32 devices in a mesh: wide: 8 (over y, x, core), narrow: 4 (over z).
Axes of the slice: x: 2, y: 2, z: 4, core: 2. Of those that a mesh axis runs over, the one named last changes fastest.
Arguments:
- tokens: bfloat16 [8192, 768], P(('wide', 'narrow')), may hold values from -6 to 6
- memory: bfloat16 [8, 512, 768], P('wide', 'narrow'), may hold values from -6 to 6
- segments: int32 [8, 1024], P('wide'), may hold values from 0 to 3, never falling along the last dimension, each value on 1 to 512 neighbouring positions
- valid_rows: int32 [8], P('wide'), may hold values from 64 to 512, as said below
- norm_gains: float32 [3, 768], replicated, may hold values from 0.5 to 1.5
- rel_table: float32 [32, 12], replicated, may hold values from -6 to 6
- self_weights: bfloat16 [4, 768, 768], P(None, None, 'narrow')
- cross_weights: bfloat16 [4, 768, 768], P(None, None, 'narrow')
- ffn_weights: bfloat16 [3, 768, 2048], P(None, None, 'narrow'), may hold values from -0.21875 to 0.21875
- cotangent: bfloat16 [8192, 768], P(('wide', 'narrow')), may hold values from -6 to 6
Outputs:
- output: bfloat16 [8192, 768], P(('wide', 'narrow'))
- tokens_grad: float32 [8192, 768], P(('wide', 'narrow'))
- memory_grad: float32 [8, 512, 768], P('wide', 'narrow')
- gains_grad: float32 [3, 768], replicated
- rel_grad: float32 [32, 12], replicated
- self_grad: float32 [4, 768, 768], P(None, 'wide', 'narrow')
- cross_grad: float32 [4, 768, 768], P(None, 'wide', 'narrow')
- ffn_grad: float32 [3, 768, 2048], P(None, 'wide', 'narrow')
- attn_row_stats: float32 [6, 768], P(None, 'wide')
- attn_col_stats: float32 [6, 768], P(None, 'narrow')
- proj_stats: float32 [2, 1536], replicated
- ffn_row_stats: float32 [3, 768], P(None, 'wide')
- ffn_col_stats: float32 [3, 2048], P(None, 'narrow')
The draws below stay inside these ranges and needn't reach their ends.
Inputs may be any that keep to these rules, and one draw needn't show every extreme that they name: `segments`: segment numbers never fall along a sequence; a segment has at most 512 tokens. memory rows below valid_rows of a sequence are real, the others padding; some sequence has 512 and some 512 // 8.
All inputs are finite; a program needn't handle non-finite values.
Results may differ from the reference program's by a relative error of at most 0.025.
The reference program's roundings to bfloat16 on the way count: a program that leaves them out, or rounds other values in their place, can miss the bound.
Values may be sent and summed in bfloat16 or wider, within the bound.
A program may use at most 128 MiB of HBM per device.

```python
import math
import jax
import jax.numpy as jnp
import numpy as np
from jax import lax

D = 768
FF = 2048
H = 12
DH = 64
BUCKETS = 32
MAX_DIST = 128
LENGTH = 1024
MEM = 512
HD = 768
SEQS = 8
TOKENS = 8192


def attention_weights(key, value_factor, out_factor):
    noise = jax.random.normal(key, (4, D, HD), jnp.float32)
    noise = jnp.clip(noise, -6.0, 6.0)
    factors = jnp.array([0.5 * D ** (-0.5), 0.5 * D ** (-0.5), value_factor * D ** (-0.5), out_factor * HD ** (-0.5)], jnp.float32)
    return (noise * factors[:, None, None]).astype(jnp.bfloat16)


def draw_self_weights(key, part):
    return attention_weights(jax.random.fold_in(key, 11), 0.8, 5.0)


def draw_cross_weights(key, part):
    return attention_weights(jax.random.fold_in(key, 23), 1.0, 6.0)


def draw_valid_rows(key, part):
    lengths = jax.random.randint(jax.random.fold_in(key, 37), (SEQS,), MEM // 8, MEM + 1)
    return lengths.at[0].set(MEM).at[1].set(MEM // 8).astype(jnp.int32)


def block_scale(own_key, shape, pieces, low, top_value):
    level, own = 1.0, jax.random.fold_in(own_key, 6)
    for position, parts in pieces:
        heights = jnp.exp(jax.random.uniform(jax.random.fold_in(own, position), (parts,), jnp.float32, low / len(pieces), top_value / len(pieces)))
        level = level * jnp.repeat(heights, shape[position] // parts).reshape([-1 if axis == position else 1 for axis in range(len(shape))])
    return level


def length_profile(count, total, limit, lean):
    loads = [(1 << 20) // math.isqrt(standing ** lean) + 1 for standing in range(2, count + 1)]
    rest, given = total - limit - (count - 1), [1] * (count - 1)
    while rest > 0:
        free = [i for i in range(count - 1) if given[i] < limit]
        mass, left = sum([loads[i] for i in free]), rest
        for i in free:
            more = min(limit - given[i], max(1, left * loads[i] // mass), rest)
            given[i] = given[i] + more
            rest = rest - more
    return np.array([limit] + given)


def uneven(stream_key, count, total, bound, lean):
    if count == 2:
        one = jax.random.randint(stream_key, (), max(1, total - bound), min(bound, total - 1) + 1)
        return jnp.stack([one, total - one])
    sizes = jnp.asarray(length_profile(count, total, bound, lean), jnp.int32)
    pairs = (count - 1) // 2
    giver, taker = sizes[1:1 + 2 * pairs:2], sizes[2:2 + 2 * pairs:2]
    room = jnp.minimum(giver - 1, bound - taker)
    passed = jax.random.randint(jax.random.fold_in(stream_key, 1), (pairs,), 0, 1 << 20) % (room + 1)
    sizes = sizes.at[1:1 + 2 * pairs:2].set(giver - passed).at[2:2 + 2 * pairs:2].set(taker + passed)
    return sizes[jax.random.permutation(jax.random.fold_in(stream_key, 2), count)]


def bell_draw(stream_key, dims, deviation, bound, shards=(), dtype=jnp.bfloat16):
    factor_of = block_scale(stream_key, dims, shards, -0.22, 0.18) if shards else 1.0
    values = jax.random.normal(stream_key, dims, jnp.float32) * deviation * factor_of
    return jnp.minimum(jnp.maximum(values, -bound), bound).astype(dtype)


def setup_inputs(seed: int = 0) -> dict:
    splits = jax.random.split(jax.random.key(seed), 11)
    tokens = bell_draw(splits[0], (TOKENS, D), 1.0, 6.0, ((0, 32),))
    memory = bell_draw(splits[1], (SEQS, MEM, D), 1.0, 6.0, ((0, 8), (1, 4)))
    segments = jax.vmap(lambda own: jnp.searchsorted(jnp.cumsum(uneven(own, 4, LENGTH, LENGTH // 2, 1)), jnp.arange(LENGTH), side="right"))(jax.random.split(splits[2], SEQS)).reshape((SEQS, LENGTH)).astype(jnp.int32)
    valid_rows = draw_valid_rows(jax.random.fold_in(splits[10], 71), 0)
    norm_gains = jnp.clip(1.0 + 0.1 * jax.random.normal(splits[4], (3, D), jnp.float32), 0.5, 1.5)
    rel_table = bell_draw(splits[5], (BUCKETS, H), 1.0, 6.0, (), jnp.float32)
    self_weights = draw_self_weights(jax.random.fold_in(splits[10], 71), 0)
    cross_weights = draw_cross_weights(jax.random.fold_in(splits[10], 71), 0)
    ffn_weights = bell_draw(splits[8], (3, D, FF), D ** -0.5, 0.21875, ((2, 4),))
    cotangent = bell_draw(splits[9], (TOKENS, D), 1.0, 6.0, ((0, 32),))
    return {"tokens": tokens, "memory": memory, "segments": segments, "valid_rows": valid_rows, "norm_gains": norm_gains, "rel_table": rel_table, "self_weights": self_weights, "cross_weights": cross_weights, "ffn_weights": ffn_weights, "cotangent": cotangent}


@jax.custom_vjp
def low(v):
    return lax.optimization_barrier(v.astype(jnp.bfloat16)).astype(jnp.float32)

@jax.custom_vjp
def low_back(v):
    return v

def low_keep(v):
    return (low(v), None)

def low_pass(kept, grad):
    return (grad,)

def back_keep(v):
    return (v, None)

def back_low(kept, grad):
    return (low(grad),)
low.defvjp(low_keep, low_pass)
low_back.defvjp(back_keep, back_low)
eps_norm = 1e-06
masked_score = -1000000000.0
highest = lax.Precision.HIGHEST

def bucket_table(seq_length, bucket_count, max_distance):
    exact_count = bucket_count // 2
    bucket_ids = np.zeros((seq_length,), np.int32)
    for distance in range(seq_length):
        if distance < exact_count:
            bucket_ids[distance] = distance
        else:
            scaled_log = math.log(distance / exact_count) / math.log(max_distance / exact_count) * (bucket_count - exact_count)
            bucket_ids[distance] = min(bucket_count - 1, exact_count + int(scaled_log))
    return bucket_ids

def both_ways(values):
    return low_back(low(values))

def rms_scaled(values, gain_row):
    return values * lax.rsqrt(lax.optimization_barrier(jnp.mean(values * values, axis=-1, keepdims=True)) + eps_norm) * gain_row

def project(left_side, right_side):
    return jnp.dot(left_side, right_side, precision=highest)

def project_back(left_side, right_side):
    return jnp.dot(left_side, right_side.T, precision=highest)

def attend(queries, key_rows, values_in, bias_terms, allowed):
    query_count = queries.shape[0]
    key_count = key_rows.shape[0]
    query_heads = queries.reshape(query_count, H, DH)
    key_heads = key_rows.reshape(key_count, H, DH)
    value_heads = values_in.reshape(key_count, H, DH)
    scores = jnp.einsum('qhd,khd->hqk', query_heads, key_heads, precision=highest) + bias_terms
    scores = low_back(scores)
    scores = jnp.where(allowed[None], scores, masked_score)
    probabilities = low(jax.nn.softmax(scores, axis=-1))
    mixed_heads = jnp.einsum('hqk,khd->qhd', probabilities, value_heads, precision=highest)
    return mixed_heads.reshape(query_count, H * DH)

def forward(segments, valid_rows, token_values, memory_values, gain_values, rel_values, self_values, cross_values, ffn_values):
    bucket_ids = jnp.asarray(bucket_table(LENGTH, BUCKETS, MAX_DIST))
    bucket_onehot = (bucket_ids[:, None] == jnp.arange(BUCKETS)[None, :]).astype(jnp.float32)
    bias_by_distance = project(bucket_onehot, rel_values)
    hidden_one = low(rms_scaled(token_values, gain_values[0]))
    q_self = both_ways(project(hidden_one, self_values[0])).reshape(SEQS, LENGTH, HD)
    k_self = both_ways(project(hidden_one, self_values[1])).reshape(SEQS, LENGTH, HD)
    v_self = both_ways(project(hidden_one, self_values[2])).reshape(SEQS, LENGTH, HD)

    def self_sequence(bias_table, seq_item):
        q_seq, k_seq, v_seq, segment_row = seq_item
        positions = jnp.arange(LENGTH)
        distance = jnp.maximum(positions[:, None] - positions[None, :], 0)
        causal = positions[None, :] <= positions[:, None]
        bias_terms = jnp.take(bias_table, distance, axis=0).transpose(2, 0, 1)
        allowed = causal & (segment_row[:, None] == segment_row[None, :])
        return attend(q_seq, k_seq, v_seq, bias_terms, allowed)
    self_step = jax.checkpoint(self_sequence)

    def self_apply(seq_item):
        return self_step(bias_by_distance, seq_item)
    self_mixed = lax.map(self_apply, (q_self, k_self, v_self, segments))
    out_self = both_ways(self_mixed.reshape(TOKENS, HD))
    state_one = token_values + low_back(project_back(out_self, self_values[3]))
    hidden_two = low(rms_scaled(state_one, gain_values[1]))
    q_cross = both_ways(project(hidden_two, cross_values[0])).reshape(SEQS, LENGTH, HD)
    memory_flat = memory_values.reshape(SEQS * MEM, D)
    k_cross = both_ways(project(memory_flat, cross_values[1])).reshape(SEQS, MEM, HD)
    v_cross = both_ways(project(memory_flat, cross_values[2])).reshape(SEQS, MEM, HD)

    def cross_sequence(seq_item):
        q_seq, k_seq, v_seq, valid_count = seq_item
        allowed = jnp.broadcast_to(jnp.arange(MEM)[None, :] < valid_count, (LENGTH, MEM))
        return attend(q_seq, k_seq, v_seq, 0.0, allowed)
    cross_mixed = lax.map(jax.checkpoint(cross_sequence), (q_cross, k_cross, v_cross, valid_rows))
    out_cross = both_ways(cross_mixed.reshape(TOKENS, HD))
    state_two = state_one + low_back(project_back(out_cross, cross_values[3]))
    hidden_three = low(rms_scaled(state_two, gain_values[2]))
    gate_values = low_back(project(hidden_three, ffn_values[0]))
    up_values = low_back(project(hidden_three, ffn_values[1]))
    activated = low(jax.nn.gelu(gate_values, approximate=True) * up_values)
    return state_two + low_back(project_back(activated, ffn_values[2]))

def reference(tokens, memory, segments, valid_rows, norm_gains, rel_table, self_weights, cross_weights, ffn_weights, cotangent):

    def wrapped(token_values, memory_values, gain_values, rel_values, self_values, cross_values, ffn_values):
        return forward(segments, valid_rows, token_values, memory_values, gain_values, rel_values, self_values, cross_values, ffn_values)
    output, pullback = jax.vjp(wrapped, tokens.astype(jnp.float32), memory.astype(jnp.float32), norm_gains, rel_table, self_weights.astype(jnp.float32), cross_weights.astype(jnp.float32), ffn_weights.astype(jnp.float32))
    gradients = pullback(cotangent.astype(jnp.float32))
    tokens_grad, memory_grad, gains_grad, rel_grad, self_grad, cross_grad, ffn_grad = gradients
    inner_grad = jnp.concatenate([self_grad[:3], cross_grad[:3]], axis=0)
    squared_attn = inner_grad * inner_grad
    outer_grad = jnp.stack([self_grad[3], cross_grad[3]])
    squared_outer = outer_grad * outer_grad
    squared_ffn = ffn_grad * ffn_grad
    attn_row_stats = lax.optimization_barrier(jnp.mean(squared_attn, axis=2))
    attn_col_stats = lax.optimization_barrier(jnp.mean(squared_attn, axis=1))
    proj_stats = jnp.concatenate([lax.optimization_barrier(jnp.mean(squared_outer, axis=2)), lax.optimization_barrier(jnp.mean(squared_outer, axis=1))], axis=1)
    ffn_row_stats = lax.optimization_barrier(jnp.mean(squared_ffn, axis=2))
    ffn_col_stats = lax.optimization_barrier(jnp.mean(squared_ffn, axis=1))
    return (output.astype(jnp.bfloat16), tokens_grad, memory_grad, gains_grad, rel_grad, self_grad, cross_grad, ffn_grad, attn_row_stats, attn_col_stats, proj_stats, ffn_row_stats, ffn_col_stats)
```

```python
import functools
import math

import jax
import jax.numpy as jnp
import numpy as np
from jax import lax
from jax.experimental import pallas as pl
from jax.experimental.pallas import tpu as pltpu
from jax.sharding import PartitionSpec as P

BUCKETS = 32
MAX_DIST = 128
EPS = 1e-06
MASKED = -1000000000.0
MESH = pl.DeviceIdType.MESH
BF = jnp.bfloat16
F32 = jnp.float32
VMEM_LIMIT = 64 * 1024 * 1024 - 65536


def bucket_table(seq_length, bucket_count, max_distance):
    exact_count = bucket_count // 2
    bucket_ids = np.zeros((seq_length,), np.int32)
    for distance in range(seq_length):
        if distance < exact_count:
            bucket_ids[distance] = distance
        else:
            scaled_log = (
                math.log(distance / exact_count)
                / math.log(max_distance / exact_count)
                * (bucket_count - exact_count)
            )
            bucket_ids[distance] = min(bucket_count - 1, exact_count + int(scaled_log))
    return bucket_ids


def mm(a, b):
    return jnp.dot(a, b, preferred_element_type=F32)


def mm_nt(a, b):
    return lax.dot_general(a, b, (((1,), (1,)), ((), ())), preferred_element_type=F32)


def mm_tn(a, b):
    return lax.dot_general(a, b, (((0,), (0,)), ((), ())), preferred_element_type=F32)


def inv_rms(v):
    return lax.rsqrt(jnp.mean(v * v, axis=-1, keepdims=True) + EPS)


def norm_back(v, gain, dh):
    r = inv_rms(v)
    gain_part = jnp.sum(dh * (v * r), axis=0, keepdims=True)
    gd = gain * dh
    dv = r * gd - v * (r * r * r) * jnp.mean(gd * v, axis=-1, keepdims=True)
    return gain_part, dv


def soft_cols(scores):
    e = jnp.exp(scores - jnp.max(scores, axis=0, keepdims=True))
    return e * (1.0 / jnp.sum(e, axis=0, keepdims=True))


def self_mask_store(mask_ref, segk_ref, segq_ref, rows, span):
    for b in range(2):
        r = lax.broadcasted_iota(jnp.int32, (span, 128), 0)
        c = lax.broadcasted_iota(jnp.int32, (span, 128), 1)
        allowed = (c + 2 * rows >= r) & (
            segk_ref[b * 128 : b * 128 + span, :] == segq_ref[:, b * 128 : b * 128 + 128]
        )
        mask_ref[b] = jnp.where(allowed, 1.0, 0.0)


def self_fwd_kernel(
    z_ref, xt_ref, tok_ref, gain_ref, w_ref, bd_ref, segq_ref, segk_ref,
    x1_ref, h1_ref, q_ref, kv_ref, o_ref, bias_ref,
    mask_ref,
):
    rows = tok_ref.shape[0]
    ext = 3 * rows
    span = 2 * rows + 128
    hw = q_ref.shape[2]
    heads = hw // 64
    j = pl.program_id(0)

    @pl.when(j == 0)
    def _():
        g = gain_ref[0:1, :]
        for t in range(2):
            v = jnp.where(z_ref[0] >= 2 - t, xt_ref[t].astype(F32), 0.0)
            h1_ref[t * rows : (t + 1) * rows, :] = (v * inv_rms(v) * g).astype(BF)
        x = tok_ref[...].astype(F32)
        x1_ref[...] = x
        h1_ref[2 * rows : ext, :] = (x * inv_rms(x) * g).astype(BF)
        self_mask_store(mask_ref, segk_ref, segq_ref, rows, span)

    q = mm(h1_ref[2 * rows : ext, :], w_ref[:, 0:hw]).astype(BF)
    kv = mm(h1_ref[...], w_ref[:, 2 * hw : 4 * hw]).astype(BF)
    q_ref[0] = q
    kv_ref[0] = kv
    parts = []
    for hh in range(heads):
        line = jnp.broadcast_to(bd_ref[0, hh : hh + 1, :], (256, 512))
        bias = pltpu.roll(line, 0, 1, stride=1, stride_axis=0)[:, 0:128]
        bias_ref[0, hh] = bias
        far = bd_ref[0, hh : hh + 1, 127:128]
        cols = []
        for b in range(2):
            k = kv[b * 128 : b * 128 + span, hh * 64 : hh * 64 + 64]
            v = kv[b * 128 : b * 128 + span, hw + hh * 64 : hw + hh * 64 + 64]
            qb = q[b * 128 : b * 128 + 128, hh * 64 : hh * 64 + 64]
            s = mm_nt(k, qb)
            s = jnp.concatenate([s[: span - 256] + far, s[span - 256 :] + bias], axis=0)
            s = jnp.where(mask_ref[b] > 0.5, s, MASKED)
            p = soft_cols(s).astype(BF)
            cols.append(mm_tn(v, p))
        parts.append(jnp.concatenate(cols, axis=1))
    o = jnp.concatenate(parts, axis=0).T.astype(BF)
    o_ref[0] = o
    x1_ref[...] += mm_nt(o, w_ref[:, hw : 2 * hw])


def self_bwd_kernel(
    g1_ref, gain_ref, w_ref, h1_ref, q_ref, kv_ref, o_ref, bias_ref, bd_ref, segq_ref, segk_ref,
    grad_ref, dh_ref, dx_ref, rel_ref,
    mask_ref, da_ref, flip_ref, acc_ref,
):
    rows = g1_ref.shape[0]
    ext = 3 * rows
    span = 2 * rows + 128
    hw = q_ref.shape[2]
    heads = hw // 64
    j = pl.program_id(0)

    @pl.when(j == 0)
    def _():
        da_ref[...] = g1_ref[...].astype(BF)
        self_mask_store(mask_ref, segk_ref, segq_ref, rows, span)
        r = lax.broadcasted_iota(jnp.int32, (256, 256), 0)
        c = lax.broadcasted_iota(jnp.int32, (256, 256), 1)
        flip_ref[...] = jnp.where(r + c == 255, 1.0, 0.0).astype(BF)
        acc_ref[...] = jnp.zeros_like(acc_ref)

    da = da_ref[...]
    q = q_ref[0]
    kv = kv_ref[0]
    do = mm(da, w_ref[:, hw : 2 * hw]).astype(BF)
    dq_parts, dk_parts, dv_parts = [], [], []
    for hh in range(heads):
        far = bd_ref[0, hh : hh + 1, 127:128]
        dq_cols, dks, dvs = [], [], []
        band = jnp.zeros((256, 128), F32)
        total = jnp.zeros((1, 128), F32)
        for b in range(2):
            k = kv[b * 128 : b * 128 + span, hh * 64 : hh * 64 + 64]
            v = kv[b * 128 : b * 128 + span, hw + hh * 64 : hw + hh * 64 + 64]
            qb = q[b * 128 : b * 128 + 128, hh * 64 : hh * 64 + 64]
            dob = do[b * 128 : b * 128 + 128, hh * 64 : hh * 64 + 64]
            s = mm_nt(k, qb)
            s = jnp.concatenate([s[: span - 256] + far, s[span - 256 :] + bias_ref[0, hh]], axis=0)
            s = jnp.where(mask_ref[b] > 0.5, s, MASKED)
            p = soft_cols(s)
            dp = mm_nt(v, dob)
            ds = (p * (dp - jnp.sum(p * dp, axis=0, keepdims=True))).astype(BF)
            dvs.append(mm(p.astype(BF), dob))
            dks.append(mm(ds, qb))
            dq_cols.append(mm_tn(k, ds))
            band = band + mm(flip_ref[...], ds[span - 256 :])
            total = total + jnp.sum(ds[: span - 256].astype(F32), axis=0, keepdims=True)
        gap = jnp.zeros((128, 64), F32)
        dk_parts.append(jnp.concatenate([dks[0], gap], 0) + jnp.concatenate([gap, dks[1]], 0))
        dv_parts.append(jnp.concatenate([dvs[0], gap], 0) + jnp.concatenate([gap, dvs[1]], 0))
        dq_parts.append(jnp.concatenate(dq_cols, axis=1))
        wide_band = jnp.concatenate([band, jnp.zeros((256, 384), F32)], axis=1)
        aligned = pltpu.roll(wide_band, 0, 1, stride=1, stride_axis=0)
        line = jnp.sum(aligned, axis=0, keepdims=True)
        lane = lax.broadcasted_iota(jnp.int32, (1, 512), 1)
        far_sum = jnp.sum(total, axis=1, keepdims=True)
        rel_ref[0, hh : hh + 1, :] = jnp.where(lane == 511, far_sum, line)
    dq = jnp.concatenate(dq_parts, axis=0).T.astype(BF)
    dkv = jnp.concatenate(dk_parts + dv_parts, axis=1).astype(BF)
    zero = jnp.zeros((rows, hw), BF)
    left = jnp.concatenate([h1_ref[2 * rows : ext, :], da], axis=0)
    right = jnp.concatenate(
        [jnp.concatenate([dq, zero], axis=1), jnp.concatenate([zero, o_ref[0]], axis=1)], axis=0
    )
    grad_ref[0, :, 0 : 2 * hw] = mm_tn(left, right).astype(BF)
    grad_ref[0, :, 2 * hw : 4 * hw] = mm_tn(h1_ref[...], dkv).astype(BF)
    acc_ref[...] += mm_nt(dkv, w_ref[:, 2 * hw : 4 * hw])
    acc_ref[2 * rows : ext, :] += mm_nt(dq, w_ref[:, 0:hw])

    @pl.when(j == 3)
    def _():
        dh_ref[...] = acc_ref[2 * rows : ext, :]
        for t in range(2):
            dx_ref[t] = acc_ref[t * rows : (t + 1) * rows, :].astype(BF)


def cross_fwd_kernel(valid_ref, x1_ref, gain_ref, w_ref, mem_ref, x2_ref, h2_ref, q_ref, kv_ref, o_ref):
    rows = x1_ref.shape[0]
    mem = mem_ref.shape[0]
    hw = q_ref.shape[2]
    heads = hw // 64
    j = pl.program_id(0)

    @pl.when(j == 0)
    def _():
        x1 = x1_ref[...]
        x2_ref[...] = x1
        h2_ref[...] = (x1 * inv_rms(x1) * gain_ref[1:2, :]).astype(BF)

    q = mm(h2_ref[...], w_ref[:, 0:hw]).astype(BF)
    kv = mm(mem_ref[...], w_ref[:, 2 * hw : 4 * hw]).astype(BF)
    q_ref[0] = q
    kv_ref[0] = kv
    allowed = lax.broadcasted_iota(jnp.int32, (mem, rows), 0) < valid_ref[0]
    parts = []
    for hh in range(heads):
        k = kv[:, hh * 64 : hh * 64 + 64]
        v = kv[:, hw + hh * 64 : hw + hh * 64 + 64]
        s = jnp.where(allowed, mm_nt(k, q[:, hh * 64 : hh * 64 + 64]), MASKED)
        parts.append(mm_tn(v, soft_cols(s).astype(BF)))
    o = jnp.concatenate(parts, axis=0).T.astype(BF)
    o_ref[0] = o
    x2_ref[...] += mm_nt(o, w_ref[:, hw : 2 * hw])


def cross_bwd_kernel(
    valid_ref, g2_ref, x1_ref, gain_ref, w_ref, mem_ref, h2_ref, q_ref, kv_ref, o_ref,
    grad_ref, g1_ref, dmem_ref, gsum_ref,
    dc_ref, dh_ref, macc_ref,
):
    rows = g2_ref.shape[0]
    mem = mem_ref.shape[0]
    hw = q_ref.shape[2]
    heads = hw // 64
    j = pl.program_id(0)

    @pl.when(j == 0)
    def _():
        dc_ref[...] = g2_ref[...].astype(BF)
        dh_ref[...] = jnp.zeros_like(dh_ref)
        macc_ref[...] = jnp.zeros_like(macc_ref)

    dc = dc_ref[...]
    q = q_ref[0]
    kv = kv_ref[0]
    do = mm(dc, w_ref[:, hw : 2 * hw]).astype(BF)
    allowed = lax.broadcasted_iota(jnp.int32, (mem, rows), 0) < valid_ref[0]
    dq_parts, dk_parts, dv_parts = [], [], []
    for hh in range(heads):
        k = kv[:, hh * 64 : hh * 64 + 64]
        v = kv[:, hw + hh * 64 : hw + hh * 64 + 64]
        qh = q[:, hh * 64 : hh * 64 + 64]
        doh = do[:, hh * 64 : hh * 64 + 64]
        p = soft_cols(jnp.where(allowed, mm_nt(k, qh), MASKED))
        dp = mm_nt(v, doh)
        ds = (p * (dp - jnp.sum(p * dp, axis=0, keepdims=True))).astype(BF)
        dv_parts.append(mm(p.astype(BF), doh))
        dk_parts.append(mm(ds, qh))
        dq_parts.append(mm_tn(k, ds))
    dq = jnp.concatenate(dq_parts, axis=0).T.astype(BF)
    dkv = jnp.concatenate(dk_parts + dv_parts, axis=1).astype(BF)
    zero = jnp.zeros((rows, hw), BF)
    left = jnp.concatenate([h2_ref[...], dc], axis=0)
    right = jnp.concatenate(
        [jnp.concatenate([dq, zero], axis=1), jnp.concatenate([zero, o_ref[0]], axis=1)], axis=0
    )
    grad_ref[0, :, 0 : 2 * hw] = mm_tn(left, right).astype(BF)
    grad_ref[0, :, 2 * hw : 4 * hw] = mm_tn(mem_ref[...], dkv).astype(BF)
    dh_ref[...] += mm_nt(dq, w_ref[:, 0:hw])
    macc_ref[...] += mm_nt(dkv, w_ref[:, 2 * hw : 4 * hw])

    @pl.when(j == 3)
    def _():
        gain_part, dv = norm_back(x1_ref[...], gain_ref[1:2, :], dh_ref[...])
        gsum_ref[...] = jnp.broadcast_to(gain_part, gsum_ref.shape)
        g1_ref[...] = g2_ref[...] + dv
        dmem_ref[...] = macc_ref[...].astype(BF)


def ffn_kernel(
    x2_ref, cot_ref, gain_ref, wa_ref, wb_ref,
    out_ref, g2_ref, grad_ref, gsum_ref,
    h3_ref, acc_ref, dh_ref,
):
    fw = wa_ref.shape[1] * 2 // 3
    j = pl.program_id(0)

    @pl.when(j == 0)
    def _():
        x2 = x2_ref[...]
        acc_ref[...] = x2
        h3_ref[...] = (x2 * inv_rms(x2) * gain_ref[2:3, :]).astype(BF)
        dh_ref[...] = jnp.zeros_like(dh_ref)

    h3 = h3_ref[...]
    df = cot_ref[...]
    wg = wa_ref[:, 0:fw]
    wu = jnp.concatenate([wa_ref[:, fw:], wb_ref[:, 0 : fw // 2]], axis=1)
    wd = wb_ref[:, fw // 2 :]
    gate = mm(h3, wg)
    up = mm(h3, wu)
    c0 = math.sqrt(2.0 / math.pi)
    gate2 = gate * gate
    t = jnp.tanh(c0 * (gate + 0.044715 * gate2 * gate))
    half = 0.5 * (1.0 + t)
    gelu = gate * half
    slope = half + 0.5 * gate * (1.0 - t * t) * (c0 * (1.0 + 3.0 * 0.044715 * gate2))
    act = (gelu * up).astype(BF)
    acc_ref[...] += mm_nt(act, wd)
    da = mm(df, wd)
    dgate = (da * up * slope).astype(BF)
    dup = (da * gelu).astype(BF)
    dgu = jnp.concatenate([dgate, dup], axis=1)
    ggu = mm_tn(h3, dgu).astype(BF)
    grad_ref[0, 0] = ggu[:, 0 : fw * 3 // 2]
    grad_ref[0, 1, :, 0 : fw // 2] = ggu[:, fw * 3 // 2 :]
    grad_ref[0, 1, :, fw // 2 :] = mm_tn(df, act).astype(BF)
    dh_ref[...] += mm_nt(dgate, wg) + mm_nt(dup, wu)

    @pl.when(j == 3)
    def _():
        out_ref[...] = acc_ref[...].astype(BF)
        gain_part, dv = norm_back(x2_ref[...], gain_ref[2:3, :], dh_ref[...])
        gsum_ref[...] = jnp.broadcast_to(gain_part, gsum_ref.shape)
        g2_ref[...] = df.astype(F32) + dv


def full(shape):
    return pl.BlockSpec(shape, lambda j: (0,) * len(shape))


def slot(shape):
    return pl.BlockSpec((1,) + shape, lambda j: (j,) + (0,) * len(shape))


def weight(chunk, shape):
    return pl.BlockSpec((None, None) + shape, lambda j: (chunk, j, 0, 0))


SMEM_SPEC = pl.BlockSpec(memory_space=pltpu.SMEM)


def grid_call(kernel, name, in_specs, out, scratch, args, flops):
    shapes = [jax.ShapeDtypeStruct(s, d) for s, d, _ in out]
    nbytes = sum(math.prod(s) * jnp.dtype(d).itemsize for s, d, _ in out) + 4 * 768 * 768 * 2
    return pl.pallas_call(
        kernel,
        name=name,
        grid=(4,),
        in_specs=in_specs,
        out_specs=[spec for _, _, spec in out],
        out_shape=shapes,
        scratch_shapes=scratch,
        compiler_params=pltpu.CompilerParams(
            dimension_semantics=("arbitrary",), vmem_limit_bytes=VMEM_LIMIT
        ),
        cost_estimate=pl.CostEstimate(flops=flops, bytes_accessed=nbytes, transcendentals=0),
    )(*args)


class Place:
    def __init__(self):
        self.w = lax.axis_index("wide")
        self.z = lax.axis_index("narrow")
        s = lax.rem(self.w, 8)
        self.s = s
        self.c = lax.rem(s, 2)
        self.x = lax.rem(s // 2, 2)
        self.y = s // 4
        dc, dx, dy = 1 - 2 * self.c, 2 * (1 - 2 * self.x), 4 * (1 - 2 * self.y)
        self.core_dev = {"wide": self.w + dc}
        self.x_dev = {"wide": self.w + dx}
        self.y_dev = {"wide": self.w + dy}
        self.sx, self.sy, self.sxy = s + dx, s + dy, s + dx + dy
        self.dc = dc

    def narrow_dev(self, k):
        return {"narrow": lax.rem(self.z + k, 4)}

    def barrier(self):
        sem = pltpu.get_barrier_semaphore()
        devs = [self.core_dev, self.x_dev, self.y_dev] + [self.narrow_dev(k) for k in (1, 2, 3)]
        for dev in devs:
            pl.semaphore_signal(sem, inc=1, device_id=dev, device_id_type=MESH)
        pl.semaphore_wait(sem, len(devs))


def remote(src, dst, send_sem, recv_sem, dev):
    return pltpu.make_async_remote_copy(
        src_ref=src, dst_ref=dst, send_sem=send_sem, recv_sem=recv_sem, device_id=dev, device_id_type=MESH
    )


def gather_kernel(
    p_ref, tok_ref, mem_ref,
    w_ref, xt_ref, mt_ref,
    stage, mstage, zs, zr, ps, pr, ts, tr, ms, mr, ls, lm,
):
    at = Place()
    z, s = at.z, at.s
    chunks = p_ref.shape[0]
    at.barrier()

    def own(c):
        return p_ref.at[c, pl.ds(2 * s, 2)]

    def up0(c):
        return remote(own(c), w_ref.at[c, 3, pl.ds(2 * s, 2)], zs.at[c, 0], zr.at[c, 3], {"narrow": z + 1})

    def down0(c):
        return remote(own(c), w_ref.at[c, 1, pl.ds(2 * s, 2)], zs.at[c, 1], zr.at[c, 1], {"narrow": z - 1})

    def tok1():
        return remote(tok_ref, xt_ref.at[1], ts.at[0], tr.at[1], {"narrow": z + 1})

    def tok2():
        return remote(tok_ref, xt_ref.at[0], ts.at[1], tr.at[0], {"narrow": z + 2})

    def memk(k):
        return remote(mem_ref, mt_ref.at[z], ms.at[k - 1], mr.at[k - 1], at.narrow_dev(k))

    def start_z(c):
        @pl.when(z < 3)
        def _():
            up0(c).start()

        @pl.when(z > 0)
        def _():
            down0(c).start()

    start_z(0)

    @pl.when(z < 3)
    def _():
        tok1().start()

    @pl.when(z < 2)
    def _():
        tok2().start()

    for c in range(1, chunks):
        start_z(c)
    for k in (1, 2, 3):
        memk(k).start()

    mem_in = pltpu.make_async_copy(mem_ref, mstage, lm.at[0])
    mem_in.start()
    loads = [pltpu.make_async_copy(p_ref.at[c], stage.at[c], ls.at[c]) for c in range(chunks)]
    for copy in loads:
        copy.start()
    mem_in.wait()
    mem_out = pltpu.make_async_copy(mstage, mt_ref.at[z], lm.at[1])
    mem_out.start()
    stores = [pltpu.make_async_copy(stage.at[c], w_ref.at[c, 0], ls.at[chunks + c]) for c in range(chunks)]
    for load, store in zip(loads, stores):
        load.wait()
        store.start()

    e0 = 1 - (z + 3) // 4
    e3 = z // 3
    e1 = (1 - z // 2) * lax.rem(z, 2)
    e2 = (z // 2) * (1 - lax.rem(z, 2))
    order = [e0 * 1 + e1 * 3 + e2 * 1 + e3 * 3, e0 * 2 + e1 * 1 + e2 * 3 + e3 * 2, e0 * 3 + e1 * 2 + e2 * 2 + e3 * 1]
    onward = {1: [(3, 2, 1), (1, 2, -1), (2, 3, -1)], 2: [(1, 2, -1), (3, 2, 1), (2, 1, 1)]}

    def forward(c, r, k):
        here, there, step = onward[k][r]
        return remote(
            w_ref.at[c, here, pl.ds(2 * s, 2)], w_ref.at[c, there, pl.ds(2 * s, 2)],
            zs.at[c, 2 + r], zr.at[c, there], {"narrow": k + step},
        )

    def piece(c, r, kind):
        sl = order[r]
        i = c * 3 + r
        table = {
            0: (2 * s, 1, at.x_dev), 1: (2 * s + 1, 1, at.x_dev), 2: (2 * at.sy + 1, 1, at.x_dev),
            3: (2 * s + 1, 1, at.y_dev), 4: (2 * s, 1, at.y_dev), 5: (2 * at.sx, 1, at.y_dev),
            6: (2 * s, 2, at.core_dev), 7: (2 * at.sx, 2, at.core_dev),
            8: (2 * at.sy, 2, at.core_dev), 9: (2 * at.sxy, 2, at.core_dev),
        }
        first, n, dev = table[kind]
        region = w_ref.at[c, sl, pl.ds(first, n)]
        return remote(region, region, ps.at[i, kind], pr.at[i, kind], dev)

    def arrived(c, r, kind):
        sl = order[r]
        i = c * 3 + r
        table = {
            0: (2 * at.sx, 1), 1: (2 * at.sx + 1, 1), 2: (2 * at.sxy + 1, 1),
            3: (2 * at.sy + 1, 1), 4: (2 * at.sy, 1), 5: (2 * at.sxy, 1),
            6: (2 * (s + at.dc), 2), 7: (2 * (at.sx + at.dc), 2),
            8: (2 * (at.sy + at.dc), 2), 9: (2 * (at.sxy + at.dc), 2),
        }
        first, n = table[kind]
        region = w_ref.at[c, sl, pl.ds(first, n)]
        remote(region, region, ps.at[i, kind], pr.at[i, kind], at.x_dev).wait_recv()

    def step0(c, r):
        sl = order[r]
        region = w_ref.at[c, sl, pl.ds(2 * s, 2)]
        remote(region, region, zs.at[c, 0], zr.at[c, sl], at.x_dev).wait_recv()
        for k in (1, 2):
            @pl.when(z == k)
            def _():
                forward(c, r, k).start()
        for kind in (0, 3, 4, 1, 6):
            piece(c, r, kind).start()

    def step1(c, r):
        arrived(c, r, 0)
        piece(c, r, 5).start()
        arrived(c, r, 3)
        piece(c, r, 2).start()
        arrived(c, r, 1)
        piece(c, r, 7).start()
        arrived(c, r, 4)
        piece(c, r, 8).start()

    def step2(c, r):
        arrived(c, r, 5)
        arrived(c, r, 2)
        piece(c, r, 9).start()

    pieces = [(c, r) for c in range(chunks) for r in range(3)]
    for t in range(len(pieces) + 2):
        if t < len(pieces):
            step0(*pieces[t])
        if 0 <= t - 1 < len(pieces):
            step1(*pieces[t - 1])
        if 0 <= t - 2 < len(pieces):
            step2(*pieces[t - 2])

    for c, r in pieces:
        for kind in (6, 7, 8, 9):
            arrived(c, r, kind)
        for kind in range(10):
            piece(c, r, kind).wait_send()
        for k in (1, 2):
            @pl.when(z == k)
            def _():
                forward(c, r, k).wait_send()
    for c in range(chunks):
        stores[c].wait()

        @pl.when(z < 3)
        def _():
            up0(c).wait_send()

        @pl.when(z > 0)
        def _():
            down0(c).wait_send()

    mem_out.wait()
    for k in (1, 2, 3):
        memk(k).wait_send()
        here = mt_ref.at[lax.rem(z + 4 - k, 4)]
        remote(here, here, ms.at[k - 1], mr.at[k - 1], at.x_dev).wait_recv()

    @pl.when(z < 3)
    def _():
        tok1().wait_send()

    @pl.when(z < 2)
    def _():
        tok2().wait_send()

    @pl.when(z > 0)
    def _():
        tok1().wait_recv()

    @pl.when(z > 1)
    def _():
        tok2().wait_recv()


def gather(packed, tokens, memory):
    rows, width = tokens.shape
    chunks = packed.shape[0]
    half = packed.shape[2]
    any_spec = pl.BlockSpec(memory_space=pl.ANY)
    dma = pltpu.SemaphoreType.DMA
    return pl.pallas_call(
        gather_kernel,
        name="gather",
        in_specs=[any_spec] * 3,
        out_specs=[any_spec] * 3,
        out_shape=[
            jax.ShapeDtypeStruct((chunks, 4) + packed.shape[1:], BF),
            jax.ShapeDtypeStruct((2, rows, width), BF),
            jax.ShapeDtypeStruct((4,) + memory.shape, BF),
        ],
        scratch_shapes=[
            pltpu.VMEM((chunks, 16, half, width), BF),
            pltpu.VMEM(memory.shape, BF),
            dma((chunks, 5)), dma((chunks, 4)),
            dma((chunks * 3, 10)), dma((chunks * 3, 10)),
            dma((2,)), dma((2,)), dma((3,)), dma((3,)), dma((2 * chunks,)), dma((2,)),
        ],
        compiler_params=pltpu.CompilerParams(
            collective_id=0, has_side_effects=True, vmem_limit_bytes=VMEM_LIMIT
        ),
    )(packed, tokens, memory)


QUARTERS = (3, 0, 2, 1)


def reduce_kernel(
    gf_ref, gc_ref, gs_ref, dx_ref, dm_ref, dh_ref, tok_ref, g1_ref, gain_ref,
    f_ref, tg_ref, mg_ref, gsum_ref,
    own, rc, xr, yr, x2, y2, zu, zd, dxr, dmr,
    lsem, cs, cr, xs, xrs, ys, yrs, x2s, x2r, y2s, y2r, us, ur, ds_, dr, dxs, dxrs, dms, dmrs,
):
    at = Place()
    z = at.z
    half = own.shape[3] // 2
    at.barrier()
    groups = [
        (2, lambda j: gf_ref.at[j, 0]), (3, lambda j: gf_ref.at[j, 1]),
        (1, lambda j: gc_ref.at[j]), (0, lambda j: gs_ref.at[j]),
    ]
    chunks = [(out, get, q) for out, get in groups for q in QUARTERS]
    n = len(chunks)

    def dx_send(t):
        return remote(dx_ref.at[t], dxr.at[t], dxs.at[t], dxrs.at[t], {"narrow": z - 2 + t})

    def dm_send(k):
        return remote(dm_ref.at[lax.rem(z + k, 4)], dmr.at[k - 1], dms.at[k - 1], dmrs.at[k - 1], at.narrow_dev(k))

    def core_send(i):
        _, get, q = chunks[i]
        src = get(lax.rem(q + 4 - z, 4)).at[:, pl.ds(1 - at.c, 1)]
        return remote(src, rc.at[i], cs.at[i], cr.at[i], at.core_dev)

    def load(i):
        _, get, q = chunks[i]
        src = get(lax.rem(q + 4 - z, 4)).at[:, pl.ds(at.c, 1)]
        return pltpu.make_async_copy(src, own.at[i], lsem.at[i])

    for i in range(n):
        load(i).start()
        core_send(i).start()
    for t in range(2):
        @pl.when(z >= 2 - t)
        def _():
            dx_send(t).start()
    for k in (1, 2, 3):
        dm_send(k).start()

    lo, hi = pl.ds(0, half), pl.ds(half, half)
    yx = 2 * at.y + at.x

    def add(ref, other):
        ref[...] = (ref[...].astype(F32) + other[...].astype(F32)).astype(BF)

    def x_send(i, yb):
        return remote(own.at[i, 2 * yb + 1 - at.x, 0, lo], xr.at[i, yb], xs.at[i, yb], xrs.at[i, yb], at.x_dev)

    def y_send(i, xb):
        return remote(own.at[i, 2 * (1 - at.y) + xb, 0, hi], yr.at[i, xb], ys.at[i, xb], yrs.at[i, xb], at.y_dev)

    def y2_send(i):
        return remote(own.at[i, 2 * (1 - at.y) + at.x, 0, lo], y2.at[i], y2s.at[i], y2r.at[i], at.y_dev)

    def x2_send(i):
        return remote(own.at[i, 2 * at.y + 1 - at.x, 0, hi], x2.at[i], x2s.at[i], x2r.at[i], at.x_dev)

    def step_b(i):
        load(i).wait()
        core_send(i).wait_recv()
        add(own.at[i], rc.at[i])
        for b in range(2):
            x_send(i, b).start()
            y_send(i, b).start()

    def step_c(i):
        for b in range(2):
            x_send(i, b).wait_recv()
            y_send(i, b).wait_recv()
            add(own.at[i, 2 * b + at.x, 0, lo], xr.at[i, b])
            add(own.at[i, 2 * at.y + b, 0, hi], yr.at[i, b])
        y2_send(i).start()
        x2_send(i).start()

    def step_d(i):
        y2_send(i).wait_recv()
        add(own.at[i, yx, 0, lo], y2.at[i])
        x2_send(i).wait_recv()
        add(own.at[i, yx, 0, hi], x2.at[i])

    def up(i, k):
        return remote(own.at[i, yx, 0], zu.at[i], us.at[i], ur.at[i], {"narrow": k + 1})

    def down(i, k):
        return remote(own.at[i, yx, 0], zd.at[i], ds_.at[i], dr.at[i], {"narrow": k - 1})

    def step_e(i, h):
        out, _, q = chunks[i]
        if h < q:
            @pl.when(z == h)
            def _():
                if h > 0:
                    up(i, 0).wait_recv()
                    add(own.at[i, yx, 0], zu.at[i])
                up(i, h).start()
        k = 3 - h
        if k > q:
            @pl.when(z == k)
            def _():
                if k < 3:
                    down(i, 3).wait_recv()
                    add(own.at[i, yx, 0], zd.at[i])
                down(i, k).start()
        if h == max(q, 3 - q):
            @pl.when(z == q)
            def _():
                total = own[i, yx, 0].astype(F32)
                if q > 0:
                    up(i, 0).wait_recv()
                    total = total + zu[i].astype(F32)
                if q < 3:
                    down(i, 3).wait_recv()
                    total = total + zd[i].astype(F32)
                f_ref[out] = total

    for t in range(n + 6):
        if t < n:
            step_b(t)
        if 0 <= t - 1 < n:
            step_c(t - 1)
        if 0 <= t - 2 < n:
            step_d(t - 2)
        for h in range(4):
            if 0 <= t - 3 - h < n:
                step_e(t - 3 - h, h)
        if t == 8:
            mg_ref[...] = dm_ref[z].astype(F32)
            for k in (1, 2, 3):
                dm_send(k).wait_recv()
                mg_ref[...] += dmr[k - 1].astype(F32)
            tg_ref[...] = dh_ref[...]
            for d in range(2):
                @pl.when(z < 2 + d)
                def _():
                    dx_send(d).wait_recv()
                    tg_ref[...] += dxr[d].astype(F32)
            gain_part, dv = norm_back(tok_ref[...].astype(F32), gain_ref[0:1, :], tg_ref[...])
            gsum_ref[...] = jnp.broadcast_to(gain_part, gsum_ref.shape)
            tg_ref[...] = g1_ref[...] + dv

    for i in range(n):
        q = chunks[i][2]
        core_send(i).wait_send()
        for b in range(2):
            x_send(i, b).wait_send()
            y_send(i, b).wait_send()
        y2_send(i).wait_send()
        x2_send(i).wait_send()

        @pl.when(z < q)
        def _():
            up(i, 0).wait_send()

        @pl.when(z > q)
        def _():
            down(i, 3).wait_send()
    for t in range(2):
        @pl.when(z >= 2 - t)
        def _():
            dx_send(t).wait_send()
    for k in (1, 2, 3):
        dm_send(k).wait_send()


def reduce_grads(gf, gc, gs, dx, dm, dh, tok, g1, gains):
    own, width = gs.shape[3:]
    half = own // 2
    rows = tok.shape[0]
    n = 16
    any_spec = pl.BlockSpec(memory_space=pl.ANY)
    vmem = pl.BlockSpec(memory_space=pltpu.VMEM)
    dma = pltpu.SemaphoreType.DMA
    return pl.pallas_call(
        reduce_kernel,
        name="reduce",
        in_specs=[any_spec] * 3 + [vmem] * 6,
        out_specs=[vmem] * 4,
        out_shape=[
            jax.ShapeDtypeStruct((4, own, width), F32),
            jax.ShapeDtypeStruct((rows, width), F32),
            jax.ShapeDtypeStruct(dm.shape[1:], F32),
            jax.ShapeDtypeStruct((8, width), F32),
        ],
        scratch_shapes=[
            pltpu.VMEM((n, 4, 1, own, width), BF), pltpu.VMEM((n, 4, 1, own, width), BF),
            pltpu.VMEM((n, 2, half, width), BF), pltpu.VMEM((n, 2, half, width), BF),
            pltpu.VMEM((n, half, width), BF), pltpu.VMEM((n, half, width), BF),
            pltpu.VMEM((n, own, width), BF), pltpu.VMEM((n, own, width), BF),
            pltpu.VMEM(dx.shape, BF), pltpu.VMEM((3,) + dm.shape[1:], BF),
            dma((n,)), dma((n,)), dma((n,)),
            dma((n, 2)), dma((n, 2)), dma((n, 2)), dma((n, 2)),
            dma((n,)), dma((n,)), dma((n,)), dma((n,)),
            dma((n,)), dma((n,)), dma((n,)), dma((n,)),
            dma((2,)), dma((2,)), dma((3,)), dma((3,)),
        ],
        compiler_params=pltpu.CompilerParams(
            collective_id=1, has_side_effects=True, vmem_limit_bytes=VMEM_LIMIT
        ),
    )(gf, gc, gs, dx, dm, dh, tok, g1, gains)


def stats_kernel(
    wide_count, f_ref, a_ref,
    rsum_ref, csum_ref, asum_ref, prow_ref, pcol_ref,
    rall, aall, call, ball, rs, rr, as_, ar, cs, cr, bs, br, ps, pr,
):
    w = lax.axis_index("wide")
    z = lax.axis_index("narrow")
    own = f_ref.shape[1]
    width = f_ref.shape[2]
    sem = pltpu.get_barrier_semaphore()

    def peer(k):
        return {"narrow": lax.rem(z + k, 4)}

    def wide_peer(k):
        return {"wide": lax.rem(w + k, wide_count)}

    def wide_loop(fn):
        if wide_count <= 8:
            for k in range(1, wide_count):
                fn(k)
        else:
            pl.loop(1, wide_count)(fn)

    for k in (1, 2, 3):
        pl.semaphore_signal(sem, inc=1, device_id=peer(k), device_id_type=MESH)
    wide_loop(lambda k: pl.semaphore_signal(sem, inc=1, device_id=wide_peer(k), device_id_type=MESH))

    lane = lax.broadcasted_iota(jnp.int32, (8, width), 1)
    row = lax.broadcasted_iota(jnp.int32, (8, width), 0)
    quarter = width // 4
    third = 2 * width // 3

    def sums(pick, sq):
        got = lax.dot_general(
            jnp.where(pick, 1.0, 0.0), sq, (((1,), (1,)), ((), ())),
            preferred_element_type=F32, precision=lax.Precision.HIGHEST,
        )
        pad = jnp.zeros((8, 128 - own), F32)
        return jnp.concatenate([got, pad], axis=1)

    sq = [f_ref[i] * f_ref[i] for i in range(4)]
    rall[z, 0:8] = sums(lane // quarter == row, sq[0])
    rall[z, 8:16] = sums(lane // quarter == row, sq[1])
    rall[z, 16:24] = sums(lane // third == row, sq[2]) + sums((lane + width) // third == row, sq[3])
    aall[z] = a_ref[...]
    call[w] = jnp.concatenate(
        [jnp.sum(v, axis=0, keepdims=True) for v in sq] + [jnp.zeros((4, width), F32)], axis=0
    )
    pl.semaphore_wait(sem, 3 + wide_count - 1)

    def r_send(k):
        return remote(rall.at[z], rall.at[z], rs.at[k - 1], rr.at[k - 1], peer(k))

    def a_send(k):
        return remote(aall.at[z], aall.at[z], as_.at[k - 1], ar.at[k - 1], peer(k))

    def c_send(k):
        return remote(call.at[w], call.at[w], cs.at[k - 1], cr.at[k - 1], wide_peer(k))

    def p_send(k):
        return remote(pcol_ref.at[z], pcol_ref.at[z], ps.at[k - 1], pr.at[k - 1], peer(k))

    def b_send(k):
        return remote(ball.at[w], ball.at[w], bs.at[k - 1], br.at[k - 1], wide_peer(k))

    for k in (1, 2, 3):
        r_send(k).start()
        a_send(k).start()
    wide_loop(lambda k: c_send(k).start())

    for k in (1, 2, 3):
        frm = lax.rem(z + 4 - k, 4)
        remote(rall.at[frm], rall.at[frm], rs.at[k - 1], rr.at[k - 1], peer(k)).wait_recv()
        remote(aall.at[frm], aall.at[frm], as_.at[k - 1], ar.at[k - 1], peer(k)).wait_recv()
    rsum = rall[0] + rall[1] + rall[2] + rall[3]
    rsum_ref[...] = rsum
    asum = aall[0] + aall[1] + aall[2] + aall[3]
    zero = jnp.zeros((1, width - 128), F32)
    ball[w] = jnp.concatenate(
        [
            asum[0:4],
            jnp.concatenate([rsum[1:2], zero], axis=1),
            jnp.concatenate([rsum[9:10], zero], axis=1),
            jnp.zeros((2, width), F32),
        ],
        axis=0,
    )
    wide_loop(lambda k: b_send(k).start())

    def c_wait(k):
        frm = lax.rem(w + wide_count - k, wide_count)
        remote(call.at[frm], call.at[frm], cs.at[k - 1], cr.at[k - 1], wide_peer(k)).wait_recv()

    wide_loop(c_wait)
    csum = lax.fori_loop(1, wide_count, lambda i, v: v + call[i], call[0])
    csum_ref[...] = csum
    pcol_ref[z] = csum
    for k in (1, 2, 3):
        p_send(k).start()

    def b_wait(k):
        frm = lax.rem(w + wide_count - k, wide_count)
        remote(ball.at[frm], ball.at[frm], bs.at[k - 1], br.at[k - 1], wide_peer(k)).wait_recv()

    wide_loop(b_wait)
    asum_ref[...] = lax.fori_loop(1, wide_count, lambda i, v: v + ball[i], ball[0])
    prow_ref[...] = ball[:, :, 0:128]
    for k in (1, 2, 3):
        frm = lax.rem(z + 4 - k, 4)
        remote(pcol_ref.at[frm], pcol_ref.at[frm], ps.at[k - 1], pr.at[k - 1], peer(k)).wait_recv()
    for k in (1, 2, 3):
        r_send(k).wait_send()
        a_send(k).wait_send()
        p_send(k).wait_send()

    def sent(k):
        c_send(k).wait_send()
        b_send(k).wait_send()

    wide_loop(sent)


def reduce_stats(wide_count, final, small):
    width = final.shape[2]
    vmem = pl.BlockSpec(memory_space=pltpu.VMEM)
    dma = pltpu.SemaphoreType.DMA
    return pl.pallas_call(
        functools.partial(stats_kernel, wide_count),
        name="stats",
        in_specs=[vmem] * 2,
        out_specs=[vmem] * 5,
        out_shape=[
            jax.ShapeDtypeStruct((24, 128), F32),
            jax.ShapeDtypeStruct((8, width), F32),
            jax.ShapeDtypeStruct((8, width), F32),
            jax.ShapeDtypeStruct((wide_count, 8, 128), F32),
            jax.ShapeDtypeStruct((4, 8, width), F32),
        ],
        scratch_shapes=[
            pltpu.VMEM((4, 24, 128), F32), pltpu.VMEM((4, 8, width), F32),
            pltpu.VMEM((wide_count, 8, width), F32), pltpu.VMEM((wide_count, 8, width), F32),
            dma((3,)), dma((3,)), dma((3,)), dma((3,)),
            dma((wide_count - 1,)), dma((wide_count - 1,)), dma((wide_count - 1,)), dma((wide_count - 1,)),
            dma((3,)), dma((3,)),
        ],
        compiler_params=pltpu.CompilerParams(collective_id=2, has_side_effects=True),
    )(final, small)


def local(
    tokens, memory, segments, valid_rows, norm_gains, rel_table,
    self_weights, cross_weights, ffn_weights, cotangent,
):
    wide_count = lax.axis_size("wide")
    assert lax.axis_size("narrow") == 4 and wide_count % 8 == 0 and segments.shape[0] == 1
    z = lax.axis_index("narrow")
    rows, width = tokens.shape
    mem_own = memory.shape[1]
    mem_len = 4 * mem_own
    hw = self_weights.shape[2]
    fw = ffn_weights.shape[2]
    heads = rel_table.shape[1] // 4
    ext = 3 * rows
    span = 2 * rows + 128
    groups = wide_count // 8
    eighth = width // 8

    def qokv(w):
        return jnp.concatenate([w[0], w[3], w[1], w[2]], axis=1)

    ffn_packed = jnp.concatenate([ffn_weights[0], ffn_weights[1], ffn_weights[2]], axis=1)
    packed = jnp.stack([qokv(self_weights), qokv(cross_weights), ffn_packed[:, :width], ffn_packed[:, width:]])
    weights, earlier, mem_all = gather(packed.reshape(4, 16, width // 16, width), tokens, memory[0])
    weights = weights.reshape(4, 4, width, width)
    mem_full = mem_all.reshape(mem_len, width)

    buckets = bucket_table(1024, BUCKETS, MAX_DIST)
    lanes = np.arange(512)
    at_lane = np.where(lanes < 128, 128 + lanes, np.maximum(lanes - 384, 0))
    pick = jnp.asarray((buckets[at_lane][None, :] == np.arange(BUCKETS)[:, None]).astype(np.float32))
    bias_line = jnp.einsum("bl,bh->hl", pick, rel_table, precision=lax.Precision.HIGHEST)
    bias_line = bias_line.reshape(4, heads, 512)
    bias_line = lax.dynamic_slice_in_dim(jnp.concatenate([bias_line, bias_line], 0), z, 4, 0)
    seg = segments[0]
    seg_q = lax.dynamic_slice_in_dim(seg, z * rows, rows, 0).reshape(1, rows)
    seg_pad = jnp.concatenate([jnp.full((2 * rows,), -1, jnp.int32), seg])
    seg_k = lax.dynamic_slice_in_dim(seg_pad, z * rows, ext, 0).reshape(ext, 1)
    z_arr = z.reshape(1)

    sq = (width, width)
    vm = pltpu.VMEM
    x1, h1, q1, kv1, o1, bias = grid_call(
        self_fwd_kernel, "self_fwd",
        [SMEM_SPEC, full((2, rows, width)), full((rows, width)), full((3, width)), weight(0, sq),
         slot((heads, 512)), full((1, rows)), full((ext, 1))],
        [((rows, width), F32, full((rows, width))), ((ext, width), BF, full((ext, width))),
         ((4, rows, hw), BF, slot((rows, hw))), ((4, ext, 2 * hw), BF, slot((ext, 2 * hw))),
         ((4, rows, hw), BF, slot((rows, hw))), ((4, heads, 256, 128), F32, slot((heads, 256, 128)))],
        [vm((2, span, 128), F32)],
        (z_arr, earlier, tokens, norm_gains, weights, bias_line, seg_q, seg_k),
        4_000_000_000,
    )
    x2, h2, q2, kv2, o2 = grid_call(
        cross_fwd_kernel, "cross_fwd",
        [SMEM_SPEC, full((rows, width)), full((3, width)), weight(1, sq), full((mem_len, width))],
        [((rows, width), F32, full((rows, width))), ((rows, width), BF, full((rows, width))),
         ((4, rows, hw), BF, slot((rows, hw))), ((4, mem_len, 2 * hw), BF, slot((mem_len, 2 * hw))),
         ((4, rows, hw), BF, slot((rows, hw)))],
        [],
        (valid_rows, x1, norm_gains, weights, mem_full),
        3_000_000_000,
    )
    output, g2, grad_f, gain3 = grid_call(
        ffn_kernel, "ffn",
        [full((rows, width)), full((rows, width)), full((3, width)), weight(2, sq), weight(3, sq)],
        [((rows, width), BF, full((rows, width))), ((rows, width), F32, full((rows, width))),
         ((4, 2, width, width), BF, slot((2, width, width))), ((8, width), F32, full((8, width)))],
        [vm((rows, width), BF), vm((rows, width), F32), vm((rows, width), F32)],
        (x2, cotangent, norm_gains, weights, weights),
        8_000_000_000,
    )
    grad_c, g1, dmem, gain2 = grid_call(
        cross_bwd_kernel, "cross_bwd",
        [SMEM_SPEC, full((rows, width)), full((rows, width)), full((3, width)), weight(1, sq),
         full((mem_len, width)), full((rows, width)), slot((rows, hw)), slot((mem_len, 2 * hw)), slot((rows, hw))],
        [((4, width, width), BF, slot((width, width))), ((rows, width), F32, full((rows, width))),
         ((mem_len, width), BF, full((mem_len, width))), ((8, width), F32, full((8, width)))],
        [vm((rows, width), BF), vm((rows, width), F32), vm((mem_len, width), F32)],
        (valid_rows, g2, x1, norm_gains, weights, mem_full, h2, q2, kv2, o2),
        6_000_000_000,
    )
    grad_s, dh1, dx, rel = grid_call(
        self_bwd_kernel, "self_bwd",
        [full((rows, width)), full((3, width)), weight(0, sq), full((ext, width)),
         slot((rows, hw)), slot((ext, 2 * hw)), slot((rows, hw)), slot((heads, 256, 128)),
         slot((heads, 512)), full((1, rows)), full((ext, 1))],
        [((4, width, width), BF, slot((width, width))), ((rows, width), F32, full((rows, width))),
         ((2, rows, width), BF, full((2, rows, width))), ((4, heads, 512), F32, slot((heads, 512)))],
        [vm((2, span, 128), F32), vm((rows, width), BF), vm((256, 256), BF), vm((ext, width), F32)],
        (g1, norm_gains, weights, h1, q1, kv1, o1, bias, bias_line, seg_q, seg_k),
        8_000_000_000,
    )

    def by_owner(g):
        lead = g.shape[:-2]
        if groups > 1:
            g = g.reshape(lead + (groups, 8, eighth // groups, width))
            g = jnp.swapaxes(g, -4, -3)
        return g.reshape(lead + (4, 2, eighth, width))

    final, tokens_grad, memory_grad, gain1 = reduce_grads(
        by_owner(grad_f), by_owner(grad_c), by_owner(grad_s), dx, dmem.reshape(4, mem_own, width),
        dh1, tokens, g1, norm_gains,
    )
    if groups > 1:
        final = lax.psum_scatter(
            final, "wide", scatter_dimension=1, tiled=True,
            axis_index_groups=[[s + 8 * g for g in range(groups)] for s in range(8)],
        )
    own = final.shape[1]

    rel_pick = jnp.asarray(
        (buckets[np.maximum(lanes - 127, 0)][:, None] == np.arange(BUCKETS)[None, :]).astype(np.float32)
    )
    rel = lax.dynamic_slice_in_dim(jnp.concatenate([rel, rel], 0), 4 - z, 4, 0)
    rel = jnp.einsum("hl,lb->bh", rel.reshape(4 * heads, 512), rel_pick, precision=lax.Precision.HIGHEST)
    rel_row = jnp.pad(rel.reshape(1, -1), ((0, 0), (0, width - BUCKETS * 4 * heads)))
    small = jnp.concatenate([gain1[:1], gain2[:1], gain3[:1], rel_row, jnp.zeros((4, width), F32)], 0)
    rsum, csum, asum, prow, pcol = reduce_stats(wide_count, final, small)

    def split(g):
        return jnp.stack([g[:, 0:hw], g[:, 2 * hw : 3 * hw], g[:, 3 * hw :], g[:, hw : 2 * hw]])

    ffn_flat = jnp.concatenate([final[2], final[3]], axis=1)
    ffn_grad = jnp.stack([ffn_flat[:, 0:fw], ffn_flat[:, fw : 2 * fw], ffn_flat[:, 2 * fw :]])
    attn_row = jnp.concatenate([rsum[0:1], rsum[2:4], rsum[8:9], rsum[10:12]], 0)[:, :own] / width
    ffn_row = rsum[16:19, :own] / (4 * fw)
    attn_col = jnp.stack(
        [csum[i, a * hw : (a + 1) * hw] for i in range(2) for a in (0, 2, 3)]
    ) / width
    ffn_cols = jnp.concatenate([csum[2], csum[3]])
    ffn_col = ffn_cols.reshape(3, fw) / width
    proj_rows = prow[:, 4:6, :own].transpose(1, 0, 2).reshape(2, width) / width
    proj_cols = pcol[:, 0:2, hw : 2 * hw].transpose(1, 0, 2).reshape(2, width) / width
    return (
        output,
        tokens_grad,
        memory_grad.reshape(1, mem_own, width),
        asum[0:3],
        asum[3, : BUCKETS * 4 * heads].reshape(BUCKETS, 4 * heads),
        split(final[0]),
        split(final[1]),
        ffn_grad,
        attn_row,
        attn_col,
        jnp.concatenate([proj_rows, proj_cols], 1),
        ffn_row,
        ffn_col,
    )


def solution(mesh):
    in_specs = (
        P(("wide", "narrow"), None),
        P("wide", "narrow", None),
        P("wide", None),
        P("wide"),
        P(),
        P(),
        P(None, None, "narrow"),
        P(None, None, "narrow"),
        P(None, None, "narrow"),
        P(("wide", "narrow"), None),
    )
    out_specs = (
        P(("wide", "narrow"), None),
        P(("wide", "narrow"), None),
        P("wide", "narrow", None),
        P(),
        P(),
        P(None, "wide", "narrow"),
        P(None, "wide", "narrow"),
        P(None, "wide", "narrow"),
        P(None, "wide"),
        P(None, "narrow"),
        P(),
        P(None, "wide"),
        P(None, "narrow"),
    )
    return jax.shard_map(local, mesh=mesh, in_specs=in_specs, out_specs=out_specs, check_vma=False)
```

```python
import functools
import math

import jax
import jax.numpy as jnp
import numpy as np
from jax import lax
from jax.experimental import pallas as pl
from jax.experimental.pallas import tpu as pltpu
from jax.sharding import PartitionSpec as P

BUCKETS = 32
MAX_DIST = 128
EPS = 1e-06
MASKED = -1000000000.0
MESH = pl.DeviceIdType.MESH
BF = jnp.bfloat16
F32 = jnp.float32
VMEM_LIMIT = 64 * 1024 * 1024 - 65536


def bucket_table(seq_length, bucket_count, max_distance):
    exact_count = bucket_count // 2
    bucket_ids = np.zeros((seq_length,), np.int32)
    for distance in range(seq_length):
        if distance < exact_count:
            bucket_ids[distance] = distance
        else:
            scaled_log = (
                math.log(distance / exact_count)
                / math.log(max_distance / exact_count)
                * (bucket_count - exact_count)
            )
            bucket_ids[distance] = min(bucket_count - 1, exact_count + int(scaled_log))
    return bucket_ids


def mm(a, b):
    return jnp.dot(a, b, preferred_element_type=F32)


def mm_nt(a, b):
    return lax.dot_general(a, b, (((1,), (1,)), ((), ())), preferred_element_type=F32)


def mm_tn(a, b):
    return lax.dot_general(a, b, (((0,), (0,)), ((), ())), preferred_element_type=F32)


def inv_rms(v):
    return lax.rsqrt(jnp.mean(v * v, axis=-1, keepdims=True) + EPS)


def norm_back(v, gain, dh):
    r = inv_rms(v)
    gain_part = jnp.sum(dh * (v * r), axis=0, keepdims=True)
    gd = gain * dh
    dv = r * gd - v * (r * r * r) * jnp.mean(gd * v, axis=-1, keepdims=True)
    return gain_part, dv


def soft_cols(scores):
    e = jnp.exp(scores - jnp.max(scores, axis=0, keepdims=True))
    return e * (1.0 / jnp.sum(e, axis=0, keepdims=True))


def self_mask_store(mask_ref, segk_ref, segq_ref, rows, span):
    for b in range(2):
        r = lax.broadcasted_iota(jnp.int32, (span, 128), 0)
        c = lax.broadcasted_iota(jnp.int32, (span, 128), 1)
        allowed = (c + 2 * rows >= r) & (
            segk_ref[b * 128 : b * 128 + span, :] == segq_ref[:, b * 128 : b * 128 + 128]
        )
        mask_ref[b] = jnp.where(allowed, 1.0, 0.0)


def self_bwd_kernel(
    g1_ref, gain_ref, w_ref, h1_ref, q_ref, kv_ref, o_ref, bias_ref, bd_ref, segq_ref, segk_ref,
    grad_ref, dh_ref, dx_ref, rel_ref,
    mask_ref, da_ref, flip_ref, acc_ref,
):
    rows = g1_ref.shape[0]
    ext = 3 * rows
    span = 2 * rows + 128
    hw = q_ref.shape[2]
    heads = hw // 64
    j = pl.program_id(0)

    @pl.when(j == 0)
    def _():
        da_ref[...] = g1_ref[...].astype(BF)
        self_mask_store(mask_ref, segk_ref, segq_ref, rows, span)
        r = lax.broadcasted_iota(jnp.int32, (256, 256), 0)
        c = lax.broadcasted_iota(jnp.int32, (256, 256), 1)
        flip_ref[...] = jnp.where(r + c == 255, 1.0, 0.0).astype(BF)
        acc_ref[...] = jnp.zeros_like(acc_ref)

    da = da_ref[...]
    q = q_ref[0]
    kv = kv_ref[0]
    do = mm(da, w_ref[:, hw : 2 * hw]).astype(BF)
    dq_parts, dk_parts, dv_parts = [], [], []
    for hh in range(heads):
        far = bd_ref[0, hh : hh + 1, 127:128]
        dq_cols, dks, dvs = [], [], []
        band = jnp.zeros((256, 128), F32)
        total = jnp.zeros((1, 128), F32)
        for b in range(2):
            k = kv[b * 128 : b * 128 + span, hh * 64 : hh * 64 + 64]
            v = kv[b * 128 : b * 128 + span, hw + hh * 64 : hw + hh * 64 + 64]
            qb = q[b * 128 : b * 128 + 128, hh * 64 : hh * 64 + 64]
            dob = do[b * 128 : b * 128 + 128, hh * 64 : hh * 64 + 64]
            s = mm_nt(k, qb)
            s = jnp.concatenate([s[: span - 256] + far, s[span - 256 :] + bias_ref[0, hh]], axis=0)
            s = jnp.where(mask_ref[b] > 0.5, s, MASKED)
            p = soft_cols(s)
            dp = mm_nt(v, dob)
            ds = (p * (dp - jnp.sum(p * dp, axis=0, keepdims=True))).astype(BF)
            dvs.append(mm(p.astype(BF), dob))
            dks.append(mm(ds, qb))
            dq_cols.append(mm_tn(k, ds))
            band = band + mm(flip_ref[...], ds[span - 256 :])
            total = total + jnp.sum(ds[: span - 256].astype(F32), axis=0, keepdims=True)
        gap = jnp.zeros((128, 64), F32)
        dk_parts.append(jnp.concatenate([dks[0], gap], 0) + jnp.concatenate([gap, dks[1]], 0))
        dv_parts.append(jnp.concatenate([dvs[0], gap], 0) + jnp.concatenate([gap, dvs[1]], 0))
        dq_parts.append(jnp.concatenate(dq_cols, axis=1))
        wide_band = jnp.concatenate([band, jnp.zeros((256, 384), F32)], axis=1)
        aligned = pltpu.roll(wide_band, 0, 1, stride=1, stride_axis=0)
        line = jnp.sum(aligned, axis=0, keepdims=True)
        lane = lax.broadcasted_iota(jnp.int32, (1, 512), 1)
        far_sum = jnp.sum(total, axis=1, keepdims=True)
        rel_ref[0, hh : hh + 1, :] = jnp.where(lane == 511, far_sum, line)
    dq = jnp.concatenate(dq_parts, axis=0).T.astype(BF)
    dkv = jnp.concatenate(dk_parts + dv_parts, axis=1).astype(BF)
    zero = jnp.zeros((rows, hw), BF)
    left = jnp.concatenate([h1_ref[2 * rows : ext, :], da], axis=0)
    right = jnp.concatenate(
        [jnp.concatenate([dq, zero], axis=1), jnp.concatenate([zero, o_ref[0]], axis=1)], axis=0
    )
    grad_ref[0, :, 0 : 2 * hw] = mm_tn(left, right).astype(BF)
    grad_ref[0, :, 2 * hw : 4 * hw] = mm_tn(h1_ref[...], dkv).astype(BF)
    acc_ref[...] += mm_nt(dkv, w_ref[:, 2 * hw : 4 * hw])
    acc_ref[2 * rows : ext, :] += mm_nt(dq, w_ref[:, 0:hw])

    @pl.when(j == 3)
    def _():
        dh_ref[...] = acc_ref[2 * rows : ext, :]
        for t in range(2):
            dx_ref[t] = acc_ref[t * rows : (t + 1) * rows, :].astype(BF)


def cross_bwd_kernel(
    valid_ref, g2_ref, x1_ref, gain_ref, w_ref, mem_ref, h2_ref, q_ref, kv_ref, o_ref,
    grad_ref, g1_ref, dmem_ref, gsum_ref,
    dc_ref, dh_ref, macc_ref,
):
    rows = g2_ref.shape[0]
    mem = mem_ref.shape[0]
    hw = q_ref.shape[2]
    heads = hw // 64
    j = pl.program_id(0)

    @pl.when(j == 0)
    def _():
        dc_ref[...] = g2_ref[...].astype(BF)
        dh_ref[...] = jnp.zeros_like(dh_ref)
        macc_ref[...] = jnp.zeros_like(macc_ref)

    dc = dc_ref[...]
    q = q_ref[0]
    kv = kv_ref[0]
    do = mm(dc, w_ref[:, hw : 2 * hw]).astype(BF)
    allowed = lax.broadcasted_iota(jnp.int32, (mem, rows), 0) < valid_ref[0]
    dq_parts, dk_parts, dv_parts = [], [], []
    for hh in range(heads):
        k = kv[:, hh * 64 : hh * 64 + 64]
        v = kv[:, hw + hh * 64 : hw + hh * 64 + 64]
        qh = q[:, hh * 64 : hh * 64 + 64]
        doh = do[:, hh * 64 : hh * 64 + 64]
        p = soft_cols(jnp.where(allowed, mm_nt(k, qh), MASKED))
        dp = mm_nt(v, doh)
        ds = (p * (dp - jnp.sum(p * dp, axis=0, keepdims=True))).astype(BF)
        dv_parts.append(mm(p.astype(BF), doh))
        dk_parts.append(mm(ds, qh))
        dq_parts.append(mm_tn(k, ds))
    dq = jnp.concatenate(dq_parts, axis=0).T.astype(BF)
    dkv = jnp.concatenate(dk_parts + dv_parts, axis=1).astype(BF)
    zero = jnp.zeros((rows, hw), BF)
    left = jnp.concatenate([h2_ref[...], dc], axis=0)
    right = jnp.concatenate(
        [jnp.concatenate([dq, zero], axis=1), jnp.concatenate([zero, o_ref[0]], axis=1)], axis=0
    )
    grad_ref[0, :, 0 : 2 * hw] = mm_tn(left, right).astype(BF)
    grad_ref[0, :, 2 * hw : 4 * hw] = mm_tn(mem_ref[...], dkv).astype(BF)
    dh_ref[...] += mm_nt(dq, w_ref[:, 0:hw])
    macc_ref[...] += mm_nt(dkv, w_ref[:, 2 * hw : 4 * hw])

    @pl.when(j == 3)
    def _():
        gain_part, dv = norm_back(x1_ref[...], gain_ref[1:2, :], dh_ref[...])
        gsum_ref[...] = jnp.broadcast_to(gain_part, gsum_ref.shape)
        g1_ref[...] = g2_ref[...] + dv
        dmem_ref[...] = macc_ref[...].astype(BF)


def ffn_kernel(
    x2_ref, cot_ref, gain_ref, wa_ref, wb_ref,
    out_ref, g2_ref, grad_ref, gsum_ref,
    h3_ref, acc_ref, dh_ref,
):
    fw = wa_ref.shape[1] * 2 // 3
    j = pl.program_id(0)

    @pl.when(j == 0)
    def _():
        x2 = x2_ref[...]
        acc_ref[...] = x2
        h3_ref[...] = (x2 * inv_rms(x2) * gain_ref[2:3, :]).astype(BF)
        dh_ref[...] = jnp.zeros_like(dh_ref)

    h3 = h3_ref[...]
    df = cot_ref[...]
    wg = wa_ref[:, 0:fw]
    wu = jnp.concatenate([wa_ref[:, fw:], wb_ref[:, 0 : fw // 2]], axis=1)
    wd = wb_ref[:, fw // 2 :]
    gate = mm(h3, wg)
    up = mm(h3, wu)
    c0 = math.sqrt(2.0 / math.pi)
    gate2 = gate * gate
    t = jnp.tanh(c0 * (gate + 0.044715 * gate2 * gate))
    half = 0.5 * (1.0 + t)
    gelu = gate * half
    slope = half + 0.5 * gate * (1.0 - t * t) * (c0 * (1.0 + 3.0 * 0.044715 * gate2))
    act = (gelu * up).astype(BF)
    acc_ref[...] += mm_nt(act, wd)
    da = mm(df, wd)
    dgate = (da * up * slope).astype(BF)
    dup = (da * gelu).astype(BF)
    dgu = jnp.concatenate([dgate, dup], axis=1)
    ggu = mm_tn(h3, dgu).astype(BF)
    grad_ref[0, 0] = ggu[:, 0 : fw * 3 // 2]
    grad_ref[0, 1, :, 0 : fw // 2] = ggu[:, fw * 3 // 2 :]
    grad_ref[0, 1, :, fw // 2 :] = mm_tn(df, act).astype(BF)
    dh_ref[...] += mm_nt(dgate, wg) + mm_nt(dup, wu)

    @pl.when(j == 3)
    def _():
        out_ref[...] = acc_ref[...].astype(BF)
        gain_part, dv = norm_back(x2_ref[...], gain_ref[2:3, :], dh_ref[...])
        gsum_ref[...] = jnp.broadcast_to(gain_part, gsum_ref.shape)
        g2_ref[...] = df.astype(F32) + dv


def full(shape):
    return pl.BlockSpec(shape, lambda j: (0,) * len(shape))


def slot(shape):
    return pl.BlockSpec((1,) + shape, lambda j: (j,) + (0,) * len(shape))


def weight(chunk, shape):
    return pl.BlockSpec((None, None) + shape, lambda j: (chunk, j, 0, 0))


SMEM_SPEC = pl.BlockSpec(memory_space=pltpu.SMEM)


def grid_call(kernel, name, in_specs, out, scratch, args, flops):
    shapes = [jax.ShapeDtypeStruct(s, d) for s, d, _ in out]
    nbytes = sum(math.prod(s) * jnp.dtype(d).itemsize for s, d, _ in out) + 4 * 768 * 768 * 2
    return pl.pallas_call(
        kernel,
        name=name,
        grid=(4,),
        in_specs=in_specs,
        out_specs=[spec for _, _, spec in out],
        out_shape=shapes,
        scratch_shapes=scratch,
        compiler_params=pltpu.CompilerParams(
            dimension_semantics=("arbitrary",), vmem_limit_bytes=VMEM_LIMIT
        ),
        cost_estimate=pl.CostEstimate(flops=flops, bytes_accessed=nbytes, transcendentals=0),
    )(*args)


class Place:
    def __init__(self):
        self.w = lax.axis_index("wide")
        self.z = lax.axis_index("narrow")
        s = lax.rem(self.w, 8)
        self.s = s
        self.c = lax.rem(s, 2)
        self.x = lax.rem(s // 2, 2)
        self.y = s // 4
        dc, dx, dy = 1 - 2 * self.c, 2 * (1 - 2 * self.x), 4 * (1 - 2 * self.y)
        self.core_dev = {"wide": self.w + dc}
        self.x_dev = {"wide": self.w + dx}
        self.y_dev = {"wide": self.w + dy}
        self.sx, self.sy, self.sxy = s + dx, s + dy, s + dx + dy
        self.dc = dc

    def narrow_dev(self, k):
        return {"narrow": lax.rem(self.z + k, 4)}

    def barrier(self):
        sem = pltpu.get_barrier_semaphore()
        devs = [self.core_dev, self.x_dev, self.y_dev] + [self.narrow_dev(k) for k in (1, 2, 3)]
        for dev in devs:
            pl.semaphore_signal(sem, inc=1, device_id=dev, device_id_type=MESH)
        pl.semaphore_wait(sem, len(devs))


def remote(src, dst, send_sem, recv_sem, dev):
    return pltpu.make_async_remote_copy(
        src_ref=src, dst_ref=dst, send_sem=send_sem, recv_sem=recv_sem, device_id=dev, device_id_type=MESH
    )


RANKS = ((0, 1, 2, 3), (1, 0, 2, 3), (2, 3, 1, 0), (3, 2, 1, 0))


def forward_kernel(
    valid_ref, tok_ref, mem_ref, gain_ref, bd_ref, segq_ref, segk_ref, ws_ref, wc_ref, wf_ref,
    w_ref, x1_ref, h1_ref, q_ref, kv_ref, o_ref, bias_ref, mfull_ref, x2_ref, h2_ref, q2_ref, kv2_ref, o2_ref,
    wv, raw, xt, mt, mask_ref, zs, zr, ps, pr, ts, tr, ms, mr, ls, fs, os_,
):
    at = Place()
    z, s = at.z, at.s
    j = pl.program_id(0)
    units = 4
    rows, width = tok_ref.shape
    ext = 3 * rows
    span = 2 * rows + 128
    hw = q_ref.shape[2]
    fw = wf_ref.shape[3]
    heads = hw // 64
    part = rows // 4
    mine = pl.ds(2 * s, 2)

    def edge(k):
        return [(d, RANKS[k + d].index(k)) for d in (1, -1) if 0 <= k + d < 4]

    def own_send(u, k, d, rank):
        return remote(
            wv.at[u, 0, mine], wv.at[u, rank, mine], zs.at[u, 0 if d > 0 else 1], zr.at[u, rank], {"narrow": k + d}
        )

    def own_sends(u, act):
        for k in range(4):
            @pl.when(z == k)
            def _():
                for d, rank in edge(k):
                    act(own_send(u, k, d, rank))

    def forwards(u, r, act):
        for k in (1, 2):
            quarter = RANKS[k][r]
            d = 1 if quarter < k else -1
            there = RANKS[k + d].index(quarter)

            @pl.when(z == k)
            def _():
                act(remote(wv.at[u, r, mine], wv.at[u, there, mine], zs.at[u, 1 + r], zr.at[u, there], {"narrow": k + d}))

    def tok_copy(hop, p):
        part_rows = pl.ds(p * part, part)
        return remote(
            tok_ref.at[part_rows], xt.at[2 - hop, part_rows], ts.at[hop - 1, p], tr.at[hop - 1, p], {"narrow": z + hop}
        )

    def tok_send(hop, parts):
        @pl.when(z < 4 - hop)
        def _():
            for p in parts:
                tok_copy(hop, p).start()

    def mem_copy(k):
        return remote(mem_ref, mt.at[z], ms.at[k - 1], mr.at[k - 1], at.narrow_dev(k))

    def piece(u, r, kind):
        first, n, dev = {
            0: (2 * s, 1, at.x_dev), 1: (2 * s + 1, 1, at.x_dev), 2: (2 * at.sy + 1, 1, at.x_dev),
            3: (2 * s + 1, 1, at.y_dev), 4: (2 * s, 1, at.y_dev), 5: (2 * at.sx, 1, at.y_dev),
            6: (2 * s, 2, at.core_dev), 7: (2 * at.sx, 2, at.core_dev),
            8: (2 * at.sy, 2, at.core_dev), 9: (2 * at.sxy, 2, at.core_dev),
        }[kind]
        region = wv.at[u, r, pl.ds(first, n)]
        i = u * 3 + r - 1
        return remote(region, region, ps.at[i, kind], pr.at[i, kind], dev)

    def arrived(u, r, kind):
        first, n = {
            0: (2 * at.sx, 1), 1: (2 * at.sx + 1, 1), 2: (2 * at.sxy + 1, 1),
            3: (2 * at.sy + 1, 1), 4: (2 * at.sy, 1), 5: (2 * at.sxy, 1),
            6: (2 * (s + at.dc), 2), 7: (2 * (at.sx + at.dc), 2),
            8: (2 * (at.sy + at.dc), 2), 9: (2 * (at.sxy + at.dc), 2),
        }[kind]
        region = wv.at[u, r, pl.ds(first, n)]
        i = u * 3 + r - 1
        remote(region, region, ps.at[i, kind], pr.at[i, kind], at.x_dev).wait_recv()

    pieces = [(u, r) for u in range(units) for r in (1, 2, 3)]

    def step0(t):
        if not 0 <= t < len(pieces):
            return
        u, r = pieces[t]
        region = wv.at[u, r, mine]
        remote(region, region, zs.at[u, 0], zr.at[u, r], at.x_dev).wait_recv()
        forwards(u, r, lambda copy: copy.start())
        for kind in (0, 3, 4, 1, 6):
            piece(u, r, kind).start()
        if t == 0:
            tok_send(1, (2, 3))
        if t == 1:
            tok_send(2, (0, 1))
        if t == 2:
            tok_send(2, (2, 3))
            own_sends(2, lambda copy: copy.start())
        if t in (3, 4, 5):
            mem_copy(t - 2).start()
        if t == 5:
            own_sends(3, lambda copy: copy.start())

    def step1(t):
        if not 0 <= t < len(pieces):
            return
        u, r = pieces[t]
        arrived(u, r, 0)
        piece(u, r, 5).start()
        arrived(u, r, 3)
        piece(u, r, 2).start()
        arrived(u, r, 1)
        piece(u, r, 7).start()
        arrived(u, r, 4)
        piece(u, r, 8).start()

    def step2(t):
        if not 0 <= t < len(pieces):
            return
        u, r = pieces[t]
        arrived(u, r, 5)
        arrived(u, r, 2)
        piece(u, r, 9).start()

    def keep(u, k):
        return pltpu.make_async_copy(wv.at[u, k], w_ref.at[u, k], os_.at[u, k])

    def step3(t):
        if not 0 <= t < len(pieces):
            return
        u, r = pieces[t]
        for kind in (6, 7, 8, 9):
            arrived(u, r, kind)
        keep(u, r).start()

    def load_raw(i):
        src = (ws_ref, wc_ref)[i]
        return pltpu.make_async_copy(src, raw.at[i], ls.at[i])

    def ffn_loads():
        cut = width - fw
        return [
            pltpu.make_async_copy(wf_ref.at[0], wv.at[2, 0, :, :, 0:fw], fs.at[0]),
            pltpu.make_async_copy(wf_ref.at[1, :, :, 0:cut], wv.at[2, 0, :, :, fw:width], fs.at[1]),
            pltpu.make_async_copy(wf_ref.at[1, :, :, cut:fw], wv.at[3, 0, :, :, 0 : fw - cut], fs.at[2]),
            pltpu.make_async_copy(wf_ref.at[2], wv.at[3, 0, :, :, fw - cut : width], fs.at[3]),
        ]

    def pack(i):
        load_raw(i).wait()
        for b in range(16):
            wv[i, 0, b] = jnp.concatenate([raw[i, 0, b], raw[i, 3, b], raw[i, 1, b], raw[i, 2, b]], axis=1)

    @pl.when(j == 0)
    def _():
        load_raw(0).start()
        load_raw(1).start()
        for copy in ffn_loads():
            copy.start()
        at.barrier()
        pack(0)
        own_sends(0, lambda copy: copy.start())
        tok_send(1, (0, 1))
        pack(1)
        own_sends(1, lambda copy: copy.start())
        for copy in ffn_loads():
            copy.wait()
        for u in range(units):
            keep(u, 0).start()
        x = tok_ref[...].astype(F32)
        x1_ref[...] = x
        h1_ref[2 * rows : ext, :] = (x * inv_rms(x) * gain_ref[0:1, :]).astype(BF)
        self_mask_store(mask_ref, segk_ref, segq_ref, rows, span)
        step0(0)
        step0(1)
        step1(0)
        step0(2)
        step1(1)
        step2(0)
        step3(0)
        step0(3)
        step1(2)
        step2(1)
        for hop in (1, 2):
            @pl.when(z >= hop)
            def _():
                for p in range(4):
                    tok_copy(hop, p).wait_recv()
        for t in range(2):
            v = jnp.where(z >= 2 - t, xt[t].astype(F32), 0.0)
            h1_ref[t * rows : (t + 1) * rows, :] = (v * inv_rms(v) * gain_ref[0:1, :]).astype(BF)

    def hook(i, first, last):
        for jj in range(first, last):
            t = 4 + jj

            @pl.when(j == jj)
            def _():
                if i == 0:
                    step3(t - 3)
                    step0(t)
                if i == 1:
                    step1(t - 1)
                if i == 2:
                    step2(t - 2)

    def flat(u, k, lo, hi):
        return wv[u, k, :, :, lo:hi].reshape(width, hi - lo)

    @pl.when(j < 4)
    def _():
        hook(0, 0, 4)
        q = mm(h1_ref[2 * rows : ext, :], flat(0, j, 0, hw)).astype(BF)
        kv = mm(h1_ref[...], flat(0, j, 2 * hw, 4 * hw)).astype(BF)
        q_ref[0] = q
        kv_ref[0] = kv
        parts = []
        for hh in range(heads):
            line = jnp.broadcast_to(bd_ref[j, hh : hh + 1, :], (256, 512))
            bias = pltpu.roll(line, 0, 1, stride=1, stride_axis=0)[:, 0:128]
            bias_ref[0, hh] = bias
            far = bd_ref[j, hh : hh + 1, 127:128]
            cols = []
            for b in range(2):
                k = kv[b * 128 : b * 128 + span, hh * 64 : hh * 64 + 64]
                v = kv[b * 128 : b * 128 + span, hw + hh * 64 : hw + hh * 64 + 64]
                qb = q[b * 128 : b * 128 + 128, hh * 64 : hh * 64 + 64]
                sc = mm_nt(k, qb)
                sc = jnp.concatenate([sc[: span - 256] + far, sc[span - 256 :] + bias], axis=0)
                sc = jnp.where(mask_ref[b] > 0.5, sc, MASKED)
                cols.append(mm_tn(v, soft_cols(sc).astype(BF)))
            parts.append(jnp.concatenate(cols, axis=1))
            if hh < 2:
                hook(1 + hh, 0, 4)
        o = jnp.concatenate(parts, axis=0).T.astype(BF)
        o_ref[0] = o
        x1_ref[...] += mm_nt(o, flat(0, j, hw, 2 * hw))

    @pl.when(j == 4)
    def _():
        x1 = x1_ref[...]
        x2_ref[...] = x1
        h2_ref[...] = (x1 * inv_rms(x1) * gain_ref[1:2, :]).astype(BF)
        mfull_ref[z] = mem_ref[...]
        for k in (1, 2, 3):
            frm = lax.rem(z + 4 - k, 4)
            remote(mt.at[frm], mt.at[frm], ms.at[k - 1], mr.at[k - 1], at.x_dev).wait_recv()
            mfull_ref[frm] = mt[frm]

    @pl.when(j >= 4)
    def _():
        hook(0, 4, 8)
        mem = mfull_ref.shape[0] * mfull_ref.shape[1]
        q = mm(h2_ref[...], flat(1, j - 4, 0, hw)).astype(BF)
        kv = mm(mfull_ref[...].reshape(mem, width), flat(1, j - 4, 2 * hw, 4 * hw)).astype(BF)
        q2_ref[0] = q
        kv2_ref[0] = kv
        allowed = lax.broadcasted_iota(jnp.int32, (mem, rows), 0) < valid_ref[0]
        parts = []
        for hh in range(heads):
            k = kv[:, hh * 64 : hh * 64 + 64]
            v = kv[:, hw + hh * 64 : hw + hh * 64 + 64]
            sc = jnp.where(allowed, mm_nt(k, q[:, hh * 64 : hh * 64 + 64]), MASKED)
            parts.append(mm_tn(v, soft_cols(sc).astype(BF)))
            if hh < 2:
                hook(1 + hh, 4, 8)
        o = jnp.concatenate(parts, axis=0).T.astype(BF)
        o2_ref[0] = o
        x2_ref[...] += mm_nt(o, flat(1, j - 4, hw, 2 * hw))

    @pl.when(j == 7)
    def _():
        for t in range(12, len(pieces) + 3):
            step0(t)
            step1(t - 1)
            step2(t - 2)
            step3(t - 3)
        for u, r in pieces:
            for kind in range(10):
                piece(u, r, kind).wait_send()
            forwards(u, r, lambda copy: copy.wait_send())
        for u in range(units):
            own_sends(u, lambda copy: copy.wait_send())
            for k in range(4):
                keep(u, k).wait()
        for hop in (1, 2):
            @pl.when(z < 4 - hop)
            def _():
                for p in range(4):
                    tok_copy(hop, p).wait_send()
        for k in (1, 2, 3):
            mem_copy(k).wait_send()


def forward(valid_rows, tokens, memory, gains, bias_line, seg_q, seg_k, ws, wc, wf):
    rows, width = tokens.shape
    mem_own = memory.shape[0]
    hw = ws.shape[3]
    heads = hw // 64
    ext = 3 * rows
    mem = 4 * mem_own
    half = width // 16
    any_spec = pl.BlockSpec(memory_space=pl.ANY)
    dma = pltpu.SemaphoreType.DMA

    def early(shape):
        return pl.BlockSpec((1,) + shape, lambda j: (jnp.minimum(j, 3),) + (0,) * len(shape))

    def late(shape):
        return pl.BlockSpec((1,) + shape, lambda j: (jnp.maximum(j - 4, 0),) + (0,) * len(shape))

    out = [
        ((4, 4, 16, half, width), BF, any_spec),
        ((rows, width), F32, full((rows, width))), ((ext, width), BF, full((ext, width))),
        ((4, rows, hw), BF, early((rows, hw))), ((4, ext, 2 * hw), BF, early((ext, 2 * hw))),
        ((4, rows, hw), BF, early((rows, hw))), ((4, heads, 256, 128), F32, early((heads, 256, 128))),
        ((4, mem_own, width), BF, full((4, mem_own, width))),
        ((rows, width), F32, full((rows, width))), ((rows, width), BF, full((rows, width))),
        ((4, rows, hw), BF, late((rows, hw))), ((4, mem, 2 * hw), BF, late((mem, 2 * hw))),
        ((4, rows, hw), BF, late((rows, hw))),
    ]
    return pl.pallas_call(
        forward_kernel,
        name="forward",
        grid=(8,),
        in_specs=[
            SMEM_SPEC, full((rows, width)), full((mem_own, width)), full((3, width)), full((4, heads, 512)),
            full((1, rows)), full((ext, 1)), any_spec, any_spec, any_spec,
        ],
        out_specs=[spec for _, _, spec in out],
        out_shape=[jax.ShapeDtypeStruct(shape, dtype) for shape, dtype, _ in out],
        scratch_shapes=[
            pltpu.VMEM((4, 4, 16, half, width), BF), pltpu.VMEM((2,) + ws.shape, BF),
            pltpu.VMEM((2, rows, width), BF), pltpu.VMEM((4, mem_own, width), BF),
            pltpu.VMEM((2, 2 * rows + 128, 128), F32),
            dma((4, 5)), dma((4, 4)), dma((12, 10)), dma((12, 10)),
            dma((2, 4)), dma((2, 4)), dma((3,)), dma((3,)), dma((2,)), dma((4,)), dma((4, 4)),
        ],
        compiler_params=pltpu.CompilerParams(
            collective_id=0, has_side_effects=True, vmem_limit_bytes=VMEM_LIMIT, dimension_semantics=("arbitrary",)
        ),
    )(valid_rows, tokens, memory, gains, bias_line, seg_q, seg_k, ws, wc, wf)


QUARTERS = (3, 0, 2, 1)


def reduce_kernel(
    gf_ref, gc_ref, gs_ref, dx_ref, dm_ref, dh_ref, tok_ref, g1_ref, gain_ref,
    f_ref, tg_ref, mg_ref, gsum_ref,
    own, rc, xr, yr, x2, y2, zu, zd, dxr, dmr,
    lsem, cs, cr, xs, xrs, ys, yrs, x2s, x2r, y2s, y2r, us, ur, ds_, dr, dxs, dxrs, dms, dmrs,
):
    at = Place()
    z = at.z
    half = own.shape[3] // 2
    at.barrier()
    groups = [
        (2, lambda j: gf_ref.at[j, 0]), (3, lambda j: gf_ref.at[j, 1]),
        (1, lambda j: gc_ref.at[j]), (0, lambda j: gs_ref.at[j]),
    ]
    chunks = [(out, get, q) for out, get in groups for q in QUARTERS]
    n = len(chunks)

    def dx_send(t):
        return remote(dx_ref.at[t], dxr.at[t], dxs.at[t], dxrs.at[t], {"narrow": z - 2 + t})

    def dm_send(k):
        return remote(dm_ref.at[lax.rem(z + k, 4)], dmr.at[k - 1], dms.at[k - 1], dmrs.at[k - 1], at.narrow_dev(k))

    e0 = 1 - (z + 3) // 4
    e3 = z // 3
    e1 = (1 - z // 2) * lax.rem(z, 2)
    e2 = (z // 2) * (1 - lax.rem(z, 2))

    def rank(q):
        return sum(e * row.index(q) for e, row in zip((e0, e1, e2, e3), RANKS))

    def core_send(i):
        _, get, q = chunks[i]
        src = get(rank(q)).at[:, pl.ds(1 - at.c, 1)]
        return remote(src, rc.at[i], cs.at[i], cr.at[i], at.core_dev)

    def load(i):
        _, get, q = chunks[i]
        src = get(rank(q)).at[:, pl.ds(at.c, 1)]
        return pltpu.make_async_copy(src, own.at[i], lsem.at[i])

    for i in range(n):
        load(i).start()
        core_send(i).start()
    for t in range(2):
        @pl.when(z >= 2 - t)
        def _():
            dx_send(t).start()
    for k in (1, 2, 3):
        dm_send(k).start()

    lo, hi = pl.ds(0, half), pl.ds(half, half)
    yx = 2 * at.y + at.x

    def add(ref, other):
        ref[...] = (ref[...].astype(F32) + other[...].astype(F32)).astype(BF)

    def x_send(i, yb):
        return remote(own.at[i, 2 * yb + 1 - at.x, 0, lo], xr.at[i, yb], xs.at[i, yb], xrs.at[i, yb], at.x_dev)

    def y_send(i, xb):
        return remote(own.at[i, 2 * (1 - at.y) + xb, 0, hi], yr.at[i, xb], ys.at[i, xb], yrs.at[i, xb], at.y_dev)

    def y2_send(i):
        return remote(own.at[i, 2 * (1 - at.y) + at.x, 0, lo], y2.at[i], y2s.at[i], y2r.at[i], at.y_dev)

    def x2_send(i):
        return remote(own.at[i, 2 * at.y + 1 - at.x, 0, hi], x2.at[i], x2s.at[i], x2r.at[i], at.x_dev)

    def step_b(i):
        load(i).wait()
        core_send(i).wait_recv()
        add(own.at[i], rc.at[i])
        for b in range(2):
            x_send(i, b).start()
            y_send(i, b).start()

    def step_c(i):
        for b in range(2):
            x_send(i, b).wait_recv()
            y_send(i, b).wait_recv()
            add(own.at[i, 2 * b + at.x, 0, lo], xr.at[i, b])
            add(own.at[i, 2 * at.y + b, 0, hi], yr.at[i, b])
        y2_send(i).start()
        x2_send(i).start()

    def step_d(i):
        y2_send(i).wait_recv()
        add(own.at[i, yx, 0, lo], y2.at[i])
        x2_send(i).wait_recv()
        add(own.at[i, yx, 0, hi], x2.at[i])

    def up(i, k):
        return remote(own.at[i, yx, 0], zu.at[i], us.at[i], ur.at[i], {"narrow": k + 1})

    def down(i, k):
        return remote(own.at[i, yx, 0], zd.at[i], ds_.at[i], dr.at[i], {"narrow": k - 1})

    def step_e(i, h):
        out, _, q = chunks[i]
        if h < q:
            @pl.when(z == h)
            def _():
                if h > 0:
                    up(i, 0).wait_recv()
                    add(own.at[i, yx, 0], zu.at[i])
                up(i, h).start()
        k = 3 - h
        if k > q:
            @pl.when(z == k)
            def _():
                if k < 3:
                    down(i, 3).wait_recv()
                    add(own.at[i, yx, 0], zd.at[i])
                down(i, k).start()
        if h == max(q, 3 - q):
            @pl.when(z == q)
            def _():
                total = own[i, yx, 0].astype(F32)
                if q > 0:
                    up(i, 0).wait_recv()
                    total = total + zu[i].astype(F32)
                if q < 3:
                    down(i, 3).wait_recv()
                    total = total + zd[i].astype(F32)
                f_ref[out] = total

    for t in range(n + 6):
        if t < n:
            step_b(t)
        if 0 <= t - 1 < n:
            step_c(t - 1)
        if 0 <= t - 2 < n:
            step_d(t - 2)
        for h in range(4):
            if 0 <= t - 3 - h < n:
                step_e(t - 3 - h, h)
        if t == 8:
            mg_ref[...] = dm_ref[z].astype(F32)
            for k in (1, 2, 3):
                dm_send(k).wait_recv()
                mg_ref[...] += dmr[k - 1].astype(F32)
            tg_ref[...] = dh_ref[...]
            for d in range(2):
                @pl.when(z < 2 + d)
                def _():
                    dx_send(d).wait_recv()
                    tg_ref[...] += dxr[d].astype(F32)
            gain_part, dv = norm_back(tok_ref[...].astype(F32), gain_ref[0:1, :], tg_ref[...])
            gsum_ref[...] = jnp.broadcast_to(gain_part, gsum_ref.shape)
            tg_ref[...] = g1_ref[...] + dv

    for i in range(n):
        q = chunks[i][2]
        core_send(i).wait_send()
        for b in range(2):
            x_send(i, b).wait_send()
            y_send(i, b).wait_send()
        y2_send(i).wait_send()
        x2_send(i).wait_send()

        @pl.when(z < q)
        def _():
            up(i, 0).wait_send()

        @pl.when(z > q)
        def _():
            down(i, 3).wait_send()
    for t in range(2):
        @pl.when(z >= 2 - t)
        def _():
            dx_send(t).wait_send()
    for k in (1, 2, 3):
        dm_send(k).wait_send()


def reduce_grads(gf, gc, gs, dx, dm, dh, tok, g1, gains):
    own, width = gs.shape[3:]
    half = own // 2
    rows = tok.shape[0]
    n = 16
    any_spec = pl.BlockSpec(memory_space=pl.ANY)
    vmem = pl.BlockSpec(memory_space=pltpu.VMEM)
    dma = pltpu.SemaphoreType.DMA
    return pl.pallas_call(
        reduce_kernel,
        name="reduce",
        in_specs=[any_spec] * 3 + [vmem] * 6,
        out_specs=[vmem] * 4,
        out_shape=[
            jax.ShapeDtypeStruct((4, own, width), F32),
            jax.ShapeDtypeStruct((rows, width), F32),
            jax.ShapeDtypeStruct(dm.shape[1:], F32),
            jax.ShapeDtypeStruct((8, width), F32),
        ],
        scratch_shapes=[
            pltpu.VMEM((n, 4, 1, own, width), BF), pltpu.VMEM((n, 4, 1, own, width), BF),
            pltpu.VMEM((n, 2, half, width), BF), pltpu.VMEM((n, 2, half, width), BF),
            pltpu.VMEM((n, half, width), BF), pltpu.VMEM((n, half, width), BF),
            pltpu.VMEM((n, own, width), BF), pltpu.VMEM((n, own, width), BF),
            pltpu.VMEM(dx.shape, BF), pltpu.VMEM((3,) + dm.shape[1:], BF),
            dma((n,)), dma((n,)), dma((n,)),
            dma((n, 2)), dma((n, 2)), dma((n, 2)), dma((n, 2)),
            dma((n,)), dma((n,)), dma((n,)), dma((n,)),
            dma((n,)), dma((n,)), dma((n,)), dma((n,)),
            dma((2,)), dma((2,)), dma((3,)), dma((3,)),
        ],
        compiler_params=pltpu.CompilerParams(
            collective_id=1, has_side_effects=True, vmem_limit_bytes=VMEM_LIMIT
        ),
    )(gf, gc, gs, dx, dm, dh, tok, g1, gains)


def stats_kernel(
    wide_count, f_ref, a_ref,
    rsum_ref, csum_ref, asum_ref, prow_ref, pcol_ref,
    rall, aall, call, ball, rs, rr, as_, ar, cs, cr, bs, br, ps, pr,
):
    w = lax.axis_index("wide")
    z = lax.axis_index("narrow")
    own = f_ref.shape[1]
    width = f_ref.shape[2]
    sem = pltpu.get_barrier_semaphore()

    def peer(k):
        return {"narrow": lax.rem(z + k, 4)}

    def wide_peer(k):
        return {"wide": lax.rem(w + k, wide_count)}

    def wide_loop(fn):
        if wide_count <= 8:
            for k in range(1, wide_count):
                fn(k)
        else:
            pl.loop(1, wide_count)(fn)

    for k in (1, 2, 3):
        pl.semaphore_signal(sem, inc=1, device_id=peer(k), device_id_type=MESH)
    wide_loop(lambda k: pl.semaphore_signal(sem, inc=1, device_id=wide_peer(k), device_id_type=MESH))

    lane = lax.broadcasted_iota(jnp.int32, (8, width), 1)
    row = lax.broadcasted_iota(jnp.int32, (8, width), 0)
    quarter = width // 4
    third = 2 * width // 3

    def sums(pick, sq):
        got = lax.dot_general(
            jnp.where(pick, 1.0, 0.0), sq, (((1,), (1,)), ((), ())),
            preferred_element_type=F32, precision=lax.Precision.HIGHEST,
        )
        pad = jnp.zeros((8, 128 - own), F32)
        return jnp.concatenate([got, pad], axis=1)

    sq = [f_ref[i] * f_ref[i] for i in range(4)]
    rall[z, 0:8] = sums(lane // quarter == row, sq[0])
    rall[z, 8:16] = sums(lane // quarter == row, sq[1])
    rall[z, 16:24] = sums(lane // third == row, sq[2]) + sums((lane + width) // third == row, sq[3])
    aall[z] = a_ref[...]
    call[w] = jnp.concatenate(
        [jnp.sum(v, axis=0, keepdims=True) for v in sq] + [jnp.zeros((4, width), F32)], axis=0
    )
    pl.semaphore_wait(sem, 3 + wide_count - 1)

    def r_send(k):
        return remote(rall.at[z], rall.at[z], rs.at[k - 1], rr.at[k - 1], peer(k))

    def a_send(k):
        return remote(aall.at[z], aall.at[z], as_.at[k - 1], ar.at[k - 1], peer(k))

    def c_send(k):
        return remote(call.at[w], call.at[w], cs.at[k - 1], cr.at[k - 1], wide_peer(k))

    def p_send(k):
        return remote(pcol_ref.at[z], pcol_ref.at[z], ps.at[k - 1], pr.at[k - 1], peer(k))

    def b_send(k):
        return remote(ball.at[w], ball.at[w], bs.at[k - 1], br.at[k - 1], wide_peer(k))

    for k in (1, 2, 3):
        r_send(k).start()
        a_send(k).start()
    wide_loop(lambda k: c_send(k).start())

    for k in (1, 2, 3):
        frm = lax.rem(z + 4 - k, 4)
        remote(rall.at[frm], rall.at[frm], rs.at[k - 1], rr.at[k - 1], peer(k)).wait_recv()
        remote(aall.at[frm], aall.at[frm], as_.at[k - 1], ar.at[k - 1], peer(k)).wait_recv()
    rsum = rall[0] + rall[1] + rall[2] + rall[3]
    rsum_ref[...] = rsum
    asum = aall[0] + aall[1] + aall[2] + aall[3]
    zero = jnp.zeros((1, width - 128), F32)
    ball[w] = jnp.concatenate(
        [
            asum[0:4],
            jnp.concatenate([rsum[1:2], zero], axis=1),
            jnp.concatenate([rsum[9:10], zero], axis=1),
            jnp.zeros((2, width), F32),
        ],
        axis=0,
    )
    wide_loop(lambda k: b_send(k).start())

    def c_wait(k):
        frm = lax.rem(w + wide_count - k, wide_count)
        remote(call.at[frm], call.at[frm], cs.at[k - 1], cr.at[k - 1], wide_peer(k)).wait_recv()

    wide_loop(c_wait)
    csum = lax.fori_loop(1, wide_count, lambda i, v: v + call[i], call[0])
    csum_ref[...] = csum
    pcol_ref[z] = csum
    for k in (1, 2, 3):
        p_send(k).start()

    def b_wait(k):
        frm = lax.rem(w + wide_count - k, wide_count)
        remote(ball.at[frm], ball.at[frm], bs.at[k - 1], br.at[k - 1], wide_peer(k)).wait_recv()

    wide_loop(b_wait)
    asum_ref[...] = lax.fori_loop(1, wide_count, lambda i, v: v + ball[i], ball[0])
    prow_ref[...] = ball[:, :, 0:128]
    for k in (1, 2, 3):
        frm = lax.rem(z + 4 - k, 4)
        remote(pcol_ref.at[frm], pcol_ref.at[frm], ps.at[k - 1], pr.at[k - 1], peer(k)).wait_recv()
    for k in (1, 2, 3):
        r_send(k).wait_send()
        a_send(k).wait_send()
        p_send(k).wait_send()

    def sent(k):
        c_send(k).wait_send()
        b_send(k).wait_send()

    wide_loop(sent)


def reduce_stats(wide_count, final, small):
    width = final.shape[2]
    vmem = pl.BlockSpec(memory_space=pltpu.VMEM)
    dma = pltpu.SemaphoreType.DMA
    return pl.pallas_call(
        functools.partial(stats_kernel, wide_count),
        name="stats",
        in_specs=[vmem] * 2,
        out_specs=[vmem] * 5,
        out_shape=[
            jax.ShapeDtypeStruct((24, 128), F32),
            jax.ShapeDtypeStruct((8, width), F32),
            jax.ShapeDtypeStruct((8, width), F32),
            jax.ShapeDtypeStruct((wide_count, 8, 128), F32),
            jax.ShapeDtypeStruct((4, 8, width), F32),
        ],
        scratch_shapes=[
            pltpu.VMEM((4, 24, 128), F32), pltpu.VMEM((4, 8, width), F32),
            pltpu.VMEM((wide_count, 8, width), F32), pltpu.VMEM((wide_count, 8, width), F32),
            dma((3,)), dma((3,)), dma((3,)), dma((3,)),
            dma((wide_count - 1,)), dma((wide_count - 1,)), dma((wide_count - 1,)), dma((wide_count - 1,)),
            dma((3,)), dma((3,)),
        ],
        compiler_params=pltpu.CompilerParams(collective_id=2, has_side_effects=True),
    )(final, small)


def local(
    tokens, memory, segments, valid_rows, norm_gains, rel_table,
    self_weights, cross_weights, ffn_weights, cotangent,
):
    wide_count = lax.axis_size("wide")
    assert lax.axis_size("narrow") == 4 and wide_count % 8 == 0 and segments.shape[0] == 1
    z = lax.axis_index("narrow")
    rows, width = tokens.shape
    mem_own = memory.shape[1]
    mem_len = 4 * mem_own
    hw = self_weights.shape[2]
    fw = ffn_weights.shape[2]
    heads = rel_table.shape[1] // 4
    ext = 3 * rows
    span = 2 * rows + 128
    groups = wide_count // 8
    eighth = width // 8

    buckets = bucket_table(1024, BUCKETS, MAX_DIST)
    lanes = np.arange(512)
    at_lane = np.where(lanes < 128, 128 + lanes, np.maximum(lanes - 384, 0))
    pick = jnp.asarray((buckets[at_lane][None, :] == np.arange(BUCKETS)[:, None]).astype(np.float32))
    bias_line = jnp.einsum("bl,bh->hl", pick, rel_table, precision=lax.Precision.HIGHEST)
    bias_line = bias_line.reshape(4, heads, 512)
    ranks = jnp.asarray(RANKS, jnp.int32)
    bias_line = jnp.take(bias_line, ranks[z], axis=0)
    seg = segments[0]
    seg_q = lax.dynamic_slice_in_dim(seg, z * rows, rows, 0).reshape(1, rows)
    seg_pad = jnp.concatenate([jnp.full((2 * rows,), -1, jnp.int32), seg])
    seg_k = lax.dynamic_slice_in_dim(seg_pad, z * rows, ext, 0).reshape(ext, 1)

    sq = (width, width)
    vm = pltpu.VMEM
    half = width // 16
    weights, x1, h1, q1, kv1, o1, bias, mem_full, x2, h2, q2, kv2, o2 = forward(
        valid_rows, tokens, memory[0], norm_gains, bias_line, seg_q, seg_k,
        self_weights.reshape(4, 16, half, hw), cross_weights.reshape(4, 16, half, hw),
        ffn_weights.reshape(3, 16, half, fw),
    )
    weights = weights.reshape(4, 4, width, width)
    mem_full = mem_full.reshape(mem_len, width)
    output, g2, grad_f, gain3 = grid_call(
        ffn_kernel, "ffn",
        [full((rows, width)), full((rows, width)), full((3, width)), weight(2, sq), weight(3, sq)],
        [((rows, width), BF, full((rows, width))), ((rows, width), F32, full((rows, width))),
         ((4, 2, width, width), BF, slot((2, width, width))), ((8, width), F32, full((8, width)))],
        [vm((rows, width), BF), vm((rows, width), F32), vm((rows, width), F32)],
        (x2, cotangent, norm_gains, weights, weights),
        8_000_000_000,
    )
    grad_c, g1, dmem, gain2 = grid_call(
        cross_bwd_kernel, "cross_bwd",
        [SMEM_SPEC, full((rows, width)), full((rows, width)), full((3, width)), weight(1, sq),
         full((mem_len, width)), full((rows, width)), slot((rows, hw)), slot((mem_len, 2 * hw)), slot((rows, hw))],
        [((4, width, width), BF, slot((width, width))), ((rows, width), F32, full((rows, width))),
         ((mem_len, width), BF, full((mem_len, width))), ((8, width), F32, full((8, width)))],
        [vm((rows, width), BF), vm((rows, width), F32), vm((mem_len, width), F32)],
        (valid_rows, g2, x1, norm_gains, weights, mem_full, h2, q2, kv2, o2),
        6_000_000_000,
    )
    grad_s, dh1, dx, rel = grid_call(
        self_bwd_kernel, "self_bwd",
        [full((rows, width)), full((3, width)), weight(0, sq), full((ext, width)),
         slot((rows, hw)), slot((ext, 2 * hw)), slot((rows, hw)), slot((heads, 256, 128)),
         slot((heads, 512)), full((1, rows)), full((ext, 1))],
        [((4, width, width), BF, slot((width, width))), ((rows, width), F32, full((rows, width))),
         ((2, rows, width), BF, full((2, rows, width))), ((4, heads, 512), F32, slot((heads, 512)))],
        [vm((2, span, 128), F32), vm((rows, width), BF), vm((256, 256), BF), vm((ext, width), F32)],
        (g1, norm_gains, weights, h1, q1, kv1, o1, bias, bias_line, seg_q, seg_k),
        8_000_000_000,
    )

    def by_owner(g):
        lead = g.shape[:-2]
        if groups > 1:
            g = g.reshape(lead + (groups, 8, eighth // groups, width))
            g = jnp.swapaxes(g, -4, -3)
        return g.reshape(lead + (4, 2, eighth, width))

    final, tokens_grad, memory_grad, gain1 = reduce_grads(
        by_owner(grad_f), by_owner(grad_c), by_owner(grad_s), dx, dmem.reshape(4, mem_own, width),
        dh1, tokens, g1, norm_gains,
    )
    if groups > 1:
        final = lax.psum_scatter(
            final, "wide", scatter_dimension=1, tiled=True,
            axis_index_groups=[[s + 8 * g for g in range(groups)] for s in range(8)],
        )
    own = final.shape[1]

    rel_pick = jnp.asarray(
        (buckets[np.maximum(lanes - 127, 0)][:, None] == np.arange(BUCKETS)[None, :]).astype(np.float32)
    )
    places = jnp.asarray([[row.index(q) for q in range(4)] for row in RANKS], jnp.int32)
    rel = jnp.take(rel, places[z], axis=0)
    rel = jnp.einsum("hl,lb->bh", rel.reshape(4 * heads, 512), rel_pick, precision=lax.Precision.HIGHEST)
    rel_row = jnp.pad(rel.reshape(1, -1), ((0, 0), (0, width - BUCKETS * 4 * heads)))
    small = jnp.concatenate([gain1[:1], gain2[:1], gain3[:1], rel_row, jnp.zeros((4, width), F32)], 0)
    rsum, csum, asum, prow, pcol = reduce_stats(wide_count, final, small)

    def split(g):
        return jnp.stack([g[:, 0:hw], g[:, 2 * hw : 3 * hw], g[:, 3 * hw :], g[:, hw : 2 * hw]])

    ffn_flat = jnp.concatenate([final[2], final[3]], axis=1)
    ffn_grad = jnp.stack([ffn_flat[:, 0:fw], ffn_flat[:, fw : 2 * fw], ffn_flat[:, 2 * fw :]])
    attn_row = jnp.concatenate([rsum[0:1], rsum[2:4], rsum[8:9], rsum[10:12]], 0)[:, :own] / width
    ffn_row = rsum[16:19, :own] / (4 * fw)
    attn_col = jnp.stack(
        [csum[i, a * hw : (a + 1) * hw] for i in range(2) for a in (0, 2, 3)]
    ) / width
    ffn_cols = jnp.concatenate([csum[2], csum[3]])
    ffn_col = ffn_cols.reshape(3, fw) / width
    proj_rows = prow[:, 4:6, :own].transpose(1, 0, 2).reshape(2, width) / width
    proj_cols = pcol[:, 0:2, hw : 2 * hw].transpose(1, 0, 2).reshape(2, width) / width
    return (
        output,
        tokens_grad,
        memory_grad.reshape(1, mem_own, width),
        asum[0:3],
        asum[3, : BUCKETS * 4 * heads].reshape(BUCKETS, 4 * heads),
        split(final[0]),
        split(final[1]),
        ffn_grad,
        attn_row,
        attn_col,
        jnp.concatenate([proj_rows, proj_cols], 1),
        ffn_row,
        ffn_col,
    )


def solution(mesh):
    in_specs = (
        P(("wide", "narrow"), None),
        P("wide", "narrow", None),
        P("wide", None),
        P("wide"),
        P(),
        P(),
        P(None, None, "narrow"),
        P(None, None, "narrow"),
        P(None, None, "narrow"),
        P(("wide", "narrow"), None),
    )
    out_specs = (
        P(("wide", "narrow"), None),
        P(("wide", "narrow"), None),
        P("wide", "narrow", None),
        P(),
        P(),
        P(None, "wide", "narrow"),
        P(None, "wide", "narrow"),
        P(None, "wide", "narrow"),
        P(None, "wide"),
        P(None, "narrow"),
        P(),
        P(None, "wide"),
        P(None, "narrow"),
    )
    return jax.shard_map(local, mesh=mesh, in_specs=in_specs, out_specs=out_specs, check_vma=False)
```

```python
import functools
import math

import jax
import jax.numpy as jnp
import numpy as np
from jax import lax
from jax.experimental import pallas as pl
from jax.experimental.pallas import tpu as pltpu
from jax.sharding import PartitionSpec as P

BUCKETS = 32
MAX_DIST = 128
EPS = 1e-06
MASKED = -1000000000.0
MESH = pl.DeviceIdType.MESH
BF = jnp.bfloat16
F32 = jnp.float32
VMEM_LIMIT = 64 * 1024 * 1024 - 65536


def bucket_table(seq_length, bucket_count, max_distance):
    exact_count = bucket_count // 2
    bucket_ids = np.zeros((seq_length,), np.int32)
    for distance in range(seq_length):
        if distance < exact_count:
            bucket_ids[distance] = distance
        else:
            scaled_log = (
                math.log(distance / exact_count)
                / math.log(max_distance / exact_count)
                * (bucket_count - exact_count)
            )
            bucket_ids[distance] = min(bucket_count - 1, exact_count + int(scaled_log))
    return bucket_ids


def mm(a, b):
    return jnp.dot(a, b, preferred_element_type=F32)


def mm_nt(a, b):
    return lax.dot_general(a, b, (((1,), (1,)), ((), ())), preferred_element_type=F32)


def mm_tn(a, b):
    return lax.dot_general(a, b, (((0,), (0,)), ((), ())), preferred_element_type=F32)


def inv_rms(v):
    return lax.rsqrt(jnp.mean(v * v, axis=-1, keepdims=True) + EPS)


def norm_back(v, gain, dh):
    r = inv_rms(v)
    gain_part = jnp.sum(dh * (v * r), axis=0, keepdims=True)
    gd = gain * dh
    dv = r * gd - v * (r * r * r) * jnp.mean(gd * v, axis=-1, keepdims=True)
    return gain_part, dv


def soft_cols(scores):
    e = jnp.exp(scores - jnp.max(scores, axis=0, keepdims=True))
    return e * (1.0 / jnp.sum(e, axis=0, keepdims=True))


def self_mask_store(mask_ref, segk_ref, segq_ref, rows, span):
    for b in range(2):
        r = lax.broadcasted_iota(jnp.int32, (span, 128), 0)
        c = lax.broadcasted_iota(jnp.int32, (span, 128), 1)
        allowed = (c + 2 * rows >= r) & (
            segk_ref[b * 128 : b * 128 + span, :] == segq_ref[:, b * 128 : b * 128 + 128]
        )
        mask_ref[b] = jnp.where(allowed, 1.0, 0.0)


def full(shape):
    return pl.BlockSpec(shape, lambda j: (0,) * len(shape))


def once(shape):
    return pl.BlockSpec(shape, lambda j: (0,) * len(shape), pipeline_mode=pl.Buffered(1))


SMEM_SPEC = pl.BlockSpec(memory_space=pltpu.SMEM)


class Place:
    def __init__(self):
        self.w = lax.axis_index("wide")
        self.z = lax.axis_index("narrow")
        s = lax.rem(self.w, 8)
        self.s = s
        self.c = lax.rem(s, 2)
        self.x = lax.rem(s // 2, 2)
        self.y = s // 4
        dc, dx, dy = 1 - 2 * self.c, 2 * (1 - 2 * self.x), 4 * (1 - 2 * self.y)
        self.core_dev = {"wide": self.w + dc}
        self.x_dev = {"wide": self.w + dx}
        self.y_dev = {"wide": self.w + dy}
        self.sx, self.sy, self.sxy = s + dx, s + dy, s + dx + dy
        self.dc = dc

    def narrow_dev(self, k):
        return {"narrow": lax.rem(self.z + k, 4)}

    def devices(self):
        return [self.core_dev, self.x_dev, self.y_dev] + [self.narrow_dev(k) for k in (1, 2, 3)]

    def signal_all(self):
        for dev in self.devices():
            pl.semaphore_signal(pltpu.get_barrier_semaphore(), inc=1, device_id=dev, device_id_type=MESH)

    def wait_all(self):
        pl.semaphore_wait(pltpu.get_barrier_semaphore(), len(self.devices()))

    def barrier(self):
        self.signal_all()
        self.wait_all()


def remote(src, dst, send_sem, recv_sem, dev):
    return pltpu.make_async_remote_copy(
        src_ref=src, dst_ref=dst, send_sem=send_sem, recv_sem=recv_sem, device_id=dev, device_id_type=MESH
    )


RANKS = ((0, 1, 2, 3), (1, 0, 2, 3), (2, 3, 1, 0), (3, 2, 1, 0))


def forward_kernel(
    valid_ref, tok_ref, mem_ref, gain_ref, bd_ref, segq_ref, segk_ref, ws_ref, wc_ref, wf_ref,
    w_ref, x1_ref, h1_ref, q_ref, kv_ref, o_ref, bias_ref, mfull_ref, x2_ref, h2_ref, q2_ref, kv2_ref, o2_ref,
    wv, raw, xt, mt, mask_ref, zs, zr, ps, pr, ts, tr, ms, mr, ls, fs, os_,
):
    at = Place()
    z, s = at.z, at.s
    j = pl.program_id(0)
    units = 4
    rows, width = tok_ref.shape
    ext = 3 * rows
    span = 2 * rows + 128
    hw = q_ref.shape[2]
    fw = wf_ref.shape[3]
    heads = hw // 64
    part = rows // 4
    mine = pl.ds(2 * s, 2)

    def edge(k):
        return [(d, RANKS[k + d].index(k)) for d in (1, -1) if 0 <= k + d < 4]

    def own_send(u, k, d, rank):
        return remote(
            wv.at[u, 0, mine], wv.at[u, rank, mine], zs.at[u, 0 if d > 0 else 1], zr.at[u, rank], {"narrow": k + d}
        )

    def own_sends(u, act):
        for k in range(4):
            @pl.when(z == k)
            def _():
                for d, rank in edge(k):
                    act(own_send(u, k, d, rank))

    def forwards(u, r, act):
        for k in (1, 2):
            quarter = RANKS[k][r]
            d = 1 if quarter < k else -1
            there = RANKS[k + d].index(quarter)

            @pl.when(z == k)
            def _():
                act(remote(wv.at[u, r, mine], wv.at[u, there, mine], zs.at[u, 1 + r], zr.at[u, there], {"narrow": k + d}))

    def tok_copy(hop, p):
        part_rows = pl.ds(p * part, part)
        return remote(
            tok_ref.at[part_rows], xt.at[2 - hop, part_rows], ts.at[hop - 1, p], tr.at[hop - 1, p], {"narrow": z + hop}
        )

    def tok_send(hop, parts):
        @pl.when(z < 4 - hop)
        def _():
            for p in parts:
                tok_copy(hop, p).start()

    def mem_copy(k):
        return remote(mem_ref, mt.at[z], ms.at[k - 1], mr.at[k - 1], at.narrow_dev(k))

    def piece(u, r, kind):
        first, n, dev = {
            0: (2 * s, 1, at.x_dev), 1: (2 * s + 1, 1, at.x_dev), 2: (2 * at.sy + 1, 1, at.x_dev),
            3: (2 * s + 1, 1, at.y_dev), 4: (2 * s, 1, at.y_dev), 5: (2 * at.sx, 1, at.y_dev),
            6: (2 * s, 2, at.core_dev), 7: (2 * at.sx, 2, at.core_dev),
            8: (2 * at.sy, 2, at.core_dev), 9: (2 * at.sxy, 2, at.core_dev),
        }[kind]
        region = wv.at[u, r, pl.ds(first, n)]
        i = u * 3 + r - 1
        return remote(region, region, ps.at[i, kind], pr.at[i, kind], dev)

    def arrived(u, r, kind):
        first, n = {
            0: (2 * at.sx, 1), 1: (2 * at.sx + 1, 1), 2: (2 * at.sxy + 1, 1),
            3: (2 * at.sy + 1, 1), 4: (2 * at.sy, 1), 5: (2 * at.sxy, 1),
            6: (2 * (s + at.dc), 2), 7: (2 * (at.sx + at.dc), 2),
            8: (2 * (at.sy + at.dc), 2), 9: (2 * (at.sxy + at.dc), 2),
        }[kind]
        region = wv.at[u, r, pl.ds(first, n)]
        i = u * 3 + r - 1
        remote(region, region, ps.at[i, kind], pr.at[i, kind], at.x_dev).wait_recv()

    pieces = [(u, r) for u in range(units) for r in (1, 2, 3)]

    def step0(t):
        if not 0 <= t < len(pieces):
            return
        u, r = pieces[t]
        region = wv.at[u, r, mine]
        remote(region, region, zs.at[u, 0], zr.at[u, r], at.x_dev).wait_recv()
        forwards(u, r, lambda copy: copy.start())
        for kind in (0, 3, 4, 1, 6):
            piece(u, r, kind).start()
        if t == 0:
            tok_send(1, (2, 3))
        if t == 1:
            tok_send(2, (0, 1))
        if t == 2:
            tok_send(2, (2, 3))
            own_sends(2, lambda copy: copy.start())
        if t in (3, 4, 5):
            mem_copy(t - 2).start()
        if t == 5:
            own_sends(3, lambda copy: copy.start())

    def step1(t):
        if not 0 <= t < len(pieces):
            return
        u, r = pieces[t]
        arrived(u, r, 0)
        piece(u, r, 5).start()
        arrived(u, r, 3)
        piece(u, r, 2).start()
        arrived(u, r, 1)
        piece(u, r, 7).start()
        arrived(u, r, 4)
        piece(u, r, 8).start()

    def step2(t):
        if not 0 <= t < len(pieces):
            return
        u, r = pieces[t]
        arrived(u, r, 5)
        arrived(u, r, 2)
        piece(u, r, 9).start()

    def keep(u, k):
        return pltpu.make_async_copy(wv.at[u, k], w_ref.at[u, k], os_.at[u, k])

    def step3(t):
        if not 0 <= t < len(pieces):
            return
        u, r = pieces[t]
        for kind in (6, 7, 8, 9):
            arrived(u, r, kind)
        keep(u, r).start()

    def load_raw(i):
        src = (ws_ref, wc_ref)[i]
        return pltpu.make_async_copy(src, raw.at[i], ls.at[i])

    def ffn_loads():
        cut = width - fw
        return [
            pltpu.make_async_copy(wf_ref.at[0], wv.at[2, 0, :, :, 0:fw], fs.at[0]),
            pltpu.make_async_copy(wf_ref.at[1, :, :, 0:cut], wv.at[2, 0, :, :, fw:width], fs.at[1]),
            pltpu.make_async_copy(wf_ref.at[1, :, :, cut:fw], wv.at[3, 0, :, :, 0 : fw - cut], fs.at[2]),
            pltpu.make_async_copy(wf_ref.at[2], wv.at[3, 0, :, :, fw - cut : width], fs.at[3]),
        ]

    def pack(i):
        load_raw(i).wait()
        for b in range(16):
            wv[i, 0, b] = jnp.concatenate([raw[i, 0, b], raw[i, 3, b], raw[i, 1, b], raw[i, 2, b]], axis=1)

    @pl.when(j == 0)
    def _():
        load_raw(0).start()
        load_raw(1).start()
        for copy in ffn_loads():
            copy.start()
        at.barrier()
        pack(0)
        own_sends(0, lambda copy: copy.start())
        tok_send(1, (0, 1))
        pack(1)
        own_sends(1, lambda copy: copy.start())
        for copy in ffn_loads():
            copy.wait()
        for u in range(units):
            keep(u, 0).start()
        x = tok_ref[...].astype(F32)
        x1_ref[...] = x
        h1_ref[2 * rows : ext, :] = (x * inv_rms(x) * gain_ref[0:1, :]).astype(BF)
        self_mask_store(mask_ref, segk_ref, segq_ref, rows, span)
        step0(0)
        step0(1)
        step1(0)
        step0(2)
        step1(1)
        step2(0)
        step3(0)
        step0(3)
        step1(2)
        step2(1)
        for hop in (1, 2):
            @pl.when(z >= hop)
            def _():
                for p in range(4):
                    tok_copy(hop, p).wait_recv()
        for t in range(2):
            v = jnp.where(z >= 2 - t, xt[t].astype(F32), 0.0)
            h1_ref[t * rows : (t + 1) * rows, :] = (v * inv_rms(v) * gain_ref[0:1, :]).astype(BF)

    def hook(i, first, last):
        for jj in range(first, last):
            t = 4 + jj

            @pl.when(j == jj)
            def _():
                if i == 0:
                    step3(t - 3)
                    step0(t)
                if i == 1:
                    step1(t - 1)
                if i == 2:
                    step2(t - 2)

    def flat(u, k, lo, hi):
        return wv[u, k, :, :, lo:hi].reshape(width, hi - lo)

    @pl.when(j < 4)
    def _():
        hook(0, 0, 4)
        q = mm(h1_ref[2 * rows : ext, :], flat(0, j, 0, hw)).astype(BF)
        kv = mm(h1_ref[...], flat(0, j, 2 * hw, 4 * hw)).astype(BF)
        q_ref[0] = q
        kv_ref[0] = kv
        parts = []
        for hh in range(heads):
            line = jnp.broadcast_to(bd_ref[j, hh : hh + 1, :], (256, 512))
            bias = pltpu.roll(line, 0, 1, stride=1, stride_axis=0)[:, 0:128]
            bias_ref[0, hh] = bias
            far = bd_ref[j, hh : hh + 1, 127:128]
            cols = []
            for b in range(2):
                k = kv[b * 128 : b * 128 + span, hh * 64 : hh * 64 + 64]
                v = kv[b * 128 : b * 128 + span, hw + hh * 64 : hw + hh * 64 + 64]
                qb = q[b * 128 : b * 128 + 128, hh * 64 : hh * 64 + 64]
                sc = mm_nt(k, qb)
                sc = jnp.concatenate([sc[: span - 256] + far, sc[span - 256 :] + bias], axis=0)
                sc = jnp.where(mask_ref[b] > 0.5, sc, MASKED)
                cols.append(mm_tn(v, soft_cols(sc).astype(BF)))
            parts.append(jnp.concatenate(cols, axis=1))
            if hh < 2:
                hook(1 + hh, 0, 4)
        o = jnp.concatenate(parts, axis=0).T.astype(BF)
        o_ref[0] = o
        x1_ref[...] += mm_nt(o, flat(0, j, hw, 2 * hw))

    @pl.when(j == 4)
    def _():
        x1 = x1_ref[...]
        x2_ref[...] = x1
        h2_ref[...] = (x1 * inv_rms(x1) * gain_ref[1:2, :]).astype(BF)
        mfull_ref[z] = mem_ref[...]
        for k in (1, 2, 3):
            frm = lax.rem(z + 4 - k, 4)
            remote(mt.at[frm], mt.at[frm], ms.at[k - 1], mr.at[k - 1], at.x_dev).wait_recv()
            mfull_ref[frm] = mt[frm]

    @pl.when(j >= 4)
    def _():
        hook(0, 4, 8)
        mem = mfull_ref.shape[0] * mfull_ref.shape[1]
        q = mm(h2_ref[...], flat(1, j - 4, 0, hw)).astype(BF)
        kv = mm(mfull_ref[...].reshape(mem, width), flat(1, j - 4, 2 * hw, 4 * hw)).astype(BF)
        q2_ref[0] = q
        kv2_ref[0] = kv
        allowed = lax.broadcasted_iota(jnp.int32, (mem, rows), 0) < valid_ref[0]
        parts = []
        for hh in range(heads):
            k = kv[:, hh * 64 : hh * 64 + 64]
            v = kv[:, hw + hh * 64 : hw + hh * 64 + 64]
            sc = jnp.where(allowed, mm_nt(k, q[:, hh * 64 : hh * 64 + 64]), MASKED)
            parts.append(mm_tn(v, soft_cols(sc).astype(BF)))
            if hh < 2:
                hook(1 + hh, 4, 8)
        o = jnp.concatenate(parts, axis=0).T.astype(BF)
        o2_ref[0] = o
        x2_ref[...] += mm_nt(o, flat(1, j - 4, hw, 2 * hw))

    @pl.when(j == 7)
    def _():
        for t in range(12, len(pieces) + 3):
            step0(t)
            step1(t - 1)
            step2(t - 2)
            step3(t - 3)
        for u, r in pieces:
            for kind in range(10):
                piece(u, r, kind).wait_send()
            forwards(u, r, lambda copy: copy.wait_send())
        for u in range(units):
            own_sends(u, lambda copy: copy.wait_send())
            for k in range(4):
                keep(u, k).wait()
        for hop in (1, 2):
            @pl.when(z < 4 - hop)
            def _():
                for p in range(4):
                    tok_copy(hop, p).wait_send()
        for k in (1, 2, 3):
            mem_copy(k).wait_send()


def forward(valid_rows, tokens, memory, gains, bias_line, seg_q, seg_k, ws, wc, wf):
    rows, width = tokens.shape
    mem_own = memory.shape[0]
    hw = ws.shape[3]
    heads = hw // 64
    ext = 3 * rows
    mem = 4 * mem_own
    half = width // 16
    any_spec = pl.BlockSpec(memory_space=pl.ANY)
    dma = pltpu.SemaphoreType.DMA

    def early(shape):
        return pl.BlockSpec((1,) + shape, lambda j: (jnp.minimum(j, 3),) + (0,) * len(shape))

    def late(shape):
        return pl.BlockSpec((1,) + shape, lambda j: (jnp.maximum(j - 4, 0),) + (0,) * len(shape))

    out = [
        ((4, 4, 16, half, width), BF, any_spec),
        ((rows, width), F32, full((rows, width))), ((ext, width), BF, full((ext, width))),
        ((4, rows, hw), BF, early((rows, hw))), ((4, ext, 2 * hw), BF, early((ext, 2 * hw))),
        ((4, rows, hw), BF, early((rows, hw))), ((4, heads, 256, 128), F32, early((heads, 256, 128))),
        ((4, mem_own, width), BF, full((4, mem_own, width))),
        ((rows, width), F32, full((rows, width))), ((rows, width), BF, full((rows, width))),
        ((4, rows, hw), BF, late((rows, hw))), ((4, mem, 2 * hw), BF, late((mem, 2 * hw))),
        ((4, rows, hw), BF, late((rows, hw))),
    ]
    return pl.pallas_call(
        forward_kernel,
        name="forward",
        grid=(8,),
        in_specs=[
            SMEM_SPEC, full((rows, width)), full((mem_own, width)), full((3, width)), full((4, heads, 512)),
            full((1, rows)), full((ext, 1)), any_spec, any_spec, any_spec,
        ],
        out_specs=[spec for _, _, spec in out],
        out_shape=[jax.ShapeDtypeStruct(shape, dtype) for shape, dtype, _ in out],
        scratch_shapes=[
            pltpu.VMEM((4, 4, 16, half, width), BF), pltpu.VMEM((2,) + ws.shape, BF),
            pltpu.VMEM((2, rows, width), BF), pltpu.VMEM((4, mem_own, width), BF),
            pltpu.VMEM((2, 2 * rows + 128, 128), F32),
            dma((4, 5)), dma((4, 4)), dma((12, 10)), dma((12, 10)),
            dma((2, 4)), dma((2, 4)), dma((3,)), dma((3,)), dma((2,)), dma((4,)), dma((4, 4)),
        ],
        compiler_params=pltpu.CompilerParams(
            collective_id=0, has_side_effects=True, vmem_limit_bytes=VMEM_LIMIT, dimension_semantics=("arbitrary",)
        ),
    )(valid_rows, tokens, memory, gains, bias_line, seg_q, seg_k, ws, wc, wf)


CHUNKS = [(2 + i % 2, i // 2) for i in range(8)] + [(1, i) for i in range(4)] + [(0, i) for i in range(4)]
HELD = 12
TICKS = [(1, 0), (2, 0), (3, 0), (4, 1), (5, 1), (6, 1), (7, 1), (8, 0), (8, 2), (9, 1), (10, 0), (10, 2), (11, 1)]


def backward_kernel(
    valid_ref, x2_ref, cot_ref, x1_ref, mem_ref, h2_ref, h1_ref, tok_ref, gain_ref, bd_ref, segq_ref, segk_ref,
    w_ref, q2_ref, kv2_ref, o2_ref, q1_ref, kv1_ref, o1_ref, bias_ref,
    out_ref, f_ref, tg_ref, mg_ref, gsum_ref, rel_ref,
    g, wbuf, acc, act_in, res, do_ref, dqt_ref, dkv_ref, mask_ref, flip_ref, dxo, dmo, rc, xr, yr, xr2, yr2, zb, dxr, dmr,
    wsem, cs, cr, xs, xrs, ys, yrs, x2s, x2r, y2s, y2r, zs, zr, dxs, dxrs, dms, dmrs,
):
    at = Place()
    z = at.z
    j = pl.program_id(0)
    rows, width = x2_ref.shape
    mem = mem_ref.shape[0]
    ext = 3 * rows
    span = 2 * rows + 128
    hw = q1_ref.shape[2]
    heads = hw // 64
    fw = wbuf.shape[2] * 2 // 3
    own_rows = g.shape[3]
    half = own_rows // 2
    n = len(CHUNKS)
    lo, hi = pl.ds(0, half), pl.ds(half, half)
    yx = 2 * at.y + at.x
    top, bottom = pl.ds(0, rows), pl.ds(2 * rows, rows)

    def w_load(unit, slot, k):
        return pltpu.make_async_copy(w_ref.at[unit, slot], wbuf.at[k], wsem.at[k])

    def held(i):
        return g.at[i % HELD]

    def add(ref, other):
        ref[...] = ref[...] + other[...]

    def core_send(i):
        return remote(held(i).at[:, pl.ds(1 - at.c, 1)], rc.at[i], cs.at[i], cr.at[i], at.core_dev)

    def x_send(i, yb):
        src = held(i).at[2 * yb + 1 - at.x, at.c, lo]
        return remote(src, xr.at[i, yb], xs.at[i, yb], xrs.at[i, yb], at.x_dev)

    def y_send(i, xb):
        src = held(i).at[2 * (1 - at.y) + xb, at.c, hi]
        return remote(src, yr.at[i, xb], ys.at[i, xb], yrs.at[i, xb], at.y_dev)

    def y2_send(i):
        return remote(held(i).at[2 * (1 - at.y) + at.x, at.c, lo], yr2.at[i], y2s.at[i], y2r.at[i], at.y_dev)

    def x2_send(i):
        return remote(held(i).at[2 * at.y + 1 - at.x, at.c, hi], xr2.at[i], x2s.at[i], x2r.at[i], at.x_dev)

    d = 1 - 2 * (z // 2)
    is_end = jnp.logical_or(z == 0, z == 3)
    is_inner = jnp.logical_or(z == 1, z == 2)

    def z_send(i, dst, step):
        unit = CHUNKS[i][0]
        return remote(held(i).at[yx, at.c], zb.at[unit, dst], zs.at[i], zr.at[unit, dst], {"narrow": z + step})

    def z_wait(i, k):
        unit = CHUNKS[i][0]
        remote(zb.at[unit, k], zb.at[unit, k], zs.at[i], zr.at[unit, k], at.x_dev).wait_recv()

    def step_b(i):
        core_send(i).wait_recv()
        add(held(i).at[:, pl.ds(at.c, 1)], rc.at[i])
        for b in range(2):
            x_send(i, b).start()
            y_send(i, b).start()

    def step_c(i):
        for b in range(2):
            x_send(i, b).wait_recv()
            y_send(i, b).wait_recv()
            add(held(i).at[2 * b + at.x, at.c, lo], xr.at[i, b])
            add(held(i).at[2 * at.y + b, at.c, hi], yr.at[i, b])
        y2_send(i).start()
        x2_send(i).start()

    def step_d(i):
        y2_send(i).wait_recv()
        add(held(i).at[yx, at.c, lo], yr2.at[i])
        x2_send(i).wait_recv()
        add(held(i).at[yx, at.c, hi], xr2.at[i])

    def step_e(i):
        @pl.when(is_end)
        def _():
            if CHUNKS[i][1] < 3:
                z_send(i, CHUNKS[i][1], d).start()

    def step_f(i):
        unit, s = CHUNKS[i]

        @pl.when(is_inner)
        def _():
            if s < 2:
                z_wait(i, s)
                add(held(i).at[yx, at.c], zb.at[unit, s])
                z_send(i, 3 + s, d).start()
            if s == 2:
                z_wait(i, 3)
                add(held(i).at[yx, at.c], zb.at[unit, 3])
                z_send(i, 2, -d).start()
            if s == 3:
                z_wait(i, 2)
                z_wait(i, 4)
                f_ref[unit] = (
                    held(i)[yx, at.c].astype(F32) + zb[unit, 2].astype(F32) + zb[unit, 4].astype(F32)
                )

        if s == 3:
            @pl.when(is_end)
            def _():
                z_wait(i, 2)
                f_ref[unit] = held(i)[yx, at.c].astype(F32) + zb[unit, 2].astype(F32)

    def sent(i):
        core_send(i).wait_send()
        for b in range(2):
            x_send(i, b).wait_send()
            y_send(i, b).wait_send()
        y2_send(i).wait_send()
        x2_send(i).wait_send()
        if CHUNKS[i][1] < 3:
            z_send(i, 0, d).wait_send()

    def tick(t):
        for k, step in enumerate((step_b, step_c, step_d, step_e, step_f)):
            if 0 <= t - k < n:
                step(t - k)

    def hook(place, first, last):
        for t, (jj, p) in enumerate(TICKS):
            if p == place and first <= jj < last:
                @pl.when(j == jj)
                def _():
                    tick(t)

    def dx_send(t):
        return remote(dxo.at[t], dxr.at[t], dxs.at[t], dxrs.at[t], {"narrow": z - 2 + t})

    def dm_send(k):
        return remote(dmo.at[lax.rem(z + k, 4)], dmr.at[k - 1], dms.at[k - 1], dmrs.at[k - 1], at.narrow_dev(k))

    @pl.when(j == 0)
    def _():
        for b in range(2):
            w_load(2 + b, 3, b).start()
        at.signal_all()
        x2 = x2_ref[...]
        acc[0:rows, :] = x2
        acc[rows : 2 * rows, :] = jnp.zeros((rows, width), F32)
        act_in[...] = (x2 * inv_rms(x2) * gain_ref[2:3, :]).astype(BF)

    @pl.when(j < 4)
    def _():
        k = 2 * lax.rem(j, 2)
        for b in range(2):
            w_load(2 + b, 3 - j, k + b).wait()

        @pl.when(j < 3)
        def _():
            for b in range(2):
                w_load(2 + b, 2 - j, 2 - k + b).start()

        @pl.when(j == 3)
        def _():
            w_load(1, 3, 0).start()

        @pl.when(j == 0)
        def _():
            at.wait_all()

        hook(0, 0, 4)
        h3 = act_in[...]
        df = cot_ref[...]
        wg = wbuf[k, :, 0:fw]
        wu = jnp.concatenate([wbuf[k, :, fw:], wbuf[k + 1, :, 0 : fw // 2]], axis=1)
        wd = wbuf[k + 1, :, fw // 2 :]
        gate = mm(h3, wg)
        up = mm(h3, wu)
        c0 = math.sqrt(2.0 / math.pi)
        gate2 = gate * gate
        t = jnp.tanh(c0 * (gate + 0.044715 * gate2 * gate))
        part = 0.5 * (1.0 + t)
        gelu = gate * part
        slope = part + 0.5 * gate * (1.0 - t * t) * (c0 * (1.0 + 3.0 * 0.044715 * gate2))
        act = (gelu * up).astype(BF)
        acc[0:rows, :] += mm_nt(act, wd)
        da = mm(df, wd)
        dgate = (da * up * slope).astype(BF)
        dup = (da * gelu).astype(BF)
        dgu = jnp.concatenate([dgate, dup], axis=1)
        ggu = mm_tn(h3, dgu).astype(BF)
        blocks = (4, 2, own_rows)
        g[2 * j] = ggu[:, 0 : fw * 3 // 2].reshape(blocks + (width,))
        g[2 * j + 1, :, :, :, 0 : fw // 2] = ggu[:, fw * 3 // 2 :].reshape(blocks + (fw // 2,))
        g[2 * j + 1, :, :, :, fw // 2 :] = mm_tn(df, act).astype(BF).reshape(blocks + (fw,))
        acc[rows : 2 * rows, :] += mm_nt(dgate, wg) + mm_nt(dup, wu)
        for jj in range(4):
            @pl.when(j == jj)
            def _():
                core_send(2 * jj).start()
                core_send(2 * jj + 1).start()

    @pl.when(j == 3)
    def _():
        out_ref[...] = acc[0:rows, :].astype(BF)
        gain_part, dv = norm_back(x2_ref[...], gain_ref[2:3, :], acc[rows : 2 * rows, :])
        gsum_ref[16:24, :] = jnp.broadcast_to(gain_part, (8, width))
        g2 = cot_ref[...].astype(F32) + dv
        res[...] = g2
        act_in[...] = g2.astype(BF)
        acc[...] = jnp.zeros_like(acc)

    @pl.when(jnp.logical_and(j >= 4, j < 8))
    def _():
        k0 = j - 4
        w_load(1, 7 - j, k0).wait()

        @pl.when(j < 7)
        def _():
            w_load(1, 6 - j, k0 + 1).start()

        @pl.when(j == 7)
        def _():
            w_load(0, 3, 0).start()

        do_ref[...] = mm(act_in[...], wbuf[k0, :, hw : 2 * hw]).astype(BF)
        for hh in range(heads):
            h_cols, v_cols = slice(hh * 64, hh * 64 + 64), slice(hw + hh * 64, hw + hh * 64 + 64)
            k = kv2_ref[0, :, h_cols]
            v = kv2_ref[0, :, v_cols]
            qh = q2_ref[0, :, h_cols]
            doh = do_ref[:, h_cols]
            allowed = lax.broadcasted_iota(jnp.int32, (mem, rows), 0) < valid_ref[0]
            p = soft_cols(jnp.where(allowed, mm_nt(k, qh), MASKED))
            dp = mm_nt(v, doh)
            ds = (p * (dp - jnp.sum(p * dp, axis=0, keepdims=True))).astype(BF)
            dkv_ref[0:mem, v_cols] = mm(p.astype(BF), doh).astype(BF)
            dkv_ref[0:mem, h_cols] = mm(ds, qh).astype(BF)
            dqt_ref[h_cols, :] = mm_tn(k, ds)
            hook(hh, 4, 8)
        dc = act_in[...]
        dq = dqt_ref[...].T.astype(BF)
        dkv = dkv_ref[0:mem, :]
        zero = jnp.zeros((rows, hw), BF)
        left = jnp.concatenate([h2_ref[...], dc], axis=0)
        right = jnp.concatenate(
            [jnp.concatenate([dq, zero], axis=1), jnp.concatenate([zero, o2_ref[0]], axis=1)], axis=0
        )
        blocks = (4, 2, own_rows, 2 * hw)
        g[4 + j, :, :, :, 0 : 2 * hw] = mm_tn(left, right).astype(BF).reshape(blocks)
        g[4 + j, :, :, :, 2 * hw : 4 * hw] = mm_tn(mem_ref[...], dkv).astype(BF).reshape(blocks)
        for jj in range(4, 8):
            @pl.when(j == jj)
            def _():
                core_send(4 + jj).start()
        acc[0:rows, :] += mm_nt(dq, wbuf[k0, :, 0:hw])
        acc[rows : rows + mem, :] += mm_nt(dkv, wbuf[k0, :, 2 * hw : 4 * hw])

    @pl.when(j == 7)
    def _():
        for k in range(4):
            dmo[k] = acc[rows + k * (mem // 4) : rows + (k + 1) * (mem // 4), :].astype(BF)
        for k in (1, 2, 3):
            dm_send(k).start()
        gain_part, dv = norm_back(x1_ref[...], gain_ref[1:2, :], acc[0:rows, :])
        gsum_ref[8:16, :] = jnp.broadcast_to(gain_part, (8, width))
        g1 = res[...] + dv
        res[...] = g1
        act_in[...] = g1.astype(BF)
        acc[...] = jnp.zeros_like(acc)
        self_mask_store(mask_ref, segk_ref, segq_ref, rows, span)
        r = lax.broadcasted_iota(jnp.int32, (256, 256), 0)
        c = lax.broadcasted_iota(jnp.int32, (256, 256), 1)
        flip_ref[...] = jnp.where(r + c == 255, 1.0, 0.0).astype(BF)

    @pl.when(j >= 8)
    def _():
        k0 = j - 8
        w_load(0, 11 - j, k0).wait()

        @pl.when(j < 11)
        def _():
            w_load(0, 10 - j, k0 + 1).start()

        do_ref[...] = mm(act_in[...], wbuf[k0, :, hw : 2 * hw]).astype(BF)
        for hh in range(heads):
            h_cols, v_cols = slice(hh * 64, hh * 64 + 64), slice(hw + hh * 64, hw + hh * 64 + 64)
            far = bd_ref[11 - j, hh : hh + 1, 127:128]
            dq_cols, dks, dvs = [], [], []
            band = jnp.zeros((256, 128), F32)
            total = jnp.zeros((1, 128), F32)
            for b in range(2):
                k = kv1_ref[0, b * 128 : b * 128 + span, h_cols]
                v = kv1_ref[0, b * 128 : b * 128 + span, v_cols]
                qb = q1_ref[0, b * 128 : b * 128 + 128, h_cols]
                dob = do_ref[b * 128 : b * 128 + 128, h_cols]
                s = mm_nt(k, qb)
                s = jnp.concatenate([s[: span - 256] + far, s[span - 256 :] + bias_ref[0, hh]], axis=0)
                s = jnp.where(mask_ref[b] > 0.5, s, MASKED)
                p = soft_cols(s)
                dp = mm_nt(v, dob)
                ds = (p * (dp - jnp.sum(p * dp, axis=0, keepdims=True))).astype(BF)
                dvs.append(mm(p.astype(BF), dob))
                dks.append(mm(ds, qb))
                dq_cols.append(mm_tn(k, ds))
                band = band + mm(flip_ref[...], ds[span - 256 :])
                total = total + jnp.sum(ds[: span - 256].astype(F32), axis=0, keepdims=True)
            gap = jnp.zeros((128, 64), F32)
            dk = jnp.concatenate([dks[0], gap], 0) + jnp.concatenate([gap, dks[1]], 0)
            dv = jnp.concatenate([dvs[0], gap], 0) + jnp.concatenate([gap, dvs[1]], 0)
            dkv_ref[:, h_cols] = dk.astype(BF)
            dkv_ref[:, v_cols] = dv.astype(BF)
            dqt_ref[h_cols, :] = jnp.concatenate(dq_cols, axis=1)
            wide_band = jnp.concatenate([band, jnp.zeros((256, 384), F32)], axis=1)
            aligned = pltpu.roll(wide_band, 0, 1, stride=1, stride_axis=0)
            line = jnp.sum(aligned, axis=0, keepdims=True)
            lane = lax.broadcasted_iota(jnp.int32, (1, 512), 1)
            far_sum = jnp.sum(total, axis=1, keepdims=True)
            rel_ref[0, hh : hh + 1, :] = jnp.where(lane == 511, far_sum, line)
            hook(hh, 8, 12)
        da = act_in[...]
        dq = dqt_ref[...].T.astype(BF)
        dkv = dkv_ref[...]
        zero = jnp.zeros((rows, hw), BF)
        left = jnp.concatenate([h1_ref[2 * rows : ext, :], da], axis=0)
        right = jnp.concatenate(
            [jnp.concatenate([dq, zero], axis=1), jnp.concatenate([zero, o1_ref[0]], axis=1)], axis=0
        )
        for jj in range(8, 12):
            @pl.when(j == jj)
            def _():
                sent(jj - 8)
        blocks = (4, 2, own_rows, 2 * hw)
        g[j - 8, :, :, :, 0 : 2 * hw] = mm_tn(left, right).astype(BF).reshape(blocks)
        g[j - 8, :, :, :, 2 * hw : 4 * hw] = mm_tn(h1_ref[...], dkv).astype(BF).reshape(blocks)
        for jj in range(8, 12):
            @pl.when(j == jj)
            def _():
                core_send(4 + jj).start()
        acc[...] += mm_nt(dkv, wbuf[k0, :, 2 * hw : 4 * hw])
        acc[2 * rows : ext, :] += mm_nt(dq, wbuf[k0, :, 0:hw])

    @pl.when(j == 11)
    def _():
        for t in range(2):
            dxo[t] = acc[t * rows : (t + 1) * rows, :].astype(BF)

            @pl.when(z >= 2 - t)
            def _():
                dx_send(t).start()
        last = n + 4
        for t in range(len(TICKS), last):
            tick(t)
            if t == len(TICKS):
                mg_ref[...] = dmo[z].astype(F32)
                for k in (1, 2, 3):
                    dm_send(k).wait_recv()
                    mg_ref[...] += dmr[k - 1].astype(F32)
            if t == last - 2:
                for k in range(2):
                    @pl.when(z < 2 + k)
                    def _():
                        dx_send(k).wait_recv()
                        acc[2 * rows : ext, :] += dxr[k].astype(F32)
                gain_part, dv = norm_back(tok_ref[...].astype(F32), gain_ref[0:1, :], acc[2 * rows : ext, :])
                gsum_ref[0:8, :] = jnp.broadcast_to(gain_part, (8, width))
                tg_ref[...] = res[...] + dv
        for i in range(n - HELD, n):
            sent(i)
        for t in range(2):
            @pl.when(z >= 2 - t)
            def _():
                dx_send(t).wait_send()
        for k in (1, 2, 3):
            dm_send(k).wait_send()


def backward(
    valid_rows, x2, cot, x1, mem_full, h2, h1, tokens, gains, bias_line, seg_q, seg_k,
    weights, q2, kv2, o2, q1, kv1, o1, bias,
):
    rows, width = x2.shape
    mem = mem_full.shape[0]
    hw = q1.shape[2]
    heads = bias_line.shape[1]
    ext = 3 * rows
    own = width // 8
    half = own // 2
    n = len(CHUNKS)
    dma = pltpu.SemaphoreType.DMA

    def slot(last, a):
        shape = a.shape[1:]
        return pl.BlockSpec(
            (1,) + shape, lambda j: (jnp.clip(last - j, 0, 3),) + (0,) * len(shape)
        )

    out = [
        ((rows, width), BF), ((4, own, width), F32), ((rows, width), F32), ((mem // 4, width), F32),
        ((24, width), F32), ((4, heads, 512), F32),
    ]
    shapes = [jax.ShapeDtypeStruct(s, d) for s, d in out]
    return pl.pallas_call(
        backward_kernel,
        name="backward",
        grid=(12,),
        in_specs=[
            SMEM_SPEC, *[once(a.shape) for a in (x2, cot, x1, mem_full, h2, h1, tokens)],
            full(gains.shape), full(bias_line.shape), full(seg_q.shape), full(seg_k.shape),
            pl.BlockSpec(memory_space=pl.ANY),
            slot(7, q2), slot(7, kv2), slot(7, o2), slot(11, q1), slot(11, kv1), slot(11, o1), slot(11, bias),
        ],
        out_specs=[*[once(s) for s, _ in out[:5]], slot(11, shapes[5])],
        out_shape=shapes,
        scratch_shapes=[
            pltpu.VMEM((HELD, 4, 2, own, width), BF), pltpu.VMEM((4, width, width), BF),
            pltpu.VMEM((ext, width), F32), pltpu.VMEM((rows, width), BF), pltpu.VMEM((rows, width), F32),
            pltpu.VMEM((rows, hw), BF), pltpu.VMEM((hw, rows), F32), pltpu.VMEM((ext, 2 * hw), BF),
            pltpu.VMEM((2, 2 * rows + 128, 128), F32), pltpu.VMEM((256, 256), BF),
            pltpu.VMEM((2, rows, width), BF), pltpu.VMEM((4, mem // 4, width), BF),
            pltpu.VMEM((n, 4, 1, own, width), BF),
            pltpu.VMEM((n, 2, half, width), BF), pltpu.VMEM((n, 2, half, width), BF),
            pltpu.VMEM((n, half, width), BF), pltpu.VMEM((n, half, width), BF),
            pltpu.VMEM((4, 5, own, width), BF),
            pltpu.VMEM((2, rows, width), BF), pltpu.VMEM((3, mem // 4, width), BF),
            dma((4,)), dma((n,)), dma((n,)),
            dma((n, 2)), dma((n, 2)), dma((n, 2)), dma((n, 2)),
            dma((n,)), dma((n,)), dma((n,)), dma((n,)),
            dma((n,)), dma((4, 5)),
            dma((2,)), dma((2,)), dma((3,)), dma((3,)),
        ],
        compiler_params=pltpu.CompilerParams(
            collective_id=1, has_side_effects=True, vmem_limit_bytes=VMEM_LIMIT, dimension_semantics=("arbitrary",)
        ),
    )(
        valid_rows, x2, cot, x1, mem_full, h2, h1, tokens, gains, bias_line, seg_q, seg_k,
        weights, q2, kv2, o2, q1, kv1, o1, bias,
    )


def stats_kernel(
    wide_count, f_ref, a_ref,
    rsum_ref, csum_ref, asum_ref, prow_ref, pcol_ref,
    rall, aall, call, ball, rs, rr, as_, ar, cs, cr, bs, br, ps, pr,
):
    w = lax.axis_index("wide")
    z = lax.axis_index("narrow")
    own = f_ref.shape[1]
    width = f_ref.shape[2]
    sem = pltpu.get_barrier_semaphore()

    def peer(k):
        return {"narrow": lax.rem(z + k, 4)}

    def wide_peer(k):
        return {"wide": lax.rem(w + k, wide_count)}

    def wide_loop(fn):
        if wide_count <= 8:
            for k in range(1, wide_count):
                fn(k)
        else:
            pl.loop(1, wide_count)(fn)

    for k in (1, 2, 3):
        pl.semaphore_signal(sem, inc=1, device_id=peer(k), device_id_type=MESH)
    wide_loop(lambda k: pl.semaphore_signal(sem, inc=1, device_id=wide_peer(k), device_id_type=MESH))

    lane = lax.broadcasted_iota(jnp.int32, (8, width), 1)
    row = lax.broadcasted_iota(jnp.int32, (8, width), 0)
    quarter = width // 4
    third = 2 * width // 3

    def sums(pick, sq):
        got = lax.dot_general(
            jnp.where(pick, 1.0, 0.0), sq, (((1,), (1,)), ((), ())),
            preferred_element_type=F32, precision=lax.Precision.HIGHEST,
        )
        pad = jnp.zeros((8, 128 - own), F32)
        return jnp.concatenate([got, pad], axis=1)

    sq = [f_ref[i] * f_ref[i] for i in range(4)]
    rall[z, 0:8] = sums(lane // quarter == row, sq[0])
    rall[z, 8:16] = sums(lane // quarter == row, sq[1])
    rall[z, 16:24] = sums(lane // third == row, sq[2]) + sums((lane + width) // third == row, sq[3])
    aall[z] = a_ref[...]
    call[w] = jnp.concatenate(
        [jnp.sum(v, axis=0, keepdims=True) for v in sq] + [jnp.zeros((4, width), F32)], axis=0
    )
    pl.semaphore_wait(sem, 3 + wide_count - 1)

    def r_send(k):
        return remote(rall.at[z], rall.at[z], rs.at[k - 1], rr.at[k - 1], peer(k))

    def a_send(k):
        return remote(aall.at[z], aall.at[z], as_.at[k - 1], ar.at[k - 1], peer(k))

    def c_send(k):
        return remote(call.at[w], call.at[w], cs.at[k - 1], cr.at[k - 1], wide_peer(k))

    def p_send(k):
        return remote(pcol_ref.at[z], pcol_ref.at[z], ps.at[k - 1], pr.at[k - 1], peer(k))

    def b_send(k):
        return remote(ball.at[w], ball.at[w], bs.at[k - 1], br.at[k - 1], wide_peer(k))

    for k in (1, 2, 3):
        r_send(k).start()
        a_send(k).start()
    wide_loop(lambda k: c_send(k).start())

    for k in (1, 2, 3):
        frm = lax.rem(z + 4 - k, 4)
        remote(rall.at[frm], rall.at[frm], rs.at[k - 1], rr.at[k - 1], peer(k)).wait_recv()
        remote(aall.at[frm], aall.at[frm], as_.at[k - 1], ar.at[k - 1], peer(k)).wait_recv()
    rsum = rall[0] + rall[1] + rall[2] + rall[3]
    rsum_ref[...] = rsum
    asum = aall[0] + aall[1] + aall[2] + aall[3]
    zero = jnp.zeros((1, width - 128), F32)
    ball[w] = jnp.concatenate(
        [
            asum[0:4],
            jnp.concatenate([rsum[1:2], zero], axis=1),
            jnp.concatenate([rsum[9:10], zero], axis=1),
            jnp.zeros((2, width), F32),
        ],
        axis=0,
    )
    wide_loop(lambda k: b_send(k).start())

    def c_wait(k):
        frm = lax.rem(w + wide_count - k, wide_count)
        remote(call.at[frm], call.at[frm], cs.at[k - 1], cr.at[k - 1], wide_peer(k)).wait_recv()

    wide_loop(c_wait)
    csum = lax.fori_loop(1, wide_count, lambda i, v: v + call[i], call[0])
    csum_ref[...] = csum
    pcol_ref[z] = csum
    for k in (1, 2, 3):
        p_send(k).start()

    def b_wait(k):
        frm = lax.rem(w + wide_count - k, wide_count)
        remote(ball.at[frm], ball.at[frm], bs.at[k - 1], br.at[k - 1], wide_peer(k)).wait_recv()

    wide_loop(b_wait)
    asum_ref[...] = lax.fori_loop(1, wide_count, lambda i, v: v + ball[i], ball[0])
    prow_ref[...] = ball[:, :, 0:128]
    for k in (1, 2, 3):
        frm = lax.rem(z + 4 - k, 4)
        remote(pcol_ref.at[frm], pcol_ref.at[frm], ps.at[k - 1], pr.at[k - 1], peer(k)).wait_recv()
    for k in (1, 2, 3):
        r_send(k).wait_send()
        a_send(k).wait_send()
        p_send(k).wait_send()

    def sent(k):
        c_send(k).wait_send()
        b_send(k).wait_send()

    wide_loop(sent)


def reduce_stats(wide_count, final, small):
    width = final.shape[2]
    vmem = pl.BlockSpec(memory_space=pltpu.VMEM)
    dma = pltpu.SemaphoreType.DMA
    return pl.pallas_call(
        functools.partial(stats_kernel, wide_count),
        name="stats",
        in_specs=[vmem] * 2,
        out_specs=[vmem] * 5,
        out_shape=[
            jax.ShapeDtypeStruct((24, 128), F32),
            jax.ShapeDtypeStruct((8, width), F32),
            jax.ShapeDtypeStruct((8, width), F32),
            jax.ShapeDtypeStruct((wide_count, 8, 128), F32),
            jax.ShapeDtypeStruct((4, 8, width), F32),
        ],
        scratch_shapes=[
            pltpu.VMEM((4, 24, 128), F32), pltpu.VMEM((4, 8, width), F32),
            pltpu.VMEM((wide_count, 8, width), F32), pltpu.VMEM((wide_count, 8, width), F32),
            dma((3,)), dma((3,)), dma((3,)), dma((3,)),
            dma((wide_count - 1,)), dma((wide_count - 1,)), dma((wide_count - 1,)), dma((wide_count - 1,)),
            dma((3,)), dma((3,)),
        ],
        compiler_params=pltpu.CompilerParams(collective_id=2, has_side_effects=True),
    )(final, small)


def local(
    tokens, memory, segments, valid_rows, norm_gains, rel_table,
    self_weights, cross_weights, ffn_weights, cotangent,
):
    wide_count = lax.axis_size("wide")
    assert lax.axis_size("narrow") == 4 and wide_count % 8 == 0 and segments.shape[0] == 1
    z = lax.axis_index("narrow")
    rows, width = tokens.shape
    mem_own = memory.shape[1]
    mem_len = 4 * mem_own
    hw = self_weights.shape[2]
    fw = ffn_weights.shape[2]
    heads = rel_table.shape[1] // 4
    ext = 3 * rows
    span = 2 * rows + 128
    groups = wide_count // 8
    eighth = width // 8

    buckets = bucket_table(1024, BUCKETS, MAX_DIST)
    lanes = np.arange(512)
    at_lane = np.where(lanes < 128, 128 + lanes, np.maximum(lanes - 384, 0))
    pick = jnp.asarray((buckets[at_lane][None, :] == np.arange(BUCKETS)[:, None]).astype(np.float32))
    bias_line = jnp.einsum("bl,bh->hl", pick, rel_table, precision=lax.Precision.HIGHEST)
    bias_line = bias_line.reshape(4, heads, 512)
    ranks = jnp.asarray(RANKS, jnp.int32)
    bias_line = jnp.take(bias_line, ranks[z], axis=0)
    seg = segments[0]
    seg_q = lax.dynamic_slice_in_dim(seg, z * rows, rows, 0).reshape(1, rows)
    seg_pad = jnp.concatenate([jnp.full((2 * rows,), -1, jnp.int32), seg])
    seg_k = lax.dynamic_slice_in_dim(seg_pad, z * rows, ext, 0).reshape(ext, 1)

    half = width // 16
    weights, x1, h1, q1, kv1, o1, bias, mem_full, x2, h2, q2, kv2, o2 = forward(
        valid_rows, tokens, memory[0], norm_gains, bias_line, seg_q, seg_k,
        self_weights.reshape(4, 16, half, hw), cross_weights.reshape(4, 16, half, hw),
        ffn_weights.reshape(3, 16, half, fw),
    )
    weights = weights.reshape(4, 4, width, width)
    mem_full = mem_full.reshape(mem_len, width)
    output, final, tokens_grad, memory_grad, gain_sums, rel = backward(
        valid_rows, x2, cotangent, x1, mem_full, h2, h1, tokens, norm_gains, bias_line, seg_q, seg_k,
        weights, q2, kv2, o2, q1, kv1, o1, bias,
    )
    if groups > 1:
        w = lax.axis_index("wide")
        mine = lax.dynamic_update_slice_in_dim(
            jnp.zeros((4, width, width), F32), final, lax.rem(w, 8) * eighth, 1
        )
        final = lax.psum_scatter(mine, "wide", scatter_dimension=1, tiled=True)
    own = final.shape[1]

    rel_pick = jnp.asarray(
        (buckets[np.maximum(lanes - 127, 0)][:, None] == np.arange(BUCKETS)[None, :]).astype(np.float32)
    )
    places = jnp.asarray([[row.index(q) for q in range(4)] for row in RANKS], jnp.int32)
    rel = jnp.take(rel, places[z], axis=0)
    rel = jnp.einsum("hl,lb->bh", rel.reshape(4 * heads, 512), rel_pick, precision=lax.Precision.HIGHEST)
    rel_row = jnp.pad(rel.reshape(1, -1), ((0, 0), (0, width - BUCKETS * 4 * heads)))
    small = jnp.concatenate([gain_sums[::8], rel_row, jnp.zeros((4, width), F32)], 0)
    rsum, csum, asum, prow, pcol = reduce_stats(wide_count, final, small)

    def split(g):
        return jnp.stack([g[:, 0:hw], g[:, 2 * hw : 3 * hw], g[:, 3 * hw :], g[:, hw : 2 * hw]])

    ffn_flat = jnp.concatenate([final[2], final[3]], axis=1)
    ffn_grad = jnp.stack([ffn_flat[:, 0:fw], ffn_flat[:, fw : 2 * fw], ffn_flat[:, 2 * fw :]])
    attn_row = jnp.concatenate([rsum[0:1], rsum[2:4], rsum[8:9], rsum[10:12]], 0)[:, :own] / width
    ffn_row = rsum[16:19, :own] / (4 * fw)
    attn_col = jnp.stack(
        [csum[i, a * hw : (a + 1) * hw] for i in range(2) for a in (0, 2, 3)]
    ) / width
    ffn_cols = jnp.concatenate([csum[2], csum[3]])
    ffn_col = ffn_cols.reshape(3, fw) / width
    proj_rows = prow[:, 4:6, :own].transpose(1, 0, 2).reshape(2, width) / width
    proj_cols = pcol[:, 0:2, hw : 2 * hw].transpose(1, 0, 2).reshape(2, width) / width
    return (
        output,
        tokens_grad,
        memory_grad.reshape(1, mem_own, width),
        asum[0:3],
        asum[3, : BUCKETS * 4 * heads].reshape(BUCKETS, 4 * heads),
        split(final[0]),
        split(final[1]),
        ffn_grad,
        attn_row,
        attn_col,
        jnp.concatenate([proj_rows, proj_cols], 1),
        ffn_row,
        ffn_col,
    )


def solution(mesh):
    in_specs = (
        P(("wide", "narrow"), None),
        P("wide", "narrow", None),
        P("wide", None),
        P("wide"),
        P(),
        P(),
        P(None, None, "narrow"),
        P(None, None, "narrow"),
        P(None, None, "narrow"),
        P(("wide", "narrow"), None),
    )
    out_specs = (
        P(("wide", "narrow"), None),
        P(("wide", "narrow"), None),
        P("wide", "narrow", None),
        P(),
        P(),
        P(None, "wide", "narrow"),
        P(None, "wide", "narrow"),
        P(None, "wide", "narrow"),
        P(None, "wide"),
        P(None, "narrow"),
        P(),
        P(None, "wide"),
        P(None, "narrow"),
    )
    return jax.shard_map(local, mesh=mesh, in_specs=in_specs, out_specs=out_specs, check_vma=False)
```

```python
import functools
import math

import jax
import jax.numpy as jnp
import numpy as np
from jax import lax
from jax.experimental import pallas as pl
from jax.experimental.pallas import tpu as pltpu
from jax.sharding import PartitionSpec as P

BUCKETS = 32
MAX_DIST = 128
EPS = 1e-06
MASKED = -1000000000.0
MESH = pl.DeviceIdType.MESH
BF = jnp.bfloat16
F32 = jnp.float32
VMEM_LIMIT = 64 * 1024 * 1024 - 65536


def bucket_table(seq_length, bucket_count, max_distance):
    exact_count = bucket_count // 2
    bucket_ids = np.zeros((seq_length,), np.int32)
    for distance in range(seq_length):
        if distance < exact_count:
            bucket_ids[distance] = distance
        else:
            scaled_log = (
                math.log(distance / exact_count)
                / math.log(max_distance / exact_count)
                * (bucket_count - exact_count)
            )
            bucket_ids[distance] = min(bucket_count - 1, exact_count + int(scaled_log))
    return bucket_ids


def mm(a, b):
    return jnp.dot(a, b, preferred_element_type=F32)


def mm_nt(a, b):
    return lax.dot_general(a, b, (((1,), (1,)), ((), ())), preferred_element_type=F32)


def mm_tn(a, b):
    return lax.dot_general(a, b, (((0,), (0,)), ((), ())), preferred_element_type=F32)


def inv_rms(v):
    return lax.rsqrt(jnp.mean(v * v, axis=-1, keepdims=True) + EPS)


def norm_back(v, gain, dh):
    r = inv_rms(v)
    gain_part = jnp.sum(dh * (v * r), axis=0, keepdims=True)
    gd = gain * dh
    dv = r * gd - v * (r * r * r) * jnp.mean(gd * v, axis=-1, keepdims=True)
    return gain_part, dv


def soft_cols(scores):
    e = jnp.exp(scores - jnp.max(scores, axis=0, keepdims=True))
    return e * (1.0 / jnp.sum(e, axis=0, keepdims=True))


def self_mask_store(mask_ref, seg_ref, z, rows, span):
    def quarter(k):
        out = jnp.full((1, rows), -1, jnp.int32)
        for kk in range(4):
            out = jnp.where(k == kk, seg_ref[:, kk * rows : (kk + 1) * rows], out)
        return out.astype(F32)

    own = quarter(z)
    keys = jnp.concatenate([quarter(z - 2), quarter(z - 1), own], axis=1)
    keys = jnp.broadcast_to(keys, (128, 3 * rows)).T
    for b in range(2):
        r = lax.broadcasted_iota(jnp.int32, (span, 128), 0)
        c = lax.broadcasted_iota(jnp.int32, (span, 128), 1)
        allowed = (c + 2 * rows >= r) & (keys[b * 128 : b * 128 + span] == own[:, b * 128 : b * 128 + 128])
        mask_ref[b] = jnp.where(allowed, 1.0, 0.0)


def full(shape):
    return pl.BlockSpec(shape, lambda j: (0,) * len(shape))


def once(shape):
    return pl.BlockSpec(shape, lambda j: (0,) * len(shape), pipeline_mode=pl.Buffered(1))


SMEM_SPEC = pl.BlockSpec(memory_space=pltpu.SMEM)


class Place:
    def __init__(self):
        self.w = lax.axis_index("wide")
        self.z = lax.axis_index("narrow")
        s = lax.rem(self.w, 8)
        self.s = s
        self.c = lax.rem(s, 2)
        self.x = lax.rem(s // 2, 2)
        self.y = s // 4
        dc, dx, dy = 1 - 2 * self.c, 2 * (1 - 2 * self.x), 4 * (1 - 2 * self.y)
        self.core_dev = {"wide": self.w + dc}
        self.x_dev = {"wide": self.w + dx}
        self.y_dev = {"wide": self.w + dy}
        self.sx, self.sy, self.sxy = s + dx, s + dy, s + dx + dy
        self.dc = dc

    def quarter(self, k):
        z = self.z
        e0, e3 = 1 - (z + 3) // 4, z // 3
        e1, e2 = (1 - z // 2) * lax.rem(z, 2), (z // 2) * (1 - lax.rem(z, 2))
        return sum(e * row[k] for e, row in zip((e0, e1, e2, e3), RANKS))

    def quarter_of(self, slot):
        return sum(jnp.where(slot == k, self.quarter(k), 0) for k in range(4))

    def narrow_dev(self, k):
        return {"narrow": lax.rem(self.z + k, 4)}

    def devices(self):
        return [self.core_dev, self.x_dev, self.y_dev] + [self.narrow_dev(k) for k in (1, 2, 3)]

    def signal_all(self):
        for dev in self.devices():
            pl.semaphore_signal(pltpu.get_barrier_semaphore(), inc=1, device_id=dev, device_id_type=MESH)

    def wait_all(self):
        pl.semaphore_wait(pltpu.get_barrier_semaphore(), len(self.devices()))

    def barrier(self):
        self.signal_all()
        self.wait_all()


def remote(src, dst, send_sem, recv_sem, dev):
    return pltpu.make_async_remote_copy(
        src_ref=src, dst_ref=dst, send_sem=send_sem, recv_sem=recv_sem, device_id=dev, device_id_type=MESH
    )


RANKS = ((0, 1, 2, 3), (1, 0, 2, 3), (2, 3, 1, 0), (3, 2, 1, 0))


def forward_kernel(
    valid_ref, tok_ref, mem_ref, gain_ref, rel_ref, pick_ref, seg_ref, ws_ref, wc_ref, wf_ref,
    w_ref, bd_ref, x1_ref, h1_ref, q_ref, kv_ref, o_ref, bias_ref, mfull_ref, x2_ref, h2_ref, q2_ref, kv2_ref, o2_ref,
    wv, lines, xt, mt, mask_ref, zs, zr, ps, pr, ts, tr, ms, mr, ls, fs, os_,
):
    at = Place()
    z, s = at.z, at.s
    j = pl.program_id(0)
    units = 4
    rows, width = tok_ref.shape
    ext = 3 * rows
    span = 2 * rows + 128
    hw = q_ref.shape[2]
    fw = wf_ref.shape[3]
    heads = hw // 64
    part = rows // 4
    half = width // 16
    mine = pl.ds(2 * s, 2)

    def edge(k):
        return [(d, RANKS[k + d].index(k)) for d in (1, -1) if 0 <= k + d < 4]

    def own_send(u, k, d, rank):
        return remote(
            wv.at[u, 0, mine], wv.at[u, rank, mine], zs.at[u, 0 if d > 0 else 1], zr.at[u, rank], {"narrow": k + d}
        )

    def own_sends(u, act):
        for k in range(4):
            @pl.when(z == k)
            def _():
                for d, rank in edge(k):
                    act(own_send(u, k, d, rank))

    def forwards(u, r, act):
        for k in (1, 2):
            quarter = RANKS[k][r]
            d = 1 if quarter < k else -1
            there = RANKS[k + d].index(quarter)

            @pl.when(z == k)
            def _():
                act(remote(wv.at[u, r, mine], wv.at[u, there, mine], zs.at[u, 1 + r], zr.at[u, there], {"narrow": k + d}))

    def tok_copy(hop, p):
        part_rows = pl.ds(p * part, part)
        return remote(
            tok_ref.at[part_rows], xt.at[2 - hop, part_rows], ts.at[hop - 1, p], tr.at[hop - 1, p], {"narrow": z + hop}
        )

    def tok_send(hop, parts):
        @pl.when(z < 4 - hop)
        def _():
            for p in parts:
                tok_copy(hop, p).start()

    def mem_copy(k):
        return remote(mem_ref, mt.at[z], ms.at[k - 1], mr.at[k - 1], at.narrow_dev(k))

    def piece(u, r, kind):
        first, n, dev = {
            0: (2 * s, 1, at.x_dev), 1: (2 * s + 1, 1, at.x_dev), 2: (2 * at.sy + 1, 1, at.x_dev),
            3: (2 * s + 1, 1, at.y_dev), 4: (2 * s, 1, at.y_dev), 5: (2 * at.sx, 1, at.y_dev),
            6: (2 * s, 2, at.core_dev), 7: (2 * at.sx, 2, at.core_dev),
            8: (2 * at.sy, 2, at.core_dev), 9: (2 * at.sxy, 2, at.core_dev),
        }[kind]
        region = wv.at[u, r, pl.ds(first, n)]
        i = u * 3 + r - 1
        return remote(region, region, ps.at[i, kind], pr.at[i, kind], dev)

    def arrived(u, r, kind):
        first, n = {
            0: (2 * at.sx, 1), 1: (2 * at.sx + 1, 1), 2: (2 * at.sxy + 1, 1),
            3: (2 * at.sy + 1, 1), 4: (2 * at.sy, 1), 5: (2 * at.sxy, 1),
            6: (2 * (s + at.dc), 2), 7: (2 * (at.sx + at.dc), 2),
            8: (2 * (at.sy + at.dc), 2), 9: (2 * (at.sxy + at.dc), 2),
        }[kind]
        region = wv.at[u, r, pl.ds(first, n)]
        i = u * 3 + r - 1
        remote(region, region, ps.at[i, kind], pr.at[i, kind], at.x_dev).wait_recv()

    pieces = [(u, r) for u in range(units) for r in (1, 2, 3)]

    def step0(t):
        if not 0 <= t < len(pieces):
            return
        u, r = pieces[t]
        region = wv.at[u, r, mine]
        remote(region, region, zs.at[u, 0], zr.at[u, r], at.x_dev).wait_recv()
        forwards(u, r, lambda copy: copy.start())
        for kind in (0, 3, 4, 1, 6):
            piece(u, r, kind).start()
        if t == 0:
            tok_send(1, (2, 3))
        if t == 1:
            tok_send(2, (0, 1))
        if t == 2:
            tok_send(2, (2, 3))
            own_sends(2, lambda copy: copy.start())
        if t in (3, 4, 5):
            mem_copy(t - 2).start()
        if t == 5:
            own_sends(3, lambda copy: copy.start())

    def step1(t):
        if not 0 <= t < len(pieces):
            return
        u, r = pieces[t]
        arrived(u, r, 0)
        piece(u, r, 5).start()
        arrived(u, r, 3)
        piece(u, r, 2).start()
        arrived(u, r, 1)
        piece(u, r, 7).start()
        arrived(u, r, 4)
        piece(u, r, 8).start()

    def step2(t):
        if not 0 <= t < len(pieces):
            return
        u, r = pieces[t]
        arrived(u, r, 5)
        arrived(u, r, 2)
        piece(u, r, 9).start()

    def keep(u, k):
        return pltpu.make_async_copy(wv.at[u, k], w_ref.at[u, k], os_.at[u, k])

    def step3(t):
        if not 0 <= t < len(pieces):
            return
        u, r = pieces[t]
        for kind in (6, 7, 8, 9):
            arrived(u, r, kind)
        keep(u, r).start()

    def attn_loads(i):
        src = (ws_ref, wc_ref)[i]
        return [
            pltpu.make_async_copy(src.at[part], wv.at[i, 0, pl.ds(4 * k, 4)], ls.at[i, k])
            for k, part in enumerate((0, 3, 1, 2))
        ]

    def ffn_loads():
        cut = width - fw
        return [
            pltpu.make_async_copy(wf_ref.at[0], wv.at[2, 0, :, :, 0:fw], fs.at[0]),
            pltpu.make_async_copy(wf_ref.at[1, :, :, 0:cut], wv.at[2, 0, :, :, fw:width], fs.at[1]),
            pltpu.make_async_copy(wf_ref.at[1, :, :, cut:fw], wv.at[3, 0, :, :, 0 : fw - cut], fs.at[2]),
            pltpu.make_async_copy(wf_ref.at[2], wv.at[3, 0, :, :, fw - cut : width], fs.at[3]),
        ]

    @pl.when(j == 0)
    def _():
        at.signal_all()
        for copy in attn_loads(0) + attn_loads(1) + ffn_loads():
            copy.start()
        at.wait_all()
        for copy in attn_loads(0):
            copy.wait()
        own_sends(0, lambda copy: copy.start())
        tok_send(1, (0, 1))
        for copy in attn_loads(1):
            copy.wait()
        own_sends(1, lambda copy: copy.start())
        for copy in ffn_loads():
            copy.wait()
        for u in range(units):
            keep(u, 0).start()
        x = tok_ref[...].astype(F32)
        x1_ref[...] = x
        h1_ref[2 * rows : ext, :] = (x * inv_rms(x) * gain_ref[0:1, :]).astype(BF)
        self_mask_store(mask_ref, seg_ref, z, rows, span)
        lines[...] = lax.dot_general(
            rel_ref[...], pick_ref[...], (((1,), (0,)), ((), ())),
            preferred_element_type=F32, precision=lax.Precision.HIGHEST,
        )
        for k in range(4):
            first = at.quarter(k) * heads
            for hh in range(heads):
                bd_ref[k, hh : hh + 1, :] = lines[pl.ds(first + hh, 1), :]
        step0(0)
        step0(1)
        step1(0)
        step0(2)
        step1(1)
        step2(0)
        step3(0)
        step0(3)
        step1(2)
        step2(1)
        for hop in (1, 2):
            @pl.when(z >= hop)
            def _():
                for p in range(4):
                    tok_copy(hop, p).wait_recv()
        for t in range(2):
            v = jnp.where(z >= 2 - t, xt[t].astype(F32), 0.0)
            h1_ref[t * rows : (t + 1) * rows, :] = (v * inv_rms(v) * gain_ref[0:1, :]).astype(BF)

    def hook(i, first, last):
        for jj in range(first, last):
            t = 4 + jj

            @pl.when(j == jj)
            def _():
                if i == 0:
                    step3(t - 3)
                    step0(t)
                if i == 1:
                    step1(t - 1)
                if i == 2:
                    step2(t - 2)

    def flat(u, k, lo, hi):
        return wv[u, k, lo // half : hi // half].reshape(hi - lo, width)

    @pl.when(j < 4)
    def _():
        hook(0, 0, 4)
        q = mm_nt(h1_ref[2 * rows : ext, :], flat(0, j, 0, hw)).astype(BF)
        kv = mm_nt(h1_ref[...], flat(0, j, 2 * hw, 4 * hw)).astype(BF)
        q_ref[0] = q
        kv_ref[0] = kv
        parts = []
        for hh in range(heads):
            line = jnp.broadcast_to(bd_ref[j, hh : hh + 1, :], (256, 512))
            bias = pltpu.roll(line, 0, 1, stride=1, stride_axis=0)[:, 0:128]
            bias_ref[0, hh] = bias
            far = bd_ref[j, hh : hh + 1, 127:128]
            cols = []
            for b in range(2):
                k = kv[b * 128 : b * 128 + span, hh * 64 : hh * 64 + 64]
                v = kv[b * 128 : b * 128 + span, hw + hh * 64 : hw + hh * 64 + 64]
                qb = q[b * 128 : b * 128 + 128, hh * 64 : hh * 64 + 64]
                sc = mm_nt(k, qb)
                sc = jnp.concatenate([sc[: span - 256] + far, sc[span - 256 :] + bias], axis=0)
                sc = jnp.where(mask_ref[b] > 0.5, sc, MASKED)
                cols.append(mm_tn(v, soft_cols(sc).astype(BF)))
            parts.append(jnp.concatenate(cols, axis=1))
            if hh < 2:
                hook(1 + hh, 0, 4)
        o = jnp.concatenate(parts, axis=0).T.astype(BF)
        o_ref[0] = o
        x1_ref[...] += mm(o, flat(0, j, hw, 2 * hw))

    @pl.when(j == 4)
    def _():
        x1 = x1_ref[...]
        x2_ref[...] = x1
        h2_ref[...] = (x1 * inv_rms(x1) * gain_ref[1:2, :]).astype(BF)
        mfull_ref[z] = mem_ref[...]
        for k in (1, 2, 3):
            frm = lax.rem(z + 4 - k, 4)
            remote(mt.at[frm], mt.at[frm], ms.at[k - 1], mr.at[k - 1], at.x_dev).wait_recv()
            mfull_ref[frm] = mt[frm]

    @pl.when(j >= 4)
    def _():
        hook(0, 4, 8)
        mem = mfull_ref.shape[0] * mfull_ref.shape[1]
        q = mm_nt(h2_ref[...], flat(1, j - 4, 0, hw)).astype(BF)
        kv = mm_nt(mfull_ref[...].reshape(mem, width), flat(1, j - 4, 2 * hw, 4 * hw)).astype(BF)
        q2_ref[0] = q
        kv2_ref[0] = kv
        allowed = lax.broadcasted_iota(jnp.int32, (mem, rows), 0) < valid_ref[0]
        parts = []
        for hh in range(heads):
            k = kv[:, hh * 64 : hh * 64 + 64]
            v = kv[:, hw + hh * 64 : hw + hh * 64 + 64]
            sc = jnp.where(allowed, mm_nt(k, q[:, hh * 64 : hh * 64 + 64]), MASKED)
            parts.append(mm_tn(v, soft_cols(sc).astype(BF)))
            if hh < 2:
                hook(1 + hh, 4, 8)
        o = jnp.concatenate(parts, axis=0).T.astype(BF)
        o2_ref[0] = o
        x2_ref[...] += mm(o, flat(1, j - 4, hw, 2 * hw))

    @pl.when(j == 7)
    def _():
        for t in range(12, len(pieces) + 3):
            step0(t)
            step1(t - 1)
            step2(t - 2)
            step3(t - 3)
        for u, r in pieces:
            for kind in range(10):
                piece(u, r, kind).wait_send()
            forwards(u, r, lambda copy: copy.wait_send())
        for u in range(units):
            own_sends(u, lambda copy: copy.wait_send())
            for k in range(4):
                keep(u, k).wait()
        for hop in (1, 2):
            @pl.when(z < 4 - hop)
            def _():
                for p in range(4):
                    tok_copy(hop, p).wait_send()
        for k in (1, 2, 3):
            mem_copy(k).wait_send()


def forward(valid_rows, tokens, memory, gains, rel, pick, seg, ws, wc, wf):
    rows, width = tokens.shape
    mem_own = memory.shape[0]
    hw = 4 * ws.shape[2]
    heads = hw // 64
    ext = 3 * rows
    mem = 4 * mem_own
    half = width // 16
    any_spec = pl.BlockSpec(memory_space=pl.ANY)
    dma = pltpu.SemaphoreType.DMA

    def early(shape):
        return pl.BlockSpec((1,) + shape, lambda j: (jnp.minimum(j, 3),) + (0,) * len(shape))

    def late(shape):
        return pl.BlockSpec((1,) + shape, lambda j: (jnp.maximum(j - 4, 0),) + (0,) * len(shape))

    out = [
        ((4, 4, 16, half, width), BF, any_spec), ((4, heads, 512), F32, full((4, heads, 512))),
        ((rows, width), F32, full((rows, width))), ((ext, width), BF, full((ext, width))),
        ((4, rows, hw), BF, early((rows, hw))), ((4, ext, 2 * hw), BF, early((ext, 2 * hw))),
        ((4, rows, hw), BF, early((rows, hw))), ((4, heads, 256, 128), F32, early((heads, 256, 128))),
        ((4, mem_own, width), BF, full((4, mem_own, width))),
        ((rows, width), F32, full((rows, width))), ((rows, width), BF, full((rows, width))),
        ((4, rows, hw), BF, late((rows, hw))), ((4, mem, 2 * hw), BF, late((mem, 2 * hw))),
        ((4, rows, hw), BF, late((rows, hw))),
    ]
    return pl.pallas_call(
        forward_kernel,
        name="forward",
        grid=(8,),
        in_specs=[
            SMEM_SPEC, full((rows, width)), full((mem_own, width)), full((3, width)),
            full(rel.shape), full(pick.shape), full(seg.shape), any_spec, any_spec, any_spec,
        ],
        out_specs=[spec for _, _, spec in out],
        out_shape=[jax.ShapeDtypeStruct(shape, dtype) for shape, dtype, _ in out],
        scratch_shapes=[
            pltpu.VMEM((4, 4, 16, half, width), BF), pltpu.VMEM((4 * heads, 512), F32),
            pltpu.VMEM((2, rows, width), BF), pltpu.VMEM((4, mem_own, width), BF),
            pltpu.VMEM((2, 2 * rows + 128, 128), F32),
            dma((4, 5)), dma((4, 4)), dma((12, 10)), dma((12, 10)),
            dma((2, 4)), dma((2, 4)), dma((3,)), dma((3,)), dma((2, 4)), dma((4,)), dma((4, 4)),
        ],
        compiler_params=pltpu.CompilerParams(
            collective_id=0, has_side_effects=True, vmem_limit_bytes=VMEM_LIMIT, dimension_semantics=("arbitrary",)
        ),
    )(valid_rows, tokens, memory, gains, rel, pick, seg, ws, wc, wf)


CHUNKS = [(2 + i % 2, i // 2) for i in range(8)] + [(1, i) for i in range(4)] + [(0, i) for i in range(4)]
HELD = 12
TICKS = [(1, 0), (2, 0), (3, 0), (4, 1), (5, 1), (6, 1), (7, 1), (8, 0), (8, 2), (9, 1), (10, 0), (10, 2), (11, 1)]


def backward_kernel(
    valid_ref, x2_ref, cot_ref, x1_ref, mem_ref, h2_ref, h1_ref, tok_ref, gain_ref, bd_ref, seg_ref, pick_ref,
    w_ref, q2_ref, kv2_ref, o2_ref, q1_ref, kv1_ref, o1_ref, bias_ref,
    out_ref, f_ref, tg_ref, mg_ref, small_ref,
    g, wbuf, acc, act_in, res, gsum_ref, rel_ref, do_ref, dqt_ref, dkv_ref, mask_ref, flip_ref, dxo, dmo, rc, xr, yr, xr2, yr2, zb, dxr, dmr,
    wsem, cs, cr, xs, xrs, ys, yrs, x2s, x2r, y2s, y2r, zs, zr, dxs, dxrs, dms, dmrs,
):
    at = Place()
    z = at.z
    j = pl.program_id(0)
    rows, width = x2_ref.shape
    mem = mem_ref.shape[0]
    ext = 3 * rows
    span = 2 * rows + 128
    hw = q1_ref.shape[2]
    heads = hw // 64
    fw = wbuf.shape[2] * 2 // 3
    own_rows = g.shape[3]
    half = own_rows // 2
    n = len(CHUNKS)
    lo, hi = pl.ds(0, half), pl.ds(half, half)
    yx = 2 * at.y + at.x
    top, bottom = pl.ds(0, rows), pl.ds(2 * rows, rows)

    def w_load(unit, slot, k):
        return pltpu.make_async_copy(w_ref.at[unit, slot], wbuf.at[k], wsem.at[k])

    def held(i):
        return g.at[i % HELD]

    def add(ref, other):
        ref[...] = ref[...] + other[...]

    def core_send(i):
        return remote(held(i).at[:, pl.ds(1 - at.c, 1)], rc.at[i], cs.at[i], cr.at[i], at.core_dev)

    def x_send(i, yb):
        src = held(i).at[2 * yb + 1 - at.x, at.c, lo]
        return remote(src, xr.at[i, yb], xs.at[i, yb], xrs.at[i, yb], at.x_dev)

    def y_send(i, xb):
        src = held(i).at[2 * (1 - at.y) + xb, at.c, hi]
        return remote(src, yr.at[i, xb], ys.at[i, xb], yrs.at[i, xb], at.y_dev)

    def y2_send(i):
        return remote(held(i).at[2 * (1 - at.y) + at.x, at.c, lo], yr2.at[i], y2s.at[i], y2r.at[i], at.y_dev)

    def x2_send(i):
        return remote(held(i).at[2 * at.y + 1 - at.x, at.c, hi], xr2.at[i], x2s.at[i], x2r.at[i], at.x_dev)

    d = 1 - 2 * (z // 2)
    is_end = jnp.logical_or(z == 0, z == 3)
    is_inner = jnp.logical_or(z == 1, z == 2)

    def z_send(i, dst, step):
        unit = CHUNKS[i][0]
        return remote(held(i).at[yx, at.c], zb.at[unit, dst], zs.at[i], zr.at[unit, dst], {"narrow": z + step})

    def z_wait(i, k):
        unit = CHUNKS[i][0]
        remote(zb.at[unit, k], zb.at[unit, k], zs.at[i], zr.at[unit, k], at.x_dev).wait_recv()

    def step_b(i):
        core_send(i).wait_recv()
        add(held(i).at[:, pl.ds(at.c, 1)], rc.at[i])
        for b in range(2):
            x_send(i, b).start()
            y_send(i, b).start()

    def step_c(i):
        for b in range(2):
            x_send(i, b).wait_recv()
            y_send(i, b).wait_recv()
            add(held(i).at[2 * b + at.x, at.c, lo], xr.at[i, b])
            add(held(i).at[2 * at.y + b, at.c, hi], yr.at[i, b])
        y2_send(i).start()
        x2_send(i).start()

    def step_d(i):
        y2_send(i).wait_recv()
        add(held(i).at[yx, at.c, lo], yr2.at[i])
        x2_send(i).wait_recv()
        add(held(i).at[yx, at.c, hi], xr2.at[i])

    def step_e(i):
        @pl.when(is_end)
        def _():
            if CHUNKS[i][1] < 3:
                z_send(i, CHUNKS[i][1], d).start()

    def step_f(i):
        unit, s = CHUNKS[i]

        @pl.when(is_inner)
        def _():
            if s < 2:
                z_wait(i, s)
                add(held(i).at[yx, at.c], zb.at[unit, s])
                z_send(i, 3 + s, d).start()
            if s == 2:
                z_wait(i, 3)
                add(held(i).at[yx, at.c], zb.at[unit, 3])
                z_send(i, 2, -d).start()
            if s == 3:
                z_wait(i, 2)
                z_wait(i, 4)
                f_ref[unit] = (
                    held(i)[yx, at.c].astype(F32) + zb[unit, 2].astype(F32) + zb[unit, 4].astype(F32)
                )

        if s == 3:
            @pl.when(is_end)
            def _():
                z_wait(i, 2)
                f_ref[unit] = held(i)[yx, at.c].astype(F32) + zb[unit, 2].astype(F32)

    def sent(i):
        core_send(i).wait_send()
        for b in range(2):
            x_send(i, b).wait_send()
            y_send(i, b).wait_send()
        y2_send(i).wait_send()
        x2_send(i).wait_send()
        if CHUNKS[i][1] < 3:
            z_send(i, 0, d).wait_send()

    def tick(t):
        for k, step in enumerate((step_b, step_c, step_d, step_e, step_f)):
            if 0 <= t - k < n:
                step(t - k)

    def hook(place, first, last):
        for t, (jj, p) in enumerate(TICKS):
            if p == place and first <= jj < last:
                @pl.when(j == jj)
                def _():
                    tick(t)

    def dx_send(t):
        return remote(dxo.at[t], dxr.at[t], dxs.at[t], dxrs.at[t], {"narrow": z - 2 + t})

    def dm_send(k):
        return remote(dmo.at[lax.rem(z + k, 4)], dmr.at[k - 1], dms.at[k - 1], dmrs.at[k - 1], at.narrow_dev(k))

    @pl.when(j == 0)
    def _():
        for b in range(2):
            w_load(2 + b, 3, b).start()
        at.signal_all()
        x2 = x2_ref[...]
        acc[0:rows, :] = x2
        acc[rows : 2 * rows, :] = jnp.zeros((rows, width), F32)
        act_in[...] = (x2 * inv_rms(x2) * gain_ref[2:3, :]).astype(BF)

    @pl.when(j < 4)
    def _():
        k = 2 * lax.rem(j, 2)
        for b in range(2):
            w_load(2 + b, 3 - j, k + b).wait()

        @pl.when(j < 3)
        def _():
            for b in range(2):
                w_load(2 + b, 2 - j, 2 - k + b).start()

        @pl.when(j == 3)
        def _():
            w_load(1, 3, 0).start()

        @pl.when(j == 0)
        def _():
            at.wait_all()

        hook(0, 0, 4)
        h3 = act_in[...]
        df = cot_ref[...]
        wg = wbuf[k, :, 0:fw]
        wu = jnp.concatenate([wbuf[k, :, fw:], wbuf[k + 1, :, 0 : fw // 2]], axis=1)
        wd = wbuf[k + 1, :, fw // 2 :]
        gate = mm(h3, wg)
        up = mm(h3, wu)
        c0 = math.sqrt(2.0 / math.pi)
        gate2 = gate * gate
        t = jnp.tanh(c0 * (gate + 0.044715 * gate2 * gate))
        part = 0.5 * (1.0 + t)
        gelu = gate * part
        slope = part + 0.5 * gate * (1.0 - t * t) * (c0 * (1.0 + 3.0 * 0.044715 * gate2))
        act = (gelu * up).astype(BF)
        acc[0:rows, :] += mm_nt(act, wd)
        da = mm(df, wd)
        dgate = (da * up * slope).astype(BF)
        dup = (da * gelu).astype(BF)
        dgu = jnp.concatenate([dgate, dup], axis=1)
        ggu = mm_tn(h3, dgu).astype(BF)
        blocks = (4, 2, own_rows)
        g[2 * j] = ggu[:, 0 : fw * 3 // 2].reshape(blocks + (width,))
        g[2 * j + 1, :, :, :, 0 : fw // 2] = ggu[:, fw * 3 // 2 :].reshape(blocks + (fw // 2,))
        g[2 * j + 1, :, :, :, fw // 2 :] = mm_tn(df, act).astype(BF).reshape(blocks + (fw,))
        acc[rows : 2 * rows, :] += mm_nt(dgate, wg) + mm_nt(dup, wu)
        for jj in range(4):
            @pl.when(j == jj)
            def _():
                core_send(2 * jj).start()
                core_send(2 * jj + 1).start()

    @pl.when(j == 3)
    def _():
        out_ref[...] = acc[0:rows, :].astype(BF)
        gain_part, dv = norm_back(x2_ref[...], gain_ref[2:3, :], acc[rows : 2 * rows, :])
        gsum_ref[16:24, :] = jnp.broadcast_to(gain_part, (8, width))
        g2 = cot_ref[...].astype(F32) + dv
        res[...] = g2
        act_in[...] = g2.astype(BF)
        acc[...] = jnp.zeros_like(acc)

    @pl.when(jnp.logical_and(j >= 4, j < 8))
    def _():
        k0 = j - 4
        w_load(1, 7 - j, k0).wait()

        @pl.when(j < 7)
        def _():
            w_load(1, 6 - j, k0 + 1).start()

        @pl.when(j == 7)
        def _():
            w_load(0, 3, 0).start()

        do_ref[...] = mm_nt(act_in[...], wbuf[k0, hw : 2 * hw, :]).astype(BF)
        for hh in range(heads):
            h_cols, v_cols = slice(hh * 64, hh * 64 + 64), slice(hw + hh * 64, hw + hh * 64 + 64)
            k = kv2_ref[0, :, h_cols]
            v = kv2_ref[0, :, v_cols]
            qh = q2_ref[0, :, h_cols]
            doh = do_ref[:, h_cols]
            allowed = lax.broadcasted_iota(jnp.int32, (mem, rows), 0) < valid_ref[0]
            p = soft_cols(jnp.where(allowed, mm_nt(k, qh), MASKED))
            dp = mm_nt(v, doh)
            ds = (p * (dp - jnp.sum(p * dp, axis=0, keepdims=True))).astype(BF)
            dkv_ref[0:mem, v_cols] = mm(p.astype(BF), doh).astype(BF)
            dkv_ref[0:mem, h_cols] = mm(ds, qh).astype(BF)
            dqt_ref[h_cols, :] = mm_tn(k, ds)
            hook(hh, 4, 8)
        dc = act_in[...]
        dq = dqt_ref[...].T.astype(BF)
        dkv = dkv_ref[0:mem, :]
        zero = jnp.zeros((rows, hw), BF)
        left = jnp.concatenate([h2_ref[...], dc], axis=0)
        right = jnp.concatenate(
            [jnp.concatenate([dq, zero], axis=1), jnp.concatenate([zero, o2_ref[0]], axis=1)], axis=0
        )
        blocks = (4, 2, own_rows, 2 * hw)
        g[4 + j, :, :, :, 0 : 2 * hw] = mm_tn(left, right).astype(BF).reshape(blocks)
        g[4 + j, :, :, :, 2 * hw : 4 * hw] = mm_tn(mem_ref[...], dkv).astype(BF).reshape(blocks)
        for jj in range(4, 8):
            @pl.when(j == jj)
            def _():
                core_send(4 + jj).start()
        acc[0:rows, :] += mm(dq, wbuf[k0, 0:hw, :])
        acc[rows : rows + mem, :] += mm(dkv, wbuf[k0, 2 * hw : 4 * hw, :])

    @pl.when(j == 7)
    def _():
        for k in range(4):
            dmo[k] = acc[rows + k * (mem // 4) : rows + (k + 1) * (mem // 4), :].astype(BF)
        for k in (1, 2, 3):
            dm_send(k).start()
        gain_part, dv = norm_back(x1_ref[...], gain_ref[1:2, :], acc[0:rows, :])
        gsum_ref[8:16, :] = jnp.broadcast_to(gain_part, (8, width))
        g1 = res[...] + dv
        res[...] = g1
        act_in[...] = g1.astype(BF)
        acc[...] = jnp.zeros_like(acc)
        self_mask_store(mask_ref, seg_ref, z, rows, span)
        rel_ref[...] = jnp.zeros_like(rel_ref)
        r = lax.broadcasted_iota(jnp.int32, (256, 256), 0)
        c = lax.broadcasted_iota(jnp.int32, (256, 256), 1)
        flip_ref[...] = jnp.where(r + c == 255, 1.0, 0.0).astype(BF)

    @pl.when(j >= 8)
    def _():
        k0 = j - 8
        w_load(0, 11 - j, k0).wait()

        @pl.when(j < 11)
        def _():
            w_load(0, 10 - j, k0 + 1).start()

        do_ref[...] = mm_nt(act_in[...], wbuf[k0, hw : 2 * hw, :]).astype(BF)
        for hh in range(heads):
            h_cols, v_cols = slice(hh * 64, hh * 64 + 64), slice(hw + hh * 64, hw + hh * 64 + 64)
            far = bd_ref[11 - j, hh : hh + 1, 127:128]
            dq_cols, dks, dvs = [], [], []
            band = jnp.zeros((256, 128), F32)
            total = jnp.zeros((1, 128), F32)
            for b in range(2):
                k = kv1_ref[0, b * 128 : b * 128 + span, h_cols]
                v = kv1_ref[0, b * 128 : b * 128 + span, v_cols]
                qb = q1_ref[0, b * 128 : b * 128 + 128, h_cols]
                dob = do_ref[b * 128 : b * 128 + 128, h_cols]
                s = mm_nt(k, qb)
                s = jnp.concatenate([s[: span - 256] + far, s[span - 256 :] + bias_ref[0, hh]], axis=0)
                s = jnp.where(mask_ref[b] > 0.5, s, MASKED)
                p = soft_cols(s)
                dp = mm_nt(v, dob)
                ds = (p * (dp - jnp.sum(p * dp, axis=0, keepdims=True))).astype(BF)
                dvs.append(mm(p.astype(BF), dob))
                dks.append(mm(ds, qb))
                dq_cols.append(mm_tn(k, ds))
                band = band + mm(flip_ref[...], ds[span - 256 :])
                total = total + jnp.sum(ds[: span - 256].astype(F32), axis=0, keepdims=True)
            gap = jnp.zeros((128, 64), F32)
            dk = jnp.concatenate([dks[0], gap], 0) + jnp.concatenate([gap, dks[1]], 0)
            dv = jnp.concatenate([dvs[0], gap], 0) + jnp.concatenate([gap, dvs[1]], 0)
            dkv_ref[:, h_cols] = dk.astype(BF)
            dkv_ref[:, v_cols] = dv.astype(BF)
            dqt_ref[h_cols, :] = jnp.concatenate(dq_cols, axis=1)
            wide_band = jnp.concatenate([band, jnp.zeros((256, 384), F32)], axis=1)
            aligned = pltpu.roll(wide_band, 0, 1, stride=1, stride_axis=0)
            line = jnp.sum(aligned, axis=0, keepdims=True)
            lane = lax.broadcasted_iota(jnp.int32, (1, 512), 1)
            far_sum = jnp.sum(total, axis=1, keepdims=True)
            rel_ref[pl.ds(at.quarter_of(11 - j) * heads + hh, 1), :] = jnp.where(lane == 511, far_sum, line)
            hook(hh, 8, 12)
        da = act_in[...]
        dq = dqt_ref[...].T.astype(BF)
        dkv = dkv_ref[...]
        zero = jnp.zeros((rows, hw), BF)
        left = jnp.concatenate([h1_ref[2 * rows : ext, :], da], axis=0)
        right = jnp.concatenate(
            [jnp.concatenate([dq, zero], axis=1), jnp.concatenate([zero, o1_ref[0]], axis=1)], axis=0
        )
        for jj in range(8, 12):
            @pl.when(j == jj)
            def _():
                sent(jj - 8)
        blocks = (4, 2, own_rows, 2 * hw)
        g[j - 8, :, :, :, 0 : 2 * hw] = mm_tn(left, right).astype(BF).reshape(blocks)
        g[j - 8, :, :, :, 2 * hw : 4 * hw] = mm_tn(h1_ref[...], dkv).astype(BF).reshape(blocks)
        for jj in range(8, 12):
            @pl.when(j == jj)
            def _():
                core_send(4 + jj).start()
        acc[...] += mm(dkv, wbuf[k0, 2 * hw : 4 * hw, :])
        acc[2 * rows : ext, :] += mm(dq, wbuf[k0, 0:hw, :])

    @pl.when(j == 11)
    def _():
        for t in range(2):
            dxo[t] = acc[t * rows : (t + 1) * rows, :].astype(BF)

            @pl.when(z >= 2 - t)
            def _():
                dx_send(t).start()
        last = n + 4
        for t in range(len(TICKS), last):
            tick(t)
            if t == len(TICKS):
                mg_ref[...] = dmo[z].astype(F32)
                for k in (1, 2, 3):
                    dm_send(k).wait_recv()
                    mg_ref[...] += dmr[k - 1].astype(F32)
            if t == last - 2:
                for k in range(2):
                    @pl.when(z < 2 + k)
                    def _():
                        dx_send(k).wait_recv()
                        acc[2 * rows : ext, :] += dxr[k].astype(F32)
                gain_part, dv = norm_back(tok_ref[...].astype(F32), gain_ref[0:1, :], acc[2 * rows : ext, :])
                rel = lax.dot_general(
                    rel_ref[...], pick_ref[...], (((1,), (0,)), ((), ())),
                    preferred_element_type=F32, precision=lax.Precision.HIGHEST,
                )
                gains = [gain_part, gsum_ref[8:9, :], gsum_ref[16:17, :], jnp.zeros((5, width), F32)]
                small_ref[...] = jnp.concatenate([jnp.concatenate(gains, axis=0), rel[0:8], rel[8:16]], axis=1)
                tg_ref[...] = res[...] + dv
        for i in range(n - HELD, n):
            sent(i)
        for t in range(2):
            @pl.when(z >= 2 - t)
            def _():
                dx_send(t).wait_send()
        for k in (1, 2, 3):
            dm_send(k).wait_send()


def backward(
    valid_rows, x2, cot, x1, mem_full, h2, h1, tokens, gains, bias_line, seg, pick,
    weights, q2, kv2, o2, q1, kv1, o1, bias,
):
    rows, width = x2.shape
    mem = mem_full.shape[0]
    hw = q1.shape[2]
    ext = 3 * rows
    own = width // 8
    half = own // 2
    n = len(CHUNKS)
    dma = pltpu.SemaphoreType.DMA

    def slot(last, a):
        shape = a.shape[1:]
        return pl.BlockSpec(
            (1,) + shape, lambda j: (jnp.clip(last - j, 0, 3),) + (0,) * len(shape)
        )

    out = [
        ((rows, width), BF), ((4, own, width), F32), ((rows, width), F32), ((mem // 4, width), F32),
        ((8, width + 256), F32),
    ]
    shapes = [jax.ShapeDtypeStruct(s, d) for s, d in out]
    return pl.pallas_call(
        backward_kernel,
        name="backward",
        grid=(12,),
        in_specs=[
            SMEM_SPEC, *[once(a.shape) for a in (x2, cot, x1, mem_full, h2, h1, tokens)],
            full(gains.shape), full(bias_line.shape), full(seg.shape), full(pick.shape),
            pl.BlockSpec(memory_space=pl.ANY),
            slot(7, q2), slot(7, kv2), slot(7, o2), slot(11, q1), slot(11, kv1), slot(11, o1), slot(11, bias),
        ],
        out_specs=[once(s) for s, _ in out],
        out_shape=shapes,
        scratch_shapes=[
            pltpu.VMEM((HELD, 4, 2, own, width), BF), pltpu.VMEM((4, width, width), BF),
            pltpu.VMEM((ext, width), F32), pltpu.VMEM((rows, width), BF), pltpu.VMEM((rows, width), F32),
            pltpu.VMEM((24, width), F32), pltpu.VMEM((16, 512), F32),
            pltpu.VMEM((rows, hw), BF), pltpu.VMEM((hw, rows), F32), pltpu.VMEM((ext, 2 * hw), BF),
            pltpu.VMEM((2, 2 * rows + 128, 128), F32), pltpu.VMEM((256, 256), BF),
            pltpu.VMEM((2, rows, width), BF), pltpu.VMEM((4, mem // 4, width), BF),
            pltpu.VMEM((n, 4, 1, own, width), BF),
            pltpu.VMEM((n, 2, half, width), BF), pltpu.VMEM((n, 2, half, width), BF),
            pltpu.VMEM((n, half, width), BF), pltpu.VMEM((n, half, width), BF),
            pltpu.VMEM((4, 5, own, width), BF),
            pltpu.VMEM((2, rows, width), BF), pltpu.VMEM((3, mem // 4, width), BF),
            dma((4,)), dma((n,)), dma((n,)),
            dma((n, 2)), dma((n, 2)), dma((n, 2)), dma((n, 2)),
            dma((n,)), dma((n,)), dma((n,)), dma((n,)),
            dma((n,)), dma((4, 5)),
            dma((2,)), dma((2,)), dma((3,)), dma((3,)),
        ],
        compiler_params=pltpu.CompilerParams(
            collective_id=1, has_side_effects=True, vmem_limit_bytes=VMEM_LIMIT, dimension_semantics=("arbitrary",)
        ),
    )(
        valid_rows, x2, cot, x1, mem_full, h2, h1, tokens, gains, bias_line, seg, pick,
        weights, q2, kv2, o2, q1, kv1, o1, bias,
    )


def stats_kernel(
    wide_count, f_ref, a_ref,
    rsum_ref, csum_ref, asum_ref, pcol_ref,
    rall, aall, call, ball, rs, rr, as_, ar, cs, cr, bs, br, ps, pr,
):
    w = lax.axis_index("wide")
    z = lax.axis_index("narrow")
    own = f_ref.shape[1]
    width = f_ref.shape[2]
    sem = pltpu.get_barrier_semaphore()

    def peer(k):
        return {"narrow": lax.rem(z + k, 4)}

    def wide_peer(k):
        return {"wide": lax.rem(w + k, wide_count)}

    def wide_loop(fn):
        if wide_count <= 8:
            for k in range(1, wide_count):
                fn(k)
        else:
            pl.loop(1, wide_count)(fn)

    for k in (1, 2, 3):
        pl.semaphore_signal(sem, inc=1, device_id=peer(k), device_id_type=MESH)
    wide_loop(lambda k: pl.semaphore_signal(sem, inc=1, device_id=wide_peer(k), device_id_type=MESH))

    lane = lax.broadcasted_iota(jnp.int32, (8, width), 1)
    row = lax.broadcasted_iota(jnp.int32, (8, width), 0)
    quarter = width // 4
    third = 2 * width // 3

    def sums(pick, sq):
        got = lax.dot_general(
            jnp.where(pick, 1.0, 0.0), sq, (((1,), (1,)), ((), ())),
            preferred_element_type=F32, precision=lax.Precision.HIGHEST,
        )
        pad = jnp.zeros((8, 128 - own), F32)
        return jnp.concatenate([got, pad], axis=1)

    sq = [f_ref[i] * f_ref[i] for i in range(4)]
    rall[z, 0:8] = sums(lane // quarter == row, sq[0])
    rall[z, 8:16] = sums(lane // quarter == row, sq[1])
    rall[z, 16:24] = sums(lane // third == row, sq[2]) + sums((lane + width) // third == row, sq[3])
    aall[z] = a_ref[...]
    call[w] = jnp.concatenate(
        [jnp.sum(v, axis=0, keepdims=True) for v in sq] + [jnp.zeros((4, width), F32)], axis=0
    )
    pl.semaphore_wait(sem, 3 + wide_count - 1)

    def r_send(k):
        return remote(rall.at[z], rall.at[z], rs.at[k - 1], rr.at[k - 1], peer(k))

    def a_send(k):
        return remote(aall.at[z], aall.at[z], as_.at[k - 1], ar.at[k - 1], peer(k))

    def c_send(k):
        return remote(call.at[w], call.at[w], cs.at[k - 1], cr.at[k - 1], wide_peer(k))

    def p_send(k):
        return remote(pcol_ref.at[z], pcol_ref.at[z], ps.at[k - 1], pr.at[k - 1], peer(k))

    def b_send(k):
        return remote(ball.at[w], ball.at[w], bs.at[k - 1], br.at[k - 1], wide_peer(k))

    for k in (1, 2, 3):
        r_send(k).start()
        a_send(k).start()
    wide_loop(lambda k: c_send(k).start())

    for k in (1, 2, 3):
        frm = lax.rem(z + 4 - k, 4)
        remote(rall.at[frm], rall.at[frm], rs.at[k - 1], rr.at[k - 1], peer(k)).wait_recv()
        remote(aall.at[frm], aall.at[frm], as_.at[k - 1], ar.at[k - 1], peer(k)).wait_recv()
    rsum = rall[0] + rall[1] + rall[2] + rall[3]
    rsum_ref[...] = rsum
    asum = aall[0] + aall[1] + aall[2] + aall[3]
    zero = jnp.zeros((8, width - 128), F32)
    rows = jnp.concatenate([rsum[0:8], zero], axis=1)
    more = jnp.concatenate([rsum[8:16], zero], axis=1)
    shift = own * w
    left = jnp.concatenate(
        [
            asum[0:3, 0:width],
            pltpu.roll(rows, shift, 1)[1:2], pltpu.roll(more, shift, 1)[1:2],
            jnp.zeros((3, width), F32),
        ],
        axis=0,
    )
    ball[w] = jnp.concatenate([left, asum[:, width:]], axis=1)
    wide_loop(lambda k: b_send(k).start())

    def c_wait(k):
        frm = lax.rem(w + wide_count - k, wide_count)
        remote(call.at[frm], call.at[frm], cs.at[k - 1], cr.at[k - 1], wide_peer(k)).wait_recv()

    wide_loop(c_wait)
    csum = lax.fori_loop(1, wide_count, lambda i, v: v + call[i], call[0])
    csum_ref[...] = csum
    pcol_ref[z] = csum
    for k in (1, 2, 3):
        p_send(k).start()

    def b_wait(k):
        frm = lax.rem(w + wide_count - k, wide_count)
        remote(ball.at[frm], ball.at[frm], bs.at[k - 1], br.at[k - 1], wide_peer(k)).wait_recv()

    wide_loop(b_wait)
    asum_ref[...] = lax.fori_loop(1, wide_count, lambda i, v: v + ball[i], ball[0])
    for k in (1, 2, 3):
        frm = lax.rem(z + 4 - k, 4)
        remote(pcol_ref.at[frm], pcol_ref.at[frm], ps.at[k - 1], pr.at[k - 1], peer(k)).wait_recv()
    for k in (1, 2, 3):
        r_send(k).wait_send()
        a_send(k).wait_send()
        p_send(k).wait_send()

    def sent(k):
        c_send(k).wait_send()
        b_send(k).wait_send()

    wide_loop(sent)


def reduce_stats(wide_count, final, small):
    width = final.shape[2]
    vmem = pl.BlockSpec(memory_space=pltpu.VMEM)
    dma = pltpu.SemaphoreType.DMA
    return pl.pallas_call(
        functools.partial(stats_kernel, wide_count),
        name="stats",
        in_specs=[vmem] * 2,
        out_specs=[vmem] * 4,
        out_shape=[
            jax.ShapeDtypeStruct((24, 128), F32),
            jax.ShapeDtypeStruct((8, width), F32),
            jax.ShapeDtypeStruct(small.shape, F32),
            jax.ShapeDtypeStruct((4, 8, width), F32),
        ],
        scratch_shapes=[
            pltpu.VMEM((4, 24, 128), F32), pltpu.VMEM((4,) + small.shape, F32),
            pltpu.VMEM((wide_count, 8, width), F32), pltpu.VMEM((wide_count,) + small.shape, F32),
            dma((3,)), dma((3,)), dma((3,)), dma((3,)),
            dma((wide_count - 1,)), dma((wide_count - 1,)), dma((wide_count - 1,)), dma((wide_count - 1,)),
            dma((3,)), dma((3,)),
        ],
        compiler_params=pltpu.CompilerParams(collective_id=2, has_side_effects=True),
    )(final, small)


def finish_kernel(
    out_ref, tg_ref, mg_ref, f_ref, rsum_ref, csum_ref, asum_ref, pcol_ref,
    out_o, tg_o, mg_o, gains_o, rel_o, self_o, cross_o, ffn_o, arow_o, acol_o, proj_o, frow_o, fcol_o,
):
    own, width = f_ref.shape[1:]
    hw = self_o.shape[2]
    fw = ffn_o.shape[2]
    out_o[...] = out_ref[...]
    tg_o[...] = tg_ref[...]
    mg_o[...] = mg_ref[...]
    gains_o[...] = asum_ref[0:3, 0:width]
    rel = jnp.concatenate([asum_ref[:, width : width + 128], asum_ref[:, width + 128 : width + 256]], axis=0)
    rel_o[...] = rel[0 : rel_o.shape[0], 0 : rel_o.shape[1]]
    for ref, i in ((self_o, 0), (cross_o, 1)):
        for m, part in enumerate((0, 2, 3, 1)):
            ref[m] = f_ref[i, :, part * hw : (part + 1) * hw]
    cut = width - fw
    ffn_o[0] = f_ref[2, :, 0:fw]
    ffn_o[1, :, 0:cut] = f_ref[2, :, fw:width]
    ffn_o[1, :, cut:fw] = f_ref[3, :, 0 : fw - cut]
    ffn_o[2] = f_ref[3, :, fw - cut : width]
    rsum = rsum_ref[...]
    arow = jnp.concatenate([rsum[0:1], rsum[2:4], rsum[8:9], rsum[10:12]], axis=0)
    arow_o[...] = arow[:, 0:own] * (1.0 / width)
    frow_o[...] = rsum[16:19, 0:own] * (1.0 / (4 * fw))
    scale = 1.0 / width
    for i in range(2):
        for m, part in enumerate((0, 2, 3)):
            acol_o[3 * i + m : 3 * i + m + 1, :] = csum_ref[i : i + 1, part * hw : (part + 1) * hw] * scale
    fcol_o[0:1, :] = csum_ref[2:3, 0:fw] * scale
    fcol_o[1:2, 0:cut] = csum_ref[2:3, fw:width] * scale
    fcol_o[1:2, cut:fw] = csum_ref[3:4, 0 : fw - cut] * scale
    fcol_o[2:3, :] = csum_ref[3:4, fw - cut : width] * scale
    for i in range(2):
        cols = jnp.concatenate([pcol_ref[k, i : i + 1, hw : 2 * hw] for k in range(4)], axis=1)
        proj_o[i : i + 1, 0:width] = asum_ref[3 + i : 4 + i, 0:width] * scale
        proj_o[i : i + 1, width : 2 * width] = cols * scale


def finish(shapes, *args):
    vmem = pl.BlockSpec(memory_space=pltpu.VMEM)
    return pl.pallas_call(
        finish_kernel,
        name="finish",
        in_specs=[vmem] * len(args),
        out_specs=[vmem] * len(shapes),
        out_shape=[jax.ShapeDtypeStruct(s, d) for s, d in shapes],
    )(*args)


def local(
    tokens, memory, segments, valid_rows, norm_gains, rel_table,
    self_weights, cross_weights, ffn_weights, cotangent,
):
    wide_count = lax.axis_size("wide")
    assert lax.axis_size("narrow") == 4 and wide_count % 8 == 0 and segments.shape[0] == 1
    rows, width = tokens.shape
    mem_own = memory.shape[1]
    mem_len = 4 * mem_own
    hw = self_weights.shape[2]
    fw = ffn_weights.shape[2]
    heads = rel_table.shape[1]
    groups = wide_count // 8
    eighth = width // 8

    buckets = bucket_table(1024, BUCKETS, MAX_DIST)
    lanes = np.arange(512)
    at_lane = np.where(lanes < 128, 128 + lanes, np.maximum(lanes - 384, 0))
    pick = jnp.asarray((buckets[at_lane][None, :] == np.arange(BUCKETS)[:, None]).astype(np.float32))
    rel_pick = jnp.asarray(
        (buckets[np.maximum(lanes - 127, 0)][:, None] == np.arange(128)[None, :]).astype(np.float32)
    )

    half = width // 16
    weights, bias_line, x1, h1, q1, kv1, o1, bias, mem_full, x2, h2, q2, kv2, o2 = forward(
        valid_rows, tokens, memory[0], norm_gains, rel_table.T, pick, segments,
        jnp.swapaxes(self_weights, 1, 2).reshape(4, 4, hw // 4, width),
        jnp.swapaxes(cross_weights, 1, 2).reshape(4, 4, hw // 4, width),
        ffn_weights.reshape(3, 16, half, fw),
    )
    weights = weights.reshape(4, 4, width, width)
    mem_full = mem_full.reshape(mem_len, width)
    output, final, tokens_grad, memory_grad, small = backward(
        valid_rows, x2, cotangent, x1, mem_full, h2, h1, tokens, norm_gains, bias_line, segments, rel_pick,
        weights, q2, kv2, o2, q1, kv1, o1, bias,
    )
    if groups > 1:
        w = lax.axis_index("wide")
        mine = lax.dynamic_update_slice_in_dim(
            jnp.zeros((4, width, width), F32), final, lax.rem(w, 8) * eighth, 1
        )
        final = lax.psum_scatter(mine, "wide", scatter_dimension=1, tiled=True)
    own = final.shape[1]
    sums = reduce_stats(wide_count, final, small)
    shapes = [
        ((rows, width), BF), ((rows, width), F32), ((mem_own, width), F32), ((3, width), F32), ((heads, BUCKETS), F32),
        ((4, own, hw), F32), ((4, own, hw), F32), ((3, own, fw), F32),
        ((6, own), F32), ((6, hw), F32), ((2, 2 * width), F32), ((3, own), F32), ((3, fw), F32),
    ]
    outs = list(finish(shapes, output, tokens_grad, memory_grad, final, *sums))
    outs[2] = outs[2].reshape(1, mem_own, width)
    outs[4] = outs[4].T
    return tuple(outs)


def solution(mesh):
    in_specs = (
        P(("wide", "narrow"), None),
        P("wide", "narrow", None),
        P("wide", None),
        P("wide"),
        P(),
        P(),
        P(None, None, "narrow"),
        P(None, None, "narrow"),
        P(None, None, "narrow"),
        P(("wide", "narrow"), None),
    )
    out_specs = (
        P(("wide", "narrow"), None),
        P(("wide", "narrow"), None),
        P("wide", "narrow", None),
        P(),
        P(),
        P(None, "wide", "narrow"),
        P(None, "wide", "narrow"),
        P(None, "wide", "narrow"),
        P(None, "wide"),
        P(None, "narrow"),
        P(),
        P(None, "wide"),
        P(None, "narrow"),
    )
    return jax.shard_map(local, mesh=mesh, in_specs=in_specs, out_specs=out_specs, check_vma=False)
```

```python
import functools
import math

import jax
import jax.numpy as jnp
import numpy as np
from jax import lax
from jax.experimental import pallas as pl
from jax.experimental.pallas import tpu as pltpu
from jax.sharding import PartitionSpec as P

BUCKETS = 32
MAX_DIST = 128
EPS = 1e-06
MASKED = -1000000000.0
MESH = pl.DeviceIdType.MESH
BF = jnp.bfloat16
F32 = jnp.float32
VMEM_LIMIT = 64 * 1024 * 1024 - 65536


def bucket_table(seq_length, bucket_count, max_distance):
    exact_count = bucket_count // 2
    bucket_ids = np.zeros((seq_length,), np.int32)
    for distance in range(seq_length):
        if distance < exact_count:
            bucket_ids[distance] = distance
        else:
            scaled_log = (
                math.log(distance / exact_count)
                / math.log(max_distance / exact_count)
                * (bucket_count - exact_count)
            )
            bucket_ids[distance] = min(bucket_count - 1, exact_count + int(scaled_log))
    return bucket_ids


def mm(a, b):
    return jnp.dot(a, b, preferred_element_type=F32)


def mm_nt(a, b):
    return lax.dot_general(a, b, (((1,), (1,)), ((), ())), preferred_element_type=F32)


def mm_tn(a, b):
    return lax.dot_general(a, b, (((0,), (0,)), ((), ())), preferred_element_type=F32)


def inv_rms(v):
    return lax.rsqrt(jnp.mean(v * v, axis=-1, keepdims=True) + EPS)


def norm_back(v, gain, dh):
    r = inv_rms(v)
    gain_part = jnp.sum(dh * (v * r), axis=0, keepdims=True)
    gd = gain * dh
    dv = r * gd - v * (r * r * r) * jnp.mean(gd * v, axis=-1, keepdims=True)
    return gain_part, dv


def soft_cols(scores):
    e = jnp.exp(scores - jnp.max(scores, axis=0, keepdims=True))
    return e * (1.0 / jnp.sum(e, axis=0, keepdims=True))


def self_mask_store(mask_ref, seg_ref, z, rows, span):
    def quarter(k):
        out = jnp.full((1, rows), -1, jnp.int32)
        for kk in range(4):
            out = jnp.where(k == kk, seg_ref[:, kk * rows : (kk + 1) * rows], out)
        return out.astype(F32)

    own = quarter(z)
    keys = jnp.concatenate([quarter(z - 2), quarter(z - 1), own], axis=1)
    keys = jnp.broadcast_to(keys, (128, 3 * rows)).T
    for b in range(2):
        r = lax.broadcasted_iota(jnp.int32, (span, 128), 0)
        c = lax.broadcasted_iota(jnp.int32, (span, 128), 1)
        allowed = (c + 2 * rows >= r) & (keys[b * 128 : b * 128 + span] == own[:, b * 128 : b * 128 + 128])
        mask_ref[b] = jnp.where(allowed, 1.0, 0.0)


def full(shape):
    return pl.BlockSpec(shape, lambda j: (0,) * len(shape))


def once(shape):
    return pl.BlockSpec(shape, lambda j: (0,) * len(shape), pipeline_mode=pl.Buffered(1))


SMEM_SPEC = pl.BlockSpec(memory_space=pltpu.SMEM)


class Place:
    def __init__(self):
        self.w = lax.axis_index("wide")
        self.z = lax.axis_index("narrow")
        s = lax.rem(self.w, 8)
        self.s = s
        self.c = lax.rem(s, 2)
        self.x = lax.rem(s // 2, 2)
        self.y = s // 4
        dc, dx, dy = 1 - 2 * self.c, 2 * (1 - 2 * self.x), 4 * (1 - 2 * self.y)
        self.core_dev = {"wide": self.w + dc}
        self.x_dev = {"wide": self.w + dx}
        self.y_dev = {"wide": self.w + dy}
        self.sx, self.sy, self.sxy = s + dx, s + dy, s + dx + dy
        self.dc = dc

    def quarter(self, k):
        z = self.z
        e0, e3 = 1 - (z + 3) // 4, z // 3
        e1, e2 = (1 - z // 2) * lax.rem(z, 2), (z // 2) * (1 - lax.rem(z, 2))
        return sum(e * row[k] for e, row in zip((e0, e1, e2, e3), RANKS))

    def quarter_of(self, slot):
        return sum(jnp.where(slot == k, self.quarter(k), 0) for k in range(4))

    def narrow_dev(self, k):
        return {"narrow": lax.rem(self.z + k, 4)}

    def devices(self):
        return [self.core_dev, self.x_dev, self.y_dev] + [self.narrow_dev(k) for k in (1, 2, 3)]

    def signal_all(self):
        for dev in self.devices():
            pl.semaphore_signal(pltpu.get_barrier_semaphore(), inc=1, device_id=dev, device_id_type=MESH)

    def wait_all(self):
        pl.semaphore_wait(pltpu.get_barrier_semaphore(), len(self.devices()))

    def barrier(self):
        self.signal_all()
        self.wait_all()


def remote(src, dst, send_sem, recv_sem, dev):
    return pltpu.make_async_remote_copy(
        src_ref=src, dst_ref=dst, send_sem=send_sem, recv_sem=recv_sem, device_id=dev, device_id_type=MESH
    )


RANKS = ((0, 1, 2, 3), (1, 0, 2, 3), (2, 3, 1, 0), (3, 2, 1, 0))
EARLY = 6


def forward_kernel(
    valid_ref, tok_ref, mem_ref, gain_ref, rel_ref, pick_ref, seg_ref, ws_ref, wc_ref, wf_ref,
    w_ref, bd_ref, x1_ref, h1_ref, q_ref, kv_ref, o_ref, bias_ref, mfull_ref, x2_ref, h2_ref, q2_ref, kv2_ref, o2_ref,
    wv, lines, xt, mt, mask_ref, zs, zr, ps, pr, ts, tr, ms, mr, ls, fs, os_,
):
    at = Place()
    z, s = at.z, at.s
    j = pl.program_id(0)
    units = 4
    rows, width = tok_ref.shape
    ext = 3 * rows
    span = 2 * rows + 128
    hw = q_ref.shape[2]
    fw = wf_ref.shape[3]
    heads = hw // 64
    part = rows // 4
    half = width // 16
    mine = pl.ds(2 * s, 2)

    def edge(k):
        return [(d, RANKS[k + d].index(k)) for d in (1, -1) if 0 <= k + d < 4]

    def own_send(u, k, d, rank):
        return remote(
            wv.at[u, 0, mine], wv.at[u, rank, mine], zs.at[u, 0 if d > 0 else 1], zr.at[u, rank], {"narrow": k + d}
        )

    def own_sends(u, act):
        for k in range(4):
            @pl.when(z == k)
            def _():
                for d, rank in edge(k):
                    act(own_send(u, k, d, rank))

    def forwards(u, r, act):
        for k in (1, 2):
            quarter = RANKS[k][r]
            d = 1 if quarter < k else -1
            there = RANKS[k + d].index(quarter)

            @pl.when(z == k)
            def _():
                act(remote(wv.at[u, r, mine], wv.at[u, there, mine], zs.at[u, 1 + r], zr.at[u, there], {"narrow": k + d}))

    def tok_copy(hop, p):
        part_rows = pl.ds(p * part, part)
        src = tok_ref.at[part_rows] if hop == 1 else xt.at[1, part_rows]
        return remote(src, xt.at[2 - hop, part_rows], ts.at[hop - 1, p], tr.at[hop - 1, p], {"narrow": z + 1})

    def tok_senders(hop):
        return z < 3 if hop == 1 else jnp.logical_and(z >= 1, z < 3)

    def tok_send(hop, parts):
        if hop == 2:
            @pl.when(z >= 1)
            def _():
                for p in parts:
                    tok_copy(1, p).wait_recv()

        @pl.when(tok_senders(hop))
        def _():
            for p in parts:
                tok_copy(hop, p).start()

    def mem_copy(i, d):
        k = z - d * i
        src = mem_ref if i == 0 else mt.at[k]
        place = i if d > 0 else 3 + i
        return remote(src, mt.at[k], ms.at[place], mr.at[place], {"narrow": z + d})

    def mem_sends(i, act):
        @pl.when(jnp.logical_and(z >= i, z < 3))
        def _():
            act(mem_copy(i, 1))

        @pl.when(jnp.logical_and(z >= 1, z < 4 - i))
        def _():
            act(mem_copy(i, -1))

    def mem_arrived(i):
        for d in (1, -1):
            @pl.when(z > i if d > 0 else z < 3 - i)
            def _():
                here = mt.at[z - d * (1 + i)]
                place = i if d > 0 else 3 + i
                remote(here, here, ms.at[place], mr.at[place], at.x_dev).wait_recv()

    def piece(u, r, kind):
        first, n, dev = {
            0: (2 * s, 1, at.x_dev), 1: (2 * s + 1, 1, at.x_dev), 2: (2 * at.sy + 1, 1, at.x_dev),
            3: (2 * s + 1, 1, at.y_dev), 4: (2 * s, 1, at.y_dev), 5: (2 * at.sx, 1, at.y_dev),
            6: (2 * s, 2, at.core_dev), 7: (2 * at.sx, 2, at.core_dev),
            8: (2 * at.sy, 2, at.core_dev), 9: (2 * at.sxy, 2, at.core_dev),
        }[kind]
        region = wv.at[u, r, pl.ds(first, n)]
        i = u * 3 + r - 1
        return remote(region, region, ps.at[i, kind], pr.at[i, kind], dev)

    def arrived(u, r, kind):
        first, n = {
            0: (2 * at.sx, 1), 1: (2 * at.sx + 1, 1), 2: (2 * at.sxy + 1, 1),
            3: (2 * at.sy + 1, 1), 4: (2 * at.sy, 1), 5: (2 * at.sxy, 1),
            6: (2 * (s + at.dc), 2), 7: (2 * (at.sx + at.dc), 2),
            8: (2 * (at.sy + at.dc), 2), 9: (2 * (at.sxy + at.dc), 2),
        }[kind]
        region = wv.at[u, r, pl.ds(first, n)]
        i = u * 3 + r - 1
        remote(region, region, ps.at[i, kind], pr.at[i, kind], at.x_dev).wait_recv()

    pieces = [(u, r) for u in range(units) for r in (1, 2, 3)]

    def step0(t):
        if not 0 <= t < len(pieces):
            return
        u, r = pieces[t]
        region = wv.at[u, r, mine]
        remote(region, region, zs.at[u, 0], zr.at[u, r], at.x_dev).wait_recv()
        forwards(u, r, lambda copy: copy.start())
        for kind in (0, 3, 4, 1, 6):
            piece(u, r, kind).start()
        if t == 0:
            tok_send(1, (0, 1))
        if t == 1:
            tok_send(1, (2, 3))
        if t == 2:
            own_sends(2, lambda copy: copy.start())
        if t == 3:
            tok_send(2, (0, 1))
        if t == 4:
            tok_send(2, (2, 3))
        if t == 5:
            own_sends(3, lambda copy: copy.start())
            mem_sends(0, lambda copy: copy.start())
        if t in (7, 9):
            i = (t - 5) // 2
            mem_arrived(i - 1)
            mem_sends(i, lambda copy: copy.start())

    def step1(t):
        if not 0 <= t < len(pieces):
            return
        u, r = pieces[t]
        arrived(u, r, 0)
        piece(u, r, 5).start()
        arrived(u, r, 3)
        piece(u, r, 2).start()
        arrived(u, r, 1)
        piece(u, r, 7).start()
        arrived(u, r, 4)
        piece(u, r, 8).start()

    def step2(t):
        if not 0 <= t < len(pieces):
            return
        u, r = pieces[t]
        arrived(u, r, 5)
        arrived(u, r, 2)
        piece(u, r, 9).start()

    def keep(u, k):
        return pltpu.make_async_copy(wv.at[u, k], w_ref.at[u, k], os_.at[u, k])

    def step3(t):
        if not 0 <= t < len(pieces):
            return
        u, r = pieces[t]
        for kind in (6, 7, 8, 9):
            arrived(u, r, kind)
        keep(u, r).start()

    def attn_loads(i):
        src = (ws_ref, wc_ref)[i]
        return [
            pltpu.make_async_copy(src.at[part], wv.at[i, 0, pl.ds(4 * k, 4)], ls.at[i, k])
            for k, part in enumerate((0, 3, 1, 2))
        ]

    def ffn_loads():
        cut = width - fw
        return [
            pltpu.make_async_copy(wf_ref.at[0], wv.at[2, 0, :, :, 0:fw], fs.at[0]),
            pltpu.make_async_copy(wf_ref.at[1, :, :, 0:cut], wv.at[2, 0, :, :, fw:width], fs.at[1]),
            pltpu.make_async_copy(wf_ref.at[1, :, :, cut:fw], wv.at[3, 0, :, :, 0 : fw - cut], fs.at[2]),
            pltpu.make_async_copy(wf_ref.at[2], wv.at[3, 0, :, :, fw - cut : width], fs.at[3]),
        ]

    @pl.when(j == 0)
    def _():
        at.signal_all()
        for copy in attn_loads(0) + attn_loads(1) + ffn_loads():
            copy.start()
        at.wait_all()
        for copy in attn_loads(0):
            copy.wait()
        own_sends(0, lambda copy: copy.start())
        for copy in attn_loads(1):
            copy.wait()
        own_sends(1, lambda copy: copy.start())
        for copy in ffn_loads():
            copy.wait()
        for u in range(units):
            keep(u, 0).start()
        x = tok_ref[...].astype(F32)
        x1_ref[...] = x
        h1_ref[2 * rows : ext, :] = (x * inv_rms(x) * gain_ref[0:1, :]).astype(BF)
        self_mask_store(mask_ref, seg_ref, z, rows, span)
        lines[...] = lax.dot_general(
            rel_ref[...], pick_ref[...], (((1,), (0,)), ((), ())),
            preferred_element_type=F32, precision=lax.Precision.HIGHEST,
        )
        for k in range(4):
            first = at.quarter(k) * heads
            for hh in range(heads):
                bd_ref[k, hh : hh + 1, :] = lines[pl.ds(first + hh, 1), :]
        for t in range(EARLY):
            step0(t)
            step1(t - 1)
            step2(t - 2)
            step3(t - 3)

        @pl.when(z >= 2)
        def _():
            for p in range(4):
                tok_copy(2, p).wait_recv()

        for t in range(2):
            v = jnp.where(z >= 2 - t, xt[t].astype(F32), 0.0)
            h1_ref[t * rows : (t + 1) * rows, :] = (v * inv_rms(v) * gain_ref[0:1, :]).astype(BF)

    def hook(i, first, last):
        for jj in range(first, last):
            t = EARLY + jj

            @pl.when(j == jj)
            def _():
                if i == 0:
                    step3(t - 3)
                    step0(t)
                if i == 1:
                    step1(t - 1)
                if i == 2:
                    step2(t - 2)

    def flat(u, k, lo, hi):
        return wv[u, k, lo // half : hi // half].reshape(hi - lo, width)

    @pl.when(j < 4)
    def _():
        hook(0, 0, 4)
        q = mm_nt(h1_ref[2 * rows : ext, :], flat(0, j, 0, hw)).astype(BF)
        kv = mm_nt(h1_ref[...], flat(0, j, 2 * hw, 4 * hw)).astype(BF)
        q_ref[0] = q
        kv_ref[0] = kv
        parts = []
        for hh in range(heads):
            line = jnp.broadcast_to(bd_ref[j, hh : hh + 1, :], (256, 512))
            bias = pltpu.roll(line, 0, 1, stride=1, stride_axis=0)[:, 0:128]
            bias_ref[0, hh] = bias
            far = bd_ref[j, hh : hh + 1, 127:128]
            cols = []
            for b in range(2):
                k = kv[b * 128 : b * 128 + span, hh * 64 : hh * 64 + 64]
                v = kv[b * 128 : b * 128 + span, hw + hh * 64 : hw + hh * 64 + 64]
                qb = q[b * 128 : b * 128 + 128, hh * 64 : hh * 64 + 64]
                sc = mm_nt(k, qb)
                sc = jnp.concatenate([sc[: span - 256] + far, sc[span - 256 :] + bias], axis=0)
                sc = jnp.where(mask_ref[b] > 0.5, sc, MASKED)
                cols.append(mm_tn(v, soft_cols(sc).astype(BF)))
            parts.append(jnp.concatenate(cols, axis=1))
            if hh < 2:
                hook(1 + hh, 0, 4)
        o = jnp.concatenate(parts, axis=0).T.astype(BF)
        o_ref[0] = o
        x1_ref[...] += mm(o, flat(0, j, hw, 2 * hw))

    @pl.when(j == 4)
    def _():
        x1 = x1_ref[...]
        x2_ref[...] = x1
        h2_ref[...] = (x1 * inv_rms(x1) * gain_ref[1:2, :]).astype(BF)
        mfull_ref[z] = mem_ref[...]
        mem_arrived(2)
        for k in range(4):
            @pl.when(z != k)
            def _():
                mfull_ref[k] = mt[k]

    @pl.when(j >= 4)
    def _():
        hook(0, 4, 8)
        mem = mfull_ref.shape[0] * mfull_ref.shape[1]
        q = mm_nt(h2_ref[...], flat(1, j - 4, 0, hw)).astype(BF)
        kv = mm_nt(mfull_ref[...].reshape(mem, width), flat(1, j - 4, 2 * hw, 4 * hw)).astype(BF)
        q2_ref[0] = q
        kv2_ref[0] = kv
        allowed = lax.broadcasted_iota(jnp.int32, (mem, rows), 0) < valid_ref[0]
        parts = []
        for hh in range(heads):
            k = kv[:, hh * 64 : hh * 64 + 64]
            v = kv[:, hw + hh * 64 : hw + hh * 64 + 64]
            sc = jnp.where(allowed, mm_nt(k, q[:, hh * 64 : hh * 64 + 64]), MASKED)
            parts.append(mm_tn(v, soft_cols(sc).astype(BF)))
            if hh < 2:
                hook(1 + hh, 4, 8)
        o = jnp.concatenate(parts, axis=0).T.astype(BF)
        o2_ref[0] = o
        x2_ref[...] += mm(o, flat(1, j - 4, hw, 2 * hw))

    @pl.when(j == 7)
    def _():
        for t in range(EARLY + 8, len(pieces) + 3):
            step0(t)
            step1(t - 1)
            step2(t - 2)
            step3(t - 3)
        for u, r in pieces:
            for kind in range(10):
                piece(u, r, kind).wait_send()
            forwards(u, r, lambda copy: copy.wait_send())
        for u in range(units):
            own_sends(u, lambda copy: copy.wait_send())
            for k in range(4):
                keep(u, k).wait()
        for hop in (1, 2):
            @pl.when(tok_senders(hop))
            def _():
                for p in range(4):
                    tok_copy(hop, p).wait_send()
        for i in range(3):
            mem_sends(i, lambda copy: copy.wait_send())


def forward(valid_rows, tokens, memory, gains, rel, pick, seg, ws, wc, wf):
    rows, width = tokens.shape
    mem_own = memory.shape[0]
    hw = 4 * ws.shape[2]
    heads = hw // 64
    ext = 3 * rows
    mem = 4 * mem_own
    half = width // 16
    any_spec = pl.BlockSpec(memory_space=pl.ANY)
    dma = pltpu.SemaphoreType.DMA

    def early(shape):
        return pl.BlockSpec((1,) + shape, lambda j: (jnp.minimum(j, 3),) + (0,) * len(shape))

    def late(shape):
        return pl.BlockSpec((1,) + shape, lambda j: (jnp.maximum(j - 4, 0),) + (0,) * len(shape))

    out = [
        ((4, 4, 16, half, width), BF, any_spec), ((4, heads, 512), F32, full((4, heads, 512))),
        ((rows, width), F32, full((rows, width))), ((ext, width), BF, full((ext, width))),
        ((4, rows, hw), BF, early((rows, hw))), ((4, ext, 2 * hw), BF, early((ext, 2 * hw))),
        ((4, rows, hw), BF, early((rows, hw))), ((4, heads, 256, 128), F32, early((heads, 256, 128))),
        ((4, mem_own, width), BF, full((4, mem_own, width))),
        ((rows, width), F32, full((rows, width))), ((rows, width), BF, full((rows, width))),
        ((4, rows, hw), BF, late((rows, hw))), ((4, mem, 2 * hw), BF, late((mem, 2 * hw))),
        ((4, rows, hw), BF, late((rows, hw))),
    ]
    return pl.pallas_call(
        forward_kernel,
        name="forward",
        grid=(8,),
        in_specs=[
            SMEM_SPEC, full((rows, width)), full((mem_own, width)), full((3, width)),
            full(rel.shape), full(pick.shape), full(seg.shape), any_spec, any_spec, any_spec,
        ],
        out_specs=[spec for _, _, spec in out],
        out_shape=[jax.ShapeDtypeStruct(shape, dtype) for shape, dtype, _ in out],
        scratch_shapes=[
            pltpu.VMEM((4, 4, 16, half, width), BF), pltpu.VMEM((4 * heads, 512), F32),
            pltpu.VMEM((2, rows, width), BF), pltpu.VMEM((4, mem_own, width), BF),
            pltpu.VMEM((2, 2 * rows + 128, 128), F32),
            dma((4, 5)), dma((4, 4)), dma((12, 10)), dma((12, 10)),
            dma((2, 4)), dma((2, 4)), dma((6,)), dma((6,)), dma((2, 4)), dma((4,)), dma((4, 4)),
        ],
        compiler_params=pltpu.CompilerParams(
            collective_id=0, has_side_effects=True, vmem_limit_bytes=VMEM_LIMIT, dimension_semantics=("arbitrary",)
        ),
    )(valid_rows, tokens, memory, gains, rel, pick, seg, ws, wc, wf)


CHUNKS = [(2 + i % 2, i // 2) for i in range(8)] + [(1, i) for i in range(4)] + [(0, i) for i in range(4)]
HELD = 12
TICKS = [(1, 0), (2, 0), (3, 0), (4, 1), (5, 1), (6, 1), (7, 1), (8, 0), (8, 2), (9, 1), (10, 0), (10, 2), (11, 1)]


def backward_kernel(
    valid_ref, x2_ref, cot_ref, x1_ref, mem_ref, h2_ref, h1_ref, tok_ref, gain_ref, bd_ref, seg_ref, pick_ref,
    w_ref, q2_ref, kv2_ref, o2_ref, q1_ref, kv1_ref, o1_ref, bias_ref,
    out_ref, f_ref, tg_ref, mg_ref, small_ref,
    g, wbuf, acc, act_in, res, gsum_ref, rel_ref, do_ref, dqt_ref, dkv_ref, mask_ref, flip_ref, dxo, dmo, rc, xr, yr, xr2, yr2, zb, dxr, dmr,
    wsem, cs, cr, xs, xrs, ys, yrs, x2s, x2r, y2s, y2r, zs, zr, dxs, dxrs, dms, dmrs,
):
    at = Place()
    z = at.z
    j = pl.program_id(0)
    rows, width = x2_ref.shape
    mem = mem_ref.shape[0]
    ext = 3 * rows
    span = 2 * rows + 128
    hw = q1_ref.shape[2]
    heads = hw // 64
    fw = wbuf.shape[2] * 2 // 3
    own_rows = g.shape[3]
    half = own_rows // 2
    n = len(CHUNKS)
    lo, hi = pl.ds(0, half), pl.ds(half, half)
    yx = 2 * at.y + at.x
    top, bottom = pl.ds(0, rows), pl.ds(2 * rows, rows)

    def w_load(unit, slot, k):
        return pltpu.make_async_copy(w_ref.at[unit, slot], wbuf.at[k], wsem.at[k])

    def held(i):
        return g.at[i % HELD]

    def add(ref, other):
        ref[...] = ref[...] + other[...]

    def core_send(i):
        return remote(held(i).at[:, pl.ds(1 - at.c, 1)], rc.at[i], cs.at[i], cr.at[i], at.core_dev)

    def x_send(i, yb):
        src = held(i).at[2 * yb + 1 - at.x, at.c, lo]
        return remote(src, xr.at[i, yb], xs.at[i, yb], xrs.at[i, yb], at.x_dev)

    def y_send(i, xb):
        src = held(i).at[2 * (1 - at.y) + xb, at.c, hi]
        return remote(src, yr.at[i, xb], ys.at[i, xb], yrs.at[i, xb], at.y_dev)

    def y2_send(i):
        return remote(held(i).at[2 * (1 - at.y) + at.x, at.c, lo], yr2.at[i], y2s.at[i], y2r.at[i], at.y_dev)

    def x2_send(i):
        return remote(held(i).at[2 * at.y + 1 - at.x, at.c, hi], xr2.at[i], x2s.at[i], x2r.at[i], at.x_dev)

    d = 1 - 2 * (z // 2)
    is_end = jnp.logical_or(z == 0, z == 3)
    is_inner = jnp.logical_or(z == 1, z == 2)

    def z_send(i, dst, step):
        unit = CHUNKS[i][0]
        return remote(held(i).at[yx, at.c], zb.at[unit, dst], zs.at[i], zr.at[unit, dst], {"narrow": z + step})

    def z_wait(i, k):
        unit = CHUNKS[i][0]
        remote(zb.at[unit, k], zb.at[unit, k], zs.at[i], zr.at[unit, k], at.x_dev).wait_recv()

    def step_b(i):
        core_send(i).wait_recv()
        add(held(i).at[:, pl.ds(at.c, 1)], rc.at[i])
        for b in range(2):
            x_send(i, b).start()
            y_send(i, b).start()

    def step_c(i):
        for b in range(2):
            x_send(i, b).wait_recv()
            y_send(i, b).wait_recv()
            add(held(i).at[2 * b + at.x, at.c, lo], xr.at[i, b])
            add(held(i).at[2 * at.y + b, at.c, hi], yr.at[i, b])
        y2_send(i).start()
        x2_send(i).start()

    def step_d(i):
        y2_send(i).wait_recv()
        add(held(i).at[yx, at.c, lo], yr2.at[i])
        x2_send(i).wait_recv()
        add(held(i).at[yx, at.c, hi], xr2.at[i])

    def step_e(i):
        @pl.when(is_end)
        def _():
            if CHUNKS[i][1] < 3:
                z_send(i, CHUNKS[i][1], d).start()

    def step_f(i):
        unit, s = CHUNKS[i]

        @pl.when(is_inner)
        def _():
            if s < 2:
                z_wait(i, s)
                add(held(i).at[yx, at.c], zb.at[unit, s])
                z_send(i, 3 + s, d).start()
            if s == 2:
                z_wait(i, 3)
                add(held(i).at[yx, at.c], zb.at[unit, 3])
                z_send(i, 2, -d).start()
            if s == 3:
                z_wait(i, 2)
                z_wait(i, 4)
                f_ref[unit] = (
                    held(i)[yx, at.c].astype(F32) + zb[unit, 2].astype(F32) + zb[unit, 4].astype(F32)
                )

        if s == 3:
            @pl.when(is_end)
            def _():
                z_wait(i, 2)
                f_ref[unit] = held(i)[yx, at.c].astype(F32) + zb[unit, 2].astype(F32)

    def sent(i):
        core_send(i).wait_send()
        for b in range(2):
            x_send(i, b).wait_send()
            y_send(i, b).wait_send()
        y2_send(i).wait_send()
        x2_send(i).wait_send()
        if CHUNKS[i][1] < 3:
            z_send(i, 0, d).wait_send()

    def tick(t):
        for k, step in enumerate((step_b, step_c, step_d, step_e, step_f)):
            if 0 <= t - k < n:
                step(t - k)

    def hook(place, first, last):
        for t, (jj, p) in enumerate(TICKS):
            if p == place and first <= jj < last:
                @pl.when(j == jj)
                def _():
                    tick(t)

    def dx_send(t):
        return remote(dxo.at[t], dxr.at[t], dxs.at[t], dxrs.at[t], {"narrow": z - 1})

    def dm_send(k):
        return remote(dmo.at[lax.rem(z + k, 4)], dmr.at[k - 1], dms.at[k - 1], dmrs.at[k - 1], at.narrow_dev(k))

    @pl.when(j == 0)
    def _():
        for b in range(2):
            w_load(2 + b, 3, b).start()
        at.signal_all()
        x2 = x2_ref[...]
        acc[0:rows, :] = x2
        acc[rows : 2 * rows, :] = jnp.zeros((rows, width), F32)
        act_in[...] = (x2 * inv_rms(x2) * gain_ref[2:3, :]).astype(BF)

    @pl.when(j < 4)
    def _():
        k = 2 * lax.rem(j, 2)
        for b in range(2):
            w_load(2 + b, 3 - j, k + b).wait()

        @pl.when(j < 3)
        def _():
            for b in range(2):
                w_load(2 + b, 2 - j, 2 - k + b).start()

        @pl.when(j == 3)
        def _():
            w_load(1, 3, 0).start()

        @pl.when(j == 0)
        def _():
            at.wait_all()

        hook(0, 0, 4)
        h3 = act_in[...]
        df = cot_ref[...]
        wg = wbuf[k, :, 0:fw]
        wu = jnp.concatenate([wbuf[k, :, fw:], wbuf[k + 1, :, 0 : fw // 2]], axis=1)
        wd = wbuf[k + 1, :, fw // 2 :]
        gate = mm(h3, wg)
        up = mm(h3, wu)
        c0 = math.sqrt(2.0 / math.pi)
        gate2 = gate * gate
        t = jnp.tanh(c0 * (gate + 0.044715 * gate2 * gate))
        part = 0.5 * (1.0 + t)
        gelu = gate * part
        slope = part + 0.5 * gate * (1.0 - t * t) * (c0 * (1.0 + 3.0 * 0.044715 * gate2))
        act = (gelu * up).astype(BF)
        acc[0:rows, :] += mm_nt(act, wd)
        da = mm(df, wd)
        dgate = (da * up * slope).astype(BF)
        dup = (da * gelu).astype(BF)
        dgu = jnp.concatenate([dgate, dup], axis=1)
        ggu = mm_tn(h3, dgu).astype(BF)
        blocks = (4, 2, own_rows)
        g[2 * j] = ggu[:, 0 : fw * 3 // 2].reshape(blocks + (width,))
        g[2 * j + 1, :, :, :, 0 : fw // 2] = ggu[:, fw * 3 // 2 :].reshape(blocks + (fw // 2,))
        g[2 * j + 1, :, :, :, fw // 2 :] = mm_tn(df, act).astype(BF).reshape(blocks + (fw,))
        acc[rows : 2 * rows, :] += mm_nt(dgate, wg) + mm_nt(dup, wu)
        for jj in range(4):
            @pl.when(j == jj)
            def _():
                core_send(2 * jj).start()
                core_send(2 * jj + 1).start()

    @pl.when(j == 3)
    def _():
        out_ref[...] = acc[0:rows, :].astype(BF)
        gain_part, dv = norm_back(x2_ref[...], gain_ref[2:3, :], acc[rows : 2 * rows, :])
        gsum_ref[16:24, :] = jnp.broadcast_to(gain_part, (8, width))
        g2 = cot_ref[...].astype(F32) + dv
        res[...] = g2
        act_in[...] = g2.astype(BF)
        acc[...] = jnp.zeros_like(acc)

    @pl.when(jnp.logical_and(j >= 4, j < 8))
    def _():
        k0 = j - 4
        w_load(1, 7 - j, k0).wait()

        @pl.when(j < 7)
        def _():
            w_load(1, 6 - j, k0 + 1).start()

        @pl.when(j == 7)
        def _():
            w_load(0, 3, 0).start()

        do_ref[...] = mm_nt(act_in[...], wbuf[k0, hw : 2 * hw, :]).astype(BF)
        for hh in range(heads):
            h_cols, v_cols = slice(hh * 64, hh * 64 + 64), slice(hw + hh * 64, hw + hh * 64 + 64)
            k = kv2_ref[0, :, h_cols]
            v = kv2_ref[0, :, v_cols]
            qh = q2_ref[0, :, h_cols]
            doh = do_ref[:, h_cols]
            allowed = lax.broadcasted_iota(jnp.int32, (mem, rows), 0) < valid_ref[0]
            p = soft_cols(jnp.where(allowed, mm_nt(k, qh), MASKED))
            dp = mm_nt(v, doh)
            ds = (p * (dp - jnp.sum(p * dp, axis=0, keepdims=True))).astype(BF)
            dkv_ref[0:mem, v_cols] = mm(p.astype(BF), doh).astype(BF)
            dkv_ref[0:mem, h_cols] = mm(ds, qh).astype(BF)
            dqt_ref[h_cols, :] = mm_tn(k, ds)
            hook(hh, 4, 8)
        dc = act_in[...]
        dq = dqt_ref[...].T.astype(BF)
        dkv = dkv_ref[0:mem, :]
        zero = jnp.zeros((rows, hw), BF)
        left = jnp.concatenate([h2_ref[...], dc], axis=0)
        right = jnp.concatenate(
            [jnp.concatenate([dq, zero], axis=1), jnp.concatenate([zero, o2_ref[0]], axis=1)], axis=0
        )
        blocks = (4, 2, own_rows, 2 * hw)
        g[4 + j, :, :, :, 0 : 2 * hw] = mm_tn(left, right).astype(BF).reshape(blocks)
        g[4 + j, :, :, :, 2 * hw : 4 * hw] = mm_tn(mem_ref[...], dkv).astype(BF).reshape(blocks)
        for jj in range(4, 8):
            @pl.when(j == jj)
            def _():
                core_send(4 + jj).start()
        acc[0:rows, :] += mm(dq, wbuf[k0, 0:hw, :])
        acc[rows : rows + mem, :] += mm(dkv, wbuf[k0, 2 * hw : 4 * hw, :])

    @pl.when(j == 7)
    def _():
        for k in range(4):
            dmo[k] = acc[rows + k * (mem // 4) : rows + (k + 1) * (mem // 4), :].astype(BF)
        for k in (1, 2, 3):
            dm_send(k).start()
        gain_part, dv = norm_back(x1_ref[...], gain_ref[1:2, :], acc[0:rows, :])
        gsum_ref[8:16, :] = jnp.broadcast_to(gain_part, (8, width))
        g1 = res[...] + dv
        res[...] = g1
        act_in[...] = g1.astype(BF)
        acc[...] = jnp.zeros_like(acc)
        self_mask_store(mask_ref, seg_ref, z, rows, span)
        rel_ref[...] = jnp.zeros_like(rel_ref)
        r = lax.broadcasted_iota(jnp.int32, (256, 256), 0)
        c = lax.broadcasted_iota(jnp.int32, (256, 256), 1)
        flip_ref[...] = jnp.where(r + c == 255, 1.0, 0.0).astype(BF)

    @pl.when(j >= 8)
    def _():
        k0 = j - 8
        w_load(0, 11 - j, k0).wait()

        @pl.when(j < 11)
        def _():
            w_load(0, 10 - j, k0 + 1).start()

        do_ref[...] = mm_nt(act_in[...], wbuf[k0, hw : 2 * hw, :]).astype(BF)
        for hh in range(heads):
            h_cols, v_cols = slice(hh * 64, hh * 64 + 64), slice(hw + hh * 64, hw + hh * 64 + 64)
            far = bd_ref[11 - j, hh : hh + 1, 127:128]
            dq_cols, dks, dvs = [], [], []
            band = jnp.zeros((256, 128), F32)
            total = jnp.zeros((1, 128), F32)
            for b in range(2):
                k = kv1_ref[0, b * 128 : b * 128 + span, h_cols]
                v = kv1_ref[0, b * 128 : b * 128 + span, v_cols]
                qb = q1_ref[0, b * 128 : b * 128 + 128, h_cols]
                dob = do_ref[b * 128 : b * 128 + 128, h_cols]
                s = mm_nt(k, qb)
                s = jnp.concatenate([s[: span - 256] + far, s[span - 256 :] + bias_ref[0, hh]], axis=0)
                s = jnp.where(mask_ref[b] > 0.5, s, MASKED)
                p = soft_cols(s)
                dp = mm_nt(v, dob)
                ds = (p * (dp - jnp.sum(p * dp, axis=0, keepdims=True))).astype(BF)
                dvs.append(mm(p.astype(BF), dob))
                dks.append(mm(ds, qb))
                dq_cols.append(mm_tn(k, ds))
                band = band + mm(flip_ref[...], ds[span - 256 :])
                total = total + jnp.sum(ds[: span - 256].astype(F32), axis=0, keepdims=True)
            gap = jnp.zeros((128, 64), F32)
            dk = jnp.concatenate([dks[0], gap], 0) + jnp.concatenate([gap, dks[1]], 0)
            dv = jnp.concatenate([dvs[0], gap], 0) + jnp.concatenate([gap, dvs[1]], 0)
            dkv_ref[:, h_cols] = dk.astype(BF)
            dkv_ref[:, v_cols] = dv.astype(BF)
            dqt_ref[h_cols, :] = jnp.concatenate(dq_cols, axis=1)
            wide_band = jnp.concatenate([band, jnp.zeros((256, 384), F32)], axis=1)
            aligned = pltpu.roll(wide_band, 0, 1, stride=1, stride_axis=0)
            line = jnp.sum(aligned, axis=0, keepdims=True)
            lane = lax.broadcasted_iota(jnp.int32, (1, 512), 1)
            far_sum = jnp.sum(total, axis=1, keepdims=True)
            rel_ref[pl.ds(at.quarter_of(11 - j) * heads + hh, 1), :] = jnp.where(lane == 511, far_sum, line)
            hook(hh, 8, 12)
        da = act_in[...]
        dq = dqt_ref[...].T.astype(BF)
        dkv = dkv_ref[...]
        zero = jnp.zeros((rows, hw), BF)
        left = jnp.concatenate([h1_ref[2 * rows : ext, :], da], axis=0)
        right = jnp.concatenate(
            [jnp.concatenate([dq, zero], axis=1), jnp.concatenate([zero, o1_ref[0]], axis=1)], axis=0
        )
        for jj in range(8, 12):
            @pl.when(j == jj)
            def _():
                sent(jj - 8)
        blocks = (4, 2, own_rows, 2 * hw)
        g[j - 8, :, :, :, 0 : 2 * hw] = mm_tn(left, right).astype(BF).reshape(blocks)
        g[j - 8, :, :, :, 2 * hw : 4 * hw] = mm_tn(h1_ref[...], dkv).astype(BF).reshape(blocks)
        for jj in range(8, 12):
            @pl.when(j == jj)
            def _():
                core_send(4 + jj).start()
        acc[...] += mm(dkv, wbuf[k0, 2 * hw : 4 * hw, :])
        acc[2 * rows : ext, :] += mm(dq, wbuf[k0, 0:hw, :])

    @pl.when(j == 11)
    def _():
        for t in range(2):
            dxo[t] = acc[t * rows : (t + 1) * rows, :].astype(BF)

        @pl.when(z >= 2)
        def _():
            dx_send(0).start()

        @pl.when(z == 3)
        def _():
            dx_send(1).start()
        last = n + 4
        for t in range(len(TICKS), last):
            tick(t)
            if t == len(TICKS):
                mg_ref[...] = dmo[z].astype(F32)
                for k in (1, 2, 3):
                    dm_send(k).wait_recv()
                    mg_ref[...] += dmr[k - 1].astype(F32)
            if t == len(TICKS) + 1:
                @pl.when(is_inner)
                def _():
                    dx_send(0).wait_recv()
                    add(dxo.at[1], dxr.at[0])
                    dx_send(1).start()
            if t == len(TICKS) + 3:
                @pl.when(z < 3)
                def _():
                    dx_send(1).wait_recv()
                    acc[2 * rows : ext, :] += dxr[1].astype(F32)
                gain_part, dv = norm_back(tok_ref[...].astype(F32), gain_ref[0:1, :], acc[2 * rows : ext, :])
                rel = lax.dot_general(
                    rel_ref[...], pick_ref[...], (((1,), (0,)), ((), ())),
                    preferred_element_type=F32, precision=lax.Precision.HIGHEST,
                )
                gains = [gain_part, gsum_ref[8:9, :], gsum_ref[16:17, :], jnp.zeros((5, width), F32)]
                small_ref[...] = jnp.concatenate([jnp.concatenate(gains, axis=0), rel[0:8], rel[8:16]], axis=1)
                tg_ref[...] = res[...] + dv
        for i in range(n - HELD, n):
            sent(i)
        for t in range(2):
            @pl.when(z >= 2 - t)
            def _():
                dx_send(t).wait_send()
        for k in (1, 2, 3):
            dm_send(k).wait_send()


def backward(
    valid_rows, x2, cot, x1, mem_full, h2, h1, tokens, gains, bias_line, seg, pick,
    weights, q2, kv2, o2, q1, kv1, o1, bias,
):
    rows, width = x2.shape
    mem = mem_full.shape[0]
    hw = q1.shape[2]
    ext = 3 * rows
    own = width // 8
    half = own // 2
    n = len(CHUNKS)
    dma = pltpu.SemaphoreType.DMA

    def slot(last, a):
        shape = a.shape[1:]
        return pl.BlockSpec(
            (1,) + shape, lambda j: (jnp.clip(last - j, 0, 3),) + (0,) * len(shape)
        )

    out = [
        ((rows, width), BF), ((4, own, width), F32), ((rows, width), F32), ((mem // 4, width), F32),
        ((8, width + 256), F32),
    ]
    shapes = [jax.ShapeDtypeStruct(s, d) for s, d in out]
    return pl.pallas_call(
        backward_kernel,
        name="backward",
        grid=(12,),
        in_specs=[
            SMEM_SPEC, *[once(a.shape) for a in (x2, cot, x1, mem_full, h2, h1, tokens)],
            full(gains.shape), full(bias_line.shape), full(seg.shape), full(pick.shape),
            pl.BlockSpec(memory_space=pl.ANY),
            slot(7, q2), slot(7, kv2), slot(7, o2), slot(11, q1), slot(11, kv1), slot(11, o1), slot(11, bias),
        ],
        out_specs=[once(s) for s, _ in out],
        out_shape=shapes,
        scratch_shapes=[
            pltpu.VMEM((HELD, 4, 2, own, width), BF), pltpu.VMEM((4, width, width), BF),
            pltpu.VMEM((ext, width), F32), pltpu.VMEM((rows, width), BF), pltpu.VMEM((rows, width), F32),
            pltpu.VMEM((24, width), F32), pltpu.VMEM((16, 512), F32),
            pltpu.VMEM((rows, hw), BF), pltpu.VMEM((hw, rows), F32), pltpu.VMEM((ext, 2 * hw), BF),
            pltpu.VMEM((2, 2 * rows + 128, 128), F32), pltpu.VMEM((256, 256), BF),
            pltpu.VMEM((2, rows, width), BF), pltpu.VMEM((4, mem // 4, width), BF),
            pltpu.VMEM((n, 4, 1, own, width), BF),
            pltpu.VMEM((n, 2, half, width), BF), pltpu.VMEM((n, 2, half, width), BF),
            pltpu.VMEM((n, half, width), BF), pltpu.VMEM((n, half, width), BF),
            pltpu.VMEM((4, 5, own, width), BF),
            pltpu.VMEM((2, rows, width), BF), pltpu.VMEM((3, mem // 4, width), BF),
            dma((4,)), dma((n,)), dma((n,)),
            dma((n, 2)), dma((n, 2)), dma((n, 2)), dma((n, 2)),
            dma((n,)), dma((n,)), dma((n,)), dma((n,)),
            dma((n,)), dma((4, 5)),
            dma((2,)), dma((2,)), dma((3,)), dma((3,)),
        ],
        compiler_params=pltpu.CompilerParams(
            collective_id=1, has_side_effects=True, vmem_limit_bytes=VMEM_LIMIT, dimension_semantics=("arbitrary",)
        ),
    )(
        valid_rows, x2, cot, x1, mem_full, h2, h1, tokens, gains, bias_line, seg, pick,
        weights, q2, kv2, o2, q1, kv1, o1, bias,
    )


def stats_kernel(
    wide_count, f_ref, a_ref,
    rsum_ref, csum_ref, asum_ref, pcol_ref,
    rall, aall, call, ball, rs, rr, as_, ar, cs, cr, bs, br, ps, pr,
):
    w = lax.axis_index("wide")
    z = lax.axis_index("narrow")
    own = f_ref.shape[1]
    width = f_ref.shape[2]
    sem = pltpu.get_barrier_semaphore()

    def peer(k):
        return {"narrow": lax.rem(z + k, 4)}

    def wide_peer(k):
        return {"wide": lax.rem(w + k, wide_count)}

    def wide_loop(fn):
        if wide_count <= 8:
            for k in range(1, wide_count):
                fn(k)
        else:
            pl.loop(1, wide_count)(fn)

    for k in (1, 2, 3):
        pl.semaphore_signal(sem, inc=1, device_id=peer(k), device_id_type=MESH)
    wide_loop(lambda k: pl.semaphore_signal(sem, inc=1, device_id=wide_peer(k), device_id_type=MESH))

    lane = lax.broadcasted_iota(jnp.int32, (8, width), 1)
    row = lax.broadcasted_iota(jnp.int32, (8, width), 0)
    quarter = width // 4
    third = 2 * width // 3

    def sums(pick, sq):
        got = lax.dot_general(
            jnp.where(pick, 1.0, 0.0), sq, (((1,), (1,)), ((), ())),
            preferred_element_type=F32, precision=lax.Precision.HIGHEST,
        )
        pad = jnp.zeros((8, 128 - own), F32)
        return jnp.concatenate([got, pad], axis=1)

    sq = [f_ref[i] * f_ref[i] for i in range(4)]
    rall[z, 0:8] = sums(lane // quarter == row, sq[0])
    rall[z, 8:16] = sums(lane // quarter == row, sq[1])
    rall[z, 16:24] = sums(lane // third == row, sq[2]) + sums((lane + width) // third == row, sq[3])
    aall[z] = a_ref[...]
    call[w] = jnp.concatenate(
        [jnp.sum(v, axis=0, keepdims=True) for v in sq] + [jnp.zeros((4, width), F32)], axis=0
    )
    pl.semaphore_wait(sem, 3 + wide_count - 1)

    def r_send(k):
        return remote(rall.at[z], rall.at[z], rs.at[k - 1], rr.at[k - 1], peer(k))

    def a_send(k):
        return remote(aall.at[z], aall.at[z], as_.at[k - 1], ar.at[k - 1], peer(k))

    def c_send(k):
        return remote(call.at[w], call.at[w], cs.at[k - 1], cr.at[k - 1], wide_peer(k))

    def p_send(k):
        return remote(pcol_ref.at[z], pcol_ref.at[z], ps.at[k - 1], pr.at[k - 1], peer(k))

    def b_send(k):
        return remote(ball.at[w], ball.at[w], bs.at[k - 1], br.at[k - 1], wide_peer(k))

    for k in (1, 2, 3):
        r_send(k).start()
        a_send(k).start()
    wide_loop(lambda k: c_send(k).start())

    for k in (1, 2, 3):
        frm = lax.rem(z + 4 - k, 4)
        remote(rall.at[frm], rall.at[frm], rs.at[k - 1], rr.at[k - 1], peer(k)).wait_recv()
        remote(aall.at[frm], aall.at[frm], as_.at[k - 1], ar.at[k - 1], peer(k)).wait_recv()
    rsum = rall[0] + rall[1] + rall[2] + rall[3]
    rsum_ref[...] = rsum
    asum = aall[0] + aall[1] + aall[2] + aall[3]
    zero = jnp.zeros((8, width - 128), F32)
    rows = jnp.concatenate([rsum[0:8], zero], axis=1)
    more = jnp.concatenate([rsum[8:16], zero], axis=1)
    shift = own * w
    left = jnp.concatenate(
        [
            asum[0:3, 0:width],
            pltpu.roll(rows, shift, 1)[1:2], pltpu.roll(more, shift, 1)[1:2],
            jnp.zeros((3, width), F32),
        ],
        axis=0,
    )
    ball[w] = jnp.concatenate([left, asum[:, width:]], axis=1)
    wide_loop(lambda k: b_send(k).start())

    def c_wait(k):
        frm = lax.rem(w + wide_count - k, wide_count)
        remote(call.at[frm], call.at[frm], cs.at[k - 1], cr.at[k - 1], wide_peer(k)).wait_recv()

    wide_loop(c_wait)
    csum = lax.fori_loop(1, wide_count, lambda i, v: v + call[i], call[0])
    csum_ref[...] = csum
    pcol_ref[z] = csum
    for k in (1, 2, 3):
        p_send(k).start()

    def b_wait(k):
        frm = lax.rem(w + wide_count - k, wide_count)
        remote(ball.at[frm], ball.at[frm], bs.at[k - 1], br.at[k - 1], wide_peer(k)).wait_recv()

    wide_loop(b_wait)
    asum_ref[...] = lax.fori_loop(1, wide_count, lambda i, v: v + ball[i], ball[0])
    for k in (1, 2, 3):
        frm = lax.rem(z + 4 - k, 4)
        remote(pcol_ref.at[frm], pcol_ref.at[frm], ps.at[k - 1], pr.at[k - 1], peer(k)).wait_recv()
    for k in (1, 2, 3):
        r_send(k).wait_send()
        a_send(k).wait_send()
        p_send(k).wait_send()

    def sent(k):
        c_send(k).wait_send()
        b_send(k).wait_send()

    wide_loop(sent)


def reduce_stats(wide_count, final, small):
    width = final.shape[2]
    vmem = pl.BlockSpec(memory_space=pltpu.VMEM)
    dma = pltpu.SemaphoreType.DMA
    return pl.pallas_call(
        functools.partial(stats_kernel, wide_count),
        name="stats",
        in_specs=[vmem] * 2,
        out_specs=[vmem] * 4,
        out_shape=[
            jax.ShapeDtypeStruct((24, 128), F32),
            jax.ShapeDtypeStruct((8, width), F32),
            jax.ShapeDtypeStruct(small.shape, F32),
            jax.ShapeDtypeStruct((4, 8, width), F32),
        ],
        scratch_shapes=[
            pltpu.VMEM((4, 24, 128), F32), pltpu.VMEM((4,) + small.shape, F32),
            pltpu.VMEM((wide_count, 8, width), F32), pltpu.VMEM((wide_count,) + small.shape, F32),
            dma((3,)), dma((3,)), dma((3,)), dma((3,)),
            dma((wide_count - 1,)), dma((wide_count - 1,)), dma((wide_count - 1,)), dma((wide_count - 1,)),
            dma((3,)), dma((3,)),
        ],
        compiler_params=pltpu.CompilerParams(collective_id=2, has_side_effects=True),
    )(final, small)


def finish_kernel(
    out_ref, tg_ref, mg_ref, f_ref, rsum_ref, csum_ref, asum_ref, pcol_ref,
    out_o, tg_o, mg_o, gains_o, rel_o, self_o, cross_o, ffn_o, arow_o, acol_o, proj_o, frow_o, fcol_o,
):
    own, width = f_ref.shape[1:]
    hw = self_o.shape[2]
    fw = ffn_o.shape[2]
    out_o[...] = out_ref[...]
    tg_o[...] = tg_ref[...]
    mg_o[...] = mg_ref[...]
    gains_o[...] = asum_ref[0:3, 0:width]
    rel = jnp.concatenate([asum_ref[:, width : width + 128], asum_ref[:, width + 128 : width + 256]], axis=0)
    rel_o[...] = rel[0 : rel_o.shape[0], 0 : rel_o.shape[1]]
    for ref, i in ((self_o, 0), (cross_o, 1)):
        for m, part in enumerate((0, 2, 3, 1)):
            ref[m] = f_ref[i, :, part * hw : (part + 1) * hw]
    cut = width - fw
    ffn_o[0] = f_ref[2, :, 0:fw]
    ffn_o[1, :, 0:cut] = f_ref[2, :, fw:width]
    ffn_o[1, :, cut:fw] = f_ref[3, :, 0 : fw - cut]
    ffn_o[2] = f_ref[3, :, fw - cut : width]
    rsum = rsum_ref[...]
    arow = jnp.concatenate([rsum[0:1], rsum[2:4], rsum[8:9], rsum[10:12]], axis=0)
    arow_o[...] = arow[:, 0:own] * (1.0 / width)
    frow_o[...] = rsum[16:19, 0:own] * (1.0 / (4 * fw))
    scale = 1.0 / width
    for i in range(2):
        for m, part in enumerate((0, 2, 3)):
            acol_o[3 * i + m : 3 * i + m + 1, :] = csum_ref[i : i + 1, part * hw : (part + 1) * hw] * scale
    fcol_o[0:1, :] = csum_ref[2:3, 0:fw] * scale
    fcol_o[1:2, 0:cut] = csum_ref[2:3, fw:width] * scale
    fcol_o[1:2, cut:fw] = csum_ref[3:4, 0 : fw - cut] * scale
    fcol_o[2:3, :] = csum_ref[3:4, fw - cut : width] * scale
    for i in range(2):
        cols = jnp.concatenate([pcol_ref[k, i : i + 1, hw : 2 * hw] for k in range(4)], axis=1)
        proj_o[i : i + 1, 0:width] = asum_ref[3 + i : 4 + i, 0:width] * scale
        proj_o[i : i + 1, width : 2 * width] = cols * scale


def finish(shapes, *args):
    vmem = pl.BlockSpec(memory_space=pltpu.VMEM)
    return pl.pallas_call(
        finish_kernel,
        name="finish",
        in_specs=[vmem] * len(args),
        out_specs=[vmem] * len(shapes),
        out_shape=[jax.ShapeDtypeStruct(s, d) for s, d in shapes],
    )(*args)


def local(
    tokens, memory, segments, valid_rows, norm_gains, rel_table,
    self_weights, cross_weights, ffn_weights, cotangent,
):
    wide_count = lax.axis_size("wide")
    assert lax.axis_size("narrow") == 4 and wide_count % 8 == 0 and segments.shape[0] == 1
    rows, width = tokens.shape
    mem_own = memory.shape[1]
    mem_len = 4 * mem_own
    hw = self_weights.shape[2]
    fw = ffn_weights.shape[2]
    heads = rel_table.shape[1]
    groups = wide_count // 8
    eighth = width // 8

    buckets = bucket_table(1024, BUCKETS, MAX_DIST)
    lanes = np.arange(512)
    at_lane = np.where(lanes < 128, 128 + lanes, np.maximum(lanes - 384, 0))
    pick = jnp.asarray((buckets[at_lane][None, :] == np.arange(BUCKETS)[:, None]).astype(np.float32))
    rel_pick = jnp.asarray(
        (buckets[np.maximum(lanes - 127, 0)][:, None] == np.arange(128)[None, :]).astype(np.float32)
    )

    half = width // 16
    weights, bias_line, x1, h1, q1, kv1, o1, bias, mem_full, x2, h2, q2, kv2, o2 = forward(
        valid_rows, tokens, memory[0], norm_gains, rel_table.T, pick, segments,
        jnp.swapaxes(self_weights, 1, 2).reshape(4, 4, hw // 4, width),
        jnp.swapaxes(cross_weights, 1, 2).reshape(4, 4, hw // 4, width),
        ffn_weights.reshape(3, 16, half, fw),
    )
    weights = weights.reshape(4, 4, width, width)
    mem_full = mem_full.reshape(mem_len, width)
    output, final, tokens_grad, memory_grad, small = backward(
        valid_rows, x2, cotangent, x1, mem_full, h2, h1, tokens, norm_gains, bias_line, segments, rel_pick,
        weights, q2, kv2, o2, q1, kv1, o1, bias,
    )
    if groups > 1:
        w = lax.axis_index("wide")
        mine = lax.dynamic_update_slice_in_dim(
            jnp.zeros((4, width, width), F32), final, lax.rem(w, 8) * eighth, 1
        )
        final = lax.psum_scatter(mine, "wide", scatter_dimension=1, tiled=True)
    own = final.shape[1]
    sums = reduce_stats(wide_count, final, small)
    shapes = [
        ((rows, width), BF), ((rows, width), F32), ((mem_own, width), F32), ((3, width), F32), ((heads, BUCKETS), F32),
        ((4, own, hw), F32), ((4, own, hw), F32), ((3, own, fw), F32),
        ((6, own), F32), ((6, hw), F32), ((2, 2 * width), F32), ((3, own), F32), ((3, fw), F32),
    ]
    outs = list(finish(shapes, output, tokens_grad, memory_grad, final, *sums))
    outs[2] = outs[2].reshape(1, mem_own, width)
    outs[4] = outs[4].T
    return tuple(outs)


def solution(mesh):
    in_specs = (
        P(("wide", "narrow"), None),
        P("wide", "narrow", None),
        P("wide", None),
        P("wide"),
        P(),
        P(),
        P(None, None, "narrow"),
        P(None, None, "narrow"),
        P(None, None, "narrow"),
        P(("wide", "narrow"), None),
    )
    out_specs = (
        P(("wide", "narrow"), None),
        P(("wide", "narrow"), None),
        P("wide", "narrow", None),
        P(),
        P(),
        P(None, "wide", "narrow"),
        P(None, "wide", "narrow"),
        P(None, "wide", "narrow"),
        P(None, "wide"),
        P(None, "narrow"),
        P(),
        P(None, "wide"),
        P(None, "narrow"),
    )
    return jax.shard_map(local, mesh=mesh, in_specs=in_specs, out_specs=out_specs, check_vma=False)
```

```python
import functools
import math

import jax
import jax.numpy as jnp
import numpy as np
from jax import lax
from jax.experimental import pallas as pl
from jax.experimental.pallas import tpu as pltpu
from jax.sharding import PartitionSpec as P

BUCKETS = 32
MAX_DIST = 128
EPS = 1e-06
MASKED = -1000000000.0
MESH = pl.DeviceIdType.MESH
BF = jnp.bfloat16
F32 = jnp.float32
VMEM_LIMIT = 64 * 1024 * 1024 - 65536


def bucket_table(seq_length, bucket_count, max_distance):
    exact_count = bucket_count // 2
    bucket_ids = np.zeros((seq_length,), np.int32)
    for distance in range(seq_length):
        if distance < exact_count:
            bucket_ids[distance] = distance
        else:
            scaled_log = (
                math.log(distance / exact_count)
                / math.log(max_distance / exact_count)
                * (bucket_count - exact_count)
            )
            bucket_ids[distance] = min(bucket_count - 1, exact_count + int(scaled_log))
    return bucket_ids


def mm(a, b):
    return jnp.dot(a, b, preferred_element_type=F32)


def mm_nt(a, b):
    return lax.dot_general(a, b, (((1,), (1,)), ((), ())), preferred_element_type=F32)


def mm_tn(a, b):
    return lax.dot_general(a, b, (((0,), (0,)), ((), ())), preferred_element_type=F32)


def inv_rms(v):
    return lax.rsqrt(jnp.mean(v * v, axis=-1, keepdims=True) + EPS)


def norm_back(v, gain, dh):
    r = inv_rms(v)
    gain_part = jnp.sum(dh * (v * r), axis=0, keepdims=True)
    gd = gain * dh
    dv = r * gd - v * (r * r * r) * jnp.mean(gd * v, axis=-1, keepdims=True)
    return gain_part, dv


def soft_cols(scores):
    e = jnp.exp(scores - jnp.max(scores, axis=0, keepdims=True))
    return e * (1.0 / jnp.sum(e, axis=0, keepdims=True))


def self_mask_store(mask_ref, seg_ref, z, rows, span):
    def quarter(k):
        out = jnp.full((1, rows), -1, jnp.int32)
        for kk in range(4):
            out = jnp.where(k == kk, seg_ref[:, kk * rows : (kk + 1) * rows], out)
        return out.astype(F32)

    own = quarter(z)
    keys = jnp.concatenate([quarter(z - 2), quarter(z - 1), own], axis=1)
    keys = jnp.broadcast_to(keys, (128, 3 * rows)).T
    for b in range(2):
        r = lax.broadcasted_iota(jnp.int32, (span, 128), 0)
        c = lax.broadcasted_iota(jnp.int32, (span, 128), 1)
        allowed = (c + 2 * rows >= r) & (keys[b * 128 : b * 128 + span] == own[:, b * 128 : b * 128 + 128])
        mask_ref[b] = jnp.where(allowed, 1.0, 0.0)


def full(shape):
    return pl.BlockSpec(shape, lambda j: (0,) * len(shape))


def once(shape):
    return pl.BlockSpec(shape, lambda j: (0,) * len(shape), pipeline_mode=pl.Buffered(1))


SMEM_SPEC = pl.BlockSpec(memory_space=pltpu.SMEM)


class Place:
    def __init__(self):
        self.w = lax.axis_index("wide")
        self.z = lax.axis_index("narrow")
        s = lax.rem(self.w, 8)
        self.s = s
        self.c = lax.rem(s, 2)
        self.x = lax.rem(s // 2, 2)
        self.y = s // 4
        dc, dx, dy = 1 - 2 * self.c, 2 * (1 - 2 * self.x), 4 * (1 - 2 * self.y)
        self.core_dev = {"wide": self.w + dc}
        self.x_dev = {"wide": self.w + dx}
        self.y_dev = {"wide": self.w + dy}
        self.sx, self.sy, self.sxy = s + dx, s + dy, s + dx + dy
        self.dc = dc

    def quarter(self, k):
        z = self.z
        e0, e3 = 1 - (z + 3) // 4, z // 3
        e1, e2 = (1 - z // 2) * lax.rem(z, 2), (z // 2) * (1 - lax.rem(z, 2))
        return sum(e * row[k] for e, row in zip((e0, e1, e2, e3), RANKS))

    def quarter_of(self, slot):
        return sum(jnp.where(slot == k, self.quarter(k), 0) for k in range(4))

    def narrow_dev(self, k):
        return {"narrow": lax.rem(self.z + k, 4)}

    def devices(self):
        return [self.core_dev, self.x_dev, self.y_dev] + [self.narrow_dev(k) for k in (1, 2, 3)]

    def signal_all(self):
        for dev in self.devices():
            pl.semaphore_signal(pltpu.get_barrier_semaphore(), inc=1, device_id=dev, device_id_type=MESH)

    def wait_all(self):
        pl.semaphore_wait(pltpu.get_barrier_semaphore(), len(self.devices()))

    def barrier(self):
        self.signal_all()
        self.wait_all()


def remote(src, dst, send_sem, recv_sem, dev):
    return pltpu.make_async_remote_copy(
        src_ref=src, dst_ref=dst, send_sem=send_sem, recv_sem=recv_sem, device_id=dev, device_id_type=MESH
    )


RANKS = ((0, 1, 2, 3), (1, 0, 2, 3), (2, 3, 1, 0), (3, 2, 1, 0))
EARLY = 5


def forward_kernel(
    valid_ref, tok_ref, mem_ref, gain_ref, rel_ref, pick_ref, seg_ref, ws_ref, wc_ref, wf_ref,
    w_ref, bd_ref, x1_ref, h1_ref, q_ref, kv_ref, o_ref, bias_ref, mfull_ref, x2_ref, h2_ref, q2_ref, kv2_ref, o2_ref,
    wv, lines, xt, mt, mask_ref, zs, zr, ps, pr, ts, tr, ms, mr, ls, fs, os_,
):
    at = Place()
    z, s = at.z, at.s
    j = pl.program_id(0)
    units = 4
    rows, width = tok_ref.shape
    ext = 3 * rows
    span = 2 * rows + 128
    hw = q_ref.shape[2]
    fw = wf_ref.shape[3]
    heads = hw // 64
    part = rows // 4
    half = width // 16
    mine = pl.ds(2 * s, 2)

    def edge(k):
        return [(d, RANKS[k + d].index(k)) for d in (1, -1) if 0 <= k + d < 4]

    def own_send(u, k, d, rank):
        return remote(
            wv.at[u, 0, mine], wv.at[u, rank, mine], zs.at[u, 0 if d > 0 else 1], zr.at[u, rank], {"narrow": k + d}
        )

    def own_sends(u, act):
        for k in range(4):
            @pl.when(z == k)
            def _():
                for d, rank in edge(k):
                    act(own_send(u, k, d, rank))

    def forwards(u, r, act):
        for k in (1, 2):
            quarter = RANKS[k][r]
            d = 1 if quarter < k else -1
            there = RANKS[k + d].index(quarter)

            @pl.when(z == k)
            def _():
                act(remote(wv.at[u, r, mine], wv.at[u, there, mine], zs.at[u, 1 + r], zr.at[u, there], {"narrow": k + d}))

    def tok_copy(hop, p):
        part_rows = pl.ds(p * part, part)
        src = tok_ref.at[part_rows] if hop == 1 else xt.at[1, part_rows]
        return remote(src, xt.at[2 - hop, part_rows], ts.at[hop - 1, p], tr.at[hop - 1, p], {"narrow": z + 1})

    def tok_senders(hop):
        return z < 3 if hop == 1 else jnp.logical_and(z >= 1, z < 3)

    def tok_send(hop, parts):
        if hop == 2:
            @pl.when(z >= 1)
            def _():
                for p in parts:
                    tok_copy(1, p).wait_recv()

        @pl.when(tok_senders(hop))
        def _():
            for p in parts:
                tok_copy(hop, p).start()

    def mem_copy(i, d):
        k = z - d * i
        src = mem_ref if i == 0 else mt.at[k]
        place = i if d > 0 else 3 + i
        return remote(src, mt.at[k], ms.at[place], mr.at[place], {"narrow": z + d})

    def mem_sends(i, act):
        @pl.when(jnp.logical_and(z >= i, z < 3))
        def _():
            act(mem_copy(i, 1))

        @pl.when(jnp.logical_and(z >= 1, z < 4 - i))
        def _():
            act(mem_copy(i, -1))

    def mem_arrived(i):
        for d in (1, -1):
            @pl.when(z > i if d > 0 else z < 3 - i)
            def _():
                here = mt.at[z - d * (1 + i)]
                place = i if d > 0 else 3 + i
                remote(here, here, ms.at[place], mr.at[place], at.x_dev).wait_recv()

    def piece(u, r, kind):
        first, n, dev = {
            0: (2 * s, 1, at.x_dev), 1: (2 * s + 1, 1, at.x_dev), 2: (2 * at.sy + 1, 1, at.x_dev),
            3: (2 * s + 1, 1, at.y_dev), 4: (2 * s, 1, at.y_dev), 5: (2 * at.sx, 1, at.y_dev),
            6: (2 * s, 2, at.core_dev), 7: (2 * at.sx, 2, at.core_dev),
            8: (2 * at.sy, 2, at.core_dev), 9: (2 * at.sxy, 2, at.core_dev),
        }[kind]
        region = wv.at[u, r, pl.ds(first, n)]
        i = u * 3 + r - 1
        return remote(region, region, ps.at[i, kind], pr.at[i, kind], dev)

    def arrived(u, r, kind):
        first, n = {
            0: (2 * at.sx, 1), 1: (2 * at.sx + 1, 1), 2: (2 * at.sxy + 1, 1),
            3: (2 * at.sy + 1, 1), 4: (2 * at.sy, 1), 5: (2 * at.sxy, 1),
            6: (2 * (s + at.dc), 2), 7: (2 * (at.sx + at.dc), 2),
            8: (2 * (at.sy + at.dc), 2), 9: (2 * (at.sxy + at.dc), 2),
        }[kind]
        region = wv.at[u, r, pl.ds(first, n)]
        i = u * 3 + r - 1
        remote(region, region, ps.at[i, kind], pr.at[i, kind], at.x_dev).wait_recv()

    pieces = [(u, r) for u in range(units) for r in (1, 2, 3)]

    def step0(t):
        if not 0 <= t < len(pieces):
            return
        u, r = pieces[t]
        region = wv.at[u, r, mine]
        remote(region, region, zs.at[u, 0], zr.at[u, r], at.x_dev).wait_recv()
        forwards(u, r, lambda copy: copy.start())
        for kind in (0, 3, 4, 1, 6):
            piece(u, r, kind).start()
        if t == 0:
            tok_send(1, (0, 1))
        if t == 1:
            tok_send(1, (2, 3))
        if t == 2:
            own_sends(2, lambda copy: copy.start())
        if t == 3:
            tok_send(2, (0, 1, 2, 3))
        if t == 4:
            mem_sends(0, lambda copy: copy.start())
        if t == 5:
            own_sends(3, lambda copy: copy.start())
        if t in (6, 8):
            i = (t - 4) // 2
            mem_arrived(i - 1)
            mem_sends(i, lambda copy: copy.start())

    def step1(t):
        if not 0 <= t < len(pieces):
            return
        u, r = pieces[t]
        arrived(u, r, 0)
        piece(u, r, 5).start()
        arrived(u, r, 3)
        piece(u, r, 2).start()
        arrived(u, r, 1)
        piece(u, r, 7).start()
        arrived(u, r, 4)
        piece(u, r, 8).start()

    def step2(t):
        if not 0 <= t < len(pieces):
            return
        u, r = pieces[t]
        arrived(u, r, 5)
        arrived(u, r, 2)
        piece(u, r, 9).start()

    def keep(u, k):
        return pltpu.make_async_copy(wv.at[u, k], w_ref.at[u, k], os_.at[u, k])

    def step3(t):
        if not 0 <= t < len(pieces):
            return
        u, r = pieces[t]
        for kind in (6, 7, 8, 9):
            arrived(u, r, kind)
        keep(u, r).start()

    def attn_loads(i):
        src = (ws_ref, wc_ref)[i]
        return [
            pltpu.make_async_copy(src.at[part], wv.at[i, 0, pl.ds(4 * k, 4)], ls.at[i, k])
            for k, part in enumerate((0, 3, 1, 2))
        ]

    def ffn_loads():
        cut = width - fw
        return [
            pltpu.make_async_copy(wf_ref.at[0], wv.at[2, 0, :, :, 0:fw], fs.at[0]),
            pltpu.make_async_copy(wf_ref.at[1, :, :, 0:cut], wv.at[2, 0, :, :, fw:width], fs.at[1]),
            pltpu.make_async_copy(wf_ref.at[1, :, :, cut:fw], wv.at[3, 0, :, :, 0 : fw - cut], fs.at[2]),
            pltpu.make_async_copy(wf_ref.at[2], wv.at[3, 0, :, :, fw - cut : width], fs.at[3]),
        ]

    @pl.when(j == 0)
    def _():
        at.signal_all()
        for copy in attn_loads(0) + attn_loads(1) + ffn_loads():
            copy.start()
        at.wait_all()
        for copy in attn_loads(0):
            copy.wait()
        own_sends(0, lambda copy: copy.start())
        for copy in attn_loads(1):
            copy.wait()
        own_sends(1, lambda copy: copy.start())
        for copy in ffn_loads():
            copy.wait()
        for u in range(units):
            keep(u, 0).start()
        x = tok_ref[...].astype(F32)
        x1_ref[...] = x
        h1_ref[2 * rows : ext, :] = (x * inv_rms(x) * gain_ref[0:1, :]).astype(BF)
        self_mask_store(mask_ref, seg_ref, z, rows, span)
        lines[...] = lax.dot_general(
            rel_ref[...], pick_ref[...], (((1,), (0,)), ((), ())),
            preferred_element_type=F32, precision=lax.Precision.HIGHEST,
        )
        for k in range(4):
            first = at.quarter(k) * heads
            for hh in range(heads):
                bd_ref[k, hh : hh + 1, :] = lines[pl.ds(first + hh, 1), :]
        for t in range(EARLY):
            step0(t)
            step1(t - 1)
            step2(t - 2)
            step3(t - 3)

        @pl.when(z >= 2)
        def _():
            for p in range(4):
                tok_copy(2, p).wait_recv()

        for t in range(2):
            v = jnp.where(z >= 2 - t, xt[t].astype(F32), 0.0)
            h1_ref[t * rows : (t + 1) * rows, :] = (v * inv_rms(v) * gain_ref[0:1, :]).astype(BF)

    def hook(i, first, last):
        for jj in range(first, last):
            t = EARLY + jj

            @pl.when(j == jj)
            def _():
                if i == 0:
                    step3(t - 3)
                    step0(t)
                if i == 1:
                    step1(t - 1)
                if i == 2:
                    step2(t - 2)

    def flat(u, k, lo, hi):
        return wv[u, k, lo // half : hi // half].reshape(hi - lo, width)

    @pl.when(j < 4)
    def _():
        hook(0, 0, 4)
        q = mm_nt(h1_ref[2 * rows : ext, :], flat(0, j, 0, hw)).astype(BF)
        kv = mm_nt(h1_ref[...], flat(0, j, 2 * hw, 4 * hw)).astype(BF)
        q_ref[0] = q
        kv_ref[0] = kv
        parts = []
        for hh in range(heads):
            line = jnp.broadcast_to(bd_ref[j, hh : hh + 1, :], (256, 512))
            bias = pltpu.roll(line, 0, 1, stride=1, stride_axis=0)[:, 0:128]
            bias_ref[0, hh] = bias
            far = bd_ref[j, hh : hh + 1, 127:128]
            cols = []
            for b in range(2):
                k = kv[b * 128 : b * 128 + span, hh * 64 : hh * 64 + 64]
                v = kv[b * 128 : b * 128 + span, hw + hh * 64 : hw + hh * 64 + 64]
                qb = q[b * 128 : b * 128 + 128, hh * 64 : hh * 64 + 64]
                sc = mm_nt(k, qb)
                sc = jnp.concatenate([sc[: span - 256] + far, sc[span - 256 :] + bias], axis=0)
                sc = jnp.where(mask_ref[b] > 0.5, sc, MASKED)
                cols.append(mm_tn(v, soft_cols(sc).astype(BF)))
            parts.append(jnp.concatenate(cols, axis=1))
            if hh < 2:
                hook(1 + hh, 0, 4)
        o = jnp.concatenate(parts, axis=0).T.astype(BF)
        o_ref[0] = o
        x1_ref[...] += mm(o, flat(0, j, hw, 2 * hw))

    @pl.when(j == 4)
    def _():
        x1 = x1_ref[...]
        x2_ref[...] = x1
        h2_ref[...] = (x1 * inv_rms(x1) * gain_ref[1:2, :]).astype(BF)
        mfull_ref[z] = mem_ref[...]
        mem_arrived(2)
        for k in range(4):
            @pl.when(z != k)
            def _():
                mfull_ref[k] = mt[k]

    @pl.when(j >= 4)
    def _():
        hook(0, 4, 8)
        mem = mfull_ref.shape[0] * mfull_ref.shape[1]
        q = mm_nt(h2_ref[...], flat(1, j - 4, 0, hw)).astype(BF)
        kv = mm_nt(mfull_ref[...].reshape(mem, width), flat(1, j - 4, 2 * hw, 4 * hw)).astype(BF)
        q2_ref[0] = q
        kv2_ref[0] = kv
        allowed = lax.broadcasted_iota(jnp.int32, (mem, rows), 0) < valid_ref[0]
        parts = []
        for hh in range(heads):
            k = kv[:, hh * 64 : hh * 64 + 64]
            v = kv[:, hw + hh * 64 : hw + hh * 64 + 64]
            sc = jnp.where(allowed, mm_nt(k, q[:, hh * 64 : hh * 64 + 64]), MASKED)
            parts.append(mm_tn(v, soft_cols(sc).astype(BF)))
            if hh < 2:
                hook(1 + hh, 4, 8)
        o = jnp.concatenate(parts, axis=0).T.astype(BF)
        o2_ref[0] = o
        x2_ref[...] += mm(o, flat(1, j - 4, hw, 2 * hw))

    @pl.when(j == 7)
    def _():
        for t in range(EARLY + 8, len(pieces) + 3):
            step0(t)
            step1(t - 1)
            step2(t - 2)
            step3(t - 3)
        for u, r in pieces:
            for kind in range(10):
                piece(u, r, kind).wait_send()
            forwards(u, r, lambda copy: copy.wait_send())
        for u in range(units):
            own_sends(u, lambda copy: copy.wait_send())
            for k in range(4):
                keep(u, k).wait()
        for hop in (1, 2):
            @pl.when(tok_senders(hop))
            def _():
                for p in range(4):
                    tok_copy(hop, p).wait_send()
        for i in range(3):
            mem_sends(i, lambda copy: copy.wait_send())


def forward(valid_rows, tokens, memory, gains, rel, pick, seg, ws, wc, wf):
    rows, width = tokens.shape
    mem_own = memory.shape[0]
    hw = 4 * ws.shape[2]
    heads = hw // 64
    ext = 3 * rows
    mem = 4 * mem_own
    half = width // 16
    any_spec = pl.BlockSpec(memory_space=pl.ANY)
    dma = pltpu.SemaphoreType.DMA

    def early(shape):
        return pl.BlockSpec((1,) + shape, lambda j: (jnp.minimum(j, 3),) + (0,) * len(shape))

    def late(shape):
        return pl.BlockSpec((1,) + shape, lambda j: (jnp.maximum(j - 4, 0),) + (0,) * len(shape))

    out = [
        ((4, 4, 16, half, width), BF, any_spec), ((4, heads, 512), F32, full((4, heads, 512))),
        ((rows, width), F32, full((rows, width))), ((ext, width), BF, full((ext, width))),
        ((4, rows, hw), BF, early((rows, hw))), ((4, ext, 2 * hw), BF, early((ext, 2 * hw))),
        ((4, rows, hw), BF, early((rows, hw))), ((4, heads, 256, 128), F32, early((heads, 256, 128))),
        ((4, mem_own, width), BF, full((4, mem_own, width))),
        ((rows, width), F32, full((rows, width))), ((rows, width), BF, full((rows, width))),
        ((4, rows, hw), BF, late((rows, hw))), ((4, mem, 2 * hw), BF, late((mem, 2 * hw))),
        ((4, rows, hw), BF, late((rows, hw))),
    ]
    return pl.pallas_call(
        forward_kernel,
        name="forward",
        grid=(8,),
        in_specs=[
            SMEM_SPEC, full((rows, width)), full((mem_own, width)), full((3, width)),
            full(rel.shape), full(pick.shape), full(seg.shape), any_spec, any_spec, any_spec,
        ],
        out_specs=[spec for _, _, spec in out],
        out_shape=[jax.ShapeDtypeStruct(shape, dtype) for shape, dtype, _ in out],
        scratch_shapes=[
            pltpu.VMEM((4, 4, 16, half, width), BF), pltpu.VMEM((4 * heads, 512), F32),
            pltpu.VMEM((2, rows, width), BF), pltpu.VMEM((4, mem_own, width), BF),
            pltpu.VMEM((2, 2 * rows + 128, 128), F32),
            dma((4, 5)), dma((4, 4)), dma((12, 10)), dma((12, 10)),
            dma((2, 4)), dma((2, 4)), dma((6,)), dma((6,)), dma((2, 4)), dma((4,)), dma((4, 4)),
        ],
        compiler_params=pltpu.CompilerParams(
            collective_id=0, has_side_effects=True, vmem_limit_bytes=VMEM_LIMIT, dimension_semantics=("arbitrary",)
        ),
    )(valid_rows, tokens, memory, gains, rel, pick, seg, ws, wc, wf)


CHUNKS = [(2 + i % 2, i // 2) for i in range(8)] + [(1, i) for i in range(4)] + [(0, i) for i in range(4)]
HELD = 12
LAG = 3
TICKS = [(1, 0), (2, 0), (3, 0), (4, 0), (5, 0), (6, 0), (7, 0), (8, 0), (8, 2), (9, 1), (10, 0), (10, 2), (11, 1)]


def backward_kernel(
    valid_ref, x2_ref, cot_ref, x1_ref, mem_ref, h2_ref, h1_ref, tok_ref, gain_ref, bd_ref, seg_ref, pick_ref,
    w_ref, q2_ref, kv2_ref, o2_ref, q1_ref, kv1_ref, o1_ref, bias_ref,
    out_ref, f_ref, tg_ref, mg_ref, small_ref,
    g, wbuf, acc, act_in, res, gsum_ref, rel_ref, do_ref, dqt_ref, dkv_ref, mask_ref, flip_ref, dxo, dmo, rc, xr, yr, xr2, yr2, zb, dxr, dmr,
    wsem, cs, cr, xs, xrs, ys, yrs, x2s, x2r, y2s, y2r, zs, zr, dxs, dxrs, dms, dmrs,
):
    at = Place()
    z = at.z
    j = pl.program_id(0)
    rows, width = x2_ref.shape
    mem = mem_ref.shape[0]
    ext = 3 * rows
    span = 2 * rows + 128
    hw = q1_ref.shape[2]
    heads = hw // 64
    fw = wbuf.shape[2] * 2 // 3
    own_rows = g.shape[3]
    half = own_rows // 2
    n = len(CHUNKS)
    lo, hi = pl.ds(0, half), pl.ds(half, half)
    yx = 2 * at.y + at.x
    top, bottom = pl.ds(0, rows), pl.ds(2 * rows, rows)

    def w_load(unit, slot, k):
        return pltpu.make_async_copy(w_ref.at[unit, slot], wbuf.at[k], wsem.at[k])

    def held(i):
        return g.at[i % HELD]

    def add(ref, other):
        ref[...] = ref[...] + other[...]

    def core_send(i):
        return remote(held(i).at[:, pl.ds(1 - at.c, 1)], rc.at[i], cs.at[i], cr.at[i], at.core_dev)

    def x_send(i, yb):
        src = held(i).at[2 * yb + 1 - at.x, at.c, lo]
        return remote(src, xr.at[i, yb], xs.at[i, yb], xrs.at[i, yb], at.x_dev)

    def y_send(i, xb):
        src = held(i).at[2 * (1 - at.y) + xb, at.c, hi]
        return remote(src, yr.at[i, xb], ys.at[i, xb], yrs.at[i, xb], at.y_dev)

    def y2_send(i):
        return remote(held(i).at[2 * (1 - at.y) + at.x, at.c, lo], yr2.at[i], y2s.at[i], y2r.at[i], at.y_dev)

    def x2_send(i):
        return remote(held(i).at[2 * at.y + 1 - at.x, at.c, hi], xr2.at[i], x2s.at[i], x2r.at[i], at.x_dev)

    d = 1 - 2 * (z // 2)
    is_end = jnp.logical_or(z == 0, z == 3)
    is_inner = jnp.logical_or(z == 1, z == 2)

    def z_send(i, dst, step):
        unit = CHUNKS[i][0]
        return remote(held(i).at[yx, at.c], zb.at[unit, dst], zs.at[i], zr.at[unit, dst], {"narrow": z + step})

    def z_wait(i, k):
        unit = CHUNKS[i][0]
        remote(zb.at[unit, k], zb.at[unit, k], zs.at[i], zr.at[unit, k], at.x_dev).wait_recv()

    def step_b(i):
        core_send(i).wait_recv()
        add(held(i).at[:, pl.ds(at.c, 1)], rc.at[i])
        for b in range(2):
            x_send(i, b).start()
            y_send(i, b).start()

    def step_c(i):
        for b in range(2):
            x_send(i, b).wait_recv()
            y_send(i, b).wait_recv()
            add(held(i).at[2 * b + at.x, at.c, lo], xr.at[i, b])
            add(held(i).at[2 * at.y + b, at.c, hi], yr.at[i, b])
        y2_send(i).start()
        x2_send(i).start()

    def step_d(i):
        y2_send(i).wait_recv()
        add(held(i).at[yx, at.c, lo], yr2.at[i])
        x2_send(i).wait_recv()
        add(held(i).at[yx, at.c, hi], xr2.at[i])

    def step_e(i):
        @pl.when(is_end)
        def _():
            if CHUNKS[i][1] < 3:
                z_send(i, CHUNKS[i][1], d).start()

    def step_f(i):
        unit, s = CHUNKS[i]

        @pl.when(is_inner)
        def _():
            if s < 2:
                z_wait(i, s)
                add(held(i).at[yx, at.c], zb.at[unit, s])
                z_send(i, 3 + s, d).start()
            if s == 2:
                z_wait(i, 3)
                add(held(i).at[yx, at.c], zb.at[unit, 3])
                z_send(i, 2, -d).start()
            if s == 3:
                z_wait(i, 2)
                z_wait(i, 4)
                f_ref[unit] = (
                    held(i)[yx, at.c].astype(F32) + zb[unit, 2].astype(F32) + zb[unit, 4].astype(F32)
                )

        if s == 3:
            @pl.when(is_end)
            def _():
                z_wait(i, 2)
                f_ref[unit] = held(i)[yx, at.c].astype(F32) + zb[unit, 2].astype(F32)

    def sent(i):
        core_send(i).wait_send()
        for b in range(2):
            x_send(i, b).wait_send()
            y_send(i, b).wait_send()
        y2_send(i).wait_send()
        x2_send(i).wait_send()
        if CHUNKS[i][1] < 3:
            z_send(i, 0, d).wait_send()

    def tick(t):
        for k, step in ((0, step_b), (1, step_c), (2, step_d), (2, step_e), (LAG, step_f)):
            if 0 <= t - k < n:
                step(t - k)

    def hook(place, first, last):
        for t, (jj, p) in enumerate(TICKS):
            if p == place and first <= jj < last:
                @pl.when(j == jj)
                def _():
                    tick(t)

    def dx_send(t):
        return remote(dxo.at[t], dxr.at[t], dxs.at[t], dxrs.at[t], {"narrow": z - 1})

    def dm_send(k):
        return remote(dmo.at[lax.rem(z + k, 4)], dmr.at[k - 1], dms.at[k - 1], dmrs.at[k - 1], at.narrow_dev(k))

    @pl.when(j == 0)
    def _():
        for b in range(2):
            w_load(2 + b, 3, b).start()
        at.signal_all()
        x2 = x2_ref[...]
        acc[0:rows, :] = x2
        acc[rows : 2 * rows, :] = jnp.zeros((rows, width), F32)
        act_in[...] = (x2 * inv_rms(x2) * gain_ref[2:3, :]).astype(BF)

    @pl.when(j < 4)
    def _():
        k = 2 * lax.rem(j, 2)
        for b in range(2):
            w_load(2 + b, 3 - j, k + b).wait()

        @pl.when(j < 3)
        def _():
            for b in range(2):
                w_load(2 + b, 2 - j, 2 - k + b).start()

        @pl.when(j == 3)
        def _():
            w_load(1, 3, 0).start()

        @pl.when(j == 0)
        def _():
            at.wait_all()

        hook(0, 0, 4)
        h3 = act_in[...]
        df = cot_ref[...]
        wg = wbuf[k, :, 0:fw]
        wu = jnp.concatenate([wbuf[k, :, fw:], wbuf[k + 1, :, 0 : fw // 2]], axis=1)
        wd = wbuf[k + 1, :, fw // 2 :]
        gate = mm(h3, wg)
        up = mm(h3, wu)
        c0 = math.sqrt(2.0 / math.pi)
        gate2 = gate * gate
        t = jnp.tanh(c0 * (gate + 0.044715 * gate2 * gate))
        part = 0.5 * (1.0 + t)
        gelu = gate * part
        slope = part + 0.5 * gate * (1.0 - t * t) * (c0 * (1.0 + 3.0 * 0.044715 * gate2))
        act = (gelu * up).astype(BF)
        acc[0:rows, :] += mm_nt(act, wd)
        da = mm(df, wd)
        dgate = (da * up * slope).astype(BF)
        dup = (da * gelu).astype(BF)
        dgu = jnp.concatenate([dgate, dup], axis=1)
        ggu = mm_tn(h3, dgu).astype(BF)
        blocks = (4, 2, own_rows)
        g[2 * j] = ggu[:, 0 : fw * 3 // 2].reshape(blocks + (width,))
        g[2 * j + 1, :, :, :, 0 : fw // 2] = ggu[:, fw * 3 // 2 :].reshape(blocks + (fw // 2,))
        g[2 * j + 1, :, :, :, fw // 2 :] = mm_tn(df, act).astype(BF).reshape(blocks + (fw,))
        acc[rows : 2 * rows, :] += mm_nt(dgate, wg) + mm_nt(dup, wu)
        for jj in range(4):
            @pl.when(j == jj)
            def _():
                core_send(2 * jj).start()
                core_send(2 * jj + 1).start()

    @pl.when(j == 3)
    def _():
        out_ref[...] = acc[0:rows, :].astype(BF)
        gain_part, dv = norm_back(x2_ref[...], gain_ref[2:3, :], acc[rows : 2 * rows, :])
        gsum_ref[16:24, :] = jnp.broadcast_to(gain_part, (8, width))
        g2 = cot_ref[...].astype(F32) + dv
        res[...] = g2
        act_in[...] = g2.astype(BF)
        acc[...] = jnp.zeros_like(acc)

    @pl.when(jnp.logical_and(j >= 4, j < 8))
    def _():
        k0 = j - 4
        w_load(1, 7 - j, k0).wait()

        @pl.when(j < 7)
        def _():
            w_load(1, 6 - j, k0 + 1).start()

        @pl.when(j == 7)
        def _():
            w_load(0, 3, 0).start()

        do_ref[...] = mm_nt(act_in[...], wbuf[k0, hw : 2 * hw, :]).astype(BF)
        for hh in range(heads):
            h_cols, v_cols = slice(hh * 64, hh * 64 + 64), slice(hw + hh * 64, hw + hh * 64 + 64)
            k = kv2_ref[0, :, h_cols]
            v = kv2_ref[0, :, v_cols]
            qh = q2_ref[0, :, h_cols]
            doh = do_ref[:, h_cols]
            allowed = lax.broadcasted_iota(jnp.int32, (mem, rows), 0) < valid_ref[0]
            p = soft_cols(jnp.where(allowed, mm_nt(k, qh), MASKED))
            dp = mm_nt(v, doh)
            ds = (p * (dp - jnp.sum(p * dp, axis=0, keepdims=True))).astype(BF)
            dkv_ref[0:mem, v_cols] = mm(p.astype(BF), doh).astype(BF)
            dkv_ref[0:mem, h_cols] = mm(ds, qh).astype(BF)
            dqt_ref[h_cols, :] = mm_tn(k, ds)
            hook(hh, 4, 8)
        dc = act_in[...]
        dq = dqt_ref[...].T.astype(BF)
        dkv = dkv_ref[0:mem, :]
        zero = jnp.zeros((rows, hw), BF)
        left = jnp.concatenate([h2_ref[...], dc], axis=0)
        right = jnp.concatenate(
            [jnp.concatenate([dq, zero], axis=1), jnp.concatenate([zero, o2_ref[0]], axis=1)], axis=0
        )
        blocks = (4, 2, own_rows, 2 * hw)
        g[4 + j, :, :, :, 0 : 2 * hw] = mm_tn(left, right).astype(BF).reshape(blocks)
        g[4 + j, :, :, :, 2 * hw : 4 * hw] = mm_tn(mem_ref[...], dkv).astype(BF).reshape(blocks)
        for jj in range(4, 8):
            @pl.when(j == jj)
            def _():
                core_send(4 + jj).start()
        acc[0:rows, :] += mm(dq, wbuf[k0, 0:hw, :])
        acc[rows : rows + mem, :] += mm(dkv, wbuf[k0, 2 * hw : 4 * hw, :])

    @pl.when(j == 7)
    def _():
        for k in range(4):
            dmo[k] = acc[rows + k * (mem // 4) : rows + (k + 1) * (mem // 4), :].astype(BF)
        for k in (1, 2, 3):
            dm_send(k).start()
        gain_part, dv = norm_back(x1_ref[...], gain_ref[1:2, :], acc[0:rows, :])
        gsum_ref[8:16, :] = jnp.broadcast_to(gain_part, (8, width))
        g1 = res[...] + dv
        res[...] = g1
        act_in[...] = g1.astype(BF)
        acc[...] = jnp.zeros_like(acc)
        self_mask_store(mask_ref, seg_ref, z, rows, span)
        rel_ref[...] = jnp.zeros_like(rel_ref)
        r = lax.broadcasted_iota(jnp.int32, (256, 256), 0)
        c = lax.broadcasted_iota(jnp.int32, (256, 256), 1)
        flip_ref[...] = jnp.where(r + c == 255, 1.0, 0.0).astype(BF)

    @pl.when(j >= 8)
    def _():
        k0 = j - 8
        w_load(0, 11 - j, k0).wait()

        @pl.when(j < 11)
        def _():
            w_load(0, 10 - j, k0 + 1).start()

        do_ref[...] = mm_nt(act_in[...], wbuf[k0, hw : 2 * hw, :]).astype(BF)
        for hh in range(heads):
            h_cols, v_cols = slice(hh * 64, hh * 64 + 64), slice(hw + hh * 64, hw + hh * 64 + 64)
            far = bd_ref[11 - j, hh : hh + 1, 127:128]
            dq_cols, dks, dvs = [], [], []
            band = jnp.zeros((256, 128), F32)
            total = jnp.zeros((1, 128), F32)
            for b in range(2):
                k = kv1_ref[0, b * 128 : b * 128 + span, h_cols]
                v = kv1_ref[0, b * 128 : b * 128 + span, v_cols]
                qb = q1_ref[0, b * 128 : b * 128 + 128, h_cols]
                dob = do_ref[b * 128 : b * 128 + 128, h_cols]
                s = mm_nt(k, qb)
                s = jnp.concatenate([s[: span - 256] + far, s[span - 256 :] + bias_ref[0, hh]], axis=0)
                s = jnp.where(mask_ref[b] > 0.5, s, MASKED)
                p = soft_cols(s)
                dp = mm_nt(v, dob)
                ds = (p * (dp - jnp.sum(p * dp, axis=0, keepdims=True))).astype(BF)
                dvs.append(mm(p.astype(BF), dob))
                dks.append(mm(ds, qb))
                dq_cols.append(mm_tn(k, ds))
                band = band + mm(flip_ref[...], ds[span - 256 :])
                total = total + jnp.sum(ds[: span - 256].astype(F32), axis=0, keepdims=True)
            gap = jnp.zeros((128, 64), F32)
            dk = jnp.concatenate([dks[0], gap], 0) + jnp.concatenate([gap, dks[1]], 0)
            dv = jnp.concatenate([dvs[0], gap], 0) + jnp.concatenate([gap, dvs[1]], 0)
            dkv_ref[:, h_cols] = dk.astype(BF)
            dkv_ref[:, v_cols] = dv.astype(BF)
            dqt_ref[h_cols, :] = jnp.concatenate(dq_cols, axis=1)
            wide_band = jnp.concatenate([band, jnp.zeros((256, 384), F32)], axis=1)
            aligned = pltpu.roll(wide_band, 0, 1, stride=1, stride_axis=0)
            line = jnp.sum(aligned, axis=0, keepdims=True)
            lane = lax.broadcasted_iota(jnp.int32, (1, 512), 1)
            far_sum = jnp.sum(total, axis=1, keepdims=True)
            rel_ref[pl.ds(at.quarter_of(11 - j) * heads + hh, 1), :] = jnp.where(lane == 511, far_sum, line)
            hook(hh, 8, 12)
        da = act_in[...]
        dq = dqt_ref[...].T.astype(BF)
        dkv = dkv_ref[...]
        zero = jnp.zeros((rows, hw), BF)
        left = jnp.concatenate([h1_ref[2 * rows : ext, :], da], axis=0)
        right = jnp.concatenate(
            [jnp.concatenate([dq, zero], axis=1), jnp.concatenate([zero, o1_ref[0]], axis=1)], axis=0
        )
        for jj in range(8, 12):
            @pl.when(j == jj)
            def _():
                sent(jj - 8)
        blocks = (4, 2, own_rows, 2 * hw)
        g[j - 8, :, :, :, 0 : 2 * hw] = mm_tn(left, right).astype(BF).reshape(blocks)
        g[j - 8, :, :, :, 2 * hw : 4 * hw] = mm_tn(h1_ref[...], dkv).astype(BF).reshape(blocks)
        for jj in range(8, 12):
            @pl.when(j == jj)
            def _():
                core_send(4 + jj).start()
        acc[...] += mm(dkv, wbuf[k0, 2 * hw : 4 * hw, :])
        acc[2 * rows : ext, :] += mm(dq, wbuf[k0, 0:hw, :])

    @pl.when(j == 11)
    def _():
        for t in range(2):
            dxo[t] = acc[t * rows : (t + 1) * rows, :].astype(BF)

        @pl.when(z >= 2)
        def _():
            dx_send(0).start()

        @pl.when(z == 3)
        def _():
            dx_send(1).start()
        last = n + LAG
        for t in range(len(TICKS), last):
            tick(t)
            if t == len(TICKS):
                mg_ref[...] = dmo[z].astype(F32)
                for k in (1, 2, 3):
                    dm_send(k).wait_recv()
                    mg_ref[...] += dmr[k - 1].astype(F32)
            if t == len(TICKS) + 1:
                @pl.when(is_inner)
                def _():
                    dx_send(0).wait_recv()
                    add(dxo.at[1], dxr.at[0])
                    dx_send(1).start()
            if t == len(TICKS) + 3:
                @pl.when(z < 3)
                def _():
                    dx_send(1).wait_recv()
                    acc[2 * rows : ext, :] += dxr[1].astype(F32)
                gain_part, dv = norm_back(tok_ref[...].astype(F32), gain_ref[0:1, :], acc[2 * rows : ext, :])
                rel = lax.dot_general(
                    rel_ref[...], pick_ref[...], (((1,), (0,)), ((), ())),
                    preferred_element_type=F32, precision=lax.Precision.HIGHEST,
                )
                gains = [gain_part, gsum_ref[8:9, :], gsum_ref[16:17, :], jnp.zeros((2, width), F32)]
                per = width // 128
                lines = [
                    jnp.concatenate([rel[per * k + h : per * k + h + 1] for h in range(per)], axis=1)
                    for k in range(2)
                ]
                small_ref[...] = jnp.concatenate(gains + lines + [jnp.zeros((1, width), F32)], axis=0)
                tg_ref[...] = res[...] + dv
        for i in range(n - HELD, n):
            sent(i)
        for t in range(2):
            @pl.when(z >= 2 - t)
            def _():
                dx_send(t).wait_send()
        for k in (1, 2, 3):
            dm_send(k).wait_send()


def backward(
    valid_rows, x2, cot, x1, mem_full, h2, h1, tokens, gains, bias_line, seg, pick,
    weights, q2, kv2, o2, q1, kv1, o1, bias,
):
    rows, width = x2.shape
    mem = mem_full.shape[0]
    hw = q1.shape[2]
    ext = 3 * rows
    own = width // 8
    half = own // 2
    n = len(CHUNKS)
    dma = pltpu.SemaphoreType.DMA

    def slot(last, a):
        shape = a.shape[1:]
        return pl.BlockSpec(
            (1,) + shape, lambda j: (jnp.clip(last - j, 0, 3),) + (0,) * len(shape)
        )

    out = [
        ((rows, width), BF), ((4, own, width), F32), ((rows, width), F32), ((mem // 4, width), F32),
        ((8, width), F32),
    ]
    shapes = [jax.ShapeDtypeStruct(s, d) for s, d in out]
    return pl.pallas_call(
        backward_kernel,
        name="backward",
        grid=(12,),
        in_specs=[
            SMEM_SPEC, *[once(a.shape) for a in (x2, cot, x1, mem_full, h2, h1, tokens)],
            full(gains.shape), full(bias_line.shape), full(seg.shape), full(pick.shape),
            pl.BlockSpec(memory_space=pl.ANY),
            slot(7, q2), slot(7, kv2), slot(7, o2), slot(11, q1), slot(11, kv1), slot(11, o1), slot(11, bias),
        ],
        out_specs=[once(s) for s, _ in out],
        out_shape=shapes,
        scratch_shapes=[
            pltpu.VMEM((HELD, 4, 2, own, width), BF), pltpu.VMEM((4, width, width), BF),
            pltpu.VMEM((ext, width), F32), pltpu.VMEM((rows, width), BF), pltpu.VMEM((rows, width), F32),
            pltpu.VMEM((24, width), F32), pltpu.VMEM((16, 512), F32),
            pltpu.VMEM((rows, hw), BF), pltpu.VMEM((hw, rows), F32), pltpu.VMEM((ext, 2 * hw), BF),
            pltpu.VMEM((2, 2 * rows + 128, 128), F32), pltpu.VMEM((256, 256), BF),
            pltpu.VMEM((2, rows, width), BF), pltpu.VMEM((4, mem // 4, width), BF),
            pltpu.VMEM((n, 4, 1, own, width), BF),
            pltpu.VMEM((n, 2, half, width), BF), pltpu.VMEM((n, 2, half, width), BF),
            pltpu.VMEM((n, half, width), BF), pltpu.VMEM((n, half, width), BF),
            pltpu.VMEM((4, 5, own, width), BF),
            pltpu.VMEM((2, rows, width), BF), pltpu.VMEM((3, mem // 4, width), BF),
            dma((4,)), dma((n,)), dma((n,)),
            dma((n, 2)), dma((n, 2)), dma((n, 2)), dma((n, 2)),
            dma((n,)), dma((n,)), dma((n,)), dma((n,)),
            dma((n,)), dma((4, 5)),
            dma((2,)), dma((2,)), dma((3,)), dma((3,)),
        ],
        compiler_params=pltpu.CompilerParams(
            collective_id=1, has_side_effects=True, vmem_limit_bytes=VMEM_LIMIT, dimension_semantics=("arbitrary",)
        ),
    )(
        valid_rows, x2, cot, x1, mem_full, h2, h1, tokens, gains, bias_line, seg, pick,
        weights, q2, kv2, o2, q1, kv1, o1, bias,
    )


def stats_kernel(
    wide_count, f_ref, a_ref,
    rsum_ref, csum_ref, asum_ref, pcol_ref,
    rall, aall, call, ball, rs, rr, as_, ar, cs, cr, bs, br, ps, pr,
):
    w = lax.axis_index("wide")
    z = lax.axis_index("narrow")
    own = f_ref.shape[1]
    width = f_ref.shape[2]
    sem = pltpu.get_barrier_semaphore()

    def peer(k):
        return {"narrow": lax.rem(z + k, 4)}

    def wide_peer(k):
        return {"wide": lax.rem(w + k, wide_count)}

    def wide_loop(fn):
        if wide_count <= 8:
            for k in range(1, wide_count):
                fn(k)
        else:
            pl.loop(1, wide_count)(fn)

    for k in (1, 2, 3):
        pl.semaphore_signal(sem, inc=1, device_id=peer(k), device_id_type=MESH)
    wide_loop(lambda k: pl.semaphore_signal(sem, inc=1, device_id=wide_peer(k), device_id_type=MESH))

    lane = lax.broadcasted_iota(jnp.int32, (8, width), 1)
    row = lax.broadcasted_iota(jnp.int32, (8, width), 0)
    quarter = width // 4
    third = 2 * width // 3

    def sums(pick, sq):
        got = lax.dot_general(
            jnp.where(pick, 1.0, 0.0), sq, (((1,), (1,)), ((), ())),
            preferred_element_type=F32, precision=lax.Precision.HIGHEST,
        )
        pad = jnp.zeros((8, 128 - own), F32)
        return jnp.concatenate([got, pad], axis=1)

    sq = [f_ref[i] * f_ref[i] for i in range(4)]
    rall[z, 0:8] = sums(lane // quarter == row, sq[0])
    rall[z, 8:16] = sums(lane // quarter == row, sq[1])
    rall[z, 16:24] = sums(lane // third == row, sq[2]) + sums((lane + width) // third == row, sq[3])
    aall[z] = a_ref[...]
    call[w] = jnp.concatenate(
        [jnp.sum(v, axis=0, keepdims=True) for v in sq], axis=0
    )
    pl.semaphore_wait(sem, 3 + wide_count - 1)

    def r_send(k):
        return remote(rall.at[z], rall.at[z], rs.at[k - 1], rr.at[k - 1], peer(k))

    def a_send(k):
        return remote(aall.at[z], aall.at[z], as_.at[k - 1], ar.at[k - 1], peer(k))

    def c_send(k):
        return remote(call.at[w], call.at[w], cs.at[k - 1], cr.at[k - 1], wide_peer(k))

    def p_send(k):
        return remote(pcol_ref.at[z], pcol_ref.at[z], ps.at[k - 1], pr.at[k - 1], peer(k))

    def b_send(k):
        return remote(ball.at[w], ball.at[w], bs.at[k - 1], br.at[k - 1], wide_peer(k))

    for k in (1, 2, 3):
        r_send(k).start()
        a_send(k).start()
    wide_loop(lambda k: c_send(k).start())

    for k in (1, 2, 3):
        frm = lax.rem(z + 4 - k, 4)
        remote(rall.at[frm], rall.at[frm], rs.at[k - 1], rr.at[k - 1], peer(k)).wait_recv()
        remote(aall.at[frm], aall.at[frm], as_.at[k - 1], ar.at[k - 1], peer(k)).wait_recv()
    rsum = rall[0] + rall[1] + rall[2] + rall[3]
    rsum_ref[...] = rsum
    asum = aall[0] + aall[1] + aall[2] + aall[3]
    zero = jnp.zeros((8, width - 128), F32)
    rows = jnp.concatenate([rsum[0:8], zero], axis=1)
    more = jnp.concatenate([rsum[8:16], zero], axis=1)
    shift = own * w
    ball[w] = jnp.concatenate(
        [asum[0:3], pltpu.roll(rows, shift, 1)[1:2], pltpu.roll(more, shift, 1)[1:2], asum[5:8]], axis=0
    )
    wide_loop(lambda k: b_send(k).start())

    def c_wait(k):
        frm = lax.rem(w + wide_count - k, wide_count)
        remote(call.at[frm], call.at[frm], cs.at[k - 1], cr.at[k - 1], wide_peer(k)).wait_recv()

    wide_loop(c_wait)
    csum = lax.fori_loop(1, wide_count, lambda i, v: v + call[i], call[0])
    csum_ref[...] = csum
    pcol_ref[z] = csum[:, quarter : quarter + 256]
    for k in (1, 2, 3):
        p_send(k).start()

    def b_wait(k):
        frm = lax.rem(w + wide_count - k, wide_count)
        remote(ball.at[frm], ball.at[frm], bs.at[k - 1], br.at[k - 1], wide_peer(k)).wait_recv()

    wide_loop(b_wait)
    asum_ref[...] = lax.fori_loop(1, wide_count, lambda i, v: v + ball[i], ball[0])
    for k in (1, 2, 3):
        frm = lax.rem(z + 4 - k, 4)
        remote(pcol_ref.at[frm], pcol_ref.at[frm], ps.at[k - 1], pr.at[k - 1], peer(k)).wait_recv()
    for k in (1, 2, 3):
        r_send(k).wait_send()
        a_send(k).wait_send()
        p_send(k).wait_send()

    def sent(k):
        c_send(k).wait_send()
        b_send(k).wait_send()

    wide_loop(sent)


def reduce_stats(wide_count, final, small):
    width = final.shape[2]
    vmem = pl.BlockSpec(memory_space=pltpu.VMEM)
    dma = pltpu.SemaphoreType.DMA
    return pl.pallas_call(
        functools.partial(stats_kernel, wide_count),
        name="stats",
        in_specs=[vmem] * 2,
        out_specs=[vmem] * 4,
        out_shape=[
            jax.ShapeDtypeStruct((24, 128), F32),
            jax.ShapeDtypeStruct((4, width), F32),
            jax.ShapeDtypeStruct(small.shape, F32),
            jax.ShapeDtypeStruct((4, 4, 256), F32),
        ],
        scratch_shapes=[
            pltpu.VMEM((4, 24, 128), F32), pltpu.VMEM((4,) + small.shape, F32),
            pltpu.VMEM((wide_count, 4, width), F32), pltpu.VMEM((wide_count,) + small.shape, F32),
            dma((3,)), dma((3,)), dma((3,)), dma((3,)),
            dma((wide_count - 1,)), dma((wide_count - 1,)), dma((wide_count - 1,)), dma((wide_count - 1,)),
            dma((3,)), dma((3,)),
        ],
        compiler_params=pltpu.CompilerParams(collective_id=2, has_side_effects=True),
    )(final, small)


def finish_kernel(
    out_ref, tg_ref, mg_ref, f_ref, rsum_ref, csum_ref, asum_ref, pcol_ref,
    out_o, tg_o, mg_o, gains_o, rel_o, self_o, cross_o, ffn_o, arow_o, acol_o, proj_o, frow_o, fcol_o,
):
    own, width = f_ref.shape[1:]
    hw = self_o.shape[2]
    fw = ffn_o.shape[2]
    out_o[...] = out_ref[...]
    tg_o[...] = tg_ref[...]
    mg_o[...] = mg_ref[...]
    gains_o[...] = asum_ref[0:3, 0:width]
    heads, buckets = rel_o.shape
    per = width // 128
    for h in range(heads):
        row, first = 5 + h // per, 128 * (h % per)
        rel_o[h : h + 1, :] = asum_ref[row : row + 1, first : first + buckets]
    for ref, i in ((self_o, 0), (cross_o, 1)):
        for m, part in enumerate((0, 2, 3, 1)):
            ref[m] = f_ref[i, :, part * hw : (part + 1) * hw]
    cut = width - fw
    ffn_o[0] = f_ref[2, :, 0:fw]
    ffn_o[1, :, 0:cut] = f_ref[2, :, fw:width]
    ffn_o[1, :, cut:fw] = f_ref[3, :, 0 : fw - cut]
    ffn_o[2] = f_ref[3, :, fw - cut : width]
    rsum = rsum_ref[...]
    arow = jnp.concatenate([rsum[0:1], rsum[2:4], rsum[8:9], rsum[10:12]], axis=0)
    arow_o[...] = arow[:, 0:own] * (1.0 / width)
    frow_o[...] = rsum[16:19, 0:own] * (1.0 / (4 * fw))
    scale = 1.0 / width
    for i in range(2):
        for m, part in enumerate((0, 2, 3)):
            acol_o[3 * i + m : 3 * i + m + 1, :] = csum_ref[i : i + 1, part * hw : (part + 1) * hw] * scale
    fcol_o[0:1, :] = csum_ref[2:3, 0:fw] * scale
    fcol_o[1:2, 0:cut] = csum_ref[2:3, fw:width] * scale
    fcol_o[1:2, cut:fw] = csum_ref[3:4, 0 : fw - cut] * scale
    fcol_o[2:3, :] = csum_ref[3:4, fw - cut : width] * scale
    for i in range(2):
        cols = jnp.concatenate([pcol_ref[k, i : i + 1, 0:hw] for k in range(4)], axis=1)
        proj_o[i : i + 1, 0:width] = asum_ref[3 + i : 4 + i, 0:width] * scale
        proj_o[i : i + 1, width : 2 * width] = cols * scale


def finish(shapes, *args):
    vmem = pl.BlockSpec(memory_space=pltpu.VMEM)
    return pl.pallas_call(
        finish_kernel,
        name="finish",
        in_specs=[vmem] * len(args),
        out_specs=[vmem] * len(shapes),
        out_shape=[jax.ShapeDtypeStruct(s, d) for s, d in shapes],
    )(*args)


def local(
    tokens, memory, segments, valid_rows, norm_gains, rel_table,
    self_weights, cross_weights, ffn_weights, cotangent,
):
    wide_count = lax.axis_size("wide")
    assert lax.axis_size("narrow") == 4 and wide_count % 8 == 0 and segments.shape[0] == 1
    rows, width = tokens.shape
    mem_own = memory.shape[1]
    mem_len = 4 * mem_own
    hw = self_weights.shape[2]
    fw = ffn_weights.shape[2]
    heads = rel_table.shape[1]
    groups = wide_count // 8
    eighth = width // 8

    buckets = bucket_table(1024, BUCKETS, MAX_DIST)
    lanes = np.arange(512)
    at_lane = np.where(lanes < 128, 128 + lanes, np.maximum(lanes - 384, 0))
    pick = jnp.asarray((buckets[at_lane][None, :] == np.arange(BUCKETS)[:, None]).astype(np.float32))
    rel_pick = jnp.asarray(
        (buckets[np.maximum(lanes - 127, 0)][:, None] == np.arange(128)[None, :]).astype(np.float32)
    )

    half = width // 16
    weights, bias_line, x1, h1, q1, kv1, o1, bias, mem_full, x2, h2, q2, kv2, o2 = forward(
        valid_rows, tokens, memory[0], norm_gains, rel_table.T, pick, segments,
        jnp.swapaxes(self_weights, 1, 2).reshape(4, 4, hw // 4, width),
        jnp.swapaxes(cross_weights, 1, 2).reshape(4, 4, hw // 4, width),
        ffn_weights.reshape(3, 16, half, fw),
    )
    weights = weights.reshape(4, 4, width, width)
    mem_full = mem_full.reshape(mem_len, width)
    output, final, tokens_grad, memory_grad, small = backward(
        valid_rows, x2, cotangent, x1, mem_full, h2, h1, tokens, norm_gains, bias_line, segments, rel_pick,
        weights, q2, kv2, o2, q1, kv1, o1, bias,
    )
    if groups > 1:
        w = lax.axis_index("wide")
        mine = lax.dynamic_update_slice_in_dim(
            jnp.zeros((4, width, width), F32), final, lax.rem(w, 8) * eighth, 1
        )
        final = lax.psum_scatter(mine, "wide", scatter_dimension=1, tiled=True)
    own = final.shape[1]
    sums = reduce_stats(wide_count, final, small)
    shapes = [
        ((rows, width), BF), ((rows, width), F32), ((mem_own, width), F32), ((3, width), F32), ((heads, BUCKETS), F32),
        ((4, own, hw), F32), ((4, own, hw), F32), ((3, own, fw), F32),
        ((6, own), F32), ((6, hw), F32), ((2, 2 * width), F32), ((3, own), F32), ((3, fw), F32),
    ]
    outs = list(finish(shapes, output, tokens_grad, memory_grad, final, *sums))
    outs[2] = outs[2].reshape(1, mem_own, width)
    outs[4] = outs[4].T
    return tuple(outs)


def solution(mesh):
    in_specs = (
        P(("wide", "narrow"), None),
        P("wide", "narrow", None),
        P("wide", None),
        P("wide"),
        P(),
        P(),
        P(None, None, "narrow"),
        P(None, None, "narrow"),
        P(None, None, "narrow"),
        P(("wide", "narrow"), None),
    )
    out_specs = (
        P(("wide", "narrow"), None),
        P(("wide", "narrow"), None),
        P("wide", "narrow", None),
        P(),
        P(),
        P(None, "wide", "narrow"),
        P(None, "wide", "narrow"),
        P(None, "wide", "narrow"),
        P(None, "wide"),
        P(None, "narrow"),
        P(),
        P(None, "wide"),
        P(None, "narrow"),
    )
    return jax.shard_map(local, mesh=mesh, in_specs=in_specs, out_specs=out_specs, check_vma=False)
```

```python
import functools
import math

import jax
import jax.numpy as jnp
import numpy as np
from jax import lax
from jax.experimental import pallas as pl
from jax.experimental.pallas import tpu as pltpu
from jax.sharding import PartitionSpec as P

BUCKETS = 32
MAX_DIST = 128
EPS = 1e-06
MASKED = -1000000000.0
MESH = pl.DeviceIdType.MESH
BF = jnp.bfloat16
F32 = jnp.float32
VMEM_LIMIT = 64 * 1024 * 1024 - 65536


def bucket_table(seq_length, bucket_count, max_distance):
    exact_count = bucket_count // 2
    bucket_ids = np.zeros((seq_length,), np.int32)
    for distance in range(seq_length):
        if distance < exact_count:
            bucket_ids[distance] = distance
        else:
            scaled_log = (
                math.log(distance / exact_count)
                / math.log(max_distance / exact_count)
                * (bucket_count - exact_count)
            )
            bucket_ids[distance] = min(bucket_count - 1, exact_count + int(scaled_log))
    return bucket_ids


def mm(a, b):
    return jnp.dot(a, b, preferred_element_type=F32)


def mm_nt(a, b):
    return lax.dot_general(a, b, (((1,), (1,)), ((), ())), preferred_element_type=F32)


def mm_tn(a, b):
    return lax.dot_general(a, b, (((0,), (0,)), ((), ())), preferred_element_type=F32)


def inv_rms(v):
    return lax.rsqrt(jnp.mean(v * v, axis=-1, keepdims=True) + EPS)


def norm_back(v, gain, dh):
    r = inv_rms(v)
    gain_part = jnp.sum(dh * (v * r), axis=0, keepdims=True)
    gd = gain * dh
    dv = r * gd - v * (r * r * r) * jnp.mean(gd * v, axis=-1, keepdims=True)
    return gain_part, dv


def soft_cols(scores):
    e = jnp.exp(scores - jnp.max(scores, axis=0, keepdims=True))
    return e * (1.0 / jnp.sum(e, axis=0, keepdims=True))


def self_mask_store(mask_ref, seg_ref, z, rows, span):
    def quarter(k):
        out = jnp.full((1, rows), -1, jnp.int32)
        for kk in range(4):
            out = jnp.where(k == kk, seg_ref[:, kk * rows : (kk + 1) * rows], out)
        return out.astype(F32)

    own = quarter(z)
    keys = jnp.concatenate([quarter(z - 2), quarter(z - 1), own], axis=1)
    keys = jnp.broadcast_to(keys, (128, 3 * rows)).T
    for b in range(2):
        r = lax.broadcasted_iota(jnp.int32, (span, 128), 0)
        c = lax.broadcasted_iota(jnp.int32, (span, 128), 1)
        allowed = (c + 2 * rows >= r) & (keys[b * 128 : b * 128 + span] == own[:, b * 128 : b * 128 + 128])
        mask_ref[b] = jnp.where(allowed, 1.0, 0.0)


def full(shape):
    return pl.BlockSpec(shape, lambda j: (0,) * len(shape))


def once(shape):
    return pl.BlockSpec(shape, lambda j: (0,) * len(shape), pipeline_mode=pl.Buffered(1))


SMEM_SPEC = pl.BlockSpec(memory_space=pltpu.SMEM)


class Place:
    def __init__(self):
        self.w = lax.axis_index("wide")
        self.z = lax.axis_index("narrow")
        s = lax.rem(self.w, 8)
        self.s = s
        self.c = lax.rem(s, 2)
        self.x = lax.rem(s // 2, 2)
        self.y = s // 4
        dc, dx, dy = 1 - 2 * self.c, 2 * (1 - 2 * self.x), 4 * (1 - 2 * self.y)
        self.core_dev = {"wide": self.w + dc}
        self.x_dev = {"wide": self.w + dx}
        self.y_dev = {"wide": self.w + dy}
        self.sx, self.sy, self.sxy = s + dx, s + dy, s + dx + dy
        self.dc = dc

    def quarter(self, k):
        z = self.z
        e0, e3 = 1 - (z + 3) // 4, z // 3
        e1, e2 = (1 - z // 2) * lax.rem(z, 2), (z // 2) * (1 - lax.rem(z, 2))
        return sum(e * row[k] for e, row in zip((e0, e1, e2, e3), RANKS))

    def quarter_of(self, slot):
        return sum(jnp.where(slot == k, self.quarter(k), 0) for k in range(4))

    def narrow_dev(self, k):
        return {"narrow": lax.rem(self.z + k, 4)}

    def devices(self):
        return [self.core_dev, self.x_dev, self.y_dev] + [self.narrow_dev(k) for k in (1, 2, 3)]

    def signal_all(self):
        for dev in self.devices():
            pl.semaphore_signal(pltpu.get_barrier_semaphore(), inc=1, device_id=dev, device_id_type=MESH)

    def wait_all(self):
        pl.semaphore_wait(pltpu.get_barrier_semaphore(), len(self.devices()))

    def barrier(self):
        self.signal_all()
        self.wait_all()


def remote(src, dst, send_sem, recv_sem, dev):
    return pltpu.make_async_remote_copy(
        src_ref=src, dst_ref=dst, send_sem=send_sem, recv_sem=recv_sem, device_id=dev, device_id_type=MESH
    )


RANKS = ((0, 1, 2, 3), (1, 0, 2, 3), (2, 3, 1, 0), (3, 2, 1, 0))
EARLY = 5


def forward_kernel(
    valid_ref, tok_ref, mem_ref, gain_ref, rel_ref, pick_ref, seg_ref, ws_ref, wc_ref, wf_ref,
    w_ref, bd_ref, x1_ref, h1_ref, q_ref, kv_ref, o_ref, bias_ref, mfull_ref, x2_ref, h2_ref, q2_ref, kv2_ref, o2_ref,
    wv, lines, xt, mt, mask_ref, zs, zr, ps, pr, ts, tr, ms, mr, ls, fs, os_,
):
    at = Place()
    z, s = at.z, at.s
    j = pl.program_id(0)
    units = 4
    rows, width = tok_ref.shape
    ext = 3 * rows
    span = 2 * rows + 128
    hw = q_ref.shape[2]
    fw = wf_ref.shape[3]
    heads = hw // 64
    part = rows // 4
    half = width // 16
    mine = pl.ds(2 * s, 2)

    def edge(k):
        return [(d, RANKS[k + d].index(k)) for d in (1, -1) if 0 <= k + d < 4]

    def own_send(u, k, d, rank):
        return remote(
            wv.at[u, 0, mine], wv.at[u, rank, mine], zs.at[u, 0 if d > 0 else 1], zr.at[u, rank], {"narrow": k + d}
        )

    def own_sends(u, act):
        for k in range(4):
            @pl.when(z == k)
            def _():
                for d, rank in edge(k):
                    act(own_send(u, k, d, rank))

    def forwards(u, r, act):
        for k in (1, 2):
            quarter = RANKS[k][r]
            d = 1 if quarter < k else -1
            there = RANKS[k + d].index(quarter)

            @pl.when(z == k)
            def _():
                act(remote(wv.at[u, r, mine], wv.at[u, there, mine], zs.at[u, 1 + r], zr.at[u, there], {"narrow": k + d}))

    def tok_copy(hop, p):
        part_rows = pl.ds(p * part, part)
        src = tok_ref.at[part_rows] if hop == 1 else xt.at[1, part_rows]
        return remote(src, xt.at[2 - hop, part_rows], ts.at[hop - 1, p], tr.at[hop - 1, p], {"narrow": z + 1})

    def tok_senders(hop):
        return z < 3 if hop == 1 else jnp.logical_and(z >= 1, z < 3)

    def tok_send(hop, parts):
        if hop == 2:
            @pl.when(z >= 1)
            def _():
                for p in parts:
                    tok_copy(1, p).wait_recv()

        @pl.when(tok_senders(hop))
        def _():
            for p in parts:
                tok_copy(hop, p).start()

    def mem_copy(i, d):
        k = z - d * i
        src = mem_ref if i == 0 else mt.at[k]
        place = i if d > 0 else 3 + i
        return remote(src, mt.at[k], ms.at[place], mr.at[place], {"narrow": z + d})

    def mem_sends(i, act):
        @pl.when(jnp.logical_and(z >= i, z < 3))
        def _():
            act(mem_copy(i, 1))

        @pl.when(jnp.logical_and(z >= 1, z < 4 - i))
        def _():
            act(mem_copy(i, -1))

    def mem_arrived(i):
        for d in (1, -1):
            @pl.when(z > i if d > 0 else z < 3 - i)
            def _():
                here = mt.at[z - d * (1 + i)]
                place = i if d > 0 else 3 + i
                remote(here, here, ms.at[place], mr.at[place], at.x_dev).wait_recv()

    def piece(u, r, kind):
        first, n, dev = {
            0: (2 * s, 1, at.x_dev), 1: (2 * s + 1, 1, at.x_dev), 2: (2 * at.sy + 1, 1, at.x_dev),
            3: (2 * s + 1, 1, at.y_dev), 4: (2 * s, 1, at.y_dev), 5: (2 * at.sx, 1, at.y_dev),
            6: (2 * s, 2, at.core_dev), 7: (2 * at.sx, 2, at.core_dev),
            8: (2 * at.sy, 2, at.core_dev), 9: (2 * at.sxy, 2, at.core_dev),
        }[kind]
        region = wv.at[u, r, pl.ds(first, n)]
        i = u * 3 + r - 1
        return remote(region, region, ps.at[i, kind], pr.at[i, kind], dev)

    def arrived(u, r, kind):
        first, n = {
            0: (2 * at.sx, 1), 1: (2 * at.sx + 1, 1), 2: (2 * at.sxy + 1, 1),
            3: (2 * at.sy + 1, 1), 4: (2 * at.sy, 1), 5: (2 * at.sxy, 1),
            6: (2 * (s + at.dc), 2), 7: (2 * (at.sx + at.dc), 2),
            8: (2 * (at.sy + at.dc), 2), 9: (2 * (at.sxy + at.dc), 2),
        }[kind]
        region = wv.at[u, r, pl.ds(first, n)]
        i = u * 3 + r - 1
        remote(region, region, ps.at[i, kind], pr.at[i, kind], at.x_dev).wait_recv()

    pieces = [(u, r) for u in range(units) for r in (1, 2, 3)]

    def step0(t):
        if not 0 <= t < len(pieces):
            return
        u, r = pieces[t]
        region = wv.at[u, r, mine]
        remote(region, region, zs.at[u, 0], zr.at[u, r], at.x_dev).wait_recv()
        forwards(u, r, lambda copy: copy.start())
        for kind in (0, 3, 4, 1, 6):
            piece(u, r, kind).start()
        if t == 0:
            tok_send(1, (0, 1))
        if t == 1:
            tok_send(1, (2, 3))
        if t == 2:
            own_sends(2, lambda copy: copy.start())
        if t == 3:
            tok_send(2, (0, 1, 2, 3))
        if t == 4:
            mem_sends(0, lambda copy: copy.start())
        if t == 5:
            own_sends(3, lambda copy: copy.start())
        if t in (6, 8):
            i = (t - 4) // 2
            mem_arrived(i - 1)
            mem_sends(i, lambda copy: copy.start())

    def step1(t):
        if not 0 <= t < len(pieces):
            return
        u, r = pieces[t]
        arrived(u, r, 0)
        piece(u, r, 5).start()
        arrived(u, r, 3)
        piece(u, r, 2).start()
        arrived(u, r, 1)
        piece(u, r, 7).start()
        arrived(u, r, 4)
        piece(u, r, 8).start()

    def step2(t):
        if not 0 <= t < len(pieces):
            return
        u, r = pieces[t]
        arrived(u, r, 5)
        arrived(u, r, 2)
        piece(u, r, 9).start()

    def keep(u, k):
        return pltpu.make_async_copy(wv.at[u, k], w_ref.at[u, k], os_.at[u, k])

    def step3(t):
        if not 0 <= t < len(pieces):
            return
        u, r = pieces[t]
        for kind in (6, 7, 8, 9):
            arrived(u, r, kind)
        keep(u, r).start()

    def attn_loads(i):
        src = (ws_ref, wc_ref)[i]
        return [
            pltpu.make_async_copy(src.at[part], wv.at[i, 0, pl.ds(4 * k, 4)], ls.at[i, k])
            for k, part in enumerate((0, 3, 1, 2))
        ]

    def ffn_loads():
        cut = width - fw
        return [
            pltpu.make_async_copy(wf_ref.at[0], wv.at[2, 0, :, :, 0:fw], fs.at[0]),
            pltpu.make_async_copy(wf_ref.at[1, :, :, 0:cut], wv.at[2, 0, :, :, fw:width], fs.at[1]),
            pltpu.make_async_copy(wf_ref.at[1, :, :, cut:fw], wv.at[3, 0, :, :, 0 : fw - cut], fs.at[2]),
            pltpu.make_async_copy(wf_ref.at[2], wv.at[3, 0, :, :, fw - cut : width], fs.at[3]),
        ]

    @pl.when(j == 0)
    def _():
        at.signal_all()
        for copy in attn_loads(0) + attn_loads(1) + ffn_loads():
            copy.start()
        at.wait_all()
        for copy in attn_loads(0):
            copy.wait()
        own_sends(0, lambda copy: copy.start())
        for copy in attn_loads(1):
            copy.wait()
        own_sends(1, lambda copy: copy.start())
        for copy in ffn_loads():
            copy.wait()
        for u in range(units):
            keep(u, 0).start()
        x = tok_ref[...].astype(F32)
        x1_ref[...] = x
        h1_ref[2 * rows : ext, :] = (x * inv_rms(x) * gain_ref[0:1, :]).astype(BF)
        self_mask_store(mask_ref, seg_ref, z, rows, span)
        lines[...] = lax.dot_general(
            rel_ref[...], pick_ref[...], (((1,), (0,)), ((), ())),
            preferred_element_type=F32, precision=lax.Precision.HIGHEST,
        )
        for k in range(4):
            first = at.quarter(k) * heads
            for hh in range(heads):
                bd_ref[k, hh : hh + 1, :] = lines[pl.ds(first + hh, 1), :]
        for t in range(EARLY):
            step0(t)
            step1(t - 1)
            step2(t - 2)
            step3(t - 3)

        @pl.when(z >= 2)
        def _():
            for p in range(4):
                tok_copy(2, p).wait_recv()

        for t in range(2):
            v = jnp.where(z >= 2 - t, xt[t].astype(F32), 0.0)
            h1_ref[t * rows : (t + 1) * rows, :] = (v * inv_rms(v) * gain_ref[0:1, :]).astype(BF)

    def hook(i, first, last):
        for jj in range(first, last):
            t = EARLY + jj

            @pl.when(j == jj)
            def _():
                if i == 0:
                    step3(t - 3)
                    step0(t)
                if i == 1:
                    step1(t - 1)
                if i == 2:
                    step2(t - 2)

    def flat(u, k, lo, hi):
        return wv[u, k, lo // half : hi // half].reshape(hi - lo, width)

    @pl.when(j < 4)
    def _():
        hook(0, 0, 4)
        q = mm_nt(h1_ref[2 * rows : ext, :], flat(0, j, 0, hw)).astype(BF)
        kv = mm_nt(h1_ref[...], flat(0, j, 2 * hw, 4 * hw)).astype(BF)
        q_ref[0] = q
        kv_ref[0] = kv
        parts = []
        for hh in range(heads):
            line = jnp.broadcast_to(bd_ref[j, hh : hh + 1, :], (256, 512))
            bias = pltpu.roll(line, 0, 1, stride=1, stride_axis=0)[:, 0:128]
            bias_ref[0, hh] = bias
            far = bd_ref[j, hh : hh + 1, 127:128]
            cols = []
            for b in range(2):
                k = kv[b * 128 : b * 128 + span, hh * 64 : hh * 64 + 64]
                v = kv[b * 128 : b * 128 + span, hw + hh * 64 : hw + hh * 64 + 64]
                qb = q[b * 128 : b * 128 + 128, hh * 64 : hh * 64 + 64]
                sc = mm_nt(k, qb)
                sc = jnp.concatenate([sc[: span - 256] + far, sc[span - 256 :] + bias], axis=0)
                sc = jnp.where(mask_ref[b] > 0.5, sc, MASKED)
                cols.append(mm_tn(v, soft_cols(sc).astype(BF)))
            parts.append(jnp.concatenate(cols, axis=1))
            if hh < 2:
                hook(1 + hh, 0, 4)
        o = jnp.concatenate(parts, axis=0).T.astype(BF)
        o_ref[0] = o
        x1_ref[...] += mm(o, flat(0, j, hw, 2 * hw))

    @pl.when(j == 4)
    def _():
        x1 = x1_ref[...]
        x2_ref[...] = x1
        h2_ref[...] = (x1 * inv_rms(x1) * gain_ref[1:2, :]).astype(BF)
        mfull_ref[z] = mem_ref[...]
        mem_arrived(2)
        for k in range(4):
            @pl.when(z != k)
            def _():
                mfull_ref[k] = mt[k]

    @pl.when(j >= 4)
    def _():
        hook(0, 4, 8)
        mem = mfull_ref.shape[0] * mfull_ref.shape[1]
        q = mm_nt(h2_ref[...], flat(1, j - 4, 0, hw)).astype(BF)
        kv = mm_nt(mfull_ref[...].reshape(mem, width), flat(1, j - 4, 2 * hw, 4 * hw)).astype(BF)
        q2_ref[0] = q
        kv2_ref[0] = kv
        allowed = lax.broadcasted_iota(jnp.int32, (mem, rows), 0) < valid_ref[0]
        parts = []
        for hh in range(heads):
            k = kv[:, hh * 64 : hh * 64 + 64]
            v = kv[:, hw + hh * 64 : hw + hh * 64 + 64]
            sc = jnp.where(allowed, mm_nt(k, q[:, hh * 64 : hh * 64 + 64]), MASKED)
            parts.append(mm_tn(v, soft_cols(sc).astype(BF)))
            if hh < 2:
                hook(1 + hh, 4, 8)
        o = jnp.concatenate(parts, axis=0).T.astype(BF)
        o2_ref[0] = o
        x2_ref[...] += mm(o, flat(1, j - 4, hw, 2 * hw))

    @pl.when(j == 7)
    def _():
        for t in range(EARLY + 8, len(pieces) + 3):
            step0(t)
            step1(t - 1)
            step2(t - 2)
            step3(t - 3)
        for u, r in pieces:
            for kind in range(10):
                piece(u, r, kind).wait_send()
            forwards(u, r, lambda copy: copy.wait_send())
        for u in range(units):
            own_sends(u, lambda copy: copy.wait_send())
            for k in range(4):
                keep(u, k).wait()
        for hop in (1, 2):
            @pl.when(tok_senders(hop))
            def _():
                for p in range(4):
                    tok_copy(hop, p).wait_send()
        for i in range(3):
            mem_sends(i, lambda copy: copy.wait_send())


def forward(valid_rows, tokens, memory, gains, rel, pick, seg, ws, wc, wf):
    rows, width = tokens.shape
    mem_own = memory.shape[0]
    hw = 4 * ws.shape[2]
    heads = hw // 64
    ext = 3 * rows
    mem = 4 * mem_own
    half = width // 16
    any_spec = pl.BlockSpec(memory_space=pl.ANY)
    dma = pltpu.SemaphoreType.DMA

    def early(shape):
        return pl.BlockSpec((1,) + shape, lambda j: (jnp.minimum(j, 3),) + (0,) * len(shape))

    def late(shape):
        return pl.BlockSpec((1,) + shape, lambda j: (jnp.maximum(j - 4, 0),) + (0,) * len(shape))

    out = [
        ((4, 4, 16, half, width), BF, any_spec), ((4, heads, 512), F32, full((4, heads, 512))),
        ((rows, width), F32, full((rows, width))), ((ext, width), BF, full((ext, width))),
        ((4, rows, hw), BF, early((rows, hw))), ((4, ext, 2 * hw), BF, early((ext, 2 * hw))),
        ((4, rows, hw), BF, early((rows, hw))), ((4, heads, 256, 128), F32, early((heads, 256, 128))),
        ((4, mem_own, width), BF, full((4, mem_own, width))),
        ((rows, width), F32, full((rows, width))), ((rows, width), BF, full((rows, width))),
        ((4, rows, hw), BF, late((rows, hw))), ((4, mem, 2 * hw), BF, late((mem, 2 * hw))),
        ((4, rows, hw), BF, late((rows, hw))),
    ]
    return pl.pallas_call(
        forward_kernel,
        name="forward",
        grid=(8,),
        in_specs=[
            SMEM_SPEC, full((rows, width)), full((mem_own, width)), full((3, width)),
            full(rel.shape), full(pick.shape), full(seg.shape), any_spec, any_spec, any_spec,
        ],
        out_specs=[spec for _, _, spec in out],
        out_shape=[jax.ShapeDtypeStruct(shape, dtype) for shape, dtype, _ in out],
        scratch_shapes=[
            pltpu.VMEM((4, 4, 16, half, width), BF), pltpu.VMEM((4 * heads, 512), F32),
            pltpu.VMEM((2, rows, width), BF), pltpu.VMEM((4, mem_own, width), BF),
            pltpu.VMEM((2, 2 * rows + 128, 128), F32),
            dma((4, 5)), dma((4, 4)), dma((12, 10)), dma((12, 10)),
            dma((2, 4)), dma((2, 4)), dma((6,)), dma((6,)), dma((2, 4)), dma((4,)), dma((4, 4)),
        ],
        compiler_params=pltpu.CompilerParams(
            collective_id=0, has_side_effects=True, vmem_limit_bytes=VMEM_LIMIT, dimension_semantics=("arbitrary",)
        ),
    )(valid_rows, tokens, memory, gains, rel, pick, seg, ws, wc, wf)


CHUNKS = [(2 + i % 2, i // 2) for i in range(8)] + [(1, i) for i in range(4)] + [(0, i) for i in range(4)]
HELD = 12
LAG = 4
TICKS = [(1, 0), (2, 0), (3, 0), (4, 1), (5, 1), (6, 1), (7, 1), (8, 0), (8, 2), (9, 1), (10, 0), (10, 2), (11, 1)]


def backward_kernel(
    valid_ref, x2_ref, cot_ref, x1_ref, mem_ref, h2_ref, h1_ref, tok_ref, gain_ref, bd_ref, seg_ref, pick_ref,
    w_ref, q2_ref, kv2_ref, o2_ref, q1_ref, kv1_ref, o1_ref, bias_ref,
    out_ref, f_ref, tg_ref, mg_ref, small_ref,
    g, wbuf, acc, act_in, res, gsum_ref, rel_ref, do_ref, dqt_ref, dkv_ref, mask_ref, flip_ref, dxo, dmo, rc, xr, yr, xr2, yr2, zb, dxr, dmr,
    wsem, cs, cr, xs, xrs, ys, yrs, x2s, x2r, y2s, y2r, zs, zr, dxs, dxrs, dms, dmrs,
):
    at = Place()
    z = at.z
    j = pl.program_id(0)
    rows, width = x2_ref.shape
    mem = mem_ref.shape[0]
    ext = 3 * rows
    span = 2 * rows + 128
    hw = q1_ref.shape[2]
    heads = hw // 64
    fw = wbuf.shape[2] * 2 // 3
    own_rows = g.shape[3]
    half = own_rows // 2
    n = len(CHUNKS)
    lo, hi = pl.ds(0, half), pl.ds(half, half)
    yx = 2 * at.y + at.x
    top, bottom = pl.ds(0, rows), pl.ds(2 * rows, rows)

    def w_load(unit, slot, k):
        return pltpu.make_async_copy(w_ref.at[unit, slot], wbuf.at[k], wsem.at[k])

    def held(i):
        return g.at[i % HELD]

    def add(ref, other):
        ref[...] = ref[...] + other[...]

    def core_send(i):
        return remote(held(i).at[:, pl.ds(1 - at.c, 1)], rc.at[i], cs.at[i], cr.at[i], at.core_dev)

    def x_send(i, yb):
        src = held(i).at[2 * yb + 1 - at.x, at.c, lo]
        return remote(src, xr.at[i, yb], xs.at[i, yb], xrs.at[i, yb], at.x_dev)

    def y_send(i, xb):
        src = held(i).at[2 * (1 - at.y) + xb, at.c, hi]
        return remote(src, yr.at[i, xb], ys.at[i, xb], yrs.at[i, xb], at.y_dev)

    def y2_send(i):
        return remote(held(i).at[2 * (1 - at.y) + at.x, at.c, lo], yr2.at[i], y2s.at[i], y2r.at[i], at.y_dev)

    def x2_send(i):
        return remote(held(i).at[2 * at.y + 1 - at.x, at.c, hi], xr2.at[i], x2s.at[i], x2r.at[i], at.x_dev)

    d = 1 - 2 * (z // 2)
    is_end = jnp.logical_or(z == 0, z == 3)
    is_inner = jnp.logical_or(z == 1, z == 2)

    def z_send(i, dst, step):
        unit = CHUNKS[i][0]
        return remote(held(i).at[yx, at.c], zb.at[unit, dst], zs.at[i], zr.at[unit, dst], {"narrow": z + step})

    def z_wait(i, k):
        unit = CHUNKS[i][0]
        remote(zb.at[unit, k], zb.at[unit, k], zs.at[i], zr.at[unit, k], at.x_dev).wait_recv()

    def step_b(i):
        core_send(i).wait_recv()
        add(held(i).at[:, pl.ds(at.c, 1)], rc.at[i])
        for b in range(2):
            x_send(i, b).start()
            y_send(i, b).start()

    def step_c(i):
        for b in range(2):
            x_send(i, b).wait_recv()
            y_send(i, b).wait_recv()
            add(held(i).at[2 * b + at.x, at.c, lo], xr.at[i, b])
            add(held(i).at[2 * at.y + b, at.c, hi], yr.at[i, b])
        y2_send(i).start()
        x2_send(i).start()

    def step_d(i):
        y2_send(i).wait_recv()
        add(held(i).at[yx, at.c, lo], yr2.at[i])
        x2_send(i).wait_recv()
        add(held(i).at[yx, at.c, hi], xr2.at[i])

    def step_e(i):
        @pl.when(is_end)
        def _():
            if CHUNKS[i][1] < 3:
                z_send(i, CHUNKS[i][1], d).start()

    def step_f(i):
        unit, s = CHUNKS[i]

        @pl.when(is_inner)
        def _():
            if s < 2:
                z_wait(i, s)
                add(held(i).at[yx, at.c], zb.at[unit, s])
                z_send(i, 3 + s, d).start()
            if s == 2:
                z_wait(i, 3)
                add(held(i).at[yx, at.c], zb.at[unit, 3])
                z_send(i, 2, -d).start()
            if s == 3:
                z_wait(i, 2)
                z_wait(i, 4)
                f_ref[unit] = (
                    held(i)[yx, at.c].astype(F32) + zb[unit, 2].astype(F32) + zb[unit, 4].astype(F32)
                )

        if s == 3:
            @pl.when(is_end)
            def _():
                z_wait(i, 2)
                f_ref[unit] = held(i)[yx, at.c].astype(F32) + zb[unit, 2].astype(F32)

    def sent(i):
        core_send(i).wait_send()
        for b in range(2):
            x_send(i, b).wait_send()
            y_send(i, b).wait_send()
        y2_send(i).wait_send()
        x2_send(i).wait_send()
        if CHUNKS[i][1] < 3:
            z_send(i, 0, d).wait_send()

    def tick(t):
        for k, step in ((0, step_b), (1, step_c), (2, step_d), (2, step_e), (LAG, step_f)):
            if 0 <= t - k < n:
                step(t - k)

    def hook(place, first, last):
        for t, (jj, p) in enumerate(TICKS):
            if p == place and first <= jj < last:
                @pl.when(j == jj)
                def _():
                    tick(t)

    def dx_send(t):
        return remote(dxo.at[t], dxr.at[t], dxs.at[t], dxrs.at[t], {"narrow": z - 1})

    def dm_send(k):
        return remote(dmo.at[lax.rem(z + k, 4)], dmr.at[k - 1], dms.at[k - 1], dmrs.at[k - 1], at.narrow_dev(k))

    @pl.when(j == 0)
    def _():
        for b in range(2):
            w_load(2 + b, 3, b).start()
        at.signal_all()
        x2 = x2_ref[...]
        acc[0:rows, :] = x2
        acc[rows : 2 * rows, :] = jnp.zeros((rows, width), F32)
        act_in[...] = (x2 * inv_rms(x2) * gain_ref[2:3, :]).astype(BF)

    @pl.when(j < 4)
    def _():
        k = 2 * lax.rem(j, 2)
        for b in range(2):
            w_load(2 + b, 3 - j, k + b).wait()

        @pl.when(j < 3)
        def _():
            for b in range(2):
                w_load(2 + b, 2 - j, 2 - k + b).start()

        @pl.when(j == 3)
        def _():
            w_load(1, 3, 0).start()

        @pl.when(j == 0)
        def _():
            at.wait_all()

        hook(0, 0, 4)
        h3 = act_in[...]
        df = cot_ref[...]
        wg = wbuf[k, :, 0:fw]
        wu = jnp.concatenate([wbuf[k, :, fw:], wbuf[k + 1, :, 0 : fw // 2]], axis=1)
        wd = wbuf[k + 1, :, fw // 2 :]
        gate = mm(h3, wg)
        up = mm(h3, wu)
        c0 = math.sqrt(2.0 / math.pi)
        gate2 = gate * gate
        t = jnp.tanh(c0 * (gate + 0.044715 * gate2 * gate))
        part = 0.5 * (1.0 + t)
        gelu = gate * part
        slope = part + 0.5 * gate * (1.0 - t * t) * (c0 * (1.0 + 3.0 * 0.044715 * gate2))
        act = (gelu * up).astype(BF)
        acc[0:rows, :] += mm_nt(act, wd)
        da = mm(df, wd)
        dgate = (da * up * slope).astype(BF)
        dup = (da * gelu).astype(BF)
        dgu = jnp.concatenate([dgate, dup], axis=1)
        ggu = mm_tn(h3, dgu).astype(BF)
        blocks = (4, 2, own_rows)
        g[2 * j] = ggu[:, 0 : fw * 3 // 2].reshape(blocks + (width,))
        g[2 * j + 1, :, :, :, 0 : fw // 2] = ggu[:, fw * 3 // 2 :].reshape(blocks + (fw // 2,))
        g[2 * j + 1, :, :, :, fw // 2 :] = mm_tn(df, act).astype(BF).reshape(blocks + (fw,))
        acc[rows : 2 * rows, :] += mm_nt(dgate, wg) + mm_nt(dup, wu)
        for jj in range(4):
            @pl.when(j == jj)
            def _():
                core_send(2 * jj).start()
                core_send(2 * jj + 1).start()

    @pl.when(j == 3)
    def _():
        out_ref[...] = acc[0:rows, :].astype(BF)
        gain_part, dv = norm_back(x2_ref[...], gain_ref[2:3, :], acc[rows : 2 * rows, :])
        gsum_ref[16:24, :] = jnp.broadcast_to(gain_part, (8, width))
        g2 = cot_ref[...].astype(F32) + dv
        res[...] = g2
        act_in[...] = g2.astype(BF)
        acc[...] = jnp.zeros_like(acc)

    @pl.when(jnp.logical_and(j >= 4, j < 8))
    def _():
        k0 = j - 4
        w_load(1, 7 - j, k0).wait()

        @pl.when(j < 7)
        def _():
            w_load(1, 6 - j, k0 + 1).start()

        @pl.when(j == 7)
        def _():
            w_load(0, 3, 0).start()

        do_ref[...] = mm_nt(act_in[...], wbuf[k0, hw : 2 * hw, :]).astype(BF)
        for hh in range(heads):
            h_cols, v_cols = slice(hh * 64, hh * 64 + 64), slice(hw + hh * 64, hw + hh * 64 + 64)
            k = kv2_ref[0, :, h_cols]
            v = kv2_ref[0, :, v_cols]
            qh = q2_ref[0, :, h_cols]
            doh = do_ref[:, h_cols]
            allowed = lax.broadcasted_iota(jnp.int32, (mem, rows), 0) < valid_ref[0]
            p = soft_cols(jnp.where(allowed, mm_nt(k, qh), MASKED))
            dp = mm_nt(v, doh)
            ds = (p * (dp - jnp.sum(p * dp, axis=0, keepdims=True))).astype(BF)
            dkv_ref[0:mem, v_cols] = mm(p.astype(BF), doh).astype(BF)
            dkv_ref[0:mem, h_cols] = mm(ds, qh).astype(BF)
            dqt_ref[h_cols, :] = mm_tn(k, ds)
            hook(hh, 4, 8)
        dc = act_in[...]
        dq = dqt_ref[...].T.astype(BF)
        dkv = dkv_ref[0:mem, :]
        zero = jnp.zeros((rows, hw), BF)
        left = jnp.concatenate([h2_ref[...], dc], axis=0)
        right = jnp.concatenate(
            [jnp.concatenate([dq, zero], axis=1), jnp.concatenate([zero, o2_ref[0]], axis=1)], axis=0
        )
        blocks = (4, 2, own_rows, 2 * hw)
        g[4 + j, :, :, :, 0 : 2 * hw] = mm_tn(left, right).astype(BF).reshape(blocks)
        g[4 + j, :, :, :, 2 * hw : 4 * hw] = mm_tn(mem_ref[...], dkv).astype(BF).reshape(blocks)
        for jj in range(4, 8):
            @pl.when(j == jj)
            def _():
                core_send(4 + jj).start()
        acc[0:rows, :] += mm(dq, wbuf[k0, 0:hw, :])
        acc[rows : rows + mem, :] += mm(dkv, wbuf[k0, 2 * hw : 4 * hw, :])

    @pl.when(j == 7)
    def _():
        for k in range(4):
            dmo[k] = acc[rows + k * (mem // 4) : rows + (k + 1) * (mem // 4), :].astype(BF)
        for k in (1, 2, 3):
            dm_send(k).start()
        gain_part, dv = norm_back(x1_ref[...], gain_ref[1:2, :], acc[0:rows, :])
        gsum_ref[8:16, :] = jnp.broadcast_to(gain_part, (8, width))
        g1 = res[...] + dv
        res[...] = g1
        act_in[...] = g1.astype(BF)
        acc[...] = jnp.zeros_like(acc)
        self_mask_store(mask_ref, seg_ref, z, rows, span)
        rel_ref[...] = jnp.zeros_like(rel_ref)
        r = lax.broadcasted_iota(jnp.int32, (256, 256), 0)
        c = lax.broadcasted_iota(jnp.int32, (256, 256), 1)
        flip_ref[...] = jnp.where(r + c == 255, 1.0, 0.0).astype(BF)

    @pl.when(j >= 8)
    def _():
        k0 = j - 8
        w_load(0, 11 - j, k0).wait()

        @pl.when(j < 11)
        def _():
            w_load(0, 10 - j, k0 + 1).start()

        do_ref[...] = mm_nt(act_in[...], wbuf[k0, hw : 2 * hw, :]).astype(BF)
        for hh in range(heads):
            h_cols, v_cols = slice(hh * 64, hh * 64 + 64), slice(hw + hh * 64, hw + hh * 64 + 64)
            far = bd_ref[11 - j, hh : hh + 1, 127:128]
            dq_cols, dks, dvs = [], [], []
            band = jnp.zeros((256, 128), F32)
            total = jnp.zeros((1, 128), F32)
            for b in range(2):
                k = kv1_ref[0, b * 128 : b * 128 + span, h_cols]
                v = kv1_ref[0, b * 128 : b * 128 + span, v_cols]
                qb = q1_ref[0, b * 128 : b * 128 + 128, h_cols]
                dob = do_ref[b * 128 : b * 128 + 128, h_cols]
                s = mm_nt(k, qb)
                s = jnp.concatenate([s[: span - 256] + far, s[span - 256 :] + bias_ref[0, hh]], axis=0)
                s = jnp.where(mask_ref[b] > 0.5, s, MASKED)
                p = soft_cols(s)
                dp = mm_nt(v, dob)
                ds = (p * (dp - jnp.sum(p * dp, axis=0, keepdims=True))).astype(BF)
                dvs.append(mm(p.astype(BF), dob))
                dks.append(mm(ds, qb))
                dq_cols.append(mm_tn(k, ds))
                band = band + mm(flip_ref[...], ds[span - 256 :])
                total = total + jnp.sum(ds[: span - 256].astype(F32), axis=0, keepdims=True)
            gap = jnp.zeros((128, 64), F32)
            dk = jnp.concatenate([dks[0], gap], 0) + jnp.concatenate([gap, dks[1]], 0)
            dv = jnp.concatenate([dvs[0], gap], 0) + jnp.concatenate([gap, dvs[1]], 0)
            dkv_ref[:, h_cols] = dk.astype(BF)
            dkv_ref[:, v_cols] = dv.astype(BF)
            dqt_ref[h_cols, :] = jnp.concatenate(dq_cols, axis=1)
            wide_band = jnp.concatenate([band, jnp.zeros((256, 384), F32)], axis=1)
            aligned = pltpu.roll(wide_band, 0, 1, stride=1, stride_axis=0)
            line = jnp.sum(aligned, axis=0, keepdims=True)
            lane = lax.broadcasted_iota(jnp.int32, (1, 512), 1)
            far_sum = jnp.sum(total, axis=1, keepdims=True)
            rel_ref[pl.ds(at.quarter_of(11 - j) * heads + hh, 1), :] = jnp.where(lane == 511, far_sum, line)
            hook(hh, 8, 12)
        da = act_in[...]
        dq = dqt_ref[...].T.astype(BF)
        dkv = dkv_ref[...]
        zero = jnp.zeros((rows, hw), BF)
        left = jnp.concatenate([h1_ref[2 * rows : ext, :], da], axis=0)
        right = jnp.concatenate(
            [jnp.concatenate([dq, zero], axis=1), jnp.concatenate([zero, o1_ref[0]], axis=1)], axis=0
        )
        for jj in range(8, 12):
            @pl.when(j == jj)
            def _():
                sent(jj - 8)
        blocks = (4, 2, own_rows, 2 * hw)
        g[j - 8, :, :, :, 0 : 2 * hw] = mm_tn(left, right).astype(BF).reshape(blocks)
        g[j - 8, :, :, :, 2 * hw : 4 * hw] = mm_tn(h1_ref[...], dkv).astype(BF).reshape(blocks)
        for jj in range(8, 12):
            @pl.when(j == jj)
            def _():
                core_send(4 + jj).start()
        acc[...] += mm(dkv, wbuf[k0, 2 * hw : 4 * hw, :])
        acc[2 * rows : ext, :] += mm(dq, wbuf[k0, 0:hw, :])

    @pl.when(j == 11)
    def _():
        for t in range(2):
            dxo[t] = acc[t * rows : (t + 1) * rows, :].astype(BF)

        @pl.when(z >= 2)
        def _():
            dx_send(0).start()

        @pl.when(z == 3)
        def _():
            dx_send(1).start()
        last = n + LAG
        for t in range(len(TICKS), last):
            tick(t)
            if t == len(TICKS):
                mg_ref[...] = dmo[z].astype(F32)
                for k in (1, 2, 3):
                    dm_send(k).wait_recv()
                    mg_ref[...] += dmr[k - 1].astype(F32)
            if t == len(TICKS) + 1:
                @pl.when(is_inner)
                def _():
                    dx_send(0).wait_recv()
                    add(dxo.at[1], dxr.at[0])
                    dx_send(1).start()
            if t == len(TICKS) + 3:
                @pl.when(z < 3)
                def _():
                    dx_send(1).wait_recv()
                    acc[2 * rows : ext, :] += dxr[1].astype(F32)
                gain_part, dv = norm_back(tok_ref[...].astype(F32), gain_ref[0:1, :], acc[2 * rows : ext, :])
                rel = lax.dot_general(
                    rel_ref[...], pick_ref[...], (((1,), (0,)), ((), ())),
                    preferred_element_type=F32, precision=lax.Precision.HIGHEST,
                )
                gains = [gain_part, gsum_ref[8:9, :], gsum_ref[16:17, :], jnp.zeros((2, width), F32)]
                per = width // 128
                lines = [
                    jnp.concatenate([rel[per * k + h : per * k + h + 1] for h in range(per)], axis=1)
                    for k in range(2)
                ]
                small_ref[...] = jnp.concatenate(gains + lines + [jnp.zeros((1, width), F32)], axis=0)
                tg_ref[...] = res[...] + dv
        for i in range(n - HELD, n):
            sent(i)
        for t in range(2):
            @pl.when(z >= 2 - t)
            def _():
                dx_send(t).wait_send()
        for k in (1, 2, 3):
            dm_send(k).wait_send()


def backward(
    valid_rows, x2, cot, x1, mem_full, h2, h1, tokens, gains, bias_line, seg, pick,
    weights, q2, kv2, o2, q1, kv1, o1, bias,
):
    rows, width = x2.shape
    mem = mem_full.shape[0]
    hw = q1.shape[2]
    ext = 3 * rows
    own = width // 8
    half = own // 2
    n = len(CHUNKS)
    dma = pltpu.SemaphoreType.DMA

    def slot(last, a):
        shape = a.shape[1:]
        return pl.BlockSpec(
            (1,) + shape, lambda j: (jnp.clip(last - j, 0, 3),) + (0,) * len(shape)
        )

    out = [
        ((rows, width), BF), ((4, own, width), F32), ((rows, width), F32), ((mem // 4, width), F32),
        ((8, width), F32),
    ]
    shapes = [jax.ShapeDtypeStruct(s, d) for s, d in out]
    return pl.pallas_call(
        backward_kernel,
        name="backward",
        grid=(12,),
        in_specs=[
            SMEM_SPEC, *[once(a.shape) for a in (x2, cot, x1, mem_full, h2, h1, tokens)],
            full(gains.shape), full(bias_line.shape), full(seg.shape), full(pick.shape),
            pl.BlockSpec(memory_space=pl.ANY),
            slot(7, q2), slot(7, kv2), slot(7, o2), slot(11, q1), slot(11, kv1), slot(11, o1), slot(11, bias),
        ],
        out_specs=[once(s) for s, _ in out],
        out_shape=shapes,
        scratch_shapes=[
            pltpu.VMEM((HELD, 4, 2, own, width), BF), pltpu.VMEM((4, width, width), BF),
            pltpu.VMEM((ext, width), F32), pltpu.VMEM((rows, width), BF), pltpu.VMEM((rows, width), F32),
            pltpu.VMEM((24, width), F32), pltpu.VMEM((16, 512), F32),
            pltpu.VMEM((rows, hw), BF), pltpu.VMEM((hw, rows), F32), pltpu.VMEM((ext, 2 * hw), BF),
            pltpu.VMEM((2, 2 * rows + 128, 128), F32), pltpu.VMEM((256, 256), BF),
            pltpu.VMEM((2, rows, width), BF), pltpu.VMEM((4, mem // 4, width), BF),
            pltpu.VMEM((n, 4, 1, own, width), BF),
            pltpu.VMEM((n, 2, half, width), BF), pltpu.VMEM((n, 2, half, width), BF),
            pltpu.VMEM((n, half, width), BF), pltpu.VMEM((n, half, width), BF),
            pltpu.VMEM((4, 5, own, width), BF),
            pltpu.VMEM((2, rows, width), BF), pltpu.VMEM((3, mem // 4, width), BF),
            dma((4,)), dma((n,)), dma((n,)),
            dma((n, 2)), dma((n, 2)), dma((n, 2)), dma((n, 2)),
            dma((n,)), dma((n,)), dma((n,)), dma((n,)),
            dma((n,)), dma((4, 5)),
            dma((2,)), dma((2,)), dma((3,)), dma((3,)),
        ],
        compiler_params=pltpu.CompilerParams(
            collective_id=1, has_side_effects=True, vmem_limit_bytes=VMEM_LIMIT, dimension_semantics=("arbitrary",)
        ),
    )(
        valid_rows, x2, cot, x1, mem_full, h2, h1, tokens, gains, bias_line, seg, pick,
        weights, q2, kv2, o2, q1, kv1, o1, bias,
    )


def stats_kernel(
    wide_count, f_ref, a_ref,
    rsum_ref, csum_ref, asum_ref, pcol_ref,
    rall, aall, call, ball, rs, rr, as_, ar, cs, cr, bs, br, ps, pr,
):
    w = lax.axis_index("wide")
    z = lax.axis_index("narrow")
    own = f_ref.shape[1]
    width = f_ref.shape[2]
    sem = pltpu.get_barrier_semaphore()

    def peer(k):
        return {"narrow": lax.rem(z + k, 4)}

    def wide_peer(k):
        return {"wide": lax.rem(w + k, wide_count)}

    def wide_loop(fn):
        if wide_count <= 8:
            for k in range(1, wide_count):
                fn(k)
        else:
            pl.loop(1, wide_count)(fn)

    for k in (1, 2, 3):
        pl.semaphore_signal(sem, inc=1, device_id=peer(k), device_id_type=MESH)
    wide_loop(lambda k: pl.semaphore_signal(sem, inc=1, device_id=wide_peer(k), device_id_type=MESH))

    lane = lax.broadcasted_iota(jnp.int32, (8, width), 1)
    row = lax.broadcasted_iota(jnp.int32, (8, width), 0)
    quarter = width // 4
    third = 2 * width // 3

    def sums(pick, sq):
        got = lax.dot_general(
            jnp.where(pick, 1.0, 0.0), sq, (((1,), (1,)), ((), ())),
            preferred_element_type=F32, precision=lax.Precision.HIGHEST,
        )
        pad = jnp.zeros((8, 128 - own), F32)
        return jnp.concatenate([got, pad], axis=1)

    sq = [f_ref[i] * f_ref[i] for i in range(4)]
    rall[z, 0:8] = sums(lane // quarter == row, sq[0])
    rall[z, 8:16] = sums(lane // quarter == row, sq[1])
    rall[z, 16:24] = sums(lane // third == row, sq[2]) + sums((lane + width) // third == row, sq[3])
    aall[z] = a_ref[...]
    call[w] = jnp.concatenate(
        [jnp.sum(v, axis=0, keepdims=True) for v in sq], axis=0
    )
    pl.semaphore_wait(sem, 3 + wide_count - 1)

    def r_send(k):
        return remote(rall.at[z], rall.at[z], rs.at[k - 1], rr.at[k - 1], peer(k))

    def a_send(k):
        return remote(aall.at[z], aall.at[z], as_.at[k - 1], ar.at[k - 1], peer(k))

    def c_send(k):
        return remote(call.at[w], call.at[w], cs.at[k - 1], cr.at[k - 1], wide_peer(k))

    def p_send(k):
        return remote(pcol_ref.at[z], pcol_ref.at[z], ps.at[k - 1], pr.at[k - 1], peer(k))

    def b_send(k):
        return remote(ball.at[w], ball.at[w], bs.at[k - 1], br.at[k - 1], wide_peer(k))

    for k in (1, 2, 3):
        r_send(k).start()
        a_send(k).start()
    wide_loop(lambda k: c_send(k).start())

    for k in (1, 2, 3):
        frm = lax.rem(z + 4 - k, 4)
        remote(rall.at[frm], rall.at[frm], rs.at[k - 1], rr.at[k - 1], peer(k)).wait_recv()
        remote(aall.at[frm], aall.at[frm], as_.at[k - 1], ar.at[k - 1], peer(k)).wait_recv()
    rsum = rall[0] + rall[1] + rall[2] + rall[3]
    rsum_ref[...] = rsum
    asum = aall[0] + aall[1] + aall[2] + aall[3]
    zero = jnp.zeros((8, width - 128), F32)
    rows = jnp.concatenate([rsum[0:8], zero], axis=1)
    more = jnp.concatenate([rsum[8:16], zero], axis=1)
    shift = own * w
    ball[w] = jnp.concatenate(
        [asum[0:3], pltpu.roll(rows, shift, 1)[1:2], pltpu.roll(more, shift, 1)[1:2], asum[5:8]], axis=0
    )
    wide_loop(lambda k: b_send(k).start())

    def c_wait(k):
        frm = lax.rem(w + wide_count - k, wide_count)
        remote(call.at[frm], call.at[frm], cs.at[k - 1], cr.at[k - 1], wide_peer(k)).wait_recv()

    wide_loop(c_wait)
    csum = lax.fori_loop(1, wide_count, lambda i, v: v + call[i], call[0])
    csum_ref[...] = csum
    pcol_ref[z] = csum[:, quarter : quarter + 256]
    for k in (1, 2, 3):
        p_send(k).start()

    def b_wait(k):
        frm = lax.rem(w + wide_count - k, wide_count)
        remote(ball.at[frm], ball.at[frm], bs.at[k - 1], br.at[k - 1], wide_peer(k)).wait_recv()

    wide_loop(b_wait)
    asum_ref[...] = lax.fori_loop(1, wide_count, lambda i, v: v + ball[i], ball[0])
    for k in (1, 2, 3):
        frm = lax.rem(z + 4 - k, 4)
        remote(pcol_ref.at[frm], pcol_ref.at[frm], ps.at[k - 1], pr.at[k - 1], peer(k)).wait_recv()
    for k in (1, 2, 3):
        r_send(k).wait_send()
        a_send(k).wait_send()
        p_send(k).wait_send()

    def sent(k):
        c_send(k).wait_send()
        b_send(k).wait_send()

    wide_loop(sent)


def reduce_stats(wide_count, final, small):
    width = final.shape[2]
    vmem = pl.BlockSpec(memory_space=pltpu.VMEM)
    dma = pltpu.SemaphoreType.DMA
    return pl.pallas_call(
        functools.partial(stats_kernel, wide_count),
        name="stats",
        in_specs=[vmem] * 2,
        out_specs=[vmem] * 4,
        out_shape=[
            jax.ShapeDtypeStruct((24, 128), F32),
            jax.ShapeDtypeStruct((4, width), F32),
            jax.ShapeDtypeStruct(small.shape, F32),
            jax.ShapeDtypeStruct((4, 4, 256), F32),
        ],
        scratch_shapes=[
            pltpu.VMEM((4, 24, 128), F32), pltpu.VMEM((4,) + small.shape, F32),
            pltpu.VMEM((wide_count, 4, width), F32), pltpu.VMEM((wide_count,) + small.shape, F32),
            dma((3,)), dma((3,)), dma((3,)), dma((3,)),
            dma((wide_count - 1,)), dma((wide_count - 1,)), dma((wide_count - 1,)), dma((wide_count - 1,)),
            dma((3,)), dma((3,)),
        ],
        compiler_params=pltpu.CompilerParams(collective_id=2, has_side_effects=True),
    )(final, small)


def finish_kernel(
    out_ref, tg_ref, mg_ref, f_ref, rsum_ref, csum_ref, asum_ref, pcol_ref,
    out_o, tg_o, mg_o, gains_o, rel_o, self_o, cross_o, ffn_o, arow_o, acol_o, proj_o, frow_o, fcol_o,
):
    own, width = f_ref.shape[1:]
    hw = self_o.shape[2]
    fw = ffn_o.shape[2]
    out_o[...] = out_ref[...]
    tg_o[...] = tg_ref[...]
    mg_o[...] = mg_ref[...]
    gains_o[...] = asum_ref[0:3, 0:width]
    heads, buckets = rel_o.shape
    per = width // 128
    for h in range(heads):
        row, first = 5 + h // per, 128 * (h % per)
        rel_o[h : h + 1, :] = asum_ref[row : row + 1, first : first + buckets]
    for ref, i in ((self_o, 0), (cross_o, 1)):
        for m, part in enumerate((0, 2, 3, 1)):
            ref[m] = f_ref[i, :, part * hw : (part + 1) * hw]
    cut = width - fw
    ffn_o[0] = f_ref[2, :, 0:fw]
    ffn_o[1, :, 0:cut] = f_ref[2, :, fw:width]
    ffn_o[1, :, cut:fw] = f_ref[3, :, 0 : fw - cut]
    ffn_o[2] = f_ref[3, :, fw - cut : width]
    rsum = rsum_ref[...]
    arow = jnp.concatenate([rsum[0:1], rsum[2:4], rsum[8:9], rsum[10:12]], axis=0)
    arow_o[...] = arow[:, 0:own] * (1.0 / width)
    frow_o[...] = rsum[16:19, 0:own] * (1.0 / (4 * fw))
    scale = 1.0 / width
    for i in range(2):
        for m, part in enumerate((0, 2, 3)):
            acol_o[3 * i + m : 3 * i + m + 1, :] = csum_ref[i : i + 1, part * hw : (part + 1) * hw] * scale
    fcol_o[0:1, :] = csum_ref[2:3, 0:fw] * scale
    fcol_o[1:2, 0:cut] = csum_ref[2:3, fw:width] * scale
    fcol_o[1:2, cut:fw] = csum_ref[3:4, 0 : fw - cut] * scale
    fcol_o[2:3, :] = csum_ref[3:4, fw - cut : width] * scale
    for i in range(2):
        cols = jnp.concatenate([pcol_ref[k, i : i + 1, 0:hw] for k in range(4)], axis=1)
        proj_o[i : i + 1, 0:width] = asum_ref[3 + i : 4 + i, 0:width] * scale
        proj_o[i : i + 1, width : 2 * width] = cols * scale


def finish(shapes, *args):
    vmem = pl.BlockSpec(memory_space=pltpu.VMEM)
    return pl.pallas_call(
        finish_kernel,
        name="finish",
        in_specs=[vmem] * len(args),
        out_specs=[vmem] * len(shapes),
        out_shape=[jax.ShapeDtypeStruct(s, d) for s, d in shapes],
    )(*args)


def local(
    tokens, memory, segments, valid_rows, norm_gains, rel_table,
    self_weights, cross_weights, ffn_weights, cotangent,
):
    wide_count = lax.axis_size("wide")
    assert lax.axis_size("narrow") == 4 and wide_count % 8 == 0 and segments.shape[0] == 1
    rows, width = tokens.shape
    mem_own = memory.shape[1]
    mem_len = 4 * mem_own
    hw = self_weights.shape[2]
    fw = ffn_weights.shape[2]
    heads = rel_table.shape[1]
    groups = wide_count // 8
    eighth = width // 8

    buckets = bucket_table(1024, BUCKETS, MAX_DIST)
    lanes = np.arange(512)
    at_lane = np.where(lanes < 128, 128 + lanes, np.maximum(lanes - 384, 0))
    pick = jnp.asarray((buckets[at_lane][None, :] == np.arange(BUCKETS)[:, None]).astype(np.float32))
    rel_pick = jnp.asarray(
        (buckets[np.maximum(lanes - 127, 0)][:, None] == np.arange(128)[None, :]).astype(np.float32)
    )

    half = width // 16
    weights, bias_line, x1, h1, q1, kv1, o1, bias, mem_full, x2, h2, q2, kv2, o2 = forward(
        valid_rows, tokens, memory[0], norm_gains, rel_table.T, pick, segments,
        jnp.swapaxes(self_weights, 1, 2).reshape(4, 4, hw // 4, width),
        jnp.swapaxes(cross_weights, 1, 2).reshape(4, 4, hw // 4, width),
        ffn_weights.reshape(3, 16, half, fw),
    )
    weights = weights.reshape(4, 4, width, width)
    mem_full = mem_full.reshape(mem_len, width)
    output, final, tokens_grad, memory_grad, small = backward(
        valid_rows, x2, cotangent, x1, mem_full, h2, h1, tokens, norm_gains, bias_line, segments, rel_pick,
        weights, q2, kv2, o2, q1, kv1, o1, bias,
    )
    if groups > 1:
        w = lax.axis_index("wide")
        mine = lax.dynamic_update_slice_in_dim(
            jnp.zeros((4, width, width), F32), final, lax.rem(w, 8) * eighth, 1
        )
        final = lax.psum_scatter(mine, "wide", scatter_dimension=1, tiled=True)
    own = final.shape[1]
    sums = reduce_stats(wide_count, final, small)
    shapes = [
        ((rows, width), BF), ((rows, width), F32), ((mem_own, width), F32), ((3, width), F32), ((heads, BUCKETS), F32),
        ((4, own, hw), F32), ((4, own, hw), F32), ((3, own, fw), F32),
        ((6, own), F32), ((6, hw), F32), ((2, 2 * width), F32), ((3, own), F32), ((3, fw), F32),
    ]
    outs = list(finish(shapes, output, tokens_grad, memory_grad, final, *sums))
    outs[2] = outs[2].reshape(1, mem_own, width)
    outs[4] = outs[4].T
    return tuple(outs)


def solution(mesh):
    in_specs = (
        P(("wide", "narrow"), None),
        P("wide", "narrow", None),
        P("wide", None),
        P("wide"),
        P(),
        P(),
        P(None, None, "narrow"),
        P(None, None, "narrow"),
        P(None, None, "narrow"),
        P(("wide", "narrow"), None),
    )
    out_specs = (
        P(("wide", "narrow"), None),
        P(("wide", "narrow"), None),
        P("wide", "narrow", None),
        P(),
        P(),
        P(None, "wide", "narrow"),
        P(None, "wide", "narrow"),
        P(None, "wide", "narrow"),
        P(None, "wide"),
        P(None, "narrow"),
        P(),
        P(None, "wide"),
        P(None, "narrow"),
    )
    return jax.shard_map(local, mesh=mesh, in_specs=in_specs, out_specs=out_specs, check_vma=False)
```

```python
import functools
import math

import jax
import jax.numpy as jnp
import numpy as np
from jax import lax
from jax.experimental import pallas as pl
from jax.experimental.pallas import tpu as pltpu
from jax.sharding import PartitionSpec as P

BUCKETS = 32
MAX_DIST = 128
EPS = 1e-06
MASKED = -1000000000.0
MESH = pl.DeviceIdType.MESH
BF = jnp.bfloat16
F32 = jnp.float32
VMEM_LIMIT = 64 * 1024 * 1024 - 65536


def bucket_table(seq_length, bucket_count, max_distance):
    exact_count = bucket_count // 2
    bucket_ids = np.zeros((seq_length,), np.int32)
    for distance in range(seq_length):
        if distance < exact_count:
            bucket_ids[distance] = distance
        else:
            scaled_log = (
                math.log(distance / exact_count)
                / math.log(max_distance / exact_count)
                * (bucket_count - exact_count)
            )
            bucket_ids[distance] = min(bucket_count - 1, exact_count + int(scaled_log))
    return bucket_ids


def mm(a, b):
    return jnp.dot(a, b, preferred_element_type=F32)


def mm_nt(a, b):
    return lax.dot_general(a, b, (((1,), (1,)), ((), ())), preferred_element_type=F32)


def mm_tn(a, b):
    return lax.dot_general(a, b, (((0,), (0,)), ((), ())), preferred_element_type=F32)


def inv_rms(v):
    return lax.rsqrt(jnp.mean(v * v, axis=-1, keepdims=True) + EPS)


def norm_back(v, gain, dh):
    r = inv_rms(v)
    gain_part = jnp.sum(dh * (v * r), axis=0, keepdims=True)
    gd = gain * dh
    dv = r * gd - v * (r * r * r) * jnp.mean(gd * v, axis=-1, keepdims=True)
    return gain_part, dv


def soft_cols(scores):
    e = jnp.exp(scores - jnp.max(scores, axis=0, keepdims=True))
    return e * (1.0 / jnp.sum(e, axis=0, keepdims=True))


def self_mask_store(mask_ref, seg_ref, z, rows, span):
    def quarter(k):
        out = jnp.full((1, rows), -1, jnp.int32)
        for kk in range(4):
            out = jnp.where(k == kk, seg_ref[:, kk * rows : (kk + 1) * rows], out)
        return out.astype(F32)

    own = quarter(z)
    keys = jnp.concatenate([quarter(z - 2), quarter(z - 1), own], axis=1)
    keys = jnp.broadcast_to(keys, (128, 3 * rows)).T
    for b in range(2):
        r = lax.broadcasted_iota(jnp.int32, (span, 128), 0)
        c = lax.broadcasted_iota(jnp.int32, (span, 128), 1)
        allowed = (c + 2 * rows >= r) & (keys[b * 128 : b * 128 + span] == own[:, b * 128 : b * 128 + 128])
        mask_ref[b] = jnp.where(allowed, 1.0, 0.0)


def full(shape):
    return pl.BlockSpec(shape, lambda j: (0,) * len(shape))


def once(shape):
    return pl.BlockSpec(shape, lambda j: (0,) * len(shape), pipeline_mode=pl.Buffered(1))


SMEM_SPEC = pl.BlockSpec(memory_space=pltpu.SMEM)


class Place:
    def __init__(self):
        self.w = lax.axis_index("wide")
        self.z = lax.axis_index("narrow")
        s = lax.rem(self.w, 8)
        self.s = s
        self.c = lax.rem(s, 2)
        self.x = lax.rem(s // 2, 2)
        self.y = s // 4
        dc, dx, dy = 1 - 2 * self.c, 2 * (1 - 2 * self.x), 4 * (1 - 2 * self.y)
        self.core_dev = {"wide": self.w + dc}
        self.x_dev = {"wide": self.w + dx}
        self.y_dev = {"wide": self.w + dy}
        self.sx, self.sy, self.sxy = s + dx, s + dy, s + dx + dy
        self.dc = dc

    def quarter(self, k):
        z = self.z
        e0, e3 = 1 - (z + 3) // 4, z // 3
        e1, e2 = (1 - z // 2) * lax.rem(z, 2), (z // 2) * (1 - lax.rem(z, 2))
        return sum(e * row[k] for e, row in zip((e0, e1, e2, e3), RANKS))

    def quarter_of(self, slot):
        return sum(jnp.where(slot == k, self.quarter(k), 0) for k in range(4))

    def narrow_dev(self, k):
        return {"narrow": lax.rem(self.z + k, 4)}

    def devices(self):
        return [self.core_dev, self.x_dev, self.y_dev] + [self.narrow_dev(k) for k in (1, 2, 3)]

    def signal_all(self):
        for dev in self.devices():
            pl.semaphore_signal(pltpu.get_barrier_semaphore(), inc=1, device_id=dev, device_id_type=MESH)

    def wait_all(self):
        pl.semaphore_wait(pltpu.get_barrier_semaphore(), len(self.devices()))

    def barrier(self):
        self.signal_all()
        self.wait_all()


def remote(src, dst, send_sem, recv_sem, dev):
    return pltpu.make_async_remote_copy(
        src_ref=src, dst_ref=dst, send_sem=send_sem, recv_sem=recv_sem, device_id=dev, device_id_type=MESH
    )


RANKS = ((0, 1, 2, 3), (1, 0, 2, 3), (2, 3, 1, 0), (3, 2, 1, 0))
EARLY = 5


def forward_kernel(
    valid_ref, tok_ref, mem_ref, gain_ref, rel_ref, pick_ref, seg_ref, ws_ref, wc_ref, wf_ref,
    w_ref, bd_ref, x1_ref, h1_ref, q_ref, kv_ref, o_ref, bias_ref, mfull_ref, x2_ref, h2_ref, q2_ref, kv2_ref, o2_ref,
    wv, lines, xt, mt, mask_ref, zs, zr, ps, pr, ts, tr, ms, mr, ls, fs, os_,
):
    at = Place()
    z, s = at.z, at.s
    j = pl.program_id(0)
    units = 4
    rows, width = tok_ref.shape
    ext = 3 * rows
    span = 2 * rows + 128
    hw = q_ref.shape[2]
    fw = wf_ref.shape[3]
    heads = hw // 64
    part = rows // 4
    half = width // 16
    mine = pl.ds(2 * s, 2)

    def edge(k):
        return [(d, RANKS[k + d].index(k)) for d in (1, -1) if 0 <= k + d < 4]

    def own_send(u, k, d, rank):
        return remote(
            wv.at[u, 0, mine], wv.at[u, rank, mine], zs.at[u, 0 if d > 0 else 1], zr.at[u, rank], {"narrow": k + d}
        )

    def own_sends(u, act):
        for k in range(4):
            @pl.when(z == k)
            def _():
                for d, rank in edge(k):
                    act(own_send(u, k, d, rank))

    def forwards(u, r, act):
        for k in (1, 2):
            quarter = RANKS[k][r]
            d = 1 if quarter < k else -1
            there = RANKS[k + d].index(quarter)

            @pl.when(z == k)
            def _():
                act(remote(wv.at[u, r, mine], wv.at[u, there, mine], zs.at[u, 1 + r], zr.at[u, there], {"narrow": k + d}))

    def tok_copy(hop, p):
        part_rows = pl.ds(p * part, part)
        src = tok_ref.at[part_rows] if hop == 1 else xt.at[1, part_rows]
        return remote(src, xt.at[2 - hop, part_rows], ts.at[hop - 1, p], tr.at[hop - 1, p], {"narrow": z + 1})

    def tok_senders(hop):
        return z < 3 if hop == 1 else jnp.logical_and(z >= 1, z < 3)

    def tok_send(hop, parts):
        if hop == 2:
            @pl.when(z >= 1)
            def _():
                for p in parts:
                    tok_copy(1, p).wait_recv()

        @pl.when(tok_senders(hop))
        def _():
            for p in parts:
                tok_copy(hop, p).start()

    def mem_copy(i, d):
        k = z - d * i
        src = mem_ref if i == 0 else mt.at[k]
        place = i if d > 0 else 3 + i
        return remote(src, mt.at[k], ms.at[place], mr.at[place], {"narrow": z + d})

    def mem_sends(i, act):
        @pl.when(jnp.logical_and(z >= i, z < 3))
        def _():
            act(mem_copy(i, 1))

        @pl.when(jnp.logical_and(z >= 1, z < 4 - i))
        def _():
            act(mem_copy(i, -1))

    def mem_arrived(i):
        for d in (1, -1):
            @pl.when(z > i if d > 0 else z < 3 - i)
            def _():
                here = mt.at[z - d * (1 + i)]
                place = i if d > 0 else 3 + i
                remote(here, here, ms.at[place], mr.at[place], at.x_dev).wait_recv()

    def piece(u, r, kind):
        first, n, dev = {
            0: (2 * s, 1, at.x_dev), 1: (2 * s + 1, 1, at.x_dev), 2: (2 * at.sy + 1, 1, at.x_dev),
            3: (2 * s + 1, 1, at.y_dev), 4: (2 * s, 1, at.y_dev), 5: (2 * at.sx, 1, at.y_dev),
            6: (2 * s, 2, at.core_dev), 7: (2 * at.sx, 2, at.core_dev),
            8: (2 * at.sy, 2, at.core_dev), 9: (2 * at.sxy, 2, at.core_dev),
        }[kind]
        region = wv.at[u, r, pl.ds(first, n)]
        i = u * 3 + r - 1
        return remote(region, region, ps.at[i, kind], pr.at[i, kind], dev)

    def arrived(u, r, kind):
        first, n = {
            0: (2 * at.sx, 1), 1: (2 * at.sx + 1, 1), 2: (2 * at.sxy + 1, 1),
            3: (2 * at.sy + 1, 1), 4: (2 * at.sy, 1), 5: (2 * at.sxy, 1),
            6: (2 * (s + at.dc), 2), 7: (2 * (at.sx + at.dc), 2),
            8: (2 * (at.sy + at.dc), 2), 9: (2 * (at.sxy + at.dc), 2),
        }[kind]
        region = wv.at[u, r, pl.ds(first, n)]
        i = u * 3 + r - 1
        remote(region, region, ps.at[i, kind], pr.at[i, kind], at.x_dev).wait_recv()

    pieces = [(u, r) for u in range(units) for r in (1, 2, 3)]

    def step0(t):
        if not 0 <= t < len(pieces):
            return
        u, r = pieces[t]
        region = wv.at[u, r, mine]
        remote(region, region, zs.at[u, 0], zr.at[u, r], at.x_dev).wait_recv()
        forwards(u, r, lambda copy: copy.start())
        for kind in (0, 3, 4, 1, 6):
            piece(u, r, kind).start()
        if t == 0:
            tok_send(1, (0, 1))
        if t == 1:
            tok_send(1, (2, 3))
        if t == 2:
            own_sends(2, lambda copy: copy.start())
        if t == 3:
            tok_send(2, (0, 1, 2, 3))
        if t == 4:
            mem_sends(0, lambda copy: copy.start())
        if t == 5:
            own_sends(3, lambda copy: copy.start())
        if t in (6, 8):
            i = (t - 4) // 2
            mem_arrived(i - 1)
            mem_sends(i, lambda copy: copy.start())

    def step1(t):
        if not 0 <= t < len(pieces):
            return
        u, r = pieces[t]
        arrived(u, r, 0)
        piece(u, r, 5).start()
        arrived(u, r, 3)
        piece(u, r, 2).start()
        arrived(u, r, 1)
        piece(u, r, 7).start()
        arrived(u, r, 4)
        piece(u, r, 8).start()

    def step2(t):
        if not 0 <= t < len(pieces):
            return
        u, r = pieces[t]
        arrived(u, r, 5)
        arrived(u, r, 2)
        piece(u, r, 9).start()

    def keep(u, k):
        return pltpu.make_async_copy(wv.at[u, k], w_ref.at[u, k], os_.at[u, k])

    def step3(t):
        if not 0 <= t < len(pieces):
            return
        u, r = pieces[t]
        for kind in (6, 7, 8, 9):
            arrived(u, r, kind)
        keep(u, r).start()

    def attn_loads(i):
        src = (ws_ref, wc_ref)[i]
        return [
            pltpu.make_async_copy(src.at[part], wv.at[i, 0, pl.ds(4 * k, 4)], ls.at[i, k])
            for k, part in enumerate((0, 3, 1, 2))
        ]

    def ffn_loads():
        cut = width - fw
        return [
            pltpu.make_async_copy(wf_ref.at[0], wv.at[2, 0, :, :, 0:fw], fs.at[0]),
            pltpu.make_async_copy(wf_ref.at[1, :, :, 0:cut], wv.at[2, 0, :, :, fw:width], fs.at[1]),
            pltpu.make_async_copy(wf_ref.at[1, :, :, cut:fw], wv.at[3, 0, :, :, 0 : fw - cut], fs.at[2]),
            pltpu.make_async_copy(wf_ref.at[2], wv.at[3, 0, :, :, fw - cut : width], fs.at[3]),
        ]

    @pl.when(j == 0)
    def _():
        at.signal_all()
        for copy in attn_loads(0) + attn_loads(1) + ffn_loads():
            copy.start()
        at.wait_all()
        for copy in attn_loads(0):
            copy.wait()
        own_sends(0, lambda copy: copy.start())
        for copy in attn_loads(1):
            copy.wait()
        own_sends(1, lambda copy: copy.start())
        for copy in ffn_loads():
            copy.wait()
        for u in range(units):
            keep(u, 0).start()
        x = tok_ref[...].astype(F32)
        x1_ref[...] = x
        h1_ref[2 * rows : ext, :] = (x * inv_rms(x) * gain_ref[0:1, :]).astype(BF)
        self_mask_store(mask_ref, seg_ref, z, rows, span)
        lines[...] = lax.dot_general(
            rel_ref[...], pick_ref[...], (((1,), (0,)), ((), ())),
            preferred_element_type=F32, precision=lax.Precision.HIGHEST,
        )
        for k in range(4):
            first = at.quarter(k) * heads
            for hh in range(heads):
                bd_ref[k, hh : hh + 1, :] = lines[pl.ds(first + hh, 1), :]
        for t in range(EARLY):
            step0(t)
            step1(t - 1)
            step2(t - 2)
            step3(t - 3)

        @pl.when(z >= 2)
        def _():
            for p in range(4):
                tok_copy(2, p).wait_recv()

        for t in range(2):
            v = jnp.where(z >= 2 - t, xt[t].astype(F32), 0.0)
            h1_ref[t * rows : (t + 1) * rows, :] = (v * inv_rms(v) * gain_ref[0:1, :]).astype(BF)

    def hook(i, first, last):
        for jj in range(first, last):
            t = EARLY + jj

            @pl.when(j == jj)
            def _():
                if i == 0:
                    step3(t - 3)
                    step0(t)
                if i == 1:
                    step1(t - 1)
                if i == 2:
                    step2(t - 2)

    def flat(u, k, lo, hi):
        return wv[u, k, lo // half : hi // half].reshape(hi - lo, width)

    @pl.when(j < 4)
    def _():
        hook(0, 0, 4)
        q = mm_nt(h1_ref[2 * rows : ext, :], flat(0, j, 0, hw)).astype(BF)
        kv = mm_nt(h1_ref[...], flat(0, j, 2 * hw, 4 * hw)).astype(BF)
        q_ref[0] = q
        kv_ref[0] = kv
        parts = []
        for hh in range(heads):
            line = jnp.broadcast_to(bd_ref[j, hh : hh + 1, :], (256, 512))
            bias = pltpu.roll(line, 0, 1, stride=1, stride_axis=0)[:, 0:128]
            bias_ref[0, hh] = bias
            far = bd_ref[j, hh : hh + 1, 127:128]
            cols = []
            for b in range(2):
                k = kv[b * 128 : b * 128 + span, hh * 64 : hh * 64 + 64]
                v = kv[b * 128 : b * 128 + span, hw + hh * 64 : hw + hh * 64 + 64]
                qb = q[b * 128 : b * 128 + 128, hh * 64 : hh * 64 + 64]
                sc = mm_nt(k, qb)
                sc = jnp.concatenate([sc[: span - 256] + far, sc[span - 256 :] + bias], axis=0)
                sc = jnp.where(mask_ref[b] > 0.5, sc, MASKED)
                cols.append(mm_tn(v, soft_cols(sc).astype(BF)))
            parts.append(jnp.concatenate(cols, axis=1))
            if hh < 2:
                hook(1 + hh, 0, 4)
        o = jnp.concatenate(parts, axis=0).T.astype(BF)
        o_ref[0] = o
        x1_ref[...] += mm(o, flat(0, j, hw, 2 * hw))

    @pl.when(j == 4)
    def _():
        x1 = x1_ref[...]
        x2_ref[...] = x1
        h2_ref[...] = (x1 * inv_rms(x1) * gain_ref[1:2, :]).astype(BF)
        mfull_ref[z] = mem_ref[...]
        mem_arrived(2)
        for k in range(4):
            @pl.when(z != k)
            def _():
                mfull_ref[k] = mt[k]

    @pl.when(j >= 4)
    def _():
        hook(0, 4, 8)
        mem = mfull_ref.shape[0] * mfull_ref.shape[1]
        q = mm_nt(h2_ref[...], flat(1, j - 4, 0, hw)).astype(BF)
        kv = mm_nt(mfull_ref[...].reshape(mem, width), flat(1, j - 4, 2 * hw, 4 * hw)).astype(BF)
        q2_ref[0] = q
        kv2_ref[0] = kv
        allowed = lax.broadcasted_iota(jnp.int32, (mem, rows), 0) < valid_ref[0]
        parts = []
        for hh in range(heads):
            k = kv[:, hh * 64 : hh * 64 + 64]
            v = kv[:, hw + hh * 64 : hw + hh * 64 + 64]
            sc = jnp.where(allowed, mm_nt(k, q[:, hh * 64 : hh * 64 + 64]), MASKED)
            parts.append(mm_tn(v, soft_cols(sc).astype(BF)))
            if hh < 2:
                hook(1 + hh, 4, 8)
        o = jnp.concatenate(parts, axis=0).T.astype(BF)
        o2_ref[0] = o
        x2_ref[...] += mm(o, flat(1, j - 4, hw, 2 * hw))

    @pl.when(j == 7)
    def _():
        for t in range(EARLY + 8, len(pieces) + 3):
            step0(t)
            step1(t - 1)
            step2(t - 2)
            step3(t - 3)
        for u, r in pieces:
            for kind in range(10):
                piece(u, r, kind).wait_send()
            forwards(u, r, lambda copy: copy.wait_send())
        for u in range(units):
            own_sends(u, lambda copy: copy.wait_send())
            for k in range(4):
                keep(u, k).wait()
        for hop in (1, 2):
            @pl.when(tok_senders(hop))
            def _():
                for p in range(4):
                    tok_copy(hop, p).wait_send()
        for i in range(3):
            mem_sends(i, lambda copy: copy.wait_send())


def forward(valid_rows, tokens, memory, gains, rel, pick, seg, ws, wc, wf):
    rows, width = tokens.shape
    mem_own = memory.shape[0]
    hw = 4 * ws.shape[2]
    heads = hw // 64
    ext = 3 * rows
    mem = 4 * mem_own
    half = width // 16
    any_spec = pl.BlockSpec(memory_space=pl.ANY)
    dma = pltpu.SemaphoreType.DMA

    def early(shape):
        return pl.BlockSpec((1,) + shape, lambda j: (jnp.minimum(j, 3),) + (0,) * len(shape))

    def late(shape):
        return pl.BlockSpec((1,) + shape, lambda j: (jnp.maximum(j - 4, 0),) + (0,) * len(shape))

    out = [
        ((4, 4, 16, half, width), BF, any_spec), ((4, heads, 512), F32, full((4, heads, 512))),
        ((rows, width), F32, full((rows, width))), ((ext, width), BF, full((ext, width))),
        ((4, rows, hw), BF, early((rows, hw))), ((4, ext, 2 * hw), BF, early((ext, 2 * hw))),
        ((4, rows, hw), BF, early((rows, hw))), ((4, heads, 256, 128), F32, early((heads, 256, 128))),
        ((4, mem_own, width), BF, full((4, mem_own, width))),
        ((rows, width), F32, full((rows, width))), ((rows, width), BF, full((rows, width))),
        ((4, rows, hw), BF, late((rows, hw))), ((4, mem, 2 * hw), BF, late((mem, 2 * hw))),
        ((4, rows, hw), BF, late((rows, hw))),
    ]
    return pl.pallas_call(
        forward_kernel,
        name="forward",
        grid=(8,),
        in_specs=[
            SMEM_SPEC, full((rows, width)), full((mem_own, width)), full((3, width)),
            full(rel.shape), full(pick.shape), full(seg.shape), any_spec, any_spec, any_spec,
        ],
        out_specs=[spec for _, _, spec in out],
        out_shape=[jax.ShapeDtypeStruct(shape, dtype) for shape, dtype, _ in out],
        scratch_shapes=[
            pltpu.VMEM((4, 4, 16, half, width), BF), pltpu.VMEM((4 * heads, 512), F32),
            pltpu.VMEM((2, rows, width), BF), pltpu.VMEM((4, mem_own, width), BF),
            pltpu.VMEM((2, 2 * rows + 128, 128), F32),
            dma((4, 5)), dma((4, 4)), dma((12, 10)), dma((12, 10)),
            dma((2, 4)), dma((2, 4)), dma((6,)), dma((6,)), dma((2, 4)), dma((4,)), dma((4, 4)),
        ],
        compiler_params=pltpu.CompilerParams(
            collective_id=0, has_side_effects=True, vmem_limit_bytes=VMEM_LIMIT, dimension_semantics=("arbitrary",)
        ),
    )(valid_rows, tokens, memory, gains, rel, pick, seg, ws, wc, wf)


CHUNKS = [(2 + i % 2, i // 2) for i in range(8)] + [(1, i) for i in range(4)] + [(0, i) for i in range(4)]
HELD = 12
LAG = 3
TICKS = [(1, 0), (2, 0), (3, 0), (4, 1), (5, 1), (6, 1), (7, 1), (8, 0), (8, 2), (9, 1), (10, 0), (10, 2), (11, 1)]


def backward_kernel(
    valid_ref, x2_ref, cot_ref, x1_ref, mem_ref, h2_ref, h1_ref, tok_ref, gain_ref, bd_ref, seg_ref, pick_ref,
    w_ref, q2_ref, kv2_ref, o2_ref, q1_ref, kv1_ref, o1_ref, bias_ref,
    out_ref, f_ref, tg_ref, mg_ref, small_ref,
    g, wbuf, acc, act_in, res, gsum_ref, rel_ref, do_ref, dqt_ref, dkv_ref, mask_ref, flip_ref, dxo, dmo, rc, xr, yr, xr2, yr2, zb, dxr, dmr,
    wsem, cs, cr, xs, xrs, ys, yrs, x2s, x2r, y2s, y2r, zs, zr, dxs, dxrs, dms, dmrs,
):
    at = Place()
    z = at.z
    j = pl.program_id(0)
    rows, width = x2_ref.shape
    mem = mem_ref.shape[0]
    ext = 3 * rows
    span = 2 * rows + 128
    hw = q1_ref.shape[2]
    heads = hw // 64
    fw = wbuf.shape[2] * 2 // 3
    own_rows = g.shape[3]
    half = own_rows // 2
    n = len(CHUNKS)
    lo, hi = pl.ds(0, half), pl.ds(half, half)
    yx = 2 * at.y + at.x
    top, bottom = pl.ds(0, rows), pl.ds(2 * rows, rows)

    def w_load(unit, slot, k):
        return pltpu.make_async_copy(w_ref.at[unit, slot], wbuf.at[k], wsem.at[k])

    def held(i):
        return g.at[i % HELD]

    def add(ref, other):
        ref[...] = ref[...] + other[...]

    def core_send(i):
        return remote(held(i).at[:, pl.ds(1 - at.c, 1)], rc.at[i], cs.at[i], cr.at[i], at.core_dev)

    def x_send(i, yb):
        src = held(i).at[2 * yb + 1 - at.x, at.c, lo]
        return remote(src, xr.at[i, yb], xs.at[i, yb], xrs.at[i, yb], at.x_dev)

    def y_send(i, xb):
        src = held(i).at[2 * (1 - at.y) + xb, at.c, hi]
        return remote(src, yr.at[i, xb], ys.at[i, xb], yrs.at[i, xb], at.y_dev)

    def y2_send(i):
        return remote(held(i).at[2 * (1 - at.y) + at.x, at.c, lo], yr2.at[i], y2s.at[i], y2r.at[i], at.y_dev)

    def x2_send(i):
        return remote(held(i).at[2 * at.y + 1 - at.x, at.c, hi], xr2.at[i], x2s.at[i], x2r.at[i], at.x_dev)

    d = 1 - 2 * (z // 2)
    is_end = jnp.logical_or(z == 0, z == 3)
    is_inner = jnp.logical_or(z == 1, z == 2)

    def z_send(i, dst, step):
        unit = CHUNKS[i][0]
        return remote(held(i).at[yx, at.c], zb.at[unit, dst], zs.at[i], zr.at[unit, dst], {"narrow": z + step})

    def z_wait(i, k):
        unit = CHUNKS[i][0]
        remote(zb.at[unit, k], zb.at[unit, k], zs.at[i], zr.at[unit, k], at.x_dev).wait_recv()

    def step_b(i):
        core_send(i).wait_recv()
        add(held(i).at[:, pl.ds(at.c, 1)], rc.at[i])
        for b in range(2):
            x_send(i, b).start()
            y_send(i, b).start()

    def step_c(i):
        for b in range(2):
            x_send(i, b).wait_recv()
            y_send(i, b).wait_recv()
            add(held(i).at[2 * b + at.x, at.c, lo], xr.at[i, b])
            add(held(i).at[2 * at.y + b, at.c, hi], yr.at[i, b])
        y2_send(i).start()
        x2_send(i).start()

    def step_d(i):
        y2_send(i).wait_recv()
        add(held(i).at[yx, at.c, lo], yr2.at[i])
        x2_send(i).wait_recv()
        add(held(i).at[yx, at.c, hi], xr2.at[i])

    def step_e(i):
        @pl.when(is_end)
        def _():
            if CHUNKS[i][1] < 3:
                z_send(i, CHUNKS[i][1], d).start()

    def step_f(i):
        unit, s = CHUNKS[i]

        @pl.when(is_inner)
        def _():
            if s < 2:
                z_wait(i, s)
                add(held(i).at[yx, at.c], zb.at[unit, s])
                z_send(i, 3 + s, d).start()
            if s == 2:
                z_wait(i, 3)
                add(held(i).at[yx, at.c], zb.at[unit, 3])
                z_send(i, 2, -d).start()
            if s == 3:
                z_wait(i, 2)
                z_wait(i, 4)
                f_ref[unit] = (
                    held(i)[yx, at.c].astype(F32) + zb[unit, 2].astype(F32) + zb[unit, 4].astype(F32)
                )

        if s == 3:
            @pl.when(is_end)
            def _():
                z_wait(i, 2)
                f_ref[unit] = held(i)[yx, at.c].astype(F32) + zb[unit, 2].astype(F32)

    def sent(i):
        core_send(i).wait_send()
        for b in range(2):
            x_send(i, b).wait_send()
            y_send(i, b).wait_send()
        y2_send(i).wait_send()
        x2_send(i).wait_send()
        if CHUNKS[i][1] < 3:
            z_send(i, 0, d).wait_send()

    def tick(t):
        for k, step in ((0, step_b), (1, step_c), (2, step_d), (2, step_e), (LAG, step_f)):
            if 0 <= t - k < n:
                step(t - k)

    def hook(place, first, last):
        for t, (jj, p) in enumerate(TICKS):
            if p == place and first <= jj < last:
                @pl.when(j == jj)
                def _():
                    tick(t)

    def dx_send(t):
        return remote(dxo.at[t], dxr.at[t], dxs.at[t], dxrs.at[t], {"narrow": z - 1})

    def dm_send(k):
        return remote(dmo.at[lax.rem(z + k, 4)], dmr.at[k - 1], dms.at[k - 1], dmrs.at[k - 1], at.narrow_dev(k))

    @pl.when(j == 0)
    def _():
        for b in range(2):
            w_load(2 + b, 3, b).start()
        at.signal_all()
        x2 = x2_ref[...]
        acc[0:rows, :] = x2
        acc[rows : 2 * rows, :] = jnp.zeros((rows, width), F32)
        act_in[...] = (x2 * inv_rms(x2) * gain_ref[2:3, :]).astype(BF)

    @pl.when(j < 4)
    def _():
        k = 2 * lax.rem(j, 2)
        for b in range(2):
            w_load(2 + b, 3 - j, k + b).wait()

        @pl.when(j < 3)
        def _():
            for b in range(2):
                w_load(2 + b, 2 - j, 2 - k + b).start()

        @pl.when(j == 3)
        def _():
            w_load(1, 3, 0).start()

        @pl.when(j == 0)
        def _():
            at.wait_all()

        hook(0, 0, 4)
        h3 = act_in[...]
        df = cot_ref[...]
        wg = wbuf[k, :, 0:fw]
        wu = jnp.concatenate([wbuf[k, :, fw:], wbuf[k + 1, :, 0 : fw // 2]], axis=1)
        wd = wbuf[k + 1, :, fw // 2 :]
        gate = mm(h3, wg)
        up = mm(h3, wu)
        c0 = math.sqrt(2.0 / math.pi)
        gate2 = gate * gate
        t = jnp.tanh(c0 * (gate + 0.044715 * gate2 * gate))
        part = 0.5 * (1.0 + t)
        gelu = gate * part
        slope = part + 0.5 * gate * (1.0 - t * t) * (c0 * (1.0 + 3.0 * 0.044715 * gate2))
        act = (gelu * up).astype(BF)
        acc[0:rows, :] += mm_nt(act, wd)
        da = mm(df, wd)
        dgate = (da * up * slope).astype(BF)
        dup = (da * gelu).astype(BF)
        dgu = jnp.concatenate([dgate, dup], axis=1)
        ggu = mm_tn(h3, dgu).astype(BF)
        blocks = (4, 2, own_rows)
        g[2 * j] = ggu[:, 0 : fw * 3 // 2].reshape(blocks + (width,))
        g[2 * j + 1, :, :, :, 0 : fw // 2] = ggu[:, fw * 3 // 2 :].reshape(blocks + (fw // 2,))
        g[2 * j + 1, :, :, :, fw // 2 :] = mm_tn(df, act).astype(BF).reshape(blocks + (fw,))
        acc[rows : 2 * rows, :] += mm_nt(dgate, wg) + mm_nt(dup, wu)
        for jj in range(4):
            @pl.when(j == jj)
            def _():
                core_send(2 * jj).start()
                core_send(2 * jj + 1).start()

    @pl.when(j == 3)
    def _():
        out_ref[...] = acc[0:rows, :].astype(BF)
        gain_part, dv = norm_back(x2_ref[...], gain_ref[2:3, :], acc[rows : 2 * rows, :])
        gsum_ref[16:24, :] = jnp.broadcast_to(gain_part, (8, width))
        g2 = cot_ref[...].astype(F32) + dv
        res[...] = g2
        act_in[...] = g2.astype(BF)
        acc[...] = jnp.zeros_like(acc)

    @pl.when(jnp.logical_and(j >= 4, j < 8))
    def _():
        k0 = j - 4
        w_load(1, 7 - j, k0).wait()

        @pl.when(j < 7)
        def _():
            w_load(1, 6 - j, k0 + 1).start()

        @pl.when(j == 7)
        def _():
            w_load(0, 3, 0).start()

        do_ref[...] = mm_nt(act_in[...], wbuf[k0, hw : 2 * hw, :]).astype(BF)
        for hh in range(heads):
            h_cols, v_cols = slice(hh * 64, hh * 64 + 64), slice(hw + hh * 64, hw + hh * 64 + 64)
            k = kv2_ref[0, :, h_cols]
            v = kv2_ref[0, :, v_cols]
            qh = q2_ref[0, :, h_cols]
            doh = do_ref[:, h_cols]
            allowed = lax.broadcasted_iota(jnp.int32, (mem, rows), 0) < valid_ref[0]
            p = soft_cols(jnp.where(allowed, mm_nt(k, qh), MASKED))
            dp = mm_nt(v, doh)
            ds = (p * (dp - jnp.sum(p * dp, axis=0, keepdims=True))).astype(BF)
            dkv_ref[0:mem, v_cols] = mm(p.astype(BF), doh).astype(BF)
            dkv_ref[0:mem, h_cols] = mm(ds, qh).astype(BF)
            dqt_ref[h_cols, :] = mm_tn(k, ds)
            hook(hh, 4, 8)
        dc = act_in[...]
        dq = dqt_ref[...].T.astype(BF)
        dkv = dkv_ref[0:mem, :]
        zero = jnp.zeros((rows, hw), BF)
        left = jnp.concatenate([h2_ref[...], dc], axis=0)
        right = jnp.concatenate(
            [jnp.concatenate([dq, zero], axis=1), jnp.concatenate([zero, o2_ref[0]], axis=1)], axis=0
        )
        blocks = (4, 2, own_rows, 2 * hw)
        g[4 + j, :, :, :, 0 : 2 * hw] = mm_tn(left, right).astype(BF).reshape(blocks)
        g[4 + j, :, :, :, 2 * hw : 4 * hw] = mm_tn(mem_ref[...], dkv).astype(BF).reshape(blocks)
        for jj in range(4, 8):
            @pl.when(j == jj)
            def _():
                core_send(4 + jj).start()
        acc[0:rows, :] += mm(dq, wbuf[k0, 0:hw, :])
        acc[rows : rows + mem, :] += mm(dkv, wbuf[k0, 2 * hw : 4 * hw, :])

    @pl.when(j == 7)
    def _():
        for k in range(4):
            dmo[k] = acc[rows + k * (mem // 4) : rows + (k + 1) * (mem // 4), :].astype(BF)
        for k in (1, 2, 3):
            dm_send(k).start()
        gain_part, dv = norm_back(x1_ref[...], gain_ref[1:2, :], acc[0:rows, :])
        gsum_ref[8:16, :] = jnp.broadcast_to(gain_part, (8, width))
        g1 = res[...] + dv
        res[...] = g1
        act_in[...] = g1.astype(BF)
        acc[...] = jnp.zeros_like(acc)
        self_mask_store(mask_ref, seg_ref, z, rows, span)
        rel_ref[...] = jnp.zeros_like(rel_ref)
        r = lax.broadcasted_iota(jnp.int32, (256, 256), 0)
        c = lax.broadcasted_iota(jnp.int32, (256, 256), 1)
        flip_ref[...] = jnp.where(r + c == 255, 1.0, 0.0).astype(BF)

    @pl.when(j >= 8)
    def _():
        k0 = j - 8
        w_load(0, 11 - j, k0).wait()

        @pl.when(j < 11)
        def _():
            w_load(0, 10 - j, k0 + 1).start()

        do_ref[...] = mm_nt(act_in[...], wbuf[k0, hw : 2 * hw, :]).astype(BF)
        for hh in range(heads):
            h_cols, v_cols = slice(hh * 64, hh * 64 + 64), slice(hw + hh * 64, hw + hh * 64 + 64)
            far = bd_ref[11 - j, hh : hh + 1, 127:128]
            dq_cols, dks, dvs = [], [], []
            band = jnp.zeros((256, 128), F32)
            total = jnp.zeros((1, 128), F32)
            for b in range(2):
                k = kv1_ref[0, b * 128 : b * 128 + span, h_cols]
                v = kv1_ref[0, b * 128 : b * 128 + span, v_cols]
                qb = q1_ref[0, b * 128 : b * 128 + 128, h_cols]
                dob = do_ref[b * 128 : b * 128 + 128, h_cols]
                s = mm_nt(k, qb)
                s = jnp.concatenate([s[: span - 256] + far, s[span - 256 :] + bias_ref[0, hh]], axis=0)
                s = jnp.where(mask_ref[b] > 0.5, s, MASKED)
                p = soft_cols(s)
                dp = mm_nt(v, dob)
                ds = (p * (dp - jnp.sum(p * dp, axis=0, keepdims=True))).astype(BF)
                dvs.append(mm(p.astype(BF), dob))
                dks.append(mm(ds, qb))
                dq_cols.append(mm_tn(k, ds))
                band = band + mm(flip_ref[...], ds[span - 256 :])
                total = total + jnp.sum(ds[: span - 256].astype(F32), axis=0, keepdims=True)
            gap = jnp.zeros((128, 64), F32)
            dk = jnp.concatenate([dks[0], gap], 0) + jnp.concatenate([gap, dks[1]], 0)
            dv = jnp.concatenate([dvs[0], gap], 0) + jnp.concatenate([gap, dvs[1]], 0)
            dkv_ref[:, h_cols] = dk.astype(BF)
            dkv_ref[:, v_cols] = dv.astype(BF)
            dqt_ref[h_cols, :] = jnp.concatenate(dq_cols, axis=1)
            wide_band = jnp.concatenate([band, jnp.zeros((256, 384), F32)], axis=1)
            aligned = pltpu.roll(wide_band, 0, 1, stride=1, stride_axis=0)
            line = jnp.sum(aligned, axis=0, keepdims=True)
            lane = lax.broadcasted_iota(jnp.int32, (1, 512), 1)
            far_sum = jnp.sum(total, axis=1, keepdims=True)
            rel_ref[pl.ds(at.quarter_of(11 - j) * heads + hh, 1), :] = jnp.where(lane == 511, far_sum, line)
            hook(hh, 8, 12)
        da = act_in[...]
        dq = dqt_ref[...].T.astype(BF)
        dkv = dkv_ref[...]
        zero = jnp.zeros((rows, hw), BF)
        left = jnp.concatenate([h1_ref[2 * rows : ext, :], da], axis=0)
        right = jnp.concatenate(
            [jnp.concatenate([dq, zero], axis=1), jnp.concatenate([zero, o1_ref[0]], axis=1)], axis=0
        )
        for jj in range(8, 12):
            @pl.when(j == jj)
            def _():
                sent(jj - 8)
        blocks = (4, 2, own_rows, 2 * hw)
        g[j - 8, :, :, :, 0 : 2 * hw] = mm_tn(left, right).astype(BF).reshape(blocks)
        g[j - 8, :, :, :, 2 * hw : 4 * hw] = mm_tn(h1_ref[...], dkv).astype(BF).reshape(blocks)
        for jj in range(8, 12):
            @pl.when(j == jj)
            def _():
                core_send(4 + jj).start()
        acc[...] += mm(dkv, wbuf[k0, 2 * hw : 4 * hw, :])
        acc[2 * rows : ext, :] += mm(dq, wbuf[k0, 0:hw, :])

    @pl.when(j == 11)
    def _():
        for t in range(2):
            dxo[t] = acc[t * rows : (t + 1) * rows, :].astype(BF)

        @pl.when(z >= 2)
        def _():
            dx_send(0).start()

        @pl.when(z == 3)
        def _():
            dx_send(1).start()
        last = n + LAG
        for t in range(len(TICKS), last):
            tick(t)
            if t == len(TICKS):
                mg_ref[...] = dmo[z].astype(F32)
                for k in (1, 2, 3):
                    dm_send(k).wait_recv()
                    mg_ref[...] += dmr[k - 1].astype(F32)
            if t == len(TICKS) + 1:
                @pl.when(is_inner)
                def _():
                    dx_send(0).wait_recv()
                    add(dxo.at[1], dxr.at[0])
                    dx_send(1).start()
            if t == len(TICKS) + 3:
                @pl.when(z < 3)
                def _():
                    dx_send(1).wait_recv()
                    acc[2 * rows : ext, :] += dxr[1].astype(F32)
                gain_part, dv = norm_back(tok_ref[...].astype(F32), gain_ref[0:1, :], acc[2 * rows : ext, :])
                rel = lax.dot_general(
                    rel_ref[...], pick_ref[...], (((1,), (0,)), ((), ())),
                    preferred_element_type=F32, precision=lax.Precision.HIGHEST,
                )
                gains = [gain_part, gsum_ref[8:9, :], gsum_ref[16:17, :], jnp.zeros((2, width), F32)]
                per = width // 128
                lines = [
                    jnp.concatenate([rel[per * k + h : per * k + h + 1] for h in range(per)], axis=1)
                    for k in range(2)
                ]
                small_ref[...] = jnp.concatenate(gains + lines + [jnp.zeros((1, width), F32)], axis=0)
                tg_ref[...] = res[...] + dv
        for i in range(n - HELD, n):
            sent(i)
        for t in range(2):
            @pl.when(z >= 2 - t)
            def _():
                dx_send(t).wait_send()
        for k in (1, 2, 3):
            dm_send(k).wait_send()


def backward(
    valid_rows, x2, cot, x1, mem_full, h2, h1, tokens, gains, bias_line, seg, pick,
    weights, q2, kv2, o2, q1, kv1, o1, bias,
):
    rows, width = x2.shape
    mem = mem_full.shape[0]
    hw = q1.shape[2]
    ext = 3 * rows
    own = width // 8
    half = own // 2
    n = len(CHUNKS)
    dma = pltpu.SemaphoreType.DMA

    def slot(last, a):
        shape = a.shape[1:]
        return pl.BlockSpec(
            (1,) + shape, lambda j: (jnp.clip(last - j, 0, 3),) + (0,) * len(shape)
        )

    out = [
        ((rows, width), BF), ((4, own, width), F32), ((rows, width), F32), ((mem // 4, width), F32),
        ((8, width), F32),
    ]
    shapes = [jax.ShapeDtypeStruct(s, d) for s, d in out]
    return pl.pallas_call(
        backward_kernel,
        name="backward",
        grid=(12,),
        in_specs=[
            SMEM_SPEC, *[once(a.shape) for a in (x2, cot, x1, mem_full, h2, h1, tokens)],
            full(gains.shape), full(bias_line.shape), full(seg.shape), full(pick.shape),
            pl.BlockSpec(memory_space=pl.ANY),
            slot(7, q2), slot(7, kv2), slot(7, o2), slot(11, q1), slot(11, kv1), slot(11, o1), slot(11, bias),
        ],
        out_specs=[once(s) for s, _ in out],
        out_shape=shapes,
        scratch_shapes=[
            pltpu.VMEM((HELD, 4, 2, own, width), BF), pltpu.VMEM((4, width, width), BF),
            pltpu.VMEM((ext, width), F32), pltpu.VMEM((rows, width), BF), pltpu.VMEM((rows, width), F32),
            pltpu.VMEM((24, width), F32), pltpu.VMEM((16, 512), F32),
            pltpu.VMEM((rows, hw), BF), pltpu.VMEM((hw, rows), F32), pltpu.VMEM((ext, 2 * hw), BF),
            pltpu.VMEM((2, 2 * rows + 128, 128), F32), pltpu.VMEM((256, 256), BF),
            pltpu.VMEM((2, rows, width), BF), pltpu.VMEM((4, mem // 4, width), BF),
            pltpu.VMEM((n, 4, 1, own, width), BF),
            pltpu.VMEM((n, 2, half, width), BF), pltpu.VMEM((n, 2, half, width), BF),
            pltpu.VMEM((n, half, width), BF), pltpu.VMEM((n, half, width), BF),
            pltpu.VMEM((4, 5, own, width), BF),
            pltpu.VMEM((2, rows, width), BF), pltpu.VMEM((3, mem // 4, width), BF),
            dma((4,)), dma((n,)), dma((n,)),
            dma((n, 2)), dma((n, 2)), dma((n, 2)), dma((n, 2)),
            dma((n,)), dma((n,)), dma((n,)), dma((n,)),
            dma((n,)), dma((4, 5)),
            dma((2,)), dma((2,)), dma((3,)), dma((3,)),
        ],
        compiler_params=pltpu.CompilerParams(
            collective_id=1, has_side_effects=True, vmem_limit_bytes=VMEM_LIMIT, dimension_semantics=("arbitrary",)
        ),
    )(
        valid_rows, x2, cot, x1, mem_full, h2, h1, tokens, gains, bias_line, seg, pick,
        weights, q2, kv2, o2, q1, kv1, o1, bias,
    )


def stats_kernel(
    wide_count, f_ref, a_ref,
    rsum_ref, csum_ref, asum_ref, pcol_ref,
    rall, aall, call, ball, rs, rr, as_, ar, cs, cr, bs, br, ps, pr,
):
    w = lax.axis_index("wide")
    z = lax.axis_index("narrow")
    own = f_ref.shape[1]
    width = f_ref.shape[2]
    sem = pltpu.get_barrier_semaphore()

    def peer(k):
        return {"narrow": lax.rem(z + k, 4)}

    def wide_peer(k):
        return {"wide": lax.rem(w + k, wide_count)}

    def wide_loop(fn):
        if wide_count <= 8:
            for k in range(1, wide_count):
                fn(k)
        else:
            pl.loop(1, wide_count)(fn)

    for k in (1, 2, 3):
        pl.semaphore_signal(sem, inc=1, device_id=peer(k), device_id_type=MESH)
    wide_loop(lambda k: pl.semaphore_signal(sem, inc=1, device_id=wide_peer(k), device_id_type=MESH))

    lane = lax.broadcasted_iota(jnp.int32, (8, width), 1)
    row = lax.broadcasted_iota(jnp.int32, (8, width), 0)
    quarter = width // 4
    third = 2 * width // 3

    def sums(pick, sq):
        got = lax.dot_general(
            jnp.where(pick, 1.0, 0.0), sq, (((1,), (1,)), ((), ())),
            preferred_element_type=F32, precision=lax.Precision.HIGHEST,
        )
        pad = jnp.zeros((8, 128 - own), F32)
        return jnp.concatenate([got, pad], axis=1)

    sq = [f_ref[i] * f_ref[i] for i in range(4)]
    rall[z, 0:8] = sums(lane // quarter == row, sq[0])
    rall[z, 8:16] = sums(lane // quarter == row, sq[1])
    rall[z, 16:24] = sums(lane // third == row, sq[2]) + sums((lane + width) // third == row, sq[3])
    aall[z] = a_ref[...]
    call[w] = jnp.concatenate(
        [jnp.sum(v, axis=0, keepdims=True) for v in sq], axis=0
    )
    pl.semaphore_wait(sem, 3 + wide_count - 1)

    def r_send(k):
        return remote(rall.at[z], rall.at[z], rs.at[k - 1], rr.at[k - 1], peer(k))

    def a_send(k):
        return remote(aall.at[z], aall.at[z], as_.at[k - 1], ar.at[k - 1], peer(k))

    def c_send(k):
        return remote(call.at[w], call.at[w], cs.at[k - 1], cr.at[k - 1], wide_peer(k))

    def p_send(k):
        return remote(pcol_ref.at[z], pcol_ref.at[z], ps.at[k - 1], pr.at[k - 1], peer(k))

    def b_send(k):
        return remote(ball.at[w], ball.at[w], bs.at[k - 1], br.at[k - 1], wide_peer(k))

    for k in (1, 2, 3):
        r_send(k).start()
        a_send(k).start()
    wide_loop(lambda k: c_send(k).start())

    for k in (1, 2, 3):
        frm = lax.rem(z + 4 - k, 4)
        remote(rall.at[frm], rall.at[frm], rs.at[k - 1], rr.at[k - 1], peer(k)).wait_recv()
        remote(aall.at[frm], aall.at[frm], as_.at[k - 1], ar.at[k - 1], peer(k)).wait_recv()
    rsum = rall[0] + rall[1] + rall[2] + rall[3]
    rsum_ref[...] = rsum
    asum = aall[0] + aall[1] + aall[2] + aall[3]
    zero = jnp.zeros((8, width - 128), F32)
    rows = jnp.concatenate([rsum[0:8], zero], axis=1)
    more = jnp.concatenate([rsum[8:16], zero], axis=1)
    shift = own * w
    ball[w] = jnp.concatenate(
        [asum[0:3], pltpu.roll(rows, shift, 1)[1:2], pltpu.roll(more, shift, 1)[1:2], asum[5:8]], axis=0
    )
    wide_loop(lambda k: b_send(k).start())

    def c_wait(k):
        frm = lax.rem(w + wide_count - k, wide_count)
        remote(call.at[frm], call.at[frm], cs.at[k - 1], cr.at[k - 1], wide_peer(k)).wait_recv()

    wide_loop(c_wait)
    csum = lax.fori_loop(1, wide_count, lambda i, v: v + call[i], call[0])
    csum_ref[...] = csum
    pcol_ref[z] = csum[:, quarter : quarter + 256]
    for k in (1, 2, 3):
        p_send(k).start()

    def b_wait(k):
        frm = lax.rem(w + wide_count - k, wide_count)
        remote(ball.at[frm], ball.at[frm], bs.at[k - 1], br.at[k - 1], wide_peer(k)).wait_recv()

    wide_loop(b_wait)
    asum_ref[...] = lax.fori_loop(1, wide_count, lambda i, v: v + ball[i], ball[0])
    for k in (1, 2, 3):
        frm = lax.rem(z + 4 - k, 4)
        remote(pcol_ref.at[frm], pcol_ref.at[frm], ps.at[k - 1], pr.at[k - 1], peer(k)).wait_recv()
    for k in (1, 2, 3):
        r_send(k).wait_send()
        a_send(k).wait_send()
        p_send(k).wait_send()

    def sent(k):
        c_send(k).wait_send()
        b_send(k).wait_send()

    wide_loop(sent)


def reduce_stats(wide_count, final, small):
    width = final.shape[2]
    vmem = pl.BlockSpec(memory_space=pltpu.VMEM)
    dma = pltpu.SemaphoreType.DMA
    return pl.pallas_call(
        functools.partial(stats_kernel, wide_count),
        name="stats",
        in_specs=[vmem] * 2,
        out_specs=[vmem] * 4,
        out_shape=[
            jax.ShapeDtypeStruct((24, 128), F32),
            jax.ShapeDtypeStruct((4, width), F32),
            jax.ShapeDtypeStruct(small.shape, F32),
            jax.ShapeDtypeStruct((4, 4, 256), F32),
        ],
        scratch_shapes=[
            pltpu.VMEM((4, 24, 128), F32), pltpu.VMEM((4,) + small.shape, F32),
            pltpu.VMEM((wide_count, 4, width), F32), pltpu.VMEM((wide_count,) + small.shape, F32),
            dma((3,)), dma((3,)), dma((3,)), dma((3,)),
            dma((wide_count - 1,)), dma((wide_count - 1,)), dma((wide_count - 1,)), dma((wide_count - 1,)),
            dma((3,)), dma((3,)),
        ],
        compiler_params=pltpu.CompilerParams(collective_id=2, has_side_effects=True),
    )(final, small)


def finish_kernel(
    out_ref, tg_ref, mg_ref, f_ref, rsum_ref, csum_ref, asum_ref, pcol_ref,
    out_o, tg_o, mg_o, gains_o, rel_o, self_o, cross_o, ffn_o, arow_o, acol_o, proj_o, frow_o, fcol_o,
):
    own, width = f_ref.shape[1:]
    hw = self_o.shape[2]
    fw = ffn_o.shape[2]
    out_o[...] = out_ref[...]
    tg_o[...] = tg_ref[...]
    mg_o[...] = mg_ref[...]
    gains_o[...] = asum_ref[0:3, 0:width]
    heads, buckets = rel_o.shape
    per = width // 128
    for h in range(heads):
        row, first = 5 + h // per, 128 * (h % per)
        rel_o[h : h + 1, :] = asum_ref[row : row + 1, first : first + buckets]
    for ref, i in ((self_o, 0), (cross_o, 1)):
        for m, part in enumerate((0, 2, 3, 1)):
            ref[m] = f_ref[i, :, part * hw : (part + 1) * hw]
    cut = width - fw
    ffn_o[0] = f_ref[2, :, 0:fw]
    ffn_o[1, :, 0:cut] = f_ref[2, :, fw:width]
    ffn_o[1, :, cut:fw] = f_ref[3, :, 0 : fw - cut]
    ffn_o[2] = f_ref[3, :, fw - cut : width]
    rsum = rsum_ref[...]
    arow = jnp.concatenate([rsum[0:1], rsum[2:4], rsum[8:9], rsum[10:12]], axis=0)
    arow_o[...] = arow[:, 0:own] * (1.0 / width)
    frow_o[...] = rsum[16:19, 0:own] * (1.0 / (4 * fw))
    scale = 1.0 / width
    for i in range(2):
        for m, part in enumerate((0, 2, 3)):
            acol_o[3 * i + m : 3 * i + m + 1, :] = csum_ref[i : i + 1, part * hw : (part + 1) * hw] * scale
    fcol_o[0:1, :] = csum_ref[2:3, 0:fw] * scale
    fcol_o[1:2, 0:cut] = csum_ref[2:3, fw:width] * scale
    fcol_o[1:2, cut:fw] = csum_ref[3:4, 0 : fw - cut] * scale
    fcol_o[2:3, :] = csum_ref[3:4, fw - cut : width] * scale
    for i in range(2):
        cols = jnp.concatenate([pcol_ref[k, i : i + 1, 0:hw] for k in range(4)], axis=1)
        proj_o[i : i + 1, 0:width] = asum_ref[3 + i : 4 + i, 0:width] * scale
        proj_o[i : i + 1, width : 2 * width] = cols * scale


def finish(shapes, *args):
    vmem = pl.BlockSpec(memory_space=pltpu.VMEM)
    return pl.pallas_call(
        finish_kernel,
        name="finish",
        in_specs=[vmem] * len(args),
        out_specs=[vmem] * len(shapes),
        out_shape=[jax.ShapeDtypeStruct(s, d) for s, d in shapes],
    )(*args)


def local(
    tokens, memory, segments, valid_rows, norm_gains, rel_table,
    self_weights, cross_weights, ffn_weights, cotangent,
):
    wide_count = lax.axis_size("wide")
    assert lax.axis_size("narrow") == 4 and wide_count % 8 == 0 and segments.shape[0] == 1
    rows, width = tokens.shape
    mem_own = memory.shape[1]
    mem_len = 4 * mem_own
    hw = self_weights.shape[2]
    fw = ffn_weights.shape[2]
    heads = rel_table.shape[1]
    groups = wide_count // 8
    eighth = width // 8

    buckets = bucket_table(1024, BUCKETS, MAX_DIST)
    lanes = np.arange(512)
    at_lane = np.where(lanes < 128, 128 + lanes, np.maximum(lanes - 384, 0))
    pick = jnp.asarray((buckets[at_lane][None, :] == np.arange(BUCKETS)[:, None]).astype(np.float32))
    rel_pick = jnp.asarray(
        (buckets[np.maximum(lanes - 127, 0)][:, None] == np.arange(128)[None, :]).astype(np.float32)
    )

    half = width // 16
    weights, bias_line, x1, h1, q1, kv1, o1, bias, mem_full, x2, h2, q2, kv2, o2 = forward(
        valid_rows, tokens, memory[0], norm_gains, rel_table.T, pick, segments,
        jnp.swapaxes(self_weights, 1, 2).reshape(4, 4, hw // 4, width),
        jnp.swapaxes(cross_weights, 1, 2).reshape(4, 4, hw // 4, width),
        ffn_weights.reshape(3, 16, half, fw),
    )
    weights = weights.reshape(4, 4, width, width)
    mem_full = mem_full.reshape(mem_len, width)
    output, final, tokens_grad, memory_grad, small = backward(
        valid_rows, x2, cotangent, x1, mem_full, h2, h1, tokens, norm_gains, bias_line, segments, rel_pick,
        weights, q2, kv2, o2, q1, kv1, o1, bias,
    )
    if groups > 1:
        w = lax.axis_index("wide")
        mine = lax.dynamic_update_slice_in_dim(
            jnp.zeros((4, width, width), F32), final, lax.rem(w, 8) * eighth, 1
        )
        final = lax.psum_scatter(mine, "wide", scatter_dimension=1, tiled=True)
    own = final.shape[1]
    sums = reduce_stats(wide_count, final, small)
    shapes = [
        ((rows, width), BF), ((rows, width), F32), ((mem_own, width), F32), ((3, width), F32), ((heads, BUCKETS), F32),
        ((4, own, hw), F32), ((4, own, hw), F32), ((3, own, fw), F32),
        ((6, own), F32), ((6, hw), F32), ((2, 2 * width), F32), ((3, own), F32), ((3, fw), F32),
    ]
    outs = list(finish(shapes, output, tokens_grad, memory_grad, final, *sums))
    outs[2] = outs[2].reshape(1, mem_own, width)
    outs[4] = outs[4].T
    return tuple(outs)


def solution(mesh):
    in_specs = (
        P(("wide", "narrow"), None),
        P("wide", "narrow", None),
        P("wide", None),
        P("wide"),
        P(),
        P(),
        P(None, None, "narrow"),
        P(None, None, "narrow"),
        P(None, None, "narrow"),
        P(("wide", "narrow"), None),
    )
    out_specs = (
        P(("wide", "narrow"), None),
        P(("wide", "narrow"), None),
        P("wide", "narrow", None),
        P(),
        P(),
        P(None, "wide", "narrow"),
        P(None, "wide", "narrow"),
        P(None, "wide", "narrow"),
        P(None, "wide"),
        P(None, "narrow"),
        P(),
        P(None, "wide"),
        P(None, "narrow"),
    )
    return jax.shard_map(local, mesh=mesh, in_specs=in_specs, out_specs=out_specs, check_vma=False)
```
